32 devices in a mesh: dp: 8 (over y, x, core), mp: 4 (over z).
Axes of the slice: x: 2, y: 2, z: 4, core: 2. Of those that a mesh axis runs over, the one named last changes fastest.
Arguments:
- latents: bfloat16 [8, 1023, 1536], P('dp'), may hold values from -6 to 6
- prompt_tokens: bfloat16 [8, 128, 768], P('dp'), may hold values from -6 to 6
- prompt_lengths: int32 [8], P('dp'), may hold values from 4 to 128, as said below
- timesteps: int32 [8], P('dp'), may hold values from 0 to 999
- time_weight: bfloat16 [256, 1536], P('dp'), may hold values from -0.5 to 0.5
- self_gain: float32 [1536], replicated, may hold values from 0.5 to 1.5
- self_bias: float32 [1536], replicated, may hold values from -1.75 to 1.75
- qkv_weight: bfloat16 [1536, 3, 1536], P('dp', None, 'mp'), may hold values from -0.15625 to 0.15625
- self_out_weight: bfloat16 [1536, 1536], P('mp', 'dp'), may hold values from -1.5 to 1.5
- cross_gain: float32 [1536], replicated, may hold values from 0.5 to 1.5
- cross_bias: float32 [1536], replicated, may hold values from -1.75 to 1.75
- cross_query_weight: bfloat16 [1536, 1536], P('dp', 'mp'), may hold values from -0.15625 to 0.15625
- context_weight: bfloat16 [768, 2, 1536], P('dp', None, 'mp'), may hold values from -0.21875 to 0.21875
- cross_out_weight: bfloat16 [1536, 1536], P('mp', 'dp'), may hold values from -0.75 to 0.75
- feed_gain: float32 [1536], replicated, may hold values from 0.5 to 1.5
- feed_bias: float32 [1536], replicated, may hold values from -1.75 to 1.75
- gate_up_weight: bfloat16 [1536, 2, 6144], P('dp', None, 'mp'), may hold values from -0.15625 to 0.15625
- down_weight: bfloat16 [6144, 1536], P('mp', 'dp'), may hold values from -0.109375 to 0.109375
- down_bias: float32 [1536], replicated, may hold values from -1.75 to 1.75
- cotangent: bfloat16 [8, 1024, 1536], P('dp', 'mp'), may hold values from -6 to 6
Outputs:
- output: bfloat16 [8, 1024, 1536], P('dp', 'mp')
- latents_grad: bfloat16 [8, 1023, 1536], P('dp')
- time_weight_grad: float32 [256, 1536], P('dp')
- self_gain_grad: float32 [1536], P('dp')
- self_bias_grad: float32 [1536], P('dp')
- qkv_weight_grad: float32 [1536, 3, 1536], P('dp', None, 'mp')
- self_out_grad: float32 [1536, 1536], P('mp', 'dp')
- cross_gain_grad: float32 [1536], P('dp')
- cross_bias_grad: float32 [1536], P('dp')
- cross_query_grad: float32 [1536, 1536], P('dp', 'mp')
- context_weight_grad: float32 [768, 2, 1536], P('dp', None, 'mp')
- cross_out_grad: float32 [1536, 1536], P('mp', 'dp')
- feed_gain_grad: float32 [1536], P('dp')
- feed_bias_grad: float32 [1536], P('dp')
- gate_up_grad: float32 [1536, 2, 6144], P('dp', None, 'mp')
- down_weight_grad: float32 [6144, 1536], P('mp', 'dp')
- down_bias_grad: float32 [1536], P('dp')
The draws below stay inside these ranges and needn't reach their ends.
Inputs may be any that keep to these rules, and one draw needn't show every extreme that they name: `prompt_lengths`: short prompts are far commoner than long ones; some item of every draw has all 128 tokens.
All inputs are finite; a program needn't handle non-finite values.
Results may differ from the reference program's by a relative error of at most 0.025.
Values may be sent and summed in bfloat16 or wider, within the bound.
A program may use at most 192 MiB of HBM per device.

```python
import math
import jax
import jax.numpy as jnp
from jax import lax

D = 1536
HEADS = 24
HD = 64
FF = 6144
CTX = 768
TFEAT = 256
PROMPT = 128
SEQ = 1024
FRAMES = 1023
ITEMS = 8


def draw_prompt_lengths(key, part):
    streams = jax.random.split(key, 4)
    first_draw = jax.random.randint(streams[0], (ITEMS,), 4, PROMPT + 1)
    second_draw = jax.random.randint(streams[1], (ITEMS,), 4, PROMPT + 1)
    third_draw = jax.random.randint(streams[2], (ITEMS,), 4, PROMPT + 1)
    shortest = jnp.minimum(jnp.minimum(first_draw, second_draw), third_draw)
    chosen = jax.random.randint(streams[3], (), 0, ITEMS)
    return jnp.where(jnp.arange(ITEMS) == chosen, PROMPT, shortest).astype(jnp.int32)


def with_ends(entries, stream_key, low, top_value):
    longest = entries.shape.index(max(entries.shape))
    spots = []
    for shift in (0, 1):
        where = [jax.random.randint(jax.random.fold_in(stream_key, axis), (), 0, length) for axis, length in enumerate(entries.shape)]
        where[longest] = (where[longest] + shift) % entries.shape[longest]
        spots.append(tuple(where))
    return entries.at[spots[0]].set(low).at[spots[1]].set(top_value)


def levels(stream_key, extent, cuts, low, top_value):
    loudness = 1.0
    for dim, shards_of in cuts:
        draws = jax.random.uniform(jax.random.fold_in(jax.random.fold_in(stream_key, 6), dim), (shards_of,), jnp.float32, low / len(cuts), top_value / len(cuts))
        loudness = loudness * jnp.repeat(jnp.exp(draws), extent[dim] // shards_of).reshape((-1,) + (1,) * (len(extent) - 1 - dim))
    return loudness


def scatter_about(stream_key, dims, width, reach, cuts=(), kind=jnp.bfloat16):
    level = levels(stream_key, dims, cuts, -0.22, 0.18) if cuts else 1.0
    values = jax.random.normal(stream_key, dims, jnp.float32) * width * level
    return jnp.minimum(jnp.maximum(values, -reach), reach).astype(kind)


def setup_inputs(seed: int = 0) -> dict:
    splits = jax.random.split(jax.random.key(seed), 21)
    latents = scatter_about(splits[0], (ITEMS, FRAMES, D), 1.0, 6.0, ((0, 8),))
    prompt_tokens = scatter_about(splits[1], (ITEMS, PROMPT, CTX), 1.0, 6.0, ((0, 8),))
    prompt_lengths = draw_prompt_lengths(jax.random.fold_in(splits[20], 71), 0)
    timesteps = with_ends(jax.random.randint(splits[3], (ITEMS,), 0, 1000), jax.random.fold_in(splits[3], 1), 0, 999).astype(jnp.int32)
    time_weight = scatter_about(splits[4], (TFEAT, D), (TFEAT // 2) ** -0.5, 0.5, ((0, 8),))
    self_gain = jnp.clip(1.0 + 0.1 * jax.random.normal(splits[5], (D,), jnp.float32), 0.5, 1.5)
    self_bias = scatter_about(splits[6], (D,), 0.3, 1.75, (), jnp.float32)
    qkv_weight = scatter_about(splits[7], (D, 3, HEADS * HD), D ** -0.5, 0.15625, ((0, 8), (2, 4)))
    self_out_weight = scatter_about(splits[8], (HEADS * HD, D), (HD // 4) ** -0.5, 1.5, ((0, 4), (1, 8)))
    cross_gain = jnp.clip(1.0 + 0.1 * jax.random.normal(splits[9], (D,), jnp.float32), 0.5, 1.5)
    cross_bias = scatter_about(splits[10], (D,), 0.3, 1.75, (), jnp.float32)
    cross_query_weight = scatter_about(splits[11], (D, HEADS * HD), D ** -0.5, 0.15625, ((0, 8), (1, 4)))
    context_weight = scatter_about(splits[12], (CTX, 2, HEADS * HD), CTX ** -0.5, 0.21875, ((0, 8), (2, 4)))
    cross_out_weight = scatter_about(splits[13], (HEADS * HD, D), HD ** -0.5, 0.75, ((0, 4), (1, 8)))
    feed_gain = jnp.clip(1.0 + 0.1 * jax.random.normal(splits[14], (D,), jnp.float32), 0.5, 1.5)
    feed_bias = scatter_about(splits[15], (D,), 0.3, 1.75, (), jnp.float32)
    gate_up_weight = scatter_about(splits[16], (D, 2, FF), D ** -0.5, 0.15625, ((0, 8), (2, 4)))
    down_weight = scatter_about(splits[17], (FF, D), (FF // 2) ** -0.5, 0.109375, ((0, 4), (1, 8)))
    down_bias = scatter_about(splits[18], (D,), 0.3, 1.75, (), jnp.float32)
    cotangent = scatter_about(splits[19], (ITEMS, SEQ, D), 1.0, 6.0, ((0, 8), (1, 4)))
    return dict(latents=latents, prompt_tokens=prompt_tokens, prompt_lengths=prompt_lengths, timesteps=timesteps, time_weight=time_weight, self_gain=self_gain, self_bias=self_bias, qkv_weight=qkv_weight, self_out_weight=self_out_weight, cross_gain=cross_gain, cross_bias=cross_bias, cross_query_weight=cross_query_weight, context_weight=context_weight, cross_out_weight=cross_out_weight, feed_gain=feed_gain, feed_bias=feed_bias, gate_up_weight=gate_up_weight, down_weight=down_weight, down_bias=down_bias, cotangent=cotangent)


EPS = 1e-05
NEG = -1e+30
HIGH = lax.Precision.HIGHEST

@jax.custom_vjp
def low(v):
    return lax.optimization_barrier(v.astype(jnp.bfloat16)).astype(jnp.float32)

@jax.custom_vjp
def low_back(v):
    return v

def low_keep(v):
    return (low(v), None)

def low_pass(kept, grad):
    return (grad,)

def back_keep(v):
    return (v, None)

def back_low(kept, grad):
    return (low(grad),)
low.defvjp(low_keep, low_pass)
low_back.defvjp(back_keep, back_low)

def time_features(steps_in):
    half_width = TFEAT // 2
    freqs = jnp.exp(-math.log(10000.0) * jnp.arange(half_width, dtype=jnp.float32) / half_width)
    angles = steps_in.astype(jnp.float32)[:, None] * freqs[None, :]
    return jnp.concatenate([jnp.cos(angles), jnp.sin(angles)], axis=-1)

def rope_tables():
    rotated_width = HD // 2
    half_width = rotated_width // 2
    inverse = jnp.exp(-math.log(10000.0) * jnp.arange(half_width, dtype=jnp.float32) * 2.0 / rotated_width)
    angles = jnp.arange(SEQ, dtype=jnp.float32)[:, None] * inverse[None, :]
    cosine = jnp.concatenate([jnp.cos(angles), jnp.cos(angles)], axis=-1)
    sine = jnp.concatenate([jnp.sin(angles), jnp.sin(angles)], axis=-1)
    return (cosine[:, None, :], sine[:, None, :])

def rotate(values, cosine, sine):
    rotated_width = cosine.shape[-1]
    half_width = rotated_width // 2
    first = values[..., :rotated_width]
    turned = jnp.concatenate([-first[..., half_width:], first[..., :half_width]], axis=-1)
    return jnp.concatenate([first * cosine + turned * sine, values[..., rotated_width:]], axis=-1)

def layer_norm(values, gain, bias):
    centered = values - lax.optimization_barrier(jnp.mean(values, axis=-1, keepdims=True))
    variance = lax.optimization_barrier(jnp.mean(centered * centered, axis=-1, keepdims=True))
    return centered * lax.rsqrt(variance + EPS) * gain + bias

def attend_one(operands):
    queries, key_rows, value_rows, bias_row = operands
    scores = low_back(jnp.einsum('qhe,khe->hqk', queries, key_rows, precision=HIGH) * HD ** (-0.5))
    scores = scores + bias_row[None, None, :]
    weights_p = low(jax.nn.softmax(scores, axis=-1))
    return jnp.einsum('hqk,khe->qhe', weights_p, value_rows, precision=HIGH)

def attend(queries, key_rows, value_rows, bias_rows):
    return lax.map(jax.checkpoint(attend_one), (queries, key_rows, value_rows, bias_rows))

def forward(latents_in, prompt_in, features, mask_rows, time_weight, self_gain, self_bias, qkv_weight, self_out_weight, cross_gain, cross_bias, cross_query_weight, context_weight, cross_out_weight, feed_gain, feed_bias, gate_up_weight, down_weight, down_bias):
    cosine, sine = rope_tables()
    token_row = jnp.dot(low(features), time_weight, precision=HIGH)
    residual_in = jnp.concatenate([token_row[:, None, :], latents_in], axis=1)
    normed_one = low(layer_norm(residual_in, self_gain, self_bias))
    projected = low_back(jnp.einsum('bsd,dkc->bskc', normed_one, qkv_weight, precision=HIGH))
    head_shape = (ITEMS, SEQ, HEADS, HD)
    queries = low(rotate(projected[:, :, 0].reshape(head_shape), cosine, sine))
    key_rows = low(rotate(projected[:, :, 1].reshape(head_shape), cosine, sine))
    value_rows = low(projected[:, :, 2].reshape(head_shape))
    open_rows = jnp.zeros((ITEMS, SEQ), jnp.float32)
    attended = attend(queries, key_rows, value_rows, open_rows).reshape(ITEMS, SEQ, HEADS * HD)
    attended = low(low_back(attended))
    residual_one = low_back(residual_in + jnp.einsum('bsh,hd->bsd', attended, self_out_weight, precision=HIGH))
    normed_two = low(layer_norm(residual_one, cross_gain, cross_bias))
    cross_q = low(low_back(jnp.einsum('bsd,dh->bsh', normed_two, cross_query_weight, precision=HIGH))).reshape(head_shape)
    context = low(low_back(jnp.einsum('bpc,ckh->bpkh', prompt_in, context_weight, precision=HIGH)))
    context_shape = (ITEMS, PROMPT, HEADS, HD)
    crossed = attend(cross_q, context[:, :, 0].reshape(context_shape), context[:, :, 1].reshape(context_shape), mask_rows)
    crossed = low(low_back(crossed.reshape(ITEMS, SEQ, HEADS * HD)))
    residual_two = low_back(residual_one + jnp.einsum('bsh,hd->bsd', crossed, cross_out_weight, precision=HIGH))
    normed_three = low(layer_norm(residual_two, feed_gain, feed_bias))
    gate_up = low_back(jnp.einsum('bsd,dkf->bskf', normed_three, gate_up_weight, precision=HIGH))
    hidden = low(jax.nn.silu(gate_up[:, :, 0]) * gate_up[:, :, 1])
    return residual_two + jnp.einsum('bsf,fd->bsd', hidden, down_weight, precision=HIGH) + down_bias

def reference(latents, prompt_tokens, prompt_lengths, timesteps, time_weight, self_gain, self_bias, qkv_weight, self_out_weight, cross_gain, cross_bias, cross_query_weight, context_weight, cross_out_weight, feed_gain, feed_bias, gate_up_weight, down_weight, down_bias, cotangent):
    features = time_features(timesteps)
    slots = jnp.arange(PROMPT, dtype=jnp.int32)
    mask_rows = jnp.where(slots[None, :] < prompt_lengths.astype(jnp.int32)[:, None], 0.0, NEG).astype(jnp.float32)
    prompt_in = prompt_tokens.astype(jnp.float32)
    params = (latents.astype(jnp.float32), time_weight.astype(jnp.float32), self_gain.astype(jnp.float32), self_bias.astype(jnp.float32), qkv_weight.astype(jnp.float32), self_out_weight.astype(jnp.float32), cross_gain.astype(jnp.float32), cross_bias.astype(jnp.float32), cross_query_weight.astype(jnp.float32), context_weight.astype(jnp.float32), cross_out_weight.astype(jnp.float32), feed_gain.astype(jnp.float32), feed_bias.astype(jnp.float32), gate_up_weight.astype(jnp.float32), down_weight.astype(jnp.float32), down_bias.astype(jnp.float32))

    def closed(*values):
        return forward(values[0], prompt_in, features, mask_rows, *values[1:])
    result, pull = jax.vjp(closed, *params)
    grads = pull(cotangent.astype(jnp.float32))
    return (result.astype(jnp.bfloat16), grads[0].astype(jnp.bfloat16), grads[1], grads[2], grads[3], grads[4], grads[5], grads[6], grads[7], grads[8], grads[9], grads[10], grads[11], grads[12], grads[13], grads[14], grads[15])
```

```python
import functools
import math

import jax
import jax.numpy as jnp
from jax import lax
from jax.experimental import pallas as pl
from jax.experimental.pallas import tpu as pltpu
from jax.sharding import PartitionSpec as P

HD = 64


EPS = 1e-05
NEG = -1e30


def time_features(steps_in, feature_width):
    half_width = feature_width // 2
    freqs = jnp.exp(-math.log(10000.0) * jnp.arange(half_width, dtype=jnp.float32) / half_width)
    angles = steps_in.astype(jnp.float32)[:, None] * freqs[None, :]
    return jnp.concatenate([jnp.cos(angles), jnp.sin(angles)], axis=-1)


def rope_tables(length, head_size):
    rotated_width = head_size // 2
    half_width = rotated_width // 2
    inverse = jnp.exp(
        -math.log(10000.0) * jnp.arange(half_width, dtype=jnp.float32) * 2.0 / rotated_width
    )
    angles = jnp.arange(length, dtype=jnp.float32)[:, None] * inverse[None, :]
    cosine = jnp.concatenate([jnp.cos(angles), jnp.cos(angles)], axis=-1)
    sine = jnp.concatenate([jnp.sin(angles), jnp.sin(angles)], axis=-1)
    return (cosine[:, None, :], sine[:, None, :])


def rotate(values, cosine, sine):
    rotated_width = cosine.shape[-1]
    half_width = rotated_width // 2
    first = values[..., :rotated_width]
    turned = jnp.concatenate([-first[..., half_width:], first[..., :half_width]], axis=-1)
    return jnp.concatenate([first * cosine + turned * sine, values[..., rotated_width:]], axis=-1)


def unrotate(grads_in, cosine, sine):
    rotated_width = cosine.shape[-1]
    half_width = rotated_width // 2
    first = grads_in[..., :rotated_width]
    scaled_in = first * sine
    turned = jnp.concatenate([scaled_in[..., half_width:], -scaled_in[..., :half_width]], axis=-1)
    return jnp.concatenate([first * cosine + turned, grads_in[..., rotated_width:]], axis=-1)


def layer_norm(values, gain, bias):
    centered = values - jnp.mean(values, axis=-1, keepdims=True)
    inverse = lax.rsqrt(jnp.mean(centered * centered, axis=-1, keepdims=True) + EPS)
    scaled = centered * inverse
    return (scaled * gain + bias, scaled, inverse)


def norm_back(grad_normed, scaled, inverse, gain):
    grad_scaled = grad_normed * gain
    first_mean = jnp.mean(grad_scaled, axis=-1, keepdims=True)
    second_mean = jnp.mean(grad_scaled * scaled, axis=-1, keepdims=True)
    grad_values = inverse * (grad_scaled - first_mean - scaled * second_mean)
    return (
        grad_values,
        jnp.sum(grad_normed * scaled, axis=(0, 1)),
        jnp.sum(grad_normed, axis=(0, 1)),
    )


def attend_forward(queries, key_rows, value_rows, bias_rows, block_size):
    score_scale = queries.shape[-1] ** (-0.5)

    def one_item(operands):
        item_query, item_key, item_value, item_bias = operands
        query_blocks = item_query.reshape(-1, block_size, item_query.shape[1], item_query.shape[2])

        def one_block(block_query):
            scores = jnp.einsum(
                "qhe,khe->hqk", block_query, item_key, preferred_element_type=jnp.float32
            )
            scores = scores * score_scale + item_bias[None, None, :]
            row_max = jnp.max(scores, axis=-1, keepdims=True)
            expos = jnp.exp(scores - row_max)
            row_total = jnp.sum(expos, axis=-1, keepdims=True)
            weights_p = (expos / row_total).astype(jnp.bfloat16)
            mixed = jnp.einsum(
                "hqk,khe->qhe", weights_p, item_value, preferred_element_type=jnp.float32
            )
            return (mixed, (row_max + jnp.log(row_total))[..., 0])

        mixed, log_total = lax.map(one_block, query_blocks)
        return (mixed.reshape(item_query.shape), log_total)

    return lax.map(one_item, (queries, key_rows, value_rows, bias_rows))


def attend_backward(queries, key_rows, value_rows, bias_rows, log_totals, grad_out, block_size):
    score_scale = queries.shape[-1] ** (-0.5)

    def one_item(operands):
        item_query, item_key, item_value, item_bias, item_log, item_grad = operands
        block_shape = (-1, block_size, item_query.shape[1], item_query.shape[2])
        query_blocks = item_query.reshape(block_shape)
        grad_blocks = item_grad.reshape(block_shape)

        def one_block(carry, operands_block):
            block_query, block_log, block_grad = operands_block
            scores = jnp.einsum(
                "qhe,khe->hqk", block_query, item_key, preferred_element_type=jnp.float32
            )
            scores = scores * score_scale + item_bias[None, None, :]
            probs_full = jnp.exp(scores - block_log[..., None])
            grad_probs = jnp.einsum(
                "qhe,khe->hqk", block_grad, item_value, preferred_element_type=jnp.float32
            )
            delta_row = jnp.sum(probs_full * grad_probs, axis=-1, keepdims=True)
            grad_scores = (probs_full * (grad_probs - delta_row)).astype(jnp.bfloat16)
            grad_query = (
                jnp.einsum(
                    "hqk,khe->qhe", grad_scores, item_key, preferred_element_type=jnp.float32
                )
                * score_scale
            )
            grad_key = (
                carry[0]
                + jnp.einsum(
                    "hqk,qhe->khe", grad_scores, block_query, preferred_element_type=jnp.float32
                )
                * score_scale
            )
            grad_value = carry[1] + jnp.einsum(
                "hqk,qhe->khe",
                probs_full.astype(jnp.bfloat16),
                block_grad,
                preferred_element_type=jnp.float32,
            )
            return ((grad_key, grad_value), grad_query)

        start_carry = (
            jnp.zeros(item_key.shape, jnp.float32),
            jnp.zeros(item_value.shape, jnp.float32),
        )
        (grad_key, grad_value), grad_query = lax.scan(
            one_block, start_carry, (query_blocks, item_log, grad_blocks)
        )
        return (grad_query.reshape(item_query.shape), grad_key, grad_value)

    return lax.map(one_item, (queries, key_rows, value_rows, bias_rows, log_totals, grad_out))


def per_device_general(
    latents,
    prompt_tokens,
    prompt_lengths,
    timesteps,
    time_weight,
    self_gain,
    self_bias,
    qkv_weight,
    self_out_weight,
    cross_gain,
    cross_bias,
    cross_query_weight,
    context_weight,
    cross_out_weight,
    feed_gain,
    feed_bias,
    gate_up_weight,
    down_weight,
    down_bias,
    cotangent,
):
    gathered = (
        lax.all_gather(time_weight, "dp", axis=0, tiled=True),
        lax.all_gather(qkv_weight, "dp", axis=0, tiled=True),
        lax.all_gather(self_out_weight, "dp", axis=1, tiled=True),
        lax.all_gather(cross_query_weight, "dp", axis=0, tiled=True),
        lax.all_gather(context_weight, "dp", axis=0, tiled=True),
        lax.all_gather(cross_out_weight, "dp", axis=1, tiled=True),
        lax.all_gather(gate_up_weight, "dp", axis=0, tiled=True),
        lax.all_gather(down_weight, "dp", axis=1, tiled=True),
    )
    (
        time_full,
        qkv_full,
        self_out_full,
        cross_query_full,
        context_full,
        cross_out_full,
        gate_up_full,
        down_full,
    ) = gathered
    items_here = latents.shape[0]
    seq_len = latents.shape[1] + 1
    shard_rows = seq_len // lax.axis_size("mp")
    first_row = lax.axis_index("mp") * shard_rows
    head_size = HD
    block_size = min(512, seq_len)
    features = time_features(timesteps, time_full.shape[0]).astype(jnp.bfloat16)
    token_row = jnp.dot(features, time_full, preferred_element_type=jnp.float32)
    residual_in = jnp.concatenate([token_row[:, None, :], latents.astype(jnp.float32)], axis=1)
    normed_one, scaled_one, inverse_one = layer_norm(residual_in, self_gain, self_bias)
    normed_one = normed_one.astype(jnp.bfloat16)
    projected = jnp.einsum(
        "bsd,dkc->bskc", normed_one, qkv_full, preferred_element_type=jnp.float32
    )
    heads_here = projected.shape[-1] // head_size
    head_shape = (items_here, seq_len, heads_here, head_size)
    cosine, sine = rope_tables(seq_len, head_size)
    queries = rotate(projected[:, :, 0].reshape(head_shape), cosine, sine).astype(jnp.bfloat16)
    key_rows = rotate(projected[:, :, 1].reshape(head_shape), cosine, sine).astype(jnp.bfloat16)
    value_rows = projected[:, :, 2].reshape(head_shape).astype(jnp.bfloat16)
    open_rows = jnp.zeros((items_here, seq_len), jnp.float32)
    attended, self_logs = attend_forward(queries, key_rows, value_rows, open_rows, block_size)
    attended = attended.reshape(items_here, seq_len, heads_here * head_size).astype(jnp.bfloat16)
    segment = attended
    self_branch = jnp.swapaxes(
        lax.psum_scatter(
            jnp.swapaxes(jnp.dot(segment, self_out_full, preferred_element_type=jnp.float32), 0, 1),
            "mp",
            scatter_dimension=0,
            tiled=True,
        ),
        0,
        1,
    )
    residual_one = lax.dynamic_slice_in_dim(residual_in, first_row, shard_rows, 1) + self_branch
    normed_two, scaled_two, inverse_two = layer_norm(residual_one, cross_gain, cross_bias)
    normed_two_all = lax.all_gather(normed_two.astype(jnp.bfloat16), "mp", axis=1, tiled=True)
    cross_q = (
        jnp.dot(normed_two_all, cross_query_full, preferred_element_type=jnp.float32)
        .astype(jnp.bfloat16)
        .reshape(head_shape)
    )
    context = jnp.einsum(
        "bpc,ckh->bpkh", prompt_tokens, context_full, preferred_element_type=jnp.float32
    ).astype(jnp.bfloat16)
    prompt_slots = prompt_tokens.shape[1]
    context_shape = (items_here, prompt_slots, heads_here, head_size)
    context_keys = context[:, :, 0].reshape(context_shape)
    context_values = context[:, :, 1].reshape(context_shape)
    slot_index = jnp.arange(prompt_slots, dtype=jnp.int32)
    mask_rows = jnp.where(slot_index[None, :] < prompt_lengths[:, None], 0.0, NEG).astype(
        jnp.float32
    )
    crossed, cross_logs = attend_forward(
        cross_q, context_keys, context_values, mask_rows, block_size
    )
    crossed = crossed.reshape(items_here, seq_len, heads_here * head_size).astype(jnp.bfloat16)
    segment = crossed
    cross_branch = jnp.swapaxes(
        lax.psum_scatter(
            jnp.swapaxes(
                jnp.dot(segment, cross_out_full, preferred_element_type=jnp.float32), 0, 1
            ).astype(jnp.bfloat16),
            "mp",
            scatter_dimension=0,
            tiled=True,
        ).astype(jnp.float32),
        0,
        1,
    )
    residual_two = residual_one + cross_branch
    normed_three, scaled_three, inverse_three = layer_norm(residual_two, feed_gain, feed_bias)
    normed_three_all = lax.all_gather(normed_three.astype(jnp.bfloat16), "mp", axis=1, tiled=True)
    gate_up = jnp.einsum(
        "bsd,dkf->bskf", normed_three_all, gate_up_full, preferred_element_type=jnp.float32
    )
    gate_part = gate_up[:, :, 0]
    up_part = gate_up[:, :, 1]
    hidden = (jax.nn.silu(gate_part) * up_part).astype(jnp.bfloat16)
    segment = hidden
    feed_branch = jnp.swapaxes(
        lax.psum_scatter(
            jnp.swapaxes(
                jnp.dot(segment, down_full, preferred_element_type=jnp.float32), 0, 1
            ).astype(jnp.bfloat16),
            "mp",
            scatter_dimension=0,
            tiled=True,
        ).astype(jnp.float32),
        0,
        1,
    )
    output = (residual_two + feed_branch + down_bias).astype(jnp.bfloat16)
    regathered = (
        lax.all_gather(qkv_weight, "dp", axis=0, tiled=True),
        lax.all_gather(self_out_weight, "dp", axis=1, tiled=True),
        lax.all_gather(cross_query_weight, "dp", axis=0, tiled=True),
        lax.all_gather(context_weight, "dp", axis=0, tiled=True),
        lax.all_gather(cross_out_weight, "dp", axis=1, tiled=True),
        lax.all_gather(gate_up_weight, "dp", axis=0, tiled=True),
        lax.all_gather(down_weight, "dp", axis=1, tiled=True),
    )
    (
        qkv_back,
        self_out_back,
        cross_query_back,
        context_back,
        cross_out_back,
        gate_up_back,
        down_back,
    ) = regathered
    grad_rows = lax.all_gather(cotangent, "mp", axis=1, tiled=True)
    grad_hidden = jnp.einsum(
        "bsd,fd->bsf", grad_rows, down_back, preferred_element_type=jnp.float32
    )
    sigmoid_gate = jax.nn.sigmoid(gate_part)
    grad_up = grad_hidden * gate_part * sigmoid_gate
    grad_gate = grad_hidden * up_part * sigmoid_gate * (1.0 + gate_part * (1.0 - sigmoid_gate))
    grad_gate_up = jnp.stack([grad_gate, grad_up], axis=2).astype(jnp.bfloat16)
    down_weight_grad = jnp.einsum(
        "bsf,bsd->fd", hidden, grad_rows, preferred_element_type=jnp.float32
    )
    gate_up_grad = jnp.einsum(
        "bsd,bskf->dkf", normed_three_all, grad_gate_up, preferred_element_type=jnp.float32
    )
    segment = grad_gate_up
    grad_normed_three = jnp.swapaxes(
        lax.psum_scatter(
            jnp.swapaxes(
                jnp.einsum(
                    "bskf,dkf->bsd", segment, gate_up_back, preferred_element_type=jnp.float32
                ),
                0,
                1,
            ).astype(jnp.bfloat16),
            "mp",
            scatter_dimension=0,
            tiled=True,
        ).astype(jnp.float32),
        0,
        1,
    )
    grad_two_norm, feed_gain_part, feed_bias_part = norm_back(
        grad_normed_three, scaled_three, inverse_three, feed_gain
    )
    grad_out_shard = cotangent.astype(jnp.float32)
    down_bias_part = jnp.sum(grad_out_shard, axis=(0, 1))
    grad_residual_two = (grad_out_shard + grad_two_norm).astype(jnp.bfloat16)
    grad_rows_two = lax.all_gather(grad_residual_two, "mp", axis=1, tiled=True)
    grad_crossed = jnp.einsum(
        "bsd,hd->bsh", grad_rows_two, cross_out_back, preferred_element_type=jnp.float32
    ).astype(jnp.bfloat16)
    cross_out_grad = jnp.einsum(
        "bsh,bsd->hd", crossed, grad_rows_two, preferred_element_type=jnp.float32
    )
    grad_cross_q, grad_cross_k, grad_cross_v = attend_backward(
        cross_q,
        context_keys,
        context_values,
        mask_rows,
        cross_logs,
        grad_crossed.reshape(head_shape),
        block_size,
    )
    grad_cross_q = grad_cross_q.reshape(items_here, seq_len, heads_here * head_size).astype(
        jnp.bfloat16
    )
    grad_context = (
        jnp.stack([grad_cross_k, grad_cross_v], axis=2)
        .reshape(items_here, prompt_slots, 2, heads_here * head_size)
        .astype(jnp.bfloat16)
    )
    cross_query_grad = jnp.einsum(
        "bsd,bsh->dh", normed_two_all, grad_cross_q, preferred_element_type=jnp.float32
    )
    context_weight_grad = jnp.einsum(
        "bpc,bpkh->ckh", prompt_tokens, grad_context, preferred_element_type=jnp.float32
    )
    segment = grad_cross_q
    grad_normed_two = jnp.swapaxes(
        lax.psum_scatter(
            jnp.swapaxes(
                jnp.einsum(
                    "bsh,dh->bsd", segment, cross_query_back, preferred_element_type=jnp.float32
                ),
                0,
                1,
            ).astype(jnp.bfloat16),
            "mp",
            scatter_dimension=0,
            tiled=True,
        ).astype(jnp.float32),
        0,
        1,
    )
    grad_one_norm, cross_gain_part, cross_bias_part = norm_back(
        grad_normed_two, scaled_two, inverse_two, cross_gain
    )
    grad_residual_one = (grad_residual_two.astype(jnp.float32) + grad_one_norm).astype(jnp.bfloat16)
    grad_rows_one = lax.all_gather(grad_residual_one, "mp", axis=1, tiled=True)
    grad_attended = jnp.einsum(
        "bsd,hd->bsh", grad_rows_one, self_out_back, preferred_element_type=jnp.float32
    ).astype(jnp.bfloat16)
    self_out_grad = jnp.einsum(
        "bsh,bsd->hd", attended, grad_rows_one, preferred_element_type=jnp.float32
    )
    grad_query, grad_key, grad_value = attend_backward(
        queries,
        key_rows,
        value_rows,
        open_rows,
        self_logs,
        grad_attended.reshape(head_shape),
        block_size,
    )
    grad_query = unrotate(grad_query, cosine, sine)
    grad_key = unrotate(grad_key, cosine, sine)
    grad_projected = (
        jnp.stack([grad_query, grad_key, grad_value], axis=2)
        .reshape(items_here, seq_len, 3, heads_here * head_size)
        .astype(jnp.bfloat16)
    )
    qkv_weight_grad = jnp.einsum(
        "bsd,bskc->dkc", normed_one, grad_projected, preferred_element_type=jnp.float32
    )
    grad_normed_part = jnp.einsum(
        "bskc,dkc->bsd", grad_projected, qkv_back, preferred_element_type=jnp.float32
    )
    summed = (
        lax.psum(grad_normed_part.astype(jnp.bfloat16), "mp").astype(jnp.float32),
        lax.psum(cross_gain_part.astype(jnp.bfloat16), "mp").astype(jnp.float32),
        lax.psum(cross_bias_part.astype(jnp.bfloat16), "mp").astype(jnp.float32),
        lax.psum(feed_gain_part.astype(jnp.bfloat16), "mp").astype(jnp.float32),
        lax.psum(feed_bias_part.astype(jnp.bfloat16), "mp").astype(jnp.float32),
        lax.psum(down_bias_part.astype(jnp.bfloat16), "mp").astype(jnp.float32),
    )
    grad_in_norm, self_gain_part, self_bias_part = norm_back(
        summed[0], scaled_one, inverse_one, self_gain
    )
    grad_residual_in = grad_rows_one.astype(jnp.float32) + grad_in_norm
    latents_grad = grad_residual_in[:, 1:].astype(jnp.bfloat16)
    time_weight_grad = jnp.dot(
        features.astype(jnp.float32).T, grad_residual_in[:, 0], precision=lax.Precision.HIGHEST
    )
    cross_gain_sum, cross_bias_sum, feed_gain_sum, feed_bias_sum, down_bias_sum = (
        summed[1],
        summed[2],
        summed[3],
        summed[4],
        summed[5],
    )
    reduced = (
        lax.psum_scatter(
            time_weight_grad.astype(jnp.bfloat16), "dp", scatter_dimension=0, tiled=True
        ).astype(jnp.float32),
        lax.psum_scatter(
            qkv_weight_grad.astype(jnp.bfloat16), "dp", scatter_dimension=0, tiled=True
        ).astype(jnp.float32),
        lax.psum_scatter(
            self_out_grad.astype(jnp.bfloat16), "dp", scatter_dimension=1, tiled=True
        ).astype(jnp.float32),
        lax.psum_scatter(
            cross_query_grad.astype(jnp.bfloat16), "dp", scatter_dimension=0, tiled=True
        ).astype(jnp.float32),
        lax.psum_scatter(
            context_weight_grad.astype(jnp.bfloat16), "dp", scatter_dimension=0, tiled=True
        ).astype(jnp.float32),
        lax.psum_scatter(
            cross_out_grad.astype(jnp.bfloat16), "dp", scatter_dimension=1, tiled=True
        ).astype(jnp.float32),
        lax.psum_scatter(
            gate_up_grad.astype(jnp.bfloat16), "dp", scatter_dimension=0, tiled=True
        ).astype(jnp.float32),
        lax.psum_scatter(
            down_weight_grad.astype(jnp.bfloat16), "dp", scatter_dimension=1, tiled=True
        ).astype(jnp.float32),
        lax.psum_scatter(
            self_gain_part.astype(jnp.bfloat16), "dp", scatter_dimension=0, tiled=True
        ).astype(jnp.float32),
        lax.psum_scatter(
            self_bias_part.astype(jnp.bfloat16), "dp", scatter_dimension=0, tiled=True
        ).astype(jnp.float32),
        lax.psum_scatter(
            cross_gain_sum.astype(jnp.bfloat16), "dp", scatter_dimension=0, tiled=True
        ).astype(jnp.float32),
        lax.psum_scatter(
            cross_bias_sum.astype(jnp.bfloat16), "dp", scatter_dimension=0, tiled=True
        ).astype(jnp.float32),
        lax.psum_scatter(
            feed_gain_sum.astype(jnp.bfloat16), "dp", scatter_dimension=0, tiled=True
        ).astype(jnp.float32),
        lax.psum_scatter(
            feed_bias_sum.astype(jnp.bfloat16), "dp", scatter_dimension=0, tiled=True
        ).astype(jnp.float32),
        lax.psum_scatter(
            down_bias_sum.astype(jnp.bfloat16), "dp", scatter_dimension=0, tiled=True
        ).astype(jnp.float32),
    )
    return (
        output,
        latents_grad,
        reduced[0],
        reduced[8],
        reduced[9],
        reduced[1],
        reduced[2],
        reduced[10],
        reduced[11],
        reduced[3],
        reduced[4],
        reduced[5],
        reduced[12],
        reduced[13],
        reduced[6],
        reduced[7],
        reduced[14],
    )


AXES = ("dp", "mp")
BF = jnp.bfloat16
F32 = jnp.float32


def flat_permutation(places):
    pairs = []
    for d in range(8):
        for z in range(4):
            target = places(d >> 1, d & 1, z & 1, z >> 1)
            if target is not None:
                s, c, zz, p = target
                pairs.append(((2 * s + c) * 4 + 2 * p + zz, (2 * (d >> 1) + (d & 1)) * 4 + z))
    return [(source, target) for target, source in pairs]


SWAP_CORE = flat_permutation(lambda s, c, zz, p: (s, 1 - c, zz, p))
SWAP_Z = flat_permutation(lambda s, c, zz, p: (s, c, 1 - zz, p))
SWAP_PAIR = flat_permutation(lambda s, c, zz, p: (s, c, zz, 1 - p))
SWAP_X = flat_permutation(lambda s, c, zz, p: (s ^ 1, c, zz, p))
SWAP_Y = flat_permutation(lambda s, c, zz, p: (s ^ 2, c, zz, p))
ROUTE_A = flat_permutation(lambda s, c, zz, p: (s, p, zz, c))
ROUTE_B = flat_permutation(lambda s, c, zz, p: (s, p, zz, 1 - c))
RETURN_B = flat_permutation(lambda s, c, zz, p: (s, 1 - p, zz, c))
OWNER_TO_PARTNER = flat_permutation(lambda s, c, zz, p: (s, 1 - c, zz, p) if c == p else None)
PARTNER_TO_OWNER = flat_permutation(lambda s, c, zz, p: (s, 1 - c, zz, p) if c != p else None)
OWNER_TO_PAIR = flat_permutation(lambda s, c, zz, p: (s, c, zz, 1 - p) if c == p else None)
OWNER_Z = flat_permutation(lambda s, c, zz, p: (s, c, 1 - zz, p) if c == p else None)
PARTNER_Z = flat_permutation(lambda s, c, zz, p: (s, c, 1 - zz, p) if c != p else None)


def move(values, pairs):
    return lax.ppermute(values, AXES, pairs)


def xor_blocks(values, axis, count, index):
    blocks = jnp.split(values, count, axis=axis)
    bit = 1
    while bit < count:
        flip = (index & bit) != 0
        blocks = [jnp.where(flip, blocks[j ^ bit], blocks[j]) for j in range(count)]
        bit *= 2
    return jnp.concatenate(blocks, axis=axis)


def attention_forward_kernel(head_size, query_block, turned, *refs):
    if turned:
        q_in, k_in, v_in, cos_ref, low_ref, high_ref, q_ref, k_ref, v_ref, o_ref, log_ref = refs
    else:
        q_in, k_in, v_in, bias_ref, o_ref, log_ref = refs
    scale = head_size ** (-0.5)
    length = q_in.shape[0]
    if turned:
        half = head_size // 4
        width = q_in.shape[1]

        def turn(source, target):
            @pl.loop(0, length // query_block)
            def _(step):
                rows = pl.ds(pl.multiple_of(step * query_block, query_block), query_block)
                values = source[rows, :]
                target[rows, :] = (
                    values * cos_ref[rows, :]
                    + pltpu.roll(values, width - half, 1) * low_ref[rows, :]
                    + pltpu.roll(values, half, 1) * high_ref[rows, :]
                ).astype(BF)

        turn(q_in, q_ref)
        turn(k_in, k_ref)
        v_ref[...] = v_in[...].astype(BF)
        queries, keys, values = q_ref, k_ref, v_ref
    else:
        queries, keys, values = q_in, k_in, v_in
    key_rows = keys[...]
    values_turned = values[...].astype(F32).T.astype(BF)
    lane = lax.broadcasted_iota(jnp.int32, (query_block, q_in.shape[1]), 1)

    @pl.loop(0, length // query_block)
    def _(step):
        rows = pl.ds(pl.multiple_of(step * query_block, query_block), query_block)
        block = queries[rows, :]
        parts, logs = [], []
        for head in range(2):
            mine = (lane >= head * head_size) & (lane < (head + 1) * head_size)
            masked = jnp.where(mine, block, jnp.zeros_like(block))
            scores = lax.dot_general(
                key_rows, masked, (((1,), (1,)), ((), ())), preferred_element_type=F32
            )
            scores = scores * scale
            if not turned:
                scores = scores + bias_ref[...]
            top = jnp.max(scores, axis=0, keepdims=True)
            expos = jnp.exp(scores - top)
            total = jnp.sum(expos, axis=0, keepdims=True)
            mixed = lax.dot_general(
                values_turned[head * head_size : (head + 1) * head_size, :],
                expos.astype(BF),
                (((1,), (0,)), ((), ())),
                preferred_element_type=F32,
            )
            parts.append(mixed * (1.0 / total))
            logs.append(top + jnp.log(total))
        o_ref[rows, :] = jnp.concatenate(parts, axis=0).T.astype(BF)
        log_ref[0, :, rows] = jnp.concatenate(logs, axis=0)


def attention_backward_kernel(head_size, query_block, turned, *refs):
    if turned:
        q_ref, k_ref, v_ref, d_ref, log_ref, cos_ref, low_ref, high_ref, g_ref, dk_acc, dv_acc = refs
    else:
        q_ref, k_ref, v_ref, d_ref, log_ref, bias_ref, dq_ref, g_ref, dk_acc, dv_acc = refs
    scale = head_size ** (-0.5)
    length, width = q_ref.shape
    key_count = k_ref.shape[0]
    here = pl.program_id(0)
    half = head_size // 4
    key_rows = k_ref[...]
    value_rows = v_ref[...]
    keys_turned = key_rows.astype(F32).T.astype(BF)
    lane = lax.broadcasted_iota(jnp.int32, (query_block, width), 1)
    dk_acc[...] = jnp.zeros_like(dk_acc)
    dv_acc[...] = jnp.zeros_like(dv_acc)

    def back_turn(values, rows):
        return (
            values * cos_ref[rows, :]
            - pltpu.roll(values, width - half, 1) * low_ref[rows, :]
            - pltpu.roll(values, half, 1) * high_ref[rows, :]
        )

    @pl.loop(0, length // query_block)
    def _(step):
        rows = pl.ds(pl.multiple_of(step * query_block, query_block), query_block)
        block = q_ref[rows, :]
        grads = d_ref[rows, :]
        parts = []
        for head in range(2):
            mine = (lane >= head * head_size) & (lane < (head + 1) * head_size)
            q_mine = jnp.where(mine, block, jnp.zeros_like(block))
            d_mine = jnp.where(mine, grads, jnp.zeros_like(grads))
            scores = lax.dot_general(
                key_rows, q_mine, (((1,), (1,)), ((), ())), preferred_element_type=F32
            )
            scores = scores * scale
            if not turned:
                scores = scores + bias_ref[...]
            probs = jnp.exp(scores - log_ref[0, head : head + 1, rows])
            grad_probs = lax.dot_general(
                value_rows, d_mine, (((1,), (1,)), ((), ())), preferred_element_type=F32
            )
            delta = jnp.sum(probs * grad_probs, axis=0, keepdims=True)
            grad_scores = (probs * (grad_probs - delta)).astype(BF)
            dv_acc[...] += jnp.dot(probs.astype(BF), d_mine, preferred_element_type=F32)
            dk_acc[...] += jnp.dot(grad_scores, q_mine, preferred_element_type=F32)
            parts.append(
                jnp.dot(
                    keys_turned[head * head_size : (head + 1) * head_size, :],
                    grad_scores,
                    preferred_element_type=F32,
                )
            )
        grad_query = jnp.concatenate(parts, axis=0).T * scale
        if turned:
            columns = pl.ds(pl.multiple_of(here * width, width), width)
            g_ref[rows, columns] = back_turn(grad_query, rows).astype(BF)
        else:
            dq_ref[rows, :] = grad_query.astype(BF)

    total_width = g_ref.shape[1] // (3 if turned else 2)
    first = total_width if turned else 0
    key_columns = pl.ds(pl.multiple_of(first + here * width, width), width)
    value_columns = pl.ds(pl.multiple_of(first + total_width + here * width, width), width)
    if turned:

        @pl.loop(0, key_count // query_block)
        def _(step):
            rows = pl.ds(pl.multiple_of(step * query_block, query_block), query_block)
            g_ref[rows, key_columns] = back_turn(dk_acc[rows, :] * scale, rows).astype(BF)
            g_ref[rows, value_columns] = dv_acc[rows, :].astype(BF)
    else:
        g_ref[:, key_columns] = (dk_acc[...] * scale).astype(BF)
        g_ref[:, value_columns] = dv_acc[...].astype(BF)


def self_attention(projected, tables):
    length, total = projected.shape
    pairs = total // 3 // 128
    block = lambda shift: pl.BlockSpec((length, 128), lambda i: (0, i + shift))
    fixed = pl.BlockSpec((length, 128), lambda i: (0, 0))
    wide = jax.ShapeDtypeStruct((length, total // 3), BF)
    return pl.pallas_call(
        functools.partial(attention_forward_kernel, HD, 256, True),
        grid=(pairs,),
        in_specs=[block(0), block(pairs), block(2 * pairs), fixed, fixed, fixed],
        out_specs=[block(0)] * 4 + [pl.BlockSpec((1, 2, length), lambda i: (i, 0, 0))],
        out_shape=[wide] * 4 + [jax.ShapeDtypeStruct((pairs, 2, length), F32)],
        cost_estimate=pl.CostEstimate(
            flops=4 * length * length * total // 3,
            transcendentals=length * length * total // 192,
            bytes_accessed=length * total * 8,
        ),
        name="self_attention",
    )(projected, projected, projected, *tables)


def self_attention_back(queries, keys, values, grads, logs, tables):
    length, total = queries.shape
    pairs = total // 128
    block = pl.BlockSpec((length, 128), lambda i: (0, i))
    fixed = pl.BlockSpec((length, 128), lambda i: (0, 0))
    return pl.pallas_call(
        functools.partial(attention_backward_kernel, HD, 256, True),
        grid=(pairs,),
        in_specs=[block] * 4 + [pl.BlockSpec((1, 2, length), lambda i: (i, 0, 0))] + [fixed] * 3,
        out_specs=pl.BlockSpec((length, 3 * total), lambda i: (0, 0)),
        out_shape=jax.ShapeDtypeStruct((length, 3 * total), BF),
        scratch_shapes=[pltpu.VMEM((length, 128), F32)] * 2,
        cost_estimate=pl.CostEstimate(
            flops=10 * length * length * total,
            transcendentals=length * length * total // 64,
            bytes_accessed=length * total * 16,
        ),
        name="self_attention_back",
    )(queries, keys, values, grads, logs, *tables)


def cross_attention(queries, context, bias):
    length, total = queries.shape
    slots = context.shape[0]
    pairs = total // 128
    block = pl.BlockSpec((length, 128), lambda i: (0, i))
    key_block = lambda shift: pl.BlockSpec((slots, 128), lambda i: (0, i + shift))
    return pl.pallas_call(
        functools.partial(attention_forward_kernel, HD, 512, False),
        grid=(pairs,),
        in_specs=[block, key_block(0), key_block(pairs), pl.BlockSpec((slots, 1), lambda i: (0, 0))],
        out_specs=[block, pl.BlockSpec((1, 2, length), lambda i: (i, 0, 0))],
        out_shape=[
            jax.ShapeDtypeStruct((length, total), BF),
            jax.ShapeDtypeStruct((pairs, 2, length), F32),
        ],
        cost_estimate=pl.CostEstimate(
            flops=4 * length * slots * total,
            transcendentals=length * slots * total // 64,
            bytes_accessed=length * total * 4,
        ),
        name="cross_attention",
    )(queries, context, context, bias)


def cross_attention_back(queries, context, bias, grads, logs):
    length, total = queries.shape
    slots = context.shape[0]
    pairs = total // 128
    block = pl.BlockSpec((length, 128), lambda i: (0, i))
    key_block = lambda shift: pl.BlockSpec((slots, 128), lambda i: (0, i + shift))
    return pl.pallas_call(
        functools.partial(attention_backward_kernel, HD, 512, False),
        grid=(pairs,),
        in_specs=[
            block,
            key_block(0),
            key_block(pairs),
            block,
            pl.BlockSpec((1, 2, length), lambda i: (i, 0, 0)),
            pl.BlockSpec((slots, 1), lambda i: (0, 0)),
        ],
        out_specs=[block, pl.BlockSpec((slots, 2 * total), lambda i: (0, 0))],
        out_shape=[
            jax.ShapeDtypeStruct((length, total), BF),
            jax.ShapeDtypeStruct((slots, 2 * total), BF),
        ],
        scratch_shapes=[pltpu.VMEM((slots, 128), F32)] * 2,
        cost_estimate=pl.CostEstimate(
            flops=10 * length * slots * total,
            transcendentals=length * slots * total // 64,
            bytes_accessed=length * total * 8,
        ),
        name="cross_attention_back",
    )(queries, context, context, grads, logs, bias)


def dot_nn(left, right):
    return lax.dot_general(left, right, (((1,), (0,)), ((), ())), preferred_element_type=F32)


def dot_nt(left, right):
    return lax.dot_general(left, right, (((1,), (1,)), ((), ())), preferred_element_type=F32)


def dot_tn(left, right):
    return lax.dot_general(left, right, (((0,), (0,)), ((), ())), preferred_element_type=F32)


def group_scatter(partial):
    rows = partial.shape[0] // 4
    other = move(partial[2 * rows :], SWAP_CORE)
    half = partial[: 2 * rows].astype(F32) + other.astype(F32)
    far = move(half[rows:].astype(BF), SWAP_Z)
    return half[:rows] + far.astype(F32)


def group_gather(part):
    far = move(part, SWAP_Z)
    half = jnp.concatenate([part, far], axis=0)
    return jnp.concatenate([half, move(half, SWAP_CORE)], axis=0)


def weight_spread(part, pair):
    one = move(part, ROUTE_A)
    two = move(part, ROUTE_B)
    first = jnp.where(pair == 0, one, two)
    second = jnp.where(pair == 0, two, one)
    return jnp.concatenate([first, second], axis=0)


def plane_gather(mine):
    rows = mine.shape[0] // 2
    from_x = move(mine, SWAP_X)
    from_y = move(mine, SWAP_Y)
    diag_one = move(from_x[:rows], SWAP_Y)
    diag_two = move(from_y[rows:], SWAP_X)
    return jnp.concatenate([mine, from_x, from_y, diag_one, diag_two], axis=0)


def plane_scatter(grad, pair):
    rows = grad.shape[0] // 8
    blocks = [grad[2 * rows * j : 2 * rows * (j + 1)] for j in range(4)]
    got_x = move(blocks[3][:rows], SWAP_X)
    got_y = move(blocks[3][rows:], SWAP_Y)
    to_x = jnp.concatenate(
        [
            blocks[1][:rows],
            (blocks[1][rows:].astype(F32) + got_y.astype(F32)).astype(BF),
        ],
        axis=0,
    )
    to_y = jnp.concatenate(
        [
            (blocks[2][:rows].astype(F32) + got_x.astype(F32)).astype(BF),
            blocks[2][rows:],
        ],
        axis=0,
    )
    total = (
        blocks[0].astype(F32)
        + move(to_x, SWAP_X).astype(F32)
        + move(to_y, SWAP_Y).astype(F32)
    ).astype(BF)
    first, second = total[:rows], total[rows:]
    one = move(jnp.where(pair == 0, first, second), ROUTE_A)
    two = move(jnp.where(pair == 0, second, first), RETURN_B)
    return one.astype(F32) + two.astype(F32)


def per_device_paired(
    latents,
    prompt_tokens,
    prompt_lengths,
    timesteps,
    time_weight,
    self_gain,
    self_bias,
    qkv_weight,
    self_out_weight,
    cross_gain,
    cross_bias,
    cross_query_weight,
    context_weight,
    cross_out_weight,
    feed_gain,
    feed_bias,
    gate_up_weight,
    down_weight,
    down_bias,
    cotangent,
):
    d = lax.axis_index("dp")
    z = lax.axis_index("mp")
    core, column, pair = d & 1, d >> 1, z >> 1
    shard = (z & 1) + 2 * core
    owner = core == pair
    width = latents.shape[-1]
    length = latents.shape[1] + 1
    rows = length // 4
    part_rows = qkv_weight.shape[0]

    qkv_part = qkv_weight.reshape(part_rows, -1)
    side_part = jnp.concatenate(
        [
            self_out_weight.T,
            cross_query_weight,
            cross_out_weight.T,
            context_weight.reshape(part_rows, -1),
        ],
        axis=1,
    )
    gate_up_part = gate_up_weight.reshape(part_rows, -1)
    down_part = down_weight.T
    qkv_own = weight_spread(qkv_part, pair)
    side_own = weight_spread(side_part, pair)
    gate_up_own = weight_spread(gate_up_part, pair)
    down_own = weight_spread(down_part, pair)
    qkv_full = plane_gather(qkv_own)
    side_full = plane_gather(side_own)
    gate_up_full = plane_gather(gate_up_own)
    down_full = plane_gather(down_own)
    n = cross_query_weight.shape[1]
    self_out_full = side_full[:, :n]
    cross_query_full = side_full[:, n : 2 * n]
    cross_out_full = side_full[:, 2 * n : 3 * n]
    context_full = side_full[:, 3 * n :].reshape(context_weight.shape[0] * 8, -1)

    def of_item(values):
        return jnp.where(owner, values, move(values, OWNER_TO_PARTNER))

    item_latents = of_item(latents[0])
    item_prompt = xor_blocks(of_item(prompt_tokens[0]), 1, 4, column)
    scalars = of_item(jnp.stack([prompt_lengths[0], timesteps[0]]))
    item_length, item_step = scalars[0], scalars[1]
    time_full = time_weight
    for pairs in (SWAP_CORE, SWAP_X, SWAP_Y):
        time_full = jnp.concatenate([time_full, move(time_full, pairs)], axis=0)
    feature_width = time_full.shape[0]
    item_features = time_features(item_step[None], feature_width).astype(BF)
    token_row = dot_nn(xor_blocks(item_features, 1, 8, d), time_full)
    residual_in = jnp.concatenate([token_row, item_latents.astype(F32)], axis=0)
    residual_in = xor_blocks(xor_blocks(residual_in, 0, 4, shard), 1, 4, column)
    residual_mine = residual_in[:rows]
    vectors = xor_blocks(
        jnp.stack([self_gain, self_bias, cross_gain, cross_bias, feed_gain, feed_bias, down_bias]),
        1,
        4,
        column,
    )
    gain_one, bias_one, gain_two, bias_two, gain_three, bias_three, bias_down = [
        vectors[j] for j in range(7)
    ]
    cot_mine = xor_blocks(move(cotangent[0], ROUTE_A), 1, 4, column)
    cot_all = group_gather(cot_mine)

    normed_one, _, _ = layer_norm(residual_in, gain_one, bias_one)
    normed_one = normed_one.astype(BF)
    projected = dot_nn(normed_one, qkv_full)
    cosine, sine = rope_tables(length, HD)
    quarter = HD // 4
    straight = jnp.ones((length, HD // 2), F32)
    blank = jnp.zeros((length, quarter), F32)
    cosine, sine = cosine[:, 0], sine[:, 0]
    tables = jnp.stack(
        [
            jnp.tile(jnp.concatenate([cosine, straight], axis=1), (1, 2)),
            jnp.tile(
                jnp.concatenate([-sine[:, :quarter], blank, blank, blank], axis=1), (1, 2)
            ),
            jnp.tile(
                jnp.concatenate([blank, sine[:, quarter:], blank, blank], axis=1), (1, 2)
            ),
        ]
    )
    tables = xor_blocks(tables, 1, 4, shard)
    tables = (tables[0], tables[1], tables[2])
    queries, keys, values, attended, self_logs = self_attention(projected, tables)
    residual_one = residual_mine + group_scatter(dot_nt(attended, self_out_full).astype(BF))
    normed_two, scaled_two, inverse_two = layer_norm(residual_one, gain_two, bias_two)
    normed_two_all = group_gather(normed_two.astype(BF))
    cross_q = dot_nn(normed_two_all, cross_query_full).astype(BF)
    context = dot_nn(item_prompt, context_full).astype(BF)
    slots = prompt_tokens.shape[1]
    mask = jnp.where(jnp.arange(slots, dtype=jnp.int32)[:, None] < item_length, 0.0, NEG)
    mask = mask.astype(F32)
    crossed, cross_logs = cross_attention(cross_q, context, mask)
    residual_two = residual_one + group_scatter(dot_nt(crossed, cross_out_full).astype(BF))
    normed_three, scaled_three, inverse_three = layer_norm(residual_two, gain_three, bias_three)
    normed_three_all = group_gather(normed_three.astype(BF))
    gate_up = dot_nn(normed_three_all, gate_up_full)
    hidden_width = gate_up.shape[1] // 2
    gate, up = gate_up[:, :hidden_width], gate_up[:, hidden_width:]
    sigmoid_gate = jax.nn.sigmoid(gate)
    hidden = (gate * sigmoid_gate * up).astype(BF)
    feed = group_scatter(dot_nt(hidden, down_full).astype(BF))
    output = xor_blocks((residual_two + feed + bias_down).astype(BF), 1, 4, column)
    output = move(output, ROUTE_A)

    grad_hidden = dot_nn(cot_all, down_full)
    grad_up = grad_hidden * gate * sigmoid_gate
    grad_gate = grad_hidden * up * sigmoid_gate * (1.0 + gate * (1.0 - sigmoid_gate))
    grad_gate_up = jnp.concatenate([grad_gate.astype(BF), grad_up.astype(BF)], axis=1)
    grad_normed_three = group_scatter(dot_nt(grad_gate_up, gate_up_full).astype(BF))
    down_grad = plane_scatter(dot_tn(cot_all, hidden).astype(BF), pair)
    gate_up_grad = plane_scatter(dot_tn(normed_three_all, grad_gate_up).astype(BF), pair)

    def norm_back_rows(grad_normed, scaled, inverse, gain):
        grads, gain_part, bias_part = norm_back(grad_normed[None], scaled[None], inverse[None], gain)
        return grads[0], gain_part, bias_part

    grad_norm, feed_gain_part, feed_bias_part = norm_back_rows(
        grad_normed_three, scaled_three, inverse_three, gain_three
    )
    cot_rows = cot_mine.astype(F32)
    down_bias_part = jnp.sum(cot_rows, axis=0)
    grad_two = (cot_rows + grad_norm).astype(BF)
    grad_two_all = group_gather(grad_two)
    grad_crossed = dot_nn(grad_two_all, cross_out_full).astype(BF)
    grad_cross_q, grad_context = cross_attention_back(
        cross_q, context, mask, grad_crossed, cross_logs
    )
    grad_normed_two = group_scatter(dot_nt(grad_cross_q, cross_query_full).astype(BF))
    context_grad = dot_tn(item_prompt, grad_context).astype(BF).reshape(side_full.shape[0], -1)
    cross_out_grad = dot_tn(grad_two_all, crossed).astype(BF)
    cross_query_grad = dot_tn(normed_two_all, grad_cross_q).astype(BF)
    cross_grads = plane_scatter(
        jnp.concatenate([cross_query_grad, cross_out_grad, context_grad], axis=1), pair
    )
    grad_norm, cross_gain_part, cross_bias_part = norm_back_rows(
        grad_normed_two, scaled_two, inverse_two, gain_two
    )
    grad_one = (grad_two.astype(F32) + grad_norm).astype(BF)
    grad_one_all = group_gather(grad_one)
    grad_attended = dot_nn(grad_one_all, self_out_full).astype(BF)
    grad_projected = self_attention_back(
        queries, keys, values, grad_attended, self_logs, tables
    )
    grad_normed_one = group_scatter(dot_nt(grad_projected, qkv_full).astype(BF))
    self_out_grad = plane_scatter(dot_tn(grad_one_all, attended).astype(BF), pair)
    qkv_grad = plane_scatter(dot_tn(normed_one, grad_projected).astype(BF), pair)
    _, scaled_one, inverse_one = layer_norm(residual_mine, gain_one, bias_one)
    grad_norm, self_gain_part, self_bias_part = norm_back_rows(
        grad_normed_one, scaled_one, inverse_one, gain_one
    )
    grad_in = (grad_one.astype(F32) + grad_norm).astype(BF)
    grad_in = xor_blocks(grad_in, 1, 4, column)

    from_partner = move(grad_in, PARTNER_TO_OWNER)
    first = jnp.where(core == 0, grad_in, from_partner)
    second = jnp.where(core == 0, from_partner, grad_in)
    half = jnp.concatenate([first, second], axis=0)
    far_half = move(half, OWNER_TO_PAIR)
    own_z = move(half, OWNER_Z)
    here = jnp.where(owner, half, far_half)
    there = jnp.where(owner, own_z, move(far_half, PARTNER_Z))
    even = jnp.where((z & 1) == 0, here, there)
    odd = jnp.where((z & 1) == 0, there, here)
    whole = jnp.concatenate([even[:rows], odd[:rows], even[rows:], odd[rows:]], axis=0)
    latents_grad = whole[1:]

    token_rows = whole[:1]
    steps = timesteps
    for pairs in (SWAP_CORE, SWAP_X, SWAP_Y):
        token_rows = jnp.concatenate([token_rows, move(token_rows, pairs)], axis=0)
        steps = jnp.concatenate([steps, move(steps, pairs)], axis=0)
    all_features = time_features(steps, feature_width).astype(BF)
    my_features = jnp.zeros((8, feature_width // 8), F32)
    for j in range(8):
        piece = all_features[:, j * (feature_width // 8) : (j + 1) * (feature_width // 8)]
        my_features = my_features + jnp.where(d == j, piece.astype(F32), 0.0)
    time_grad = lax.dot_general(
        my_features.astype(BF), token_rows, (((0,), (0,)), ((), ())), preferred_element_type=F32
    )

    parts = jnp.stack(
        [
            self_gain_part,
            self_bias_part,
            cross_gain_part,
            cross_bias_part,
            feed_gain_part,
            feed_bias_part,
            down_bias_part,
        ]
    )
    block = width // 4
    got = move(jnp.concatenate([parts[:, block : 2 * block], parts[:, 3 * block :]], axis=1), SWAP_X)
    keep = jnp.concatenate([parts[:, :block], parts[:, 2 * block : 3 * block]], axis=1) + got
    mine = keep[:, :block] + move(keep[:, block:], SWAP_Y)
    low_half, high_half = mine[:, : block // 2], mine[:, block // 2 :]
    other = move(jnp.where(core == 0, high_half, low_half), SWAP_CORE)
    mine = jnp.where(core == 0, low_half, high_half) + other
    mine = mine + move(mine, SWAP_Z)
    mine = mine + move(mine, SWAP_PAIR)

    return (
        output[None],
        latents_grad[None],
        time_grad,
        mine[0],
        mine[1],
        qkv_grad.reshape(qkv_weight.shape),
        self_out_grad.T,
        mine[2],
        mine[3],
        cross_grads[:, :n],
        cross_grads[:, 2 * n :].reshape(context_weight.shape),
        cross_grads[:, n : 2 * n].T,
        mine[4],
        mine[5],
        gate_up_grad.reshape(gate_up_weight.shape),
        down_grad.T,
        mine[6],
    )


def solution(mesh):
    placed = (
        P("dp", None, None),
        P("dp", None, None),
        P("dp"),
        P("dp"),
        P("dp", None),
        P(),
        P(),
        P("dp", None, "mp"),
        P("mp", "dp"),
        P(),
        P(),
        P("dp", "mp"),
        P("dp", None, "mp"),
        P("mp", "dp"),
        P(),
        P(),
        P("dp", None, "mp"),
        P("mp", "dp"),
        P(),
        P("dp", "mp", None),
    )
    paired = mesh.shape["dp"] == 8 and mesh.shape["mp"] == 4
    return jax.shard_map(
        per_device_paired if paired else per_device_general,
        mesh=mesh,
        in_specs=placed,
        out_specs=(
            P("dp", "mp", None),
            P("dp", None, None),
            P("dp", None),
            P("dp"),
            P("dp"),
            P("dp", None, "mp"),
            P("mp", "dp"),
            P("dp"),
            P("dp"),
            P("dp", "mp"),
            P("dp", None, "mp"),
            P("mp", "dp"),
            P("dp"),
            P("dp"),
            P("dp", None, "mp"),
            P("mp", "dp"),
            P("dp"),
        ),
        check_vma=False,
    )
```

```python
import functools
import math

import jax
import jax.numpy as jnp
from jax import lax
from jax.experimental import pallas as pl
from jax.experimental.pallas import tpu as pltpu
from jax.sharding import PartitionSpec as P

HD = 64


EPS = 1e-05
NEG = -1e30


def time_features(steps_in, feature_width):
    half_width = feature_width // 2
    freqs = jnp.exp(-math.log(10000.0) * jnp.arange(half_width, dtype=jnp.float32) / half_width)
    angles = steps_in.astype(jnp.float32)[:, None] * freqs[None, :]
    return jnp.concatenate([jnp.cos(angles), jnp.sin(angles)], axis=-1)


def rope_tables(length, head_size):
    rotated_width = head_size // 2
    half_width = rotated_width // 2
    inverse = jnp.exp(
        -math.log(10000.0) * jnp.arange(half_width, dtype=jnp.float32) * 2.0 / rotated_width
    )
    angles = jnp.arange(length, dtype=jnp.float32)[:, None] * inverse[None, :]
    cosine = jnp.concatenate([jnp.cos(angles), jnp.cos(angles)], axis=-1)
    sine = jnp.concatenate([jnp.sin(angles), jnp.sin(angles)], axis=-1)
    return (cosine[:, None, :], sine[:, None, :])


def rotate(values, cosine, sine):
    rotated_width = cosine.shape[-1]
    half_width = rotated_width // 2
    first = values[..., :rotated_width]
    turned = jnp.concatenate([-first[..., half_width:], first[..., :half_width]], axis=-1)
    return jnp.concatenate([first * cosine + turned * sine, values[..., rotated_width:]], axis=-1)


def unrotate(grads_in, cosine, sine):
    rotated_width = cosine.shape[-1]
    half_width = rotated_width // 2
    first = grads_in[..., :rotated_width]
    scaled_in = first * sine
    turned = jnp.concatenate([scaled_in[..., half_width:], -scaled_in[..., :half_width]], axis=-1)
    return jnp.concatenate([first * cosine + turned, grads_in[..., rotated_width:]], axis=-1)


def layer_norm(values, gain, bias):
    centered = values - jnp.mean(values, axis=-1, keepdims=True)
    inverse = lax.rsqrt(jnp.mean(centered * centered, axis=-1, keepdims=True) + EPS)
    scaled = centered * inverse
    return (scaled * gain + bias, scaled, inverse)


def norm_back(grad_normed, scaled, inverse, gain):
    grad_scaled = grad_normed * gain
    first_mean = jnp.mean(grad_scaled, axis=-1, keepdims=True)
    second_mean = jnp.mean(grad_scaled * scaled, axis=-1, keepdims=True)
    grad_values = inverse * (grad_scaled - first_mean - scaled * second_mean)
    return (
        grad_values,
        jnp.sum(grad_normed * scaled, axis=(0, 1)),
        jnp.sum(grad_normed, axis=(0, 1)),
    )


def attend_forward(queries, key_rows, value_rows, bias_rows, block_size):
    score_scale = queries.shape[-1] ** (-0.5)

    def one_item(operands):
        item_query, item_key, item_value, item_bias = operands
        query_blocks = item_query.reshape(-1, block_size, item_query.shape[1], item_query.shape[2])

        def one_block(block_query):
            scores = jnp.einsum(
                "qhe,khe->hqk", block_query, item_key, preferred_element_type=jnp.float32
            )
            scores = scores * score_scale + item_bias[None, None, :]
            row_max = jnp.max(scores, axis=-1, keepdims=True)
            expos = jnp.exp(scores - row_max)
            row_total = jnp.sum(expos, axis=-1, keepdims=True)
            weights_p = (expos / row_total).astype(jnp.bfloat16)
            mixed = jnp.einsum(
                "hqk,khe->qhe", weights_p, item_value, preferred_element_type=jnp.float32
            )
            return (mixed, (row_max + jnp.log(row_total))[..., 0])

        mixed, log_total = lax.map(one_block, query_blocks)
        return (mixed.reshape(item_query.shape), log_total)

    return lax.map(one_item, (queries, key_rows, value_rows, bias_rows))


def attend_backward(queries, key_rows, value_rows, bias_rows, log_totals, grad_out, block_size):
    score_scale = queries.shape[-1] ** (-0.5)

    def one_item(operands):
        item_query, item_key, item_value, item_bias, item_log, item_grad = operands
        block_shape = (-1, block_size, item_query.shape[1], item_query.shape[2])
        query_blocks = item_query.reshape(block_shape)
        grad_blocks = item_grad.reshape(block_shape)

        def one_block(carry, operands_block):
            block_query, block_log, block_grad = operands_block
            scores = jnp.einsum(
                "qhe,khe->hqk", block_query, item_key, preferred_element_type=jnp.float32
            )
            scores = scores * score_scale + item_bias[None, None, :]
            probs_full = jnp.exp(scores - block_log[..., None])
            grad_probs = jnp.einsum(
                "qhe,khe->hqk", block_grad, item_value, preferred_element_type=jnp.float32
            )
            delta_row = jnp.sum(probs_full * grad_probs, axis=-1, keepdims=True)
            grad_scores = (probs_full * (grad_probs - delta_row)).astype(jnp.bfloat16)
            grad_query = (
                jnp.einsum(
                    "hqk,khe->qhe", grad_scores, item_key, preferred_element_type=jnp.float32
                )
                * score_scale
            )
            grad_key = (
                carry[0]
                + jnp.einsum(
                    "hqk,qhe->khe", grad_scores, block_query, preferred_element_type=jnp.float32
                )
                * score_scale
            )
            grad_value = carry[1] + jnp.einsum(
                "hqk,qhe->khe",
                probs_full.astype(jnp.bfloat16),
                block_grad,
                preferred_element_type=jnp.float32,
            )
            return ((grad_key, grad_value), grad_query)

        start_carry = (
            jnp.zeros(item_key.shape, jnp.float32),
            jnp.zeros(item_value.shape, jnp.float32),
        )
        (grad_key, grad_value), grad_query = lax.scan(
            one_block, start_carry, (query_blocks, item_log, grad_blocks)
        )
        return (grad_query.reshape(item_query.shape), grad_key, grad_value)

    return lax.map(one_item, (queries, key_rows, value_rows, bias_rows, log_totals, grad_out))


def per_device_general(
    latents,
    prompt_tokens,
    prompt_lengths,
    timesteps,
    time_weight,
    self_gain,
    self_bias,
    qkv_weight,
    self_out_weight,
    cross_gain,
    cross_bias,
    cross_query_weight,
    context_weight,
    cross_out_weight,
    feed_gain,
    feed_bias,
    gate_up_weight,
    down_weight,
    down_bias,
    cotangent,
):
    gathered = (
        lax.all_gather(time_weight, "dp", axis=0, tiled=True),
        lax.all_gather(qkv_weight, "dp", axis=0, tiled=True),
        lax.all_gather(self_out_weight, "dp", axis=1, tiled=True),
        lax.all_gather(cross_query_weight, "dp", axis=0, tiled=True),
        lax.all_gather(context_weight, "dp", axis=0, tiled=True),
        lax.all_gather(cross_out_weight, "dp", axis=1, tiled=True),
        lax.all_gather(gate_up_weight, "dp", axis=0, tiled=True),
        lax.all_gather(down_weight, "dp", axis=1, tiled=True),
    )
    (
        time_full,
        qkv_full,
        self_out_full,
        cross_query_full,
        context_full,
        cross_out_full,
        gate_up_full,
        down_full,
    ) = gathered
    items_here = latents.shape[0]
    seq_len = latents.shape[1] + 1
    shard_rows = seq_len // lax.axis_size("mp")
    first_row = lax.axis_index("mp") * shard_rows
    head_size = HD
    block_size = min(512, seq_len)
    features = time_features(timesteps, time_full.shape[0]).astype(jnp.bfloat16)
    token_row = jnp.dot(features, time_full, preferred_element_type=jnp.float32)
    residual_in = jnp.concatenate([token_row[:, None, :], latents.astype(jnp.float32)], axis=1)
    normed_one, scaled_one, inverse_one = layer_norm(residual_in, self_gain, self_bias)
    normed_one = normed_one.astype(jnp.bfloat16)
    projected = jnp.einsum(
        "bsd,dkc->bskc", normed_one, qkv_full, preferred_element_type=jnp.float32
    )
    heads_here = projected.shape[-1] // head_size
    head_shape = (items_here, seq_len, heads_here, head_size)
    cosine, sine = rope_tables(seq_len, head_size)
    queries = rotate(projected[:, :, 0].reshape(head_shape), cosine, sine).astype(jnp.bfloat16)
    key_rows = rotate(projected[:, :, 1].reshape(head_shape), cosine, sine).astype(jnp.bfloat16)
    value_rows = projected[:, :, 2].reshape(head_shape).astype(jnp.bfloat16)
    open_rows = jnp.zeros((items_here, seq_len), jnp.float32)
    attended, self_logs = attend_forward(queries, key_rows, value_rows, open_rows, block_size)
    attended = attended.reshape(items_here, seq_len, heads_here * head_size).astype(jnp.bfloat16)
    segment = attended
    self_branch = jnp.swapaxes(
        lax.psum_scatter(
            jnp.swapaxes(jnp.dot(segment, self_out_full, preferred_element_type=jnp.float32), 0, 1),
            "mp",
            scatter_dimension=0,
            tiled=True,
        ),
        0,
        1,
    )
    residual_one = lax.dynamic_slice_in_dim(residual_in, first_row, shard_rows, 1) + self_branch
    normed_two, scaled_two, inverse_two = layer_norm(residual_one, cross_gain, cross_bias)
    normed_two_all = lax.all_gather(normed_two.astype(jnp.bfloat16), "mp", axis=1, tiled=True)
    cross_q = (
        jnp.dot(normed_two_all, cross_query_full, preferred_element_type=jnp.float32)
        .astype(jnp.bfloat16)
        .reshape(head_shape)
    )
    context = jnp.einsum(
        "bpc,ckh->bpkh", prompt_tokens, context_full, preferred_element_type=jnp.float32
    ).astype(jnp.bfloat16)
    prompt_slots = prompt_tokens.shape[1]
    context_shape = (items_here, prompt_slots, heads_here, head_size)
    context_keys = context[:, :, 0].reshape(context_shape)
    context_values = context[:, :, 1].reshape(context_shape)
    slot_index = jnp.arange(prompt_slots, dtype=jnp.int32)
    mask_rows = jnp.where(slot_index[None, :] < prompt_lengths[:, None], 0.0, NEG).astype(
        jnp.float32
    )
    crossed, cross_logs = attend_forward(
        cross_q, context_keys, context_values, mask_rows, block_size
    )
    crossed = crossed.reshape(items_here, seq_len, heads_here * head_size).astype(jnp.bfloat16)
    segment = crossed
    cross_branch = jnp.swapaxes(
        lax.psum_scatter(
            jnp.swapaxes(
                jnp.dot(segment, cross_out_full, preferred_element_type=jnp.float32), 0, 1
            ).astype(jnp.bfloat16),
            "mp",
            scatter_dimension=0,
            tiled=True,
        ).astype(jnp.float32),
        0,
        1,
    )
    residual_two = residual_one + cross_branch
    normed_three, scaled_three, inverse_three = layer_norm(residual_two, feed_gain, feed_bias)
    normed_three_all = lax.all_gather(normed_three.astype(jnp.bfloat16), "mp", axis=1, tiled=True)
    gate_up = jnp.einsum(
        "bsd,dkf->bskf", normed_three_all, gate_up_full, preferred_element_type=jnp.float32
    )
    gate_part = gate_up[:, :, 0]
    up_part = gate_up[:, :, 1]
    hidden = (jax.nn.silu(gate_part) * up_part).astype(jnp.bfloat16)
    segment = hidden
    feed_branch = jnp.swapaxes(
        lax.psum_scatter(
            jnp.swapaxes(
                jnp.dot(segment, down_full, preferred_element_type=jnp.float32), 0, 1
            ).astype(jnp.bfloat16),
            "mp",
            scatter_dimension=0,
            tiled=True,
        ).astype(jnp.float32),
        0,
        1,
    )
    output = (residual_two + feed_branch + down_bias).astype(jnp.bfloat16)
    regathered = (
        lax.all_gather(qkv_weight, "dp", axis=0, tiled=True),
        lax.all_gather(self_out_weight, "dp", axis=1, tiled=True),
        lax.all_gather(cross_query_weight, "dp", axis=0, tiled=True),
        lax.all_gather(context_weight, "dp", axis=0, tiled=True),
        lax.all_gather(cross_out_weight, "dp", axis=1, tiled=True),
        lax.all_gather(gate_up_weight, "dp", axis=0, tiled=True),
        lax.all_gather(down_weight, "dp", axis=1, tiled=True),
    )
    (
        qkv_back,
        self_out_back,
        cross_query_back,
        context_back,
        cross_out_back,
        gate_up_back,
        down_back,
    ) = regathered
    grad_rows = lax.all_gather(cotangent, "mp", axis=1, tiled=True)
    grad_hidden = jnp.einsum(
        "bsd,fd->bsf", grad_rows, down_back, preferred_element_type=jnp.float32
    )
    sigmoid_gate = jax.nn.sigmoid(gate_part)
    grad_up = grad_hidden * gate_part * sigmoid_gate
    grad_gate = grad_hidden * up_part * sigmoid_gate * (1.0 + gate_part * (1.0 - sigmoid_gate))
    grad_gate_up = jnp.stack([grad_gate, grad_up], axis=2).astype(jnp.bfloat16)
    down_weight_grad = jnp.einsum(
        "bsf,bsd->fd", hidden, grad_rows, preferred_element_type=jnp.float32
    )
    gate_up_grad = jnp.einsum(
        "bsd,bskf->dkf", normed_three_all, grad_gate_up, preferred_element_type=jnp.float32
    )
    segment = grad_gate_up
    grad_normed_three = jnp.swapaxes(
        lax.psum_scatter(
            jnp.swapaxes(
                jnp.einsum(
                    "bskf,dkf->bsd", segment, gate_up_back, preferred_element_type=jnp.float32
                ),
                0,
                1,
            ).astype(jnp.bfloat16),
            "mp",
            scatter_dimension=0,
            tiled=True,
        ).astype(jnp.float32),
        0,
        1,
    )
    grad_two_norm, feed_gain_part, feed_bias_part = norm_back(
        grad_normed_three, scaled_three, inverse_three, feed_gain
    )
    grad_out_shard = cotangent.astype(jnp.float32)
    down_bias_part = jnp.sum(grad_out_shard, axis=(0, 1))
    grad_residual_two = (grad_out_shard + grad_two_norm).astype(jnp.bfloat16)
    grad_rows_two = lax.all_gather(grad_residual_two, "mp", axis=1, tiled=True)
    grad_crossed = jnp.einsum(
        "bsd,hd->bsh", grad_rows_two, cross_out_back, preferred_element_type=jnp.float32
    ).astype(jnp.bfloat16)
    cross_out_grad = jnp.einsum(
        "bsh,bsd->hd", crossed, grad_rows_two, preferred_element_type=jnp.float32
    )
    grad_cross_q, grad_cross_k, grad_cross_v = attend_backward(
        cross_q,
        context_keys,
        context_values,
        mask_rows,
        cross_logs,
        grad_crossed.reshape(head_shape),
        block_size,
    )
    grad_cross_q = grad_cross_q.reshape(items_here, seq_len, heads_here * head_size).astype(
        jnp.bfloat16
    )
    grad_context = (
        jnp.stack([grad_cross_k, grad_cross_v], axis=2)
        .reshape(items_here, prompt_slots, 2, heads_here * head_size)
        .astype(jnp.bfloat16)
    )
    cross_query_grad = jnp.einsum(
        "bsd,bsh->dh", normed_two_all, grad_cross_q, preferred_element_type=jnp.float32
    )
    context_weight_grad = jnp.einsum(
        "bpc,bpkh->ckh", prompt_tokens, grad_context, preferred_element_type=jnp.float32
    )
    segment = grad_cross_q
    grad_normed_two = jnp.swapaxes(
        lax.psum_scatter(
            jnp.swapaxes(
                jnp.einsum(
                    "bsh,dh->bsd", segment, cross_query_back, preferred_element_type=jnp.float32
                ),
                0,
                1,
            ).astype(jnp.bfloat16),
            "mp",
            scatter_dimension=0,
            tiled=True,
        ).astype(jnp.float32),
        0,
        1,
    )
    grad_one_norm, cross_gain_part, cross_bias_part = norm_back(
        grad_normed_two, scaled_two, inverse_two, cross_gain
    )
    grad_residual_one = (grad_residual_two.astype(jnp.float32) + grad_one_norm).astype(jnp.bfloat16)
    grad_rows_one = lax.all_gather(grad_residual_one, "mp", axis=1, tiled=True)
    grad_attended = jnp.einsum(
        "bsd,hd->bsh", grad_rows_one, self_out_back, preferred_element_type=jnp.float32
    ).astype(jnp.bfloat16)
    self_out_grad = jnp.einsum(
        "bsh,bsd->hd", attended, grad_rows_one, preferred_element_type=jnp.float32
    )
    grad_query, grad_key, grad_value = attend_backward(
        queries,
        key_rows,
        value_rows,
        open_rows,
        self_logs,
        grad_attended.reshape(head_shape),
        block_size,
    )
    grad_query = unrotate(grad_query, cosine, sine)
    grad_key = unrotate(grad_key, cosine, sine)
    grad_projected = (
        jnp.stack([grad_query, grad_key, grad_value], axis=2)
        .reshape(items_here, seq_len, 3, heads_here * head_size)
        .astype(jnp.bfloat16)
    )
    qkv_weight_grad = jnp.einsum(
        "bsd,bskc->dkc", normed_one, grad_projected, preferred_element_type=jnp.float32
    )
    grad_normed_part = jnp.einsum(
        "bskc,dkc->bsd", grad_projected, qkv_back, preferred_element_type=jnp.float32
    )
    summed = (
        lax.psum(grad_normed_part.astype(jnp.bfloat16), "mp").astype(jnp.float32),
        lax.psum(cross_gain_part.astype(jnp.bfloat16), "mp").astype(jnp.float32),
        lax.psum(cross_bias_part.astype(jnp.bfloat16), "mp").astype(jnp.float32),
        lax.psum(feed_gain_part.astype(jnp.bfloat16), "mp").astype(jnp.float32),
        lax.psum(feed_bias_part.astype(jnp.bfloat16), "mp").astype(jnp.float32),
        lax.psum(down_bias_part.astype(jnp.bfloat16), "mp").astype(jnp.float32),
    )
    grad_in_norm, self_gain_part, self_bias_part = norm_back(
        summed[0], scaled_one, inverse_one, self_gain
    )
    grad_residual_in = grad_rows_one.astype(jnp.float32) + grad_in_norm
    latents_grad = grad_residual_in[:, 1:].astype(jnp.bfloat16)
    time_weight_grad = jnp.dot(
        features.astype(jnp.float32).T, grad_residual_in[:, 0], precision=lax.Precision.HIGHEST
    )
    cross_gain_sum, cross_bias_sum, feed_gain_sum, feed_bias_sum, down_bias_sum = (
        summed[1],
        summed[2],
        summed[3],
        summed[4],
        summed[5],
    )
    reduced = (
        lax.psum_scatter(
            time_weight_grad.astype(jnp.bfloat16), "dp", scatter_dimension=0, tiled=True
        ).astype(jnp.float32),
        lax.psum_scatter(
            qkv_weight_grad.astype(jnp.bfloat16), "dp", scatter_dimension=0, tiled=True
        ).astype(jnp.float32),
        lax.psum_scatter(
            self_out_grad.astype(jnp.bfloat16), "dp", scatter_dimension=1, tiled=True
        ).astype(jnp.float32),
        lax.psum_scatter(
            cross_query_grad.astype(jnp.bfloat16), "dp", scatter_dimension=0, tiled=True
        ).astype(jnp.float32),
        lax.psum_scatter(
            context_weight_grad.astype(jnp.bfloat16), "dp", scatter_dimension=0, tiled=True
        ).astype(jnp.float32),
        lax.psum_scatter(
            cross_out_grad.astype(jnp.bfloat16), "dp", scatter_dimension=1, tiled=True
        ).astype(jnp.float32),
        lax.psum_scatter(
            gate_up_grad.astype(jnp.bfloat16), "dp", scatter_dimension=0, tiled=True
        ).astype(jnp.float32),
        lax.psum_scatter(
            down_weight_grad.astype(jnp.bfloat16), "dp", scatter_dimension=1, tiled=True
        ).astype(jnp.float32),
        lax.psum_scatter(
            self_gain_part.astype(jnp.bfloat16), "dp", scatter_dimension=0, tiled=True
        ).astype(jnp.float32),
        lax.psum_scatter(
            self_bias_part.astype(jnp.bfloat16), "dp", scatter_dimension=0, tiled=True
        ).astype(jnp.float32),
        lax.psum_scatter(
            cross_gain_sum.astype(jnp.bfloat16), "dp", scatter_dimension=0, tiled=True
        ).astype(jnp.float32),
        lax.psum_scatter(
            cross_bias_sum.astype(jnp.bfloat16), "dp", scatter_dimension=0, tiled=True
        ).astype(jnp.float32),
        lax.psum_scatter(
            feed_gain_sum.astype(jnp.bfloat16), "dp", scatter_dimension=0, tiled=True
        ).astype(jnp.float32),
        lax.psum_scatter(
            feed_bias_sum.astype(jnp.bfloat16), "dp", scatter_dimension=0, tiled=True
        ).astype(jnp.float32),
        lax.psum_scatter(
            down_bias_sum.astype(jnp.bfloat16), "dp", scatter_dimension=0, tiled=True
        ).astype(jnp.float32),
    )
    return (
        output,
        latents_grad,
        reduced[0],
        reduced[8],
        reduced[9],
        reduced[1],
        reduced[2],
        reduced[10],
        reduced[11],
        reduced[3],
        reduced[4],
        reduced[5],
        reduced[12],
        reduced[13],
        reduced[6],
        reduced[7],
        reduced[14],
    )


AXES = ("dp", "mp")
BF = jnp.bfloat16
F32 = jnp.float32


def flat_permutation(places):
    pairs = []
    for d in range(8):
        for z in range(4):
            target = places(d >> 1, d & 1, z & 1, z >> 1)
            if target is not None:
                s, c, zz, p = target
                pairs.append(((2 * s + c) * 4 + 2 * p + zz, (2 * (d >> 1) + (d & 1)) * 4 + z))
    return [(source, target) for target, source in pairs]


SWAP_CORE = flat_permutation(lambda s, c, zz, p: (s, 1 - c, zz, p))
SWAP_Z = flat_permutation(lambda s, c, zz, p: (s, c, 1 - zz, p))
SWAP_PAIR = flat_permutation(lambda s, c, zz, p: (s, c, zz, 1 - p))
SWAP_X = flat_permutation(lambda s, c, zz, p: (s ^ 1, c, zz, p))
SWAP_Y = flat_permutation(lambda s, c, zz, p: (s ^ 2, c, zz, p))
ROUTE_A = flat_permutation(lambda s, c, zz, p: (s, p, zz, c))
ROUTE_B = flat_permutation(lambda s, c, zz, p: (s, p, zz, 1 - c))
RETURN_B = flat_permutation(lambda s, c, zz, p: (s, 1 - p, zz, c))
OWNER_TO_PARTNER = flat_permutation(lambda s, c, zz, p: (s, 1 - c, zz, p) if c == p else None)
PARTNER_TO_OWNER = flat_permutation(lambda s, c, zz, p: (s, 1 - c, zz, p) if c != p else None)
OWNER_TO_PAIR = flat_permutation(lambda s, c, zz, p: (s, c, zz, 1 - p) if c == p else None)
OWNER_Z = flat_permutation(lambda s, c, zz, p: (s, c, 1 - zz, p) if c == p else None)
PARTNER_Z = flat_permutation(lambda s, c, zz, p: (s, c, 1 - zz, p) if c != p else None)


def move(values, pairs):
    return lax.ppermute(values, AXES, pairs)


def xor_blocks(values, axis, count, index):
    blocks = jnp.split(values, count, axis=axis)
    bit = 1
    while bit < count:
        flip = (index & bit) != 0
        blocks = [jnp.where(flip, blocks[j ^ bit], blocks[j]) for j in range(count)]
        bit *= 2
    return jnp.concatenate(blocks, axis=axis)


def attend_pair(head_size, query_block, queries, keys, values, bias, o_ref, log_ref):
    scale = head_size ** (-0.5)
    length, width = queries.shape
    key_rows = keys[...]
    values_turned = values[...].astype(F32).T.astype(BF)
    lane = lax.broadcasted_iota(jnp.int32, (query_block, width), 1)

    @pl.loop(0, length // query_block)
    def _(step):
        rows = pl.ds(pl.multiple_of(step * query_block, query_block), query_block)
        block = queries[rows, :]
        parts, logs = [], []
        for head in range(2):
            mine = (lane >= head * head_size) & (lane < (head + 1) * head_size)
            masked = jnp.where(mine, block, jnp.zeros_like(block))
            scores = lax.dot_general(
                key_rows, masked, (((1,), (1,)), ((), ())), preferred_element_type=F32
            )
            scores = scores * scale
            if bias is not None:
                scores = scores + bias[...]
            top = jnp.max(scores, axis=0, keepdims=True)
            expos = jnp.exp(scores - top)
            total = jnp.sum(expos, axis=0, keepdims=True)
            mixed = lax.dot_general(
                values_turned[head * head_size : (head + 1) * head_size, :],
                expos.astype(BF),
                (((1,), (0,)), ((), ())),
                preferred_element_type=F32,
            )
            parts.append(mixed * (1.0 / total))
            logs.append(top + jnp.log(total))
        o_ref[rows, :] = jnp.concatenate(parts, axis=0).T.astype(BF)
        log_ref[0, :, rows] = jnp.concatenate(logs, axis=0)


def cross_attention_kernel(q_ref, k_ref, v_ref, bias_ref, o_ref, log_ref):
    attend_pair(HD, 512, q_ref, k_ref, v_ref, bias_ref, o_ref, log_ref)


def self_attention_kernel(load, *refs):
    res_ref, gain_ref, bias_ref, w_ref, cos_ref, low_ref, high_ref, part_ref = refs[:8]
    n_ref, q_ref, k_ref, v_ref, o_ref, log_ref, own_ref = refs[8:15]
    projected = refs[15]
    here = pl.program_id(0)
    place = Place()
    carried = load.begin(place, [part_ref], [own_ref], refs[16:])
    length, width = res_ref.shape
    total = w_ref.shape[1]
    block = 256

    @pl.when(here == 0)
    def _():
        greet(load.peers(place, [place.core_peer]))
        for each in carried:
            each.start()

        @pl.loop(0, length // 16)
        def _(step):
            rows = pl.ds(pl.multiple_of(step * 16, 16), 16)
            values = res_ref[rows, :]
            centered = values - jnp.mean(values, axis=-1, keepdims=True)
            inverse = lax.rsqrt(jnp.mean(centered * centered, axis=-1, keepdims=True) + EPS)
            n_ref[rows, :] = (centered * inverse * gain_ref[...] + bias_ref[...]).astype(BF)

        for part in range(3):
            columns = pl.ds(part * (total // 3), total // 3)

            @pl.loop(0, length // block)
            def _(step):
                rows = pl.ds(pl.multiple_of(step * block, block), block)
                projected[rows, columns] = jnp.dot(
                    n_ref[rows, :], w_ref[:, columns], preferred_element_type=F32
                )

    half = HD // 4

    def turn(first, target):
        columns = pl.ds(pl.multiple_of(first + here * 128, 128), 128)

        @pl.loop(0, length // block)
        def _(step):
            rows = pl.ds(pl.multiple_of(step * block, block), block)
            values = projected[rows, columns]
            target[rows, :] = (
                values * cos_ref[rows, :]
                + pltpu.roll(values, 128 - half, 1) * low_ref[rows, :]
                + pltpu.roll(values, half, 1) * high_ref[rows, :]
            ).astype(BF)

    turn(0, q_ref)
    turn(total // 3, k_ref)
    v_ref[...] = projected[
        :, pl.ds(pl.multiple_of(2 * (total // 3) + here * 128, 128), 128)
    ].astype(BF)
    attend_pair(HD, block, q_ref, k_ref, v_ref, None, o_ref, log_ref)

    @pl.when(here == pl.num_programs(0) - 1)
    def _():
        for each in carried:
            each.finish()


def attention_backward_kernel(head_size, query_block, turned, load, *refs):
    if turned:
        refs = list(refs)
        q_ref, k_ref, v_ref, d_ref, log_ref, cos_ref, low_ref, high_ref = refs[:8]
        more = (len(load.operands), len(load.outs_like))
        refs = refs[8:]
        load_ins, g_ref, refs = refs[: more[0]], refs[more[0]], refs[more[0] + 1 :]
        load_outs, refs = refs[: more[1]], refs[more[1] :]
        dk_acc, dv_acc = refs[:2]
        place = Place()
        carried = load.begin(place, load_ins, load_outs, refs[2:])

        @pl.when(pl.program_id(0) == 0)
        def _():
            greet(load.peers(place, [place.core_peer]))
            for each in carried:
                each.start()
    else:
        q_ref, k_ref, v_ref, d_ref, log_ref, bias_ref, dq_ref, g_ref, dk_acc, dv_acc = refs
    scale = head_size ** (-0.5)
    length, width = q_ref.shape
    key_count = k_ref.shape[0]
    here = pl.program_id(0)
    half = head_size // 4
    key_rows = k_ref[...]
    value_rows = v_ref[...]
    keys_turned = key_rows.astype(F32).T.astype(BF)
    lane = lax.broadcasted_iota(jnp.int32, (query_block, width), 1)
    dk_acc[...] = jnp.zeros_like(dk_acc)
    dv_acc[...] = jnp.zeros_like(dv_acc)

    def back_turn(values, rows):
        return (
            values * cos_ref[rows, :]
            - pltpu.roll(values, width - half, 1) * low_ref[rows, :]
            - pltpu.roll(values, half, 1) * high_ref[rows, :]
        )

    @pl.loop(0, length // query_block)
    def _(step):
        rows = pl.ds(pl.multiple_of(step * query_block, query_block), query_block)
        block = q_ref[rows, :]
        grads = d_ref[rows, :]
        parts = []
        for head in range(2):
            mine = (lane >= head * head_size) & (lane < (head + 1) * head_size)
            q_mine = jnp.where(mine, block, jnp.zeros_like(block))
            d_mine = jnp.where(mine, grads, jnp.zeros_like(grads))
            scores = lax.dot_general(
                key_rows, q_mine, (((1,), (1,)), ((), ())), preferred_element_type=F32
            )
            scores = scores * scale
            if not turned:
                scores = scores + bias_ref[...]
            probs = jnp.exp(scores - log_ref[0, head : head + 1, rows])
            grad_probs = lax.dot_general(
                value_rows, d_mine, (((1,), (1,)), ((), ())), preferred_element_type=F32
            )
            delta = jnp.sum(probs * grad_probs, axis=0, keepdims=True)
            grad_scores = (probs * (grad_probs - delta)).astype(BF)
            dv_acc[...] += jnp.dot(probs.astype(BF), d_mine, preferred_element_type=F32)
            dk_acc[...] += jnp.dot(grad_scores, q_mine, preferred_element_type=F32)
            parts.append(
                jnp.dot(
                    keys_turned[head * head_size : (head + 1) * head_size, :],
                    grad_scores,
                    preferred_element_type=F32,
                )
            )
        grad_query = jnp.concatenate(parts, axis=0).T * scale
        if turned:
            columns = pl.ds(pl.multiple_of(here * width, width), width)
            g_ref[rows, columns] = back_turn(grad_query, rows).astype(BF)
        else:
            dq_ref[rows, :] = grad_query.astype(BF)

    total_width = g_ref.shape[1] // (3 if turned else 2)
    first = total_width if turned else 0
    key_columns = pl.ds(pl.multiple_of(first + here * width, width), width)
    value_columns = pl.ds(pl.multiple_of(first + total_width + here * width, width), width)
    if turned:

        @pl.loop(0, key_count // query_block)
        def _(step):
            rows = pl.ds(pl.multiple_of(step * query_block, query_block), query_block)
            g_ref[rows, key_columns] = back_turn(dk_acc[rows, :] * scale, rows).astype(BF)
            g_ref[rows, value_columns] = dv_acc[rows, :].astype(BF)

        @pl.when(here == pl.num_programs(0) - 1)
        def _():
            for each in carried:
                each.finish()
    else:
        g_ref[:, key_columns] = (dk_acc[...] * scale).astype(BF)
        g_ref[:, value_columns] = dv_acc[...].astype(BF)


def self_attention(place, residual, gain, bias, weight, tables, part):
    length, width = residual.shape
    total = weight.shape[1]
    pairs = total // 3 // 128
    load = Loads((Spread, part))
    block = pl.BlockSpec((length, 128), lambda i: (0, i))
    fixed = pl.BlockSpec((length, 128), lambda i: (0, 0))
    whole = pl.BlockSpec(memory_space=pltpu.VMEM)
    wide = jax.ShapeDtypeStruct((length, total // 3), BF)
    return pl.pallas_call(
        functools.partial(self_attention_kernel, load),
        grid=(pairs,),
        in_specs=[whole] * 4 + [fixed] * 3 + [ANYWHERE],
        out_specs=[pl.BlockSpec((length, width), lambda i: (0, 0))]
        + [block] * 4
        + [pl.BlockSpec((1, 2, length), lambda i: (i, 0, 0)), ANYWHERE],
        out_shape=[jax.ShapeDtypeStruct((length, width), BF)]
        + [wide] * 4
        + [jax.ShapeDtypeStruct((pairs, 2, length), F32)]
        + load.outs_like,
        scratch_shapes=[pltpu.VMEM((length, total), F32)] + load.scratch,
        compiler_params=pltpu.CompilerParams(
            collective_id=place, has_side_effects=True, vmem_limit_bytes=60 * 2**20
        ),
        cost_estimate=pl.CostEstimate(
            flops=4 * length * length * total // 3 + 2 * length * width * total,
            transcendentals=length * length * total // 192,
            bytes_accessed=100_000_000,
        ),
        name="self_attention",
    )(residual, gain[None], bias[None], weight, *tables, part)


def self_attention_back(place, queries, keys, values, grads, logs, tables, load):
    length, total = queries.shape
    pairs = total // 128
    block = pl.BlockSpec((length, 128), lambda i: (0, i))
    fixed = pl.BlockSpec((length, 128), lambda i: (0, 0))
    return pl.pallas_call(
        functools.partial(attention_backward_kernel, HD, 256, True, load),
        grid=(pairs,),
        in_specs=[block] * 4
        + [pl.BlockSpec((1, 2, length), lambda i: (i, 0, 0))]
        + [fixed] * 3
        + [ANYWHERE] * len(load.operands),
        out_specs=[pl.BlockSpec((length, 3 * total), lambda i: (0, 0))]
        + [ANYWHERE] * len(load.outs_like),
        out_shape=[jax.ShapeDtypeStruct((length, 3 * total), BF)] + load.outs_like,
        scratch_shapes=[pltpu.VMEM((length, 128), F32)] * 2 + load.scratch,
        compiler_params=pltpu.CompilerParams(collective_id=place, has_side_effects=True),
        cost_estimate=pl.CostEstimate(
            flops=10 * length * length * total,
            transcendentals=length * length * total // 64,
            bytes_accessed=100_000_000,
        ),
        name="self_attention_back",
    )(queries, keys, values, grads, logs, *tables, *load.operands)


def cross_attention(queries, context, bias):
    length, total = queries.shape
    slots = context.shape[0]
    pairs = total // 128
    block = pl.BlockSpec((length, 128), lambda i: (0, i))
    key_block = lambda shift: pl.BlockSpec((slots, 128), lambda i: (0, i + shift))
    return pl.pallas_call(
        cross_attention_kernel,
        grid=(pairs,),
        in_specs=[block, key_block(0), key_block(pairs), pl.BlockSpec((slots, 1), lambda i: (0, 0))],
        out_specs=[block, pl.BlockSpec((1, 2, length), lambda i: (i, 0, 0))],
        out_shape=[
            jax.ShapeDtypeStruct((length, total), BF),
            jax.ShapeDtypeStruct((pairs, 2, length), F32),
        ],
        cost_estimate=pl.CostEstimate(
            flops=4 * length * slots * total,
            transcendentals=length * slots * total // 64,
            bytes_accessed=length * total * 4,
        ),
        name="cross_attention",
    )(queries, context, context, bias)


def cross_attention_back(queries, context, bias, grads, logs):
    length, total = queries.shape
    slots = context.shape[0]
    pairs = total // 128
    block = pl.BlockSpec((length, 128), lambda i: (0, i))
    key_block = lambda shift: pl.BlockSpec((slots, 128), lambda i: (0, i + shift))
    return pl.pallas_call(
        functools.partial(attention_backward_kernel, HD, 512, False, None),
        grid=(pairs,),
        in_specs=[
            block,
            key_block(0),
            key_block(pairs),
            block,
            pl.BlockSpec((1, 2, length), lambda i: (i, 0, 0)),
            pl.BlockSpec((slots, 1), lambda i: (0, 0)),
        ],
        out_specs=[block, pl.BlockSpec((slots, 2 * total), lambda i: (0, 0))],
        out_shape=[
            jax.ShapeDtypeStruct((length, total), BF),
            jax.ShapeDtypeStruct((slots, 2 * total), BF),
        ],
        scratch_shapes=[pltpu.VMEM((slots, 128), F32)] * 2,
        cost_estimate=pl.CostEstimate(
            flops=10 * length * slots * total,
            transcendentals=length * slots * total // 64,
            bytes_accessed=length * total * 8,
        ),
        name="cross_attention_back",
    )(queries, context, context, grads, logs, bias)


def dot_nn(left, right):
    return lax.dot_general(left, right, (((1,), (0,)), ((), ())), preferred_element_type=F32)


def dot_nt(left, right):
    return lax.dot_general(left, right, (((1,), (1,)), ((), ())), preferred_element_type=F32)


def dot_tn(left, right):
    return lax.dot_general(left, right, (((0,), (0,)), ((), ())), preferred_element_type=F32)


PLANE = [[0, 2, 4, 6], [1, 3, 5, 7]]


def group_sum(partial):
    rows = partial.shape[0] // 2
    half = partial[:rows].astype(F32) + move(partial[rows:], SWAP_CORE).astype(F32)
    half = half.astype(BF)
    return half.astype(F32) + move(half, SWAP_Z).astype(F32)


def both_halves(half):
    return jnp.concatenate([half, move(half, SWAP_CORE)], axis=0)


def weight_order(one, two, pair):
    first = jnp.where(pair == 0, one, two)
    second = jnp.where(pair == 0, two, one)
    return jnp.concatenate([first, second], axis=0)


def plane_gather(mine):
    return lax.all_gather(mine, "dp", axis=0, tiled=True, axis_index_groups=PLANE)


def plane_sum(grad):
    return lax.psum_scatter(
        grad, "dp", scatter_dimension=0, tiled=True, axis_index_groups=PLANE
    )


def to_owners(total, pair):
    rows = total.shape[0] // 2
    first, second = total[:rows], total[rows:]
    one = move(jnp.where(pair == 0, first, second), ROUTE_A)
    two = move(jnp.where(pair == 0, second, first), RETURN_B)
    return one.astype(F32) + two.astype(F32)


def after(values, *others):
    return lax.optimization_barrier((values, *others))[0]


class Place:
    def __init__(self):
        d = lax.axis_index("dp")
        z = lax.axis_index("mp")
        self.d, self.z = d, z
        self.core = lax.rem(d, 2)
        self.column = d // 2
        self.pair = z // 2
        self.owner = self.core == self.pair
        self.core_peer = (d + 1 - 2 * self.core, z)
        self.near_z = (d, z + 1 - 2 * lax.rem(z, 2))
        self.far_z = z + 2 - 4 * self.pair
        self.far_same = (d, self.far_z)
        self.far_other = (self.core_peer[0], self.far_z)
        self.user = (2 * self.column + self.pair, self.far_z)
        self.x_peer = (d + 2 - 4 * lax.rem(self.column, 2), z)
        self.y_peer = (d + 4 - 8 * (self.column // 2), z)
        self.x_column = self.column + 1 - 2 * lax.rem(self.column, 2)
        self.y_column = self.column + 2 - 4 * (self.column // 2)


def greet(peers):
    barrier = pltpu.get_barrier_semaphore()
    for peer in peers:
        pl.semaphore_signal(
            barrier, inc=1, device_id=peer, device_id_type=pl.DeviceIdType.MESH
        )
    pl.semaphore_wait(barrier, len(peers))


def send(source, target, sent, got, peer):
    return pltpu.make_async_remote_copy(
        src_ref=source,
        dst_ref=target,
        send_sem=sent,
        recv_sem=got,
        device_id=peer,
        device_id_type=pl.DeviceIdType.MESH,
    )


class Spread:
    scratch = [pltpu.SemaphoreType.DMA((2,)), pltpu.SemaphoreType.DMA((3,)), pltpu.SemaphoreType.DMA]
    late = True

    @staticmethod
    def outs(part):
        return [jax.ShapeDtypeStruct((2 * part.shape[0], part.shape[1]), BF)]

    @staticmethod
    def peers(place):
        return [place.far_same, place.far_other]

    def __init__(self, place, ins, outs, sems):
        self.place = place
        (self.part,), (self.own,), (self.sent, self.got, self.here) = ins, outs, sems

    def target(self, sender):
        rows = self.part.shape[0]
        return self.own.at[pl.ds(pl.multiple_of(sender * rows, rows), rows)]

    def far(self, sender):
        return send(
            self.part, self.target(sender), self.sent.at[0], self.got.at[sender], self.place.user
        )

    def near(self, sender):
        return send(
            self.part, self.target(sender), self.sent.at[1], self.got.at[2], self.place.core_peer
        )

    def local(self):
        return pltpu.make_async_copy(self.part, self.target(self.place.core), self.here)

    def start(self):
        place = self.place
        self.far(place.core).start()

        @pl.when(place.owner)
        def _():
            self.local().start()

        @pl.when(jnp.logical_not(place.owner))
        def _():
            self.near(place.core).start()

    def middle(self):
        pass

    def finish(self):
        place = self.place

        @pl.when(place.owner)
        def _():
            self.local().wait()
            self.near(1 - place.core).wait_recv()

        @pl.when(jnp.logical_not(place.owner))
        def _():
            self.near(place.core).wait_send()
            self.far(0).wait_recv()
            self.far(1).wait_recv()

        self.far(place.core).wait_send()


class Plane:
    scratch = [
        pltpu.SemaphoreType.DMA((2, 3)),
        pltpu.SemaphoreType.DMA((2, 3)),
        pltpu.SemaphoreType.DMA,
    ]
    late = False

    @staticmethod
    def outs(own):
        return [jax.ShapeDtypeStruct((4 * own.shape[0], own.shape[1]), BF)]

    @staticmethod
    def peers(place):
        return [place.x_peer, place.y_peer]

    def __init__(self, place, ins, outs, sems):
        self.place = place
        (self.own,), (self.full,), (self.sent, self.got, self.here) = ins, outs, sems
        self.rows = self.own.shape[0] // 2

    def target(self, column, part):
        rows = self.rows
        return self.full.at[pl.ds(pl.multiple_of((2 * column + part) * rows, rows), rows)]

    def one(self, way, part):
        place = self.place
        peer = place.x_peer if way == 0 else place.y_peer
        return send(
            self.own.at[pl.ds(part * self.rows, self.rows)],
            self.target(place.column, part),
            self.sent.at[way, part],
            self.got.at[way, part],
            peer,
        )

    def two(self, way):
        place = self.place
        if way == 0:
            spot = self.target(place.y_column, 1)
            return send(spot, spot, self.sent.at[0, 2], self.got.at[0, 2], place.x_peer)
        spot = self.target(place.x_column, 0)
        return send(spot, spot, self.sent.at[1, 2], self.got.at[1, 2], place.y_peer)

    def local(self):
        rows = self.own.shape[0]
        place = self.full.at[pl.ds(pl.multiple_of(self.place.column * rows, rows), rows)]
        return pltpu.make_async_copy(self.own, place, self.here)

    def start(self):
        for way in range(2):
            self.one(way, way).start()
        for way in range(2):
            self.one(way, 1 - way).start()
        self.local().start()

    def middle(self):
        self.one(0, 0).wait_recv()
        self.two(1).start()
        self.one(1, 1).wait_recv()
        self.two(0).start()

    def finish(self):
        self.local().wait()
        for way in range(2):
            self.one(way, 1 - way).wait_recv()
            self.two(way).wait_recv()
            self.two(way).wait_send()
            for part in range(2):
                self.one(way, part).wait_send()


class Return:
    scratch = [pltpu.SemaphoreType.DMA((2,)), pltpu.SemaphoreType.DMA((2,))]
    late = True

    @staticmethod
    def outs(total):
        shape = jax.ShapeDtypeStruct((total.shape[0] // 2, total.shape[1]), BF)
        return [shape, shape]

    @staticmethod
    def peers(place):
        return [place.far_same, place.far_other]

    def __init__(self, place, ins, outs, sems):
        self.place = place
        (self.total,), (self.near, self.far), (self.sent, self.got) = ins, outs, sems

    def part(self, which):
        rows = self.near.shape[0]
        return self.total.at[pl.ds(pl.multiple_of(which * rows, rows), rows)]

    def to_near(self):
        place = self.place
        return send(
            self.part(1 - place.core), self.near, self.sent.at[0], self.got.at[0], place.core_peer
        )

    def to_far(self, same):
        place = self.place
        which = place.core if same else 1 - place.core
        peer = place.far_same if same else place.far_other
        return send(
            self.part(which), self.far, self.sent.at[0 if same else 1], self.got.at[1], peer
        )

    def start(self):
        place = self.place

        @pl.when(place.owner)
        def _():
            self.to_near().start()

        @pl.when(jnp.logical_not(place.owner))
        def _():
            self.to_far(True).start()
            self.to_far(False).start()

    def middle(self):
        pass

    def finish(self):
        place = self.place

        @pl.when(place.owner)
        def _():
            self.to_near().wait_send()
            self.to_far(True).wait_recv()

        @pl.when(jnp.logical_not(place.owner))
        def _():
            self.to_far(True).wait_send()
            self.to_far(False).wait_send()
            self.to_near().wait_recv()
            self.to_far(False).wait_recv()


class Swap:
    scratch = [pltpu.SemaphoreType.DMA, pltpu.SemaphoreType.DMA]
    late = True
    way = None

    @staticmethod
    def outs(values):
        return [jax.ShapeDtypeStruct(values.shape, values.dtype)]

    @classmethod
    def peers(cls, place):
        return {
            "core": [place.core_peer],
            "z": [place.near_z],
            "route": [place.far_same, place.far_other],
        }[cls.way]

    def __init__(self, place, ins, outs, sems):
        self.place = place
        peer = {"core": place.core_peer, "z": place.near_z, "route": place.far_other}[self.way]
        self.copy = send(ins[0], outs[0], sems[0], sems[1], peer)

    def each(self, act):
        if self.way != "route":
            act()
            return

        @pl.when(jnp.logical_not(self.place.owner))
        def _():
            act()

    def start(self):
        self.each(lambda: self.copy.start())

    def middle(self):
        pass

    def finish(self):
        self.each(lambda: self.copy.wait())


class SwapCore(Swap):
    way = "core"


class SwapNear(Swap):
    way = "z"


class SwapRoute(Swap):
    way = "route"


class Loads:
    def __init__(self, *loads):
        self.loads = loads
        self.operands = [operand for _, operand in loads]
        self.outs_like = [out for kind, operand in loads for out in kind.outs(operand)]
        self.scratch = [sem for kind, _ in loads for sem in kind.scratch]

    def peers(self, place, base):
        found = {id(peer): peer for peer in base}
        for kind, _ in self.loads:
            for peer in kind.peers(place):
                found[id(peer)] = peer
        return list(found.values())

    def begin(self, place, ins, outs, sems):
        result, at, sem_at = [], 0, 0
        for (kind, operand), source in zip(self.loads, ins):
            count, sem_count = len(kind.outs(operand)), len(kind.scratch)
            result.append(
                kind(
                    place,
                    [source],
                    outs[at : at + count],
                    sems[sem_at : sem_at + sem_count],
                )
            )
            at, sem_at = at + count, sem_at + sem_count
        return result


ANYWHERE = pl.BlockSpec(memory_space=pl.ANY)


def returned(total, near, far, core, owner):
    rows = near.shape[0]
    mine = jnp.where(core == 0, total[:rows], total[rows:])
    return jnp.where(owner, mine, near).astype(F32) + far.astype(F32)


def exchange_kernel(kind, chunks, load, *refs):
    refs = list(refs)
    place = Place()
    more = (len(load.operands), len(load.outs_like))
    ins, refs = refs[:5], refs[5:]
    load_ins, refs = refs[: more[0]], refs[more[0] :]
    outs, refs = refs[:2], refs[2:]
    load_outs, refs = refs[: more[1]], refs[more[1] :]
    rest, refs = refs[:11], refs[11:]
    if kind == "norm":
        a_ref, w_ref, res_ref, gain_ref, bias_ref = ins
        res_out, all_ref = outs
    else:
        a_ref, w_ref, res_ref, up_ref, gain_ref = ins
        all_ref, sum_ref = outs
    carried = load.begin(place, load_ins, load_outs, refs)
    mine, given, near, half, far, send_near, got_near, send_far, got_far, send_all, got_all = rest
    rows = mine.shape[0]
    width = mine.shape[1]
    chunk = rows // chunks
    core_peer, far_peer = place.core_peer, place.near_z
    copy = send
    greet(load.peers(place, [core_peer, far_peer]))
    for each in carried:
        if not each.late:
            each.start()

    def near_copy(k):
        part = pl.ds(k * chunk, chunk)
        return copy(given.at[part], near.at[part], send_near.at[k], got_near.at[k], core_peer)

    def far_copy(k):
        part = pl.ds(k * chunk, chunk)
        return copy(half.at[part], far.at[part], send_far.at[k], got_far.at[k], far_peer)

    def all_copy(k):
        return copy(
            all_ref.at[pl.ds(k * chunk, chunk)],
            all_ref.at[pl.ds(rows + k * chunk, chunk)],
            send_all.at[k],
            got_all.at[k],
            core_peer,
        )

    block = 2 * chunk
    tile = 256

    def product(first, target, start):
        @pl.loop(0, width // tile)
        def _(step):
            columns = pl.ds(pl.multiple_of(step * tile, tile), tile)
            target[pl.ds(start, block), columns] = lax.dot_general(
                a_ref[pl.ds(first, block), :],
                w_ref[columns, :],
                (((1,), (1,)), ((), ())),
                preferred_element_type=F32,
            ).astype(target.dtype)

    step_rows = 16
    for m in range(chunks // 2):
        product(rows + m * block, given, m * block)
        for k in (2 * m, 2 * m + 1):
            near_copy(k).start()
        product(m * block, mine, m * block)
        for k in (2 * m, 2 * m + 1):
            near_copy(k).wait_recv()

            @pl.loop(0, chunk // step_rows)
            def _(step):
                part = pl.ds(pl.multiple_of(k * chunk + step * step_rows, step_rows), step_rows)
                half[part, :] = (mine[part, :] + near[part, :].astype(F32)).astype(BF)

            far_copy(k).start()
    for each in carried:
        if each.late:
            each.start()
    if kind != "norm":
        sum_ref[...] = jnp.zeros_like(sum_ref)
    for k in range(chunks):
        far_copy(k).wait_recv()

        @pl.loop(0, chunk // step_rows)
        def _(step):
            part = pl.ds(pl.multiple_of(k * chunk + step * step_rows, step_rows), step_rows)
            total = half[part, :].astype(F32) + far[part, :].astype(F32)
            if kind == "norm":
                values = res_ref[part, :] + total
                res_out[part, :] = values
            else:
                values = res_ref[part, :]
            centered = values - jnp.mean(values, axis=-1, keepdims=True)
            inverse = lax.rsqrt(jnp.mean(centered * centered, axis=-1, keepdims=True) + EPS)
            scaled = centered * inverse
            if kind == "norm":
                all_ref[part, :] = (scaled * gain_ref[...] + bias_ref[...]).astype(BF)
            else:
                grad_scaled = total * gain_ref[...]
                first_mean = jnp.mean(grad_scaled, axis=-1, keepdims=True)
                second_mean = jnp.mean(grad_scaled * scaled, axis=-1, keepdims=True)
                grads = inverse * (grad_scaled - first_mean - scaled * second_mean)
                all_ref[part, :] = (up_ref[part, :].astype(F32) + grads).astype(BF)
                product_rows = total * scaled
                sum_ref[0] += product_rows[:8] + product_rows[8:]
                sum_ref[1] += total[:8] + total[8:]

        if k == 1:
            for each in carried:
                each.middle()
        if kind != "half":
            all_copy(k).start()
    for k in range(chunks):
        near_copy(k).wait_send()
        far_copy(k).wait_send()
        if kind != "half":
            all_copy(k).wait_send()
            all_copy(k).wait_recv()
    for each in carried:
        each.finish()


def exchange(kind, place, a, w, residual, *others, load=Loads()):
    length, depth = a.shape
    width = w.shape[0]
    rows = length // 2
    chunks = 4
    whole = pl.BlockSpec(memory_space=pltpu.VMEM)
    if kind == "norm":
        gain, bias = others
        operands = (a, w, residual, gain[None], bias[None])
        outs = [
            jax.ShapeDtypeStruct((rows, width), F32),
            jax.ShapeDtypeStruct((length, width), BF),
        ]
    else:
        up, gain = others
        operands = (a, w, residual, up, gain[None])
        outs = [
            jax.ShapeDtypeStruct((rows if kind == "half" else length, width), BF),
            jax.ShapeDtypeStruct((2, 8, width), F32),
        ]
    specs = [whole] * 5 + [ANYWHERE] * len(load.operands)
    out_specs = [whole] * 2 + [ANYWHERE] * len(load.outs_like)
    operands += tuple(load.operands)
    outs = outs + load.outs_like
    return pl.pallas_call(
        functools.partial(exchange_kernel, kind, chunks, load),
        in_specs=specs,
        out_specs=out_specs,
        out_shape=outs,
        scratch_shapes=[
            pltpu.VMEM((rows, width), F32),
            pltpu.VMEM((rows, width), BF),
            pltpu.VMEM((rows, width), BF),
            pltpu.VMEM((rows, width), BF),
            pltpu.VMEM((rows, width), BF),
        ]
        + [pltpu.SemaphoreType.DMA((chunks,))] * 6
        + load.scratch,
        compiler_params=pltpu.CompilerParams(
            collective_id=place, has_side_effects=True, vmem_limit_bytes=60 * 2**20
        ),
        cost_estimate=pl.CostEstimate(
            flops=2 * length * depth * width,
            transcendentals=0,
            bytes_accessed=100_000_000,
        ),
        name="exchange_" + kind,
    )(*operands)


def spread_kernel(load, chunks, *refs):
    refs = list(refs)
    more = (len(load.operands), len(load.outs_like))
    half_ref, refs = refs[0], refs[1:]
    load_ins, refs = refs[: more[0]], refs[more[0] :]
    (out_ref, token_ref), refs = refs[:2], refs[2:]
    load_outs, refs = refs[: more[1]], refs[more[1] :]
    (sent, got, send_token, got_token), refs = refs[:4], refs[4:]
    place = Place()
    carried = load.begin(place, load_ins, load_outs, refs)
    d, core, pair = place.d, place.core, place.pair
    inner_z = lax.rem(place.z, 2)
    plane_peers = [(lax.rem(d + j, 8), place.z) for j in range(1, 8)]
    greet([place.near_z, place.far_same, place.far_other] + plane_peers)
    rows = half_ref.shape[0]
    chunk = rows // chunks

    def spot(which, k):
        return out_ref.at[pl.ds(pl.multiple_of(which * rows + k * chunk, chunk), chunk)]

    def owner_copy(k, which):
        source = half_ref.at[pl.ds(k * chunk, chunk)]
        return send(source, spot(which, k), sent.at[0, k], got.at[0, k], place.core_peer)

    def pair_copy(k, which):
        source = half_ref.at[pl.ds(k * chunk, chunk)]
        return send(source, spot(which, k), sent.at[1, k], got.at[1, k], place.user)

    def pass_copy(k, which):
        return send(spot(which, k), spot(which, k), sent.at[2, k], got.at[2, k], place.near_z)

    @pl.when(core == inner_z)
    def _():
        for k in range(chunks):
            pair_copy(k, core).start()

    for each in carried:
        each.start()

    @pl.when(core != pair)
    def _():
        for k in range(chunks):
            owner_copy(k, core).start()

    @pl.when(core == pair)
    def _():
        @pl.loop(0, rows // 16)
        def _(step):
            first = pl.multiple_of(step * 16, 16)
            out_ref[pl.ds(pl.multiple_of(core * rows + first, 16), 16), :] = half_ref[
                pl.ds(first, 16), :
            ]

        for k in range(chunks):
            owner_copy(k, 1 - core).wait_recv()

    @pl.when(core != pair)
    def _():
        for k in range(chunks):
            pair_copy(k, inner_z).wait_recv()
            pass_copy(k, inner_z).start()
        for k in range(chunks):
            pass_copy(k, 1 - inner_z).wait_recv()

    head = 16
    token_ref[pl.ds(pl.multiple_of(d * head, head), head), :] = out_ref[pl.ds(0, head), :]

    def token_copy(j, sender):
        return send(
            out_ref.at[pl.ds(0, head)],
            token_ref.at[pl.ds(pl.multiple_of(sender * head, head), head)],
            send_token.at[j - 1],
            got_token.at[j - 1],
            plane_peers[j - 1],
        )

    for j in range(1, 8):
        token_copy(j, d).start()

    @pl.when(core != pair)
    def _():
        for k in range(chunks):
            pass_copy(k, inner_z).wait_send()
            owner_copy(k, core).wait_send()

    @pl.when(core == inner_z)
    def _():
        for k in range(chunks):
            pair_copy(k, core).wait_send()

    for j in range(1, 8):
        token_copy(j, d).wait_send()
        token_copy(j, lax.rem(d + 8 - j, 8)).wait_recv()
    for each in carried:
        each.finish()


def spread_gradient(place, half, load):
    rows, width = half.shape
    chunks = 4
    whole = pl.BlockSpec(memory_space=pltpu.VMEM)
    return pl.pallas_call(
        functools.partial(spread_kernel, load, chunks),
        in_specs=[whole] + [ANYWHERE] * len(load.operands),
        out_specs=[whole] * 2 + [ANYWHERE] * len(load.outs_like),
        out_shape=[
            jax.ShapeDtypeStruct((2 * rows, width), BF),
            jax.ShapeDtypeStruct((8 * 16, width), BF),
        ]
        + load.outs_like,
        scratch_shapes=[
            pltpu.SemaphoreType.DMA((3, chunks)),
            pltpu.SemaphoreType.DMA((3, chunks)),
            pltpu.SemaphoreType.DMA((7,)),
            pltpu.SemaphoreType.DMA((7,)),
        ]
        + load.scratch,
        compiler_params=pltpu.CompilerParams(
            collective_id=place, has_side_effects=True, vmem_limit_bytes=60 * 2**20
        ),
        cost_estimate=pl.CostEstimate(flops=0, transcendentals=0, bytes_accessed=100_000_000),
        name="spread_gradient",
    )(half, *load.operands)


def feed_kernel(n_ref, cot_ref, gate_ref, up_ref, down_ref, hidden_ref, grad_ref):
    here = pl.program_id(0)
    length = n_ref.shape[0]
    tile = gate_ref.shape[1]
    half = grad_ref.shape[1] // 2
    block = 256
    gate_columns = pl.ds(pl.multiple_of(here * tile, tile), tile)
    up_columns = pl.ds(pl.multiple_of(half + here * tile, tile), tile)

    @pl.loop(0, length // block)
    def _(step):
        rows = pl.ds(pl.multiple_of(step * block, block), block)
        gate = jnp.dot(n_ref[rows, :], gate_ref[...], preferred_element_type=F32)
        up = jnp.dot(n_ref[rows, :], up_ref[...], preferred_element_type=F32)
        grad = jnp.dot(cot_ref[rows, :], down_ref[...], preferred_element_type=F32)
        sigmoid = jax.nn.sigmoid(gate)
        silu = gate * sigmoid
        hidden_ref[rows, :] = (silu * up).astype(BF)
        grad_ref[rows, gate_columns] = (
            grad * up * sigmoid * (1.0 + gate * (1.0 - sigmoid))
        ).astype(BF)
        grad_ref[rows, up_columns] = (grad * silu).astype(BF)


def feed_forward(normed, cot, gate_up, down):
    length, width = normed.shape
    hidden_width = down.shape[1]
    tile = 256
    steps = hidden_width // tile
    fixed = pl.BlockSpec((length, width), lambda j: (0, 0))
    return pl.pallas_call(
        feed_kernel,
        grid=(steps,),
        in_specs=[
            fixed,
            fixed,
            pl.BlockSpec((width, tile), lambda j: (0, j)),
            pl.BlockSpec((width, tile), lambda j: (0, j + steps)),
            pl.BlockSpec((width, tile), lambda j: (0, j)),
        ],
        out_specs=[
            pl.BlockSpec((length, tile), lambda j: (0, j)),
            pl.BlockSpec((length, 2 * hidden_width), lambda j: (0, 0)),
        ],
        out_shape=[
            jax.ShapeDtypeStruct((length, hidden_width), BF),
            jax.ShapeDtypeStruct((length, 2 * hidden_width), BF),
        ],
        compiler_params=pltpu.CompilerParams(vmem_limit_bytes=60 * 2**20),
        cost_estimate=pl.CostEstimate(
            flops=6 * length * width * hidden_width,
            transcendentals=length * hidden_width,
            bytes_accessed=30_000_000,
        ),
        name="feed_forward",
    )(normed, cot, gate_up, gate_up, down)


def front_kernel(
    qkv_part,
    side_part,
    latents,
    prompt,
    time_part,
    facts,
    qkv_full,
    side_own,
    latents_too,
    prompt_too,
    time_full,
    facts_full,
    send_far,
    got_far,
    send_near,
    got_near,
    here,
    send_plane,
    got_plane,
    send_swap,
    got_swap,
    send_small,
    got_small,
):
    d = lax.axis_index("dp")
    z = lax.axis_index("mp")
    core = lax.rem(d, 2)
    column = d // 2
    pair = z // 2
    far_z = z + 2 - 4 * pair
    core_peer = (d + 1 - 2 * core, z)
    x_peer = (d + 2 - 4 * lax.rem(column, 2), z)
    y_peer = (d + 4 - 8 * (column // 2), z)
    x_column = column + 1 - 2 * lax.rem(column, 2)
    y_column = column + 2 - 4 * (column // 2)
    owner = core == pair
    barrier = pltpu.get_barrier_semaphore()
    plane_peers = [(lax.rem(d + j, 8), z) for j in range(1, 8)]
    peers = [(d, far_z), (core_peer[0], far_z)] + plane_peers
    for peer in peers:
        pl.semaphore_signal(
            barrier, inc=1, device_id=peer, device_id_type=pl.DeviceIdType.MESH
        )
    pl.semaphore_wait(barrier, len(peers))
    rows = qkv_part.shape[0]
    piece = rows // 2

    def copy(source, target, send, got, peer):
        return pltpu.make_async_remote_copy(
            src_ref=source,
            dst_ref=target,
            send_sem=send,
            recv_sem=got,
            device_id=peer,
            device_id_type=pl.DeviceIdType.MESH,
        )

    def part_copy(k, sender, send, got, peer):
        if k < 2:
            return copy(
                qkv_part.at[pl.ds(k * piece, piece)],
                qkv_full.at[pl.ds((2 * column + sender) * rows + k * piece, piece)],
                send,
                got,
                peer,
            )
        return copy(side_part, side_own.at[pl.ds(sender * rows, rows)], send, got, peer)

    user = 2 * column + pair
    swaps = [
        copy(latents, latents_too, send_swap.at[0], got_swap.at[0], core_peer),
        copy(prompt, prompt_too, send_swap.at[1], got_swap.at[1], core_peer),
    ]
    swaps[0].start()
    far_parts = [
        part_copy(k, core, send_far.at[k], got_far.at[core, k], (user, far_z)) for k in range(3)
    ]
    for part in far_parts:
        part.start()
    near_parts = [
        part_copy(k, core, send_near.at[k], got_near.at[k], core_peer) for k in range(3)
    ]
    own_parts = [
        pltpu.make_async_copy(
            qkv_part, qkv_full.at[pl.ds((2 * column + core) * rows, rows)], here.at[0]
        ),
        pltpu.make_async_copy(side_part, side_own.at[pl.ds(core * rows, rows)], here.at[1]),
    ]

    @pl.when(owner)
    def _():
        for part in own_parts:
            part.start()

    @pl.when(jnp.logical_not(owner))
    def _():
        for part in near_parts:
            part.start()

    swaps[1].start()

    def small_copies(sender, j, peer):
        result = []
        for which, (part, whole) in enumerate(((time_part, time_full), (facts, facts_full))):
            count = part.shape[0]
            place = whole.at[pl.ds(sender * count, count)]
            result.append(
                copy(part, place, send_small.at[which, j - 1], got_small.at[which, j - 1], peer)
            )
        return result

    small_own = [
        pltpu.make_async_copy(
            part, whole.at[pl.ds(d * part.shape[0], part.shape[0])], here.at[2 + which]
        )
        for which, (part, whole) in enumerate(((time_part, time_full), (facts, facts_full)))
    ]
    for part in small_own:
        part.start()
    for j in range(1, 8):
        for part in small_copies(d, j, plane_peers[j - 1]):
            part.start()

    def await_part(k, sender):
        @pl.when(owner)
        def _():
            @pl.when(core == sender)
            def _():
                if k == 0:
                    own_parts[0].wait()
                if k == 2:
                    own_parts[1].wait()

            @pl.when(core != sender)
            def _():
                part_copy(k, sender, send_near.at[k], got_near.at[k], core_peer).wait_recv()

        @pl.when(jnp.logical_not(owner))
        def _():
            part_copy(k, sender, send_far.at[k], got_far.at[sender, k], core_peer).wait_recv()

    def plane_copy(stage, way, k, sender):
        peer = x_peer if way == 0 else y_peer
        if stage == 0:
            source = column
        else:
            source = y_column if way == 0 else x_column
        place = pl.ds((2 * source + sender) * rows + k * piece, piece)
        slot = 4 * stage + 2 * sender + k
        return copy(
            qkv_full.at[place],
            qkv_full.at[place],
            send_plane.at[way, slot],
            got_plane.at[way, slot],
            peer,
        )

    for k in range(2):
        for sender in range(2):
            await_part(k, sender)
            plane_copy(0, 0, k, sender).start()
            plane_copy(0, 1, k, sender).start()
    for k in range(2):
        plane_copy(0, 0, k, 0).wait_recv()
        plane_copy(1, 1, k, 0).start()
        plane_copy(0, 1, k, 1).wait_recv()
        plane_copy(1, 0, k, 1).start()
        plane_copy(0, 0, k, 1).wait_recv()
        plane_copy(0, 1, k, 0).wait_recv()
    for k in range(2):
        plane_copy(1, 1, k, 0).wait_recv()
        plane_copy(1, 0, k, 1).wait_recv()
    for sender in range(2):
        await_part(2, sender)
    for part in swaps:
        part.wait()
    for part in small_own:
        part.wait()
    for j in range(1, 8):
        sender = lax.rem(d + 8 - j, 8)
        for part in small_copies(sender, j, plane_peers[j - 1]):
            part.wait_recv()
        for part in small_copies(d, j, plane_peers[j - 1]):
            part.wait_send()
    for part in far_parts:
        part.wait_send()

    @pl.when(jnp.logical_not(owner))
    def _():
        for part in near_parts:
            part.wait_send()

    for k in range(2):
        for sender in range(2):
            plane_copy(0, 0, k, sender).wait_send()
            plane_copy(0, 1, k, sender).wait_send()
        plane_copy(1, 1, k, 0).wait_send()
        plane_copy(1, 0, k, 1).wait_send()


def front(qkv_part, side_part, latents, prompt, time_part, facts):
    place = pl.BlockSpec(memory_space=pl.ANY)
    rows = qkv_part.shape[0]
    return pl.pallas_call(
        front_kernel,
        in_specs=[place] * 6,
        out_specs=[place] * 6,
        out_shape=(
            jax.ShapeDtypeStruct((8 * rows, qkv_part.shape[1]), BF),
            jax.ShapeDtypeStruct((2 * rows, side_part.shape[1]), BF),
            jax.ShapeDtypeStruct(latents.shape, BF),
            jax.ShapeDtypeStruct(prompt.shape, BF),
            jax.ShapeDtypeStruct((8 * time_part.shape[0], time_part.shape[1]), BF),
            jax.ShapeDtypeStruct((8 * facts.shape[0], facts.shape[1]), facts.dtype),
        ),
        scratch_shapes=[
            pltpu.SemaphoreType.DMA((3,)),
            pltpu.SemaphoreType.DMA((2, 3)),
            pltpu.SemaphoreType.DMA((3,)),
            pltpu.SemaphoreType.DMA((3,)),
            pltpu.SemaphoreType.DMA((4,)),
            pltpu.SemaphoreType.DMA((2, 8)),
            pltpu.SemaphoreType.DMA((2, 8)),
            pltpu.SemaphoreType.DMA((2,)),
            pltpu.SemaphoreType.DMA((2,)),
            pltpu.SemaphoreType.DMA((2, 7)),
            pltpu.SemaphoreType.DMA((2, 7)),
        ],
        compiler_params=pltpu.CompilerParams(collective_id=5, has_side_effects=True),
        cost_estimate=pl.CostEstimate(flops=0, transcendentals=0, bytes_accessed=100_000_000),
        name="front",
    )(qkv_part, side_part, latents, prompt, time_part, facts)


def per_device_paired(
    latents,
    prompt_tokens,
    prompt_lengths,
    timesteps,
    time_weight,
    self_gain,
    self_bias,
    qkv_weight,
    self_out_weight,
    cross_gain,
    cross_bias,
    cross_query_weight,
    context_weight,
    cross_out_weight,
    feed_gain,
    feed_bias,
    gate_up_weight,
    down_weight,
    down_bias,
    cotangent,
):
    d = lax.axis_index("dp")
    z = lax.axis_index("mp")
    core, pair = d & 1, z >> 1
    owner = core == pair
    length = latents.shape[1] + 1
    rows = length // 4
    half_rows = length // 2
    part_rows = qkv_weight.shape[0]
    n = cross_query_weight.shape[1]

    side_part = jnp.concatenate(
        [
            self_out_weight.T,
            cross_query_weight,
            cross_out_weight.T,
            context_weight.reshape(part_rows, -1),
        ],
        axis=1,
    )
    facts = jnp.zeros((8, 128), jnp.int32)
    facts = facts.at[0].set(prompt_lengths[0]).at[1].set(timesteps[0])
    qkv_full, side_own, latents_too, prompt_too, time_full, facts_full = front(
        qkv_weight.reshape(part_rows, -1),
        side_part,
        latents[0],
        prompt_tokens[0],
        time_weight,
        facts,
    )
    side_full = plane_gather(side_own)
    self_out_full = side_full[:, :n]
    cross_query_full = side_full[:, n : 2 * n]
    cross_out_full = side_full[:, 2 * n : 3 * n]
    context_full = side_full[:, 3 * n :].reshape(context_weight.shape[0] * 8, -1)

    item_latents = jnp.where(owner, latents[0], latents_too)
    item_prompt = jnp.where(owner, prompt_tokens[0], prompt_too)
    facts_full = facts_full.reshape(8, 8, 128)[:, :2, 0]
    item_facts = lax.dynamic_index_in_dim(facts_full, d - core + pair, 0, False)
    item_length, item_step = item_facts[0], item_facts[1]
    feature_width = time_full.shape[0]
    item_features = time_features(item_step[None], feature_width).astype(BF)
    token_row = dot_nn(item_features, time_full)
    residual_in = jnp.concatenate([token_row, item_latents.astype(F32)], axis=0)
    residual_in = xor_blocks(residual_in, 0, 2, core)
    residual_mine = residual_in[:half_rows]
    cosine, sine = rope_tables(length, HD)
    quarter = HD // 4
    straight = jnp.ones((length, HD // 2), F32)
    blank = jnp.zeros((length, quarter), F32)
    cosine, sine = cosine[:, 0], sine[:, 0]
    tables = jnp.stack(
        [
            jnp.tile(jnp.concatenate([cosine, straight], axis=1), (1, 2)),
            jnp.tile(
                jnp.concatenate([-sine[:, :quarter], blank, blank, blank], axis=1), (1, 2)
            ),
            jnp.tile(
                jnp.concatenate([blank, sine[:, quarter:], blank, blank], axis=1), (1, 2)
            ),
        ]
    )
    tables = xor_blocks(tables, 1, 2, core)
    tables = (tables[0], tables[1], tables[2])
    normed_one, queries, keys, values, attended, self_logs, gate_up_own = self_attention(
        6, residual_in, self_gain, self_bias, qkv_full, tables, gate_up_weight.reshape(part_rows, -1)
    )
    gate_up_full = plane_gather(gate_up_own)
    cot_shard = move(after(cotangent[0], attended), ROUTE_A)
    residual_one, normed_two_all, down_own = exchange(
        "norm",
        0,
        attended,
        self_out_full,
        residual_mine,
        cross_gain,
        cross_bias,
        load=Loads((Spread, down_weight.T)),
    )
    cot_shard = after(cot_shard, normed_two_all)
    cot_far = move(cot_shard, SWAP_Z)
    odd = (z & 1) == 1
    cross_q = dot_nn(normed_two_all, cross_query_full).astype(BF)
    context = dot_nn(item_prompt, context_full).astype(BF)
    slots = prompt_tokens.shape[1]
    mask = jnp.where(jnp.arange(slots, dtype=jnp.int32)[:, None] < item_length, 0.0, NEG)
    mask = mask.astype(F32)
    crossed, cross_logs = cross_attention(cross_q, context, mask)
    cot_far = after(cot_far, crossed)
    cot_mine = jnp.concatenate(
        [jnp.where(odd, cot_far, cot_shard), jnp.where(odd, cot_shard, cot_far)], axis=0
    )
    cot_other = move(cot_mine, SWAP_CORE)
    residual_two, normed_three_all, down_full = exchange(
        "norm",
        1,
        crossed,
        cross_out_full,
        residual_one,
        feed_gain,
        feed_bias,
        load=Loads((Plane, down_own)),
    )
    cot_all = jnp.concatenate([cot_mine, after(cot_other, normed_three_all)], axis=0)
    hidden, grad_gate_up = feed_forward(normed_three_all, cot_all, gate_up_full, down_full)

    gate_up_local = dot_tn(normed_three_all, grad_gate_up).astype(BF)
    gate_up_sums = plane_sum(gate_up_local)
    split = gate_up_weight.shape[2]
    gate_sums, up_sums = gate_up_sums[:, :split], gate_up_sums[:, split:]
    grad_two_all, feed_sums = exchange(
        "back",
        2,
        after(grad_gate_up, gate_up_local),
        gate_up_full,
        residual_two,
        cot_mine,
        feed_gain,
    )
    down_bias_part = jnp.sum(cot_mine.astype(F32), axis=0)
    hidden = after(hidden, grad_two_all)
    down_local = dot_tn(cot_all, hidden).astype(BF)
    down_sums = plane_sum(down_local)
    feed = dot_nt(hidden, down_full).astype(BF)
    grad_crossed = dot_nn(grad_two_all, cross_out_full).astype(BF)
    grad_cross_q, grad_context = cross_attention_back(
        cross_q, context, mask, grad_crossed, cross_logs
    )
    context_grad = dot_tn(item_prompt, grad_context).astype(BF).reshape(side_full.shape[0], -1)
    cross_out_grad = dot_tn(grad_two_all, crossed).astype(BF)
    cross_query_grad = dot_tn(normed_two_all, grad_cross_q).astype(BF)
    cross_local = jnp.concatenate([cross_query_grad, cross_out_grad, context_grad], axis=1)
    grad_one_all, cross_sums, gate_near, gate_far, feed_near = exchange(
        "back",
        3,
        after(grad_cross_q, down_local, feed),
        cross_query_full,
        residual_one,
        grad_two_all[:half_rows],
        cross_gain,
        load=Loads((Return, gate_sums), (SwapCore, feed[half_rows:])),
    )
    feed_half = feed[:half_rows].astype(F32) + feed_near.astype(F32)
    feed_here = jnp.where(odd, feed_half[rows:], feed_half[:rows])
    feed_away = jnp.where(odd, feed_half[:rows], feed_half[rows:]).astype(BF)
    grad_attended = dot_nn(grad_one_all, self_out_full).astype(BF)
    grad_projected, up_near, up_far, feed_far = self_attention_back(
        7,
        queries,
        keys,
        values,
        grad_attended,
        self_logs,
        tables,
        Loads((Return, up_sums), (SwapNear, feed_away)),
    )
    residual_here = jnp.where(odd, residual_two[rows:], residual_two[:rows])
    output_here = (residual_here + feed_here + feed_far.astype(F32) + down_bias).astype(BF)
    cross_total = plane_sum(cross_local)
    self_out_local = dot_tn(grad_one_all, attended).astype(BF)
    self_out_total = plane_sum(after(self_out_local, cross_total))
    qkv_local = dot_tn(normed_one, grad_projected).astype(BF)
    qkv_total = plane_sum(qkv_local)
    side_total = jnp.concatenate([cross_total, self_out_total], axis=1)
    grad_in, self_sums, down_near, down_far, side_near, side_far, output_far = exchange(
        "half",
        4,
        after(grad_projected, qkv_local),
        qkv_full,
        residual_mine,
        grad_one_all[:half_rows],
        self_gain,
        load=Loads((Return, down_sums), (Return, side_total), (SwapRoute, output_here)),
    )
    whole, token_rows, qkv_near, qkv_far = spread_gradient(
        8, grad_in, Loads((Return, qkv_total))
    )
    output = jnp.where(owner, output_here, output_far)
    latents_grad = whole[1:]

    token_rows = token_rows.reshape(8, 16, -1)[:, 0]
    all_features = time_features(facts_full[:, 1], feature_width).astype(BF)
    my_features = jnp.zeros((8, feature_width // 8), F32)
    for j in range(8):
        piece = all_features[:, j * (feature_width // 8) : (j + 1) * (feature_width // 8)]
        my_features = my_features + jnp.where(d == j, piece.astype(F32), 0.0)
    time_grad = lax.dot_general(
        my_features.astype(BF), token_rows, (((0,), (0,)), ((), ())), preferred_element_type=F32
    )

    sums = jnp.concatenate(
        [
            jnp.sum(self_sums, axis=1),
            jnp.sum(cross_sums, axis=1),
            jnp.sum(feed_sums, axis=1),
            down_bias_part[None],
        ],
        axis=0,
    )
    sums = xor_blocks(sums, 1, 8, d)
    for pairs in (SWAP_Y, SWAP_X, SWAP_CORE):
        middle = sums.shape[1] // 2
        sums = sums[:, :middle] + move(sums[:, middle:], pairs)
    sums = sums + move(sums, SWAP_PAIR)

    side_grads = returned(side_total, side_near, side_far, core, owner)
    qkv_grad = returned(qkv_total, qkv_near, qkv_far, core, owner)
    gate_grad = returned(gate_sums, gate_near, gate_far, core, owner)
    up_grad = returned(up_sums, up_near, up_far, core, owner)
    down_grad = returned(down_sums, down_near, down_far, core, owner)
    return (
        output[None],
        latents_grad[None],
        time_grad,
        sums[0],
        sums[1],
        qkv_grad.reshape(qkv_weight.shape),
        side_grads[:, 2 * n + context_weight.size // part_rows :].T,
        sums[2],
        sums[3],
        side_grads[:, :n],
        side_grads[:, 2 * n : 2 * n + context_weight.size // part_rows].reshape(
            context_weight.shape
        ),
        side_grads[:, n : 2 * n].T,
        sums[4],
        sums[5],
        jnp.stack([gate_grad, up_grad], axis=1),
        down_grad.T,
        sums[6],
    )


def solution(mesh):
    placed = (
        P("dp", None, None),
        P("dp", None, None),
        P("dp"),
        P("dp"),
        P("dp", None),
        P(),
        P(),
        P("dp", None, "mp"),
        P("mp", "dp"),
        P(),
        P(),
        P("dp", "mp"),
        P("dp", None, "mp"),
        P("mp", "dp"),
        P(),
        P(),
        P("dp", None, "mp"),
        P("mp", "dp"),
        P(),
        P("dp", "mp", None),
    )
    paired = mesh.shape["dp"] == 8 and mesh.shape["mp"] == 4
    return jax.shard_map(
        per_device_paired if paired else per_device_general,
        mesh=mesh,
        in_specs=placed,
        out_specs=(
            P("dp", "mp", None),
            P("dp", None, None),
            P("dp", None),
            P("dp"),
            P("dp"),
            P("dp", None, "mp"),
            P("mp", "dp"),
            P("dp"),
            P("dp"),
            P("dp", "mp"),
            P("dp", None, "mp"),
            P("mp", "dp"),
            P("dp"),
            P("dp"),
            P("dp", None, "mp"),
            P("mp", "dp"),
            P("dp"),
        ),
        check_vma=False,
    )
```

```python
import functools
import math

import jax
import jax.numpy as jnp
import numpy as np
from jax import lax
from jax.experimental import pallas as pl
from jax.experimental.pallas import tpu as pltpu
from jax.sharding import PartitionSpec as P

HD = 64


EPS = 1e-05
NEG = -1e30


def time_features(steps_in, feature_width):
    half_width = feature_width // 2
    freqs = jnp.exp(-math.log(10000.0) * jnp.arange(half_width, dtype=jnp.float32) / half_width)
    angles = steps_in.astype(jnp.float32)[:, None] * freqs[None, :]
    return jnp.concatenate([jnp.cos(angles), jnp.sin(angles)], axis=-1)


def rope_tables(length, head_size):
    rotated_width = head_size // 2
    half_width = rotated_width // 2
    inverse = jnp.exp(
        -math.log(10000.0) * jnp.arange(half_width, dtype=jnp.float32) * 2.0 / rotated_width
    )
    angles = jnp.arange(length, dtype=jnp.float32)[:, None] * inverse[None, :]
    cosine = jnp.concatenate([jnp.cos(angles), jnp.cos(angles)], axis=-1)
    sine = jnp.concatenate([jnp.sin(angles), jnp.sin(angles)], axis=-1)
    return (cosine[:, None, :], sine[:, None, :])


def rotate(values, cosine, sine):
    rotated_width = cosine.shape[-1]
    half_width = rotated_width // 2
    first = values[..., :rotated_width]
    turned = jnp.concatenate([-first[..., half_width:], first[..., :half_width]], axis=-1)
    return jnp.concatenate([first * cosine + turned * sine, values[..., rotated_width:]], axis=-1)


def unrotate(grads_in, cosine, sine):
    rotated_width = cosine.shape[-1]
    half_width = rotated_width // 2
    first = grads_in[..., :rotated_width]
    scaled_in = first * sine
    turned = jnp.concatenate([scaled_in[..., half_width:], -scaled_in[..., :half_width]], axis=-1)
    return jnp.concatenate([first * cosine + turned, grads_in[..., rotated_width:]], axis=-1)


def layer_norm(values, gain, bias):
    centered = values - jnp.mean(values, axis=-1, keepdims=True)
    inverse = lax.rsqrt(jnp.mean(centered * centered, axis=-1, keepdims=True) + EPS)
    scaled = centered * inverse
    return (scaled * gain + bias, scaled, inverse)


def norm_back(grad_normed, scaled, inverse, gain):
    grad_scaled = grad_normed * gain
    first_mean = jnp.mean(grad_scaled, axis=-1, keepdims=True)
    second_mean = jnp.mean(grad_scaled * scaled, axis=-1, keepdims=True)
    grad_values = inverse * (grad_scaled - first_mean - scaled * second_mean)
    return (
        grad_values,
        jnp.sum(grad_normed * scaled, axis=(0, 1)),
        jnp.sum(grad_normed, axis=(0, 1)),
    )


def attend_forward(queries, key_rows, value_rows, bias_rows, block_size):
    score_scale = queries.shape[-1] ** (-0.5)

    def one_item(operands):
        item_query, item_key, item_value, item_bias = operands
        query_blocks = item_query.reshape(-1, block_size, item_query.shape[1], item_query.shape[2])

        def one_block(block_query):
            scores = jnp.einsum(
                "qhe,khe->hqk", block_query, item_key, preferred_element_type=jnp.float32
            )
            scores = scores * score_scale + item_bias[None, None, :]
            row_max = jnp.max(scores, axis=-1, keepdims=True)
            expos = jnp.exp(scores - row_max)
            row_total = jnp.sum(expos, axis=-1, keepdims=True)
            weights_p = (expos / row_total).astype(jnp.bfloat16)
            mixed = jnp.einsum(
                "hqk,khe->qhe", weights_p, item_value, preferred_element_type=jnp.float32
            )
            return (mixed, (row_max + jnp.log(row_total))[..., 0])

        mixed, log_total = lax.map(one_block, query_blocks)
        return (mixed.reshape(item_query.shape), log_total)

    return lax.map(one_item, (queries, key_rows, value_rows, bias_rows))


def attend_backward(queries, key_rows, value_rows, bias_rows, log_totals, grad_out, block_size):
    score_scale = queries.shape[-1] ** (-0.5)

    def one_item(operands):
        item_query, item_key, item_value, item_bias, item_log, item_grad = operands
        block_shape = (-1, block_size, item_query.shape[1], item_query.shape[2])
        query_blocks = item_query.reshape(block_shape)
        grad_blocks = item_grad.reshape(block_shape)

        def one_block(carry, operands_block):
            block_query, block_log, block_grad = operands_block
            scores = jnp.einsum(
                "qhe,khe->hqk", block_query, item_key, preferred_element_type=jnp.float32
            )
            scores = scores * score_scale + item_bias[None, None, :]
            probs_full = jnp.exp(scores - block_log[..., None])
            grad_probs = jnp.einsum(
                "qhe,khe->hqk", block_grad, item_value, preferred_element_type=jnp.float32
            )
            delta_row = jnp.sum(probs_full * grad_probs, axis=-1, keepdims=True)
            grad_scores = (probs_full * (grad_probs - delta_row)).astype(jnp.bfloat16)
            grad_query = (
                jnp.einsum(
                    "hqk,khe->qhe", grad_scores, item_key, preferred_element_type=jnp.float32
                )
                * score_scale
            )
            grad_key = (
                carry[0]
                + jnp.einsum(
                    "hqk,qhe->khe", grad_scores, block_query, preferred_element_type=jnp.float32
                )
                * score_scale
            )
            grad_value = carry[1] + jnp.einsum(
                "hqk,qhe->khe",
                probs_full.astype(jnp.bfloat16),
                block_grad,
                preferred_element_type=jnp.float32,
            )
            return ((grad_key, grad_value), grad_query)

        start_carry = (
            jnp.zeros(item_key.shape, jnp.float32),
            jnp.zeros(item_value.shape, jnp.float32),
        )
        (grad_key, grad_value), grad_query = lax.scan(
            one_block, start_carry, (query_blocks, item_log, grad_blocks)
        )
        return (grad_query.reshape(item_query.shape), grad_key, grad_value)

    return lax.map(one_item, (queries, key_rows, value_rows, bias_rows, log_totals, grad_out))


def per_device_general(
    latents,
    prompt_tokens,
    prompt_lengths,
    timesteps,
    time_weight,
    self_gain,
    self_bias,
    qkv_weight,
    self_out_weight,
    cross_gain,
    cross_bias,
    cross_query_weight,
    context_weight,
    cross_out_weight,
    feed_gain,
    feed_bias,
    gate_up_weight,
    down_weight,
    down_bias,
    cotangent,
):
    gathered = (
        lax.all_gather(time_weight, "dp", axis=0, tiled=True),
        lax.all_gather(qkv_weight, "dp", axis=0, tiled=True),
        lax.all_gather(self_out_weight, "dp", axis=1, tiled=True),
        lax.all_gather(cross_query_weight, "dp", axis=0, tiled=True),
        lax.all_gather(context_weight, "dp", axis=0, tiled=True),
        lax.all_gather(cross_out_weight, "dp", axis=1, tiled=True),
        lax.all_gather(gate_up_weight, "dp", axis=0, tiled=True),
        lax.all_gather(down_weight, "dp", axis=1, tiled=True),
    )
    (
        time_full,
        qkv_full,
        self_out_full,
        cross_query_full,
        context_full,
        cross_out_full,
        gate_up_full,
        down_full,
    ) = gathered
    items_here = latents.shape[0]
    seq_len = latents.shape[1] + 1
    shard_rows = seq_len // lax.axis_size("mp")
    first_row = lax.axis_index("mp") * shard_rows
    head_size = HD
    block_size = min(512, seq_len)
    features = time_features(timesteps, time_full.shape[0]).astype(jnp.bfloat16)
    token_row = jnp.dot(features, time_full, preferred_element_type=jnp.float32)
    residual_in = jnp.concatenate([token_row[:, None, :], latents.astype(jnp.float32)], axis=1)
    normed_one, scaled_one, inverse_one = layer_norm(residual_in, self_gain, self_bias)
    normed_one = normed_one.astype(jnp.bfloat16)
    projected = jnp.einsum(
        "bsd,dkc->bskc", normed_one, qkv_full, preferred_element_type=jnp.float32
    )
    heads_here = projected.shape[-1] // head_size
    head_shape = (items_here, seq_len, heads_here, head_size)
    cosine, sine = rope_tables(seq_len, head_size)
    queries = rotate(projected[:, :, 0].reshape(head_shape), cosine, sine).astype(jnp.bfloat16)
    key_rows = rotate(projected[:, :, 1].reshape(head_shape), cosine, sine).astype(jnp.bfloat16)
    value_rows = projected[:, :, 2].reshape(head_shape).astype(jnp.bfloat16)
    open_rows = jnp.zeros((items_here, seq_len), jnp.float32)
    attended, self_logs = attend_forward(queries, key_rows, value_rows, open_rows, block_size)
    attended = attended.reshape(items_here, seq_len, heads_here * head_size).astype(jnp.bfloat16)
    segment = attended
    self_branch = jnp.swapaxes(
        lax.psum_scatter(
            jnp.swapaxes(jnp.dot(segment, self_out_full, preferred_element_type=jnp.float32), 0, 1),
            "mp",
            scatter_dimension=0,
            tiled=True,
        ),
        0,
        1,
    )
    residual_one = lax.dynamic_slice_in_dim(residual_in, first_row, shard_rows, 1) + self_branch
    normed_two, scaled_two, inverse_two = layer_norm(residual_one, cross_gain, cross_bias)
    normed_two_all = lax.all_gather(normed_two.astype(jnp.bfloat16), "mp", axis=1, tiled=True)
    cross_q = (
        jnp.dot(normed_two_all, cross_query_full, preferred_element_type=jnp.float32)
        .astype(jnp.bfloat16)
        .reshape(head_shape)
    )
    context = jnp.einsum(
        "bpc,ckh->bpkh", prompt_tokens, context_full, preferred_element_type=jnp.float32
    ).astype(jnp.bfloat16)
    prompt_slots = prompt_tokens.shape[1]
    context_shape = (items_here, prompt_slots, heads_here, head_size)
    context_keys = context[:, :, 0].reshape(context_shape)
    context_values = context[:, :, 1].reshape(context_shape)
    slot_index = jnp.arange(prompt_slots, dtype=jnp.int32)
    mask_rows = jnp.where(slot_index[None, :] < prompt_lengths[:, None], 0.0, NEG).astype(
        jnp.float32
    )
    crossed, cross_logs = attend_forward(
        cross_q, context_keys, context_values, mask_rows, block_size
    )
    crossed = crossed.reshape(items_here, seq_len, heads_here * head_size).astype(jnp.bfloat16)
    segment = crossed
    cross_branch = jnp.swapaxes(
        lax.psum_scatter(
            jnp.swapaxes(
                jnp.dot(segment, cross_out_full, preferred_element_type=jnp.float32), 0, 1
            ).astype(jnp.bfloat16),
            "mp",
            scatter_dimension=0,
            tiled=True,
        ).astype(jnp.float32),
        0,
        1,
    )
    residual_two = residual_one + cross_branch
    normed_three, scaled_three, inverse_three = layer_norm(residual_two, feed_gain, feed_bias)
    normed_three_all = lax.all_gather(normed_three.astype(jnp.bfloat16), "mp", axis=1, tiled=True)
    gate_up = jnp.einsum(
        "bsd,dkf->bskf", normed_three_all, gate_up_full, preferred_element_type=jnp.float32
    )
    gate_part = gate_up[:, :, 0]
    up_part = gate_up[:, :, 1]
    hidden = (jax.nn.silu(gate_part) * up_part).astype(jnp.bfloat16)
    segment = hidden
    feed_branch = jnp.swapaxes(
        lax.psum_scatter(
            jnp.swapaxes(
                jnp.dot(segment, down_full, preferred_element_type=jnp.float32), 0, 1
            ).astype(jnp.bfloat16),
            "mp",
            scatter_dimension=0,
            tiled=True,
        ).astype(jnp.float32),
        0,
        1,
    )
    output = (residual_two + feed_branch + down_bias).astype(jnp.bfloat16)
    regathered = (
        lax.all_gather(qkv_weight, "dp", axis=0, tiled=True),
        lax.all_gather(self_out_weight, "dp", axis=1, tiled=True),
        lax.all_gather(cross_query_weight, "dp", axis=0, tiled=True),
        lax.all_gather(context_weight, "dp", axis=0, tiled=True),
        lax.all_gather(cross_out_weight, "dp", axis=1, tiled=True),
        lax.all_gather(gate_up_weight, "dp", axis=0, tiled=True),
        lax.all_gather(down_weight, "dp", axis=1, tiled=True),
    )
    (
        qkv_back,
        self_out_back,
        cross_query_back,
        context_back,
        cross_out_back,
        gate_up_back,
        down_back,
    ) = regathered
    grad_rows = lax.all_gather(cotangent, "mp", axis=1, tiled=True)
    grad_hidden = jnp.einsum(
        "bsd,fd->bsf", grad_rows, down_back, preferred_element_type=jnp.float32
    )
    sigmoid_gate = jax.nn.sigmoid(gate_part)
    grad_up = grad_hidden * gate_part * sigmoid_gate
    grad_gate = grad_hidden * up_part * sigmoid_gate * (1.0 + gate_part * (1.0 - sigmoid_gate))
    grad_gate_up = jnp.stack([grad_gate, grad_up], axis=2).astype(jnp.bfloat16)
    down_weight_grad = jnp.einsum(
        "bsf,bsd->fd", hidden, grad_rows, preferred_element_type=jnp.float32
    )
    gate_up_grad = jnp.einsum(
        "bsd,bskf->dkf", normed_three_all, grad_gate_up, preferred_element_type=jnp.float32
    )
    segment = grad_gate_up
    grad_normed_three = jnp.swapaxes(
        lax.psum_scatter(
            jnp.swapaxes(
                jnp.einsum(
                    "bskf,dkf->bsd", segment, gate_up_back, preferred_element_type=jnp.float32
                ),
                0,
                1,
            ).astype(jnp.bfloat16),
            "mp",
            scatter_dimension=0,
            tiled=True,
        ).astype(jnp.float32),
        0,
        1,
    )
    grad_two_norm, feed_gain_part, feed_bias_part = norm_back(
        grad_normed_three, scaled_three, inverse_three, feed_gain
    )
    grad_out_shard = cotangent.astype(jnp.float32)
    down_bias_part = jnp.sum(grad_out_shard, axis=(0, 1))
    grad_residual_two = (grad_out_shard + grad_two_norm).astype(jnp.bfloat16)
    grad_rows_two = lax.all_gather(grad_residual_two, "mp", axis=1, tiled=True)
    grad_crossed = jnp.einsum(
        "bsd,hd->bsh", grad_rows_two, cross_out_back, preferred_element_type=jnp.float32
    ).astype(jnp.bfloat16)
    cross_out_grad = jnp.einsum(
        "bsh,bsd->hd", crossed, grad_rows_two, preferred_element_type=jnp.float32
    )
    grad_cross_q, grad_cross_k, grad_cross_v = attend_backward(
        cross_q,
        context_keys,
        context_values,
        mask_rows,
        cross_logs,
        grad_crossed.reshape(head_shape),
        block_size,
    )
    grad_cross_q = grad_cross_q.reshape(items_here, seq_len, heads_here * head_size).astype(
        jnp.bfloat16
    )
    grad_context = (
        jnp.stack([grad_cross_k, grad_cross_v], axis=2)
        .reshape(items_here, prompt_slots, 2, heads_here * head_size)
        .astype(jnp.bfloat16)
    )
    cross_query_grad = jnp.einsum(
        "bsd,bsh->dh", normed_two_all, grad_cross_q, preferred_element_type=jnp.float32
    )
    context_weight_grad = jnp.einsum(
        "bpc,bpkh->ckh", prompt_tokens, grad_context, preferred_element_type=jnp.float32
    )
    segment = grad_cross_q
    grad_normed_two = jnp.swapaxes(
        lax.psum_scatter(
            jnp.swapaxes(
                jnp.einsum(
                    "bsh,dh->bsd", segment, cross_query_back, preferred_element_type=jnp.float32
                ),
                0,
                1,
            ).astype(jnp.bfloat16),
            "mp",
            scatter_dimension=0,
            tiled=True,
        ).astype(jnp.float32),
        0,
        1,
    )
    grad_one_norm, cross_gain_part, cross_bias_part = norm_back(
        grad_normed_two, scaled_two, inverse_two, cross_gain
    )
    grad_residual_one = (grad_residual_two.astype(jnp.float32) + grad_one_norm).astype(jnp.bfloat16)
    grad_rows_one = lax.all_gather(grad_residual_one, "mp", axis=1, tiled=True)
    grad_attended = jnp.einsum(
        "bsd,hd->bsh", grad_rows_one, self_out_back, preferred_element_type=jnp.float32
    ).astype(jnp.bfloat16)
    self_out_grad = jnp.einsum(
        "bsh,bsd->hd", attended, grad_rows_one, preferred_element_type=jnp.float32
    )
    grad_query, grad_key, grad_value = attend_backward(
        queries,
        key_rows,
        value_rows,
        open_rows,
        self_logs,
        grad_attended.reshape(head_shape),
        block_size,
    )
    grad_query = unrotate(grad_query, cosine, sine)
    grad_key = unrotate(grad_key, cosine, sine)
    grad_projected = (
        jnp.stack([grad_query, grad_key, grad_value], axis=2)
        .reshape(items_here, seq_len, 3, heads_here * head_size)
        .astype(jnp.bfloat16)
    )
    qkv_weight_grad = jnp.einsum(
        "bsd,bskc->dkc", normed_one, grad_projected, preferred_element_type=jnp.float32
    )
    grad_normed_part = jnp.einsum(
        "bskc,dkc->bsd", grad_projected, qkv_back, preferred_element_type=jnp.float32
    )
    summed = (
        lax.psum(grad_normed_part.astype(jnp.bfloat16), "mp").astype(jnp.float32),
        lax.psum(cross_gain_part.astype(jnp.bfloat16), "mp").astype(jnp.float32),
        lax.psum(cross_bias_part.astype(jnp.bfloat16), "mp").astype(jnp.float32),
        lax.psum(feed_gain_part.astype(jnp.bfloat16), "mp").astype(jnp.float32),
        lax.psum(feed_bias_part.astype(jnp.bfloat16), "mp").astype(jnp.float32),
        lax.psum(down_bias_part.astype(jnp.bfloat16), "mp").astype(jnp.float32),
    )
    grad_in_norm, self_gain_part, self_bias_part = norm_back(
        summed[0], scaled_one, inverse_one, self_gain
    )
    grad_residual_in = grad_rows_one.astype(jnp.float32) + grad_in_norm
    latents_grad = grad_residual_in[:, 1:].astype(jnp.bfloat16)
    time_weight_grad = jnp.dot(
        features.astype(jnp.float32).T, grad_residual_in[:, 0], precision=lax.Precision.HIGHEST
    )
    cross_gain_sum, cross_bias_sum, feed_gain_sum, feed_bias_sum, down_bias_sum = (
        summed[1],
        summed[2],
        summed[3],
        summed[4],
        summed[5],
    )
    reduced = (
        lax.psum_scatter(
            time_weight_grad.astype(jnp.bfloat16), "dp", scatter_dimension=0, tiled=True
        ).astype(jnp.float32),
        lax.psum_scatter(
            qkv_weight_grad.astype(jnp.bfloat16), "dp", scatter_dimension=0, tiled=True
        ).astype(jnp.float32),
        lax.psum_scatter(
            self_out_grad.astype(jnp.bfloat16), "dp", scatter_dimension=1, tiled=True
        ).astype(jnp.float32),
        lax.psum_scatter(
            cross_query_grad.astype(jnp.bfloat16), "dp", scatter_dimension=0, tiled=True
        ).astype(jnp.float32),
        lax.psum_scatter(
            context_weight_grad.astype(jnp.bfloat16), "dp", scatter_dimension=0, tiled=True
        ).astype(jnp.float32),
        lax.psum_scatter(
            cross_out_grad.astype(jnp.bfloat16), "dp", scatter_dimension=1, tiled=True
        ).astype(jnp.float32),
        lax.psum_scatter(
            gate_up_grad.astype(jnp.bfloat16), "dp", scatter_dimension=0, tiled=True
        ).astype(jnp.float32),
        lax.psum_scatter(
            down_weight_grad.astype(jnp.bfloat16), "dp", scatter_dimension=1, tiled=True
        ).astype(jnp.float32),
        lax.psum_scatter(
            self_gain_part.astype(jnp.bfloat16), "dp", scatter_dimension=0, tiled=True
        ).astype(jnp.float32),
        lax.psum_scatter(
            self_bias_part.astype(jnp.bfloat16), "dp", scatter_dimension=0, tiled=True
        ).astype(jnp.float32),
        lax.psum_scatter(
            cross_gain_sum.astype(jnp.bfloat16), "dp", scatter_dimension=0, tiled=True
        ).astype(jnp.float32),
        lax.psum_scatter(
            cross_bias_sum.astype(jnp.bfloat16), "dp", scatter_dimension=0, tiled=True
        ).astype(jnp.float32),
        lax.psum_scatter(
            feed_gain_sum.astype(jnp.bfloat16), "dp", scatter_dimension=0, tiled=True
        ).astype(jnp.float32),
        lax.psum_scatter(
            feed_bias_sum.astype(jnp.bfloat16), "dp", scatter_dimension=0, tiled=True
        ).astype(jnp.float32),
        lax.psum_scatter(
            down_bias_sum.astype(jnp.bfloat16), "dp", scatter_dimension=0, tiled=True
        ).astype(jnp.float32),
    )
    return (
        output,
        latents_grad,
        reduced[0],
        reduced[8],
        reduced[9],
        reduced[1],
        reduced[2],
        reduced[10],
        reduced[11],
        reduced[3],
        reduced[4],
        reduced[5],
        reduced[12],
        reduced[13],
        reduced[6],
        reduced[7],
        reduced[14],
    )


AXES = ("dp", "mp")
BF = jnp.bfloat16
F32 = jnp.float32


def flat_permutation(places):
    pairs = []
    for d in range(8):
        for z in range(4):
            target = places(d >> 1, d & 1, z & 1, z >> 1)
            if target is not None:
                s, c, zz, p = target
                pairs.append(((2 * s + c) * 4 + 2 * p + zz, (2 * (d >> 1) + (d & 1)) * 4 + z))
    return [(source, target) for target, source in pairs]


SWAP_CORE = flat_permutation(lambda s, c, zz, p: (s, 1 - c, zz, p))
SWAP_Z = flat_permutation(lambda s, c, zz, p: (s, c, 1 - zz, p))
SWAP_PAIR = flat_permutation(lambda s, c, zz, p: (s, c, zz, 1 - p))
SWAP_X = flat_permutation(lambda s, c, zz, p: (s ^ 1, c, zz, p))
SWAP_Y = flat_permutation(lambda s, c, zz, p: (s ^ 2, c, zz, p))
ROUTE_A = flat_permutation(lambda s, c, zz, p: (s, p, zz, c))
ROUTE_B = flat_permutation(lambda s, c, zz, p: (s, p, zz, 1 - c))
RETURN_B = flat_permutation(lambda s, c, zz, p: (s, 1 - p, zz, c))
OWNER_TO_PARTNER = flat_permutation(lambda s, c, zz, p: (s, 1 - c, zz, p) if c == p else None)
PARTNER_TO_OWNER = flat_permutation(lambda s, c, zz, p: (s, 1 - c, zz, p) if c != p else None)
OWNER_TO_PAIR = flat_permutation(lambda s, c, zz, p: (s, c, zz, 1 - p) if c == p else None)
OWNER_Z = flat_permutation(lambda s, c, zz, p: (s, c, 1 - zz, p) if c == p else None)
PARTNER_Z = flat_permutation(lambda s, c, zz, p: (s, c, 1 - zz, p) if c != p else None)


def move(values, pairs):
    return lax.ppermute(values, AXES, pairs)


def xor_blocks(values, axis, count, index):
    blocks = jnp.split(values, count, axis=axis)
    bit = 1
    while bit < count:
        flip = (index & bit) != 0
        blocks = [jnp.where(flip, blocks[j ^ bit], blocks[j]) for j in range(count)]
        bit *= 2
    return jnp.concatenate(blocks, axis=axis)


def attend_pair(head_size, query_block, queries, keys, values, bias, o_ref, log_ref):
    scale = head_size ** (-0.5)
    length, width = queries.shape
    key_rows = keys[...]
    values_turned = values[...].astype(F32).T.astype(BF)
    lane = lax.broadcasted_iota(jnp.int32, (query_block, width), 1)

    @pl.loop(0, length // query_block)
    def _(step):
        rows = pl.ds(pl.multiple_of(step * query_block, query_block), query_block)
        block = queries[rows, :]
        parts, logs = [], []
        for head in range(2):
            mine = (lane >= head * head_size) & (lane < (head + 1) * head_size)
            masked = jnp.where(mine, block, jnp.zeros_like(block))
            scores = lax.dot_general(
                key_rows, masked, (((1,), (1,)), ((), ())), preferred_element_type=F32
            )
            scores = scores * scale
            if bias is not None:
                scores = scores + bias[...]
            top = jnp.max(scores, axis=0, keepdims=True)
            expos = jnp.exp(scores - top)
            total = jnp.sum(expos, axis=0, keepdims=True)
            mixed = lax.dot_general(
                values_turned[head * head_size : (head + 1) * head_size, :],
                expos.astype(BF),
                (((1,), (0,)), ((), ())),
                preferred_element_type=F32,
            )
            parts.append(mixed * (1.0 / total))
            logs.append(top + jnp.log(total))
        o_ref[rows, :] = jnp.concatenate(parts, axis=0).T.astype(BF)
        log_ref[0, :, rows] = jnp.concatenate(logs, axis=0)


def cross_attention_kernel(q_ref, k_ref, v_ref, bias_ref, o_ref, log_ref):
    attend_pair(HD, 512, q_ref, k_ref, v_ref, bias_ref, o_ref, log_ref)


def attention_backward_kernel(head_size, query_block, turned, load, *refs):
    if turned:
        refs = list(refs)
        q_ref, k_ref, v_ref, d_ref, log_ref, base_ref, steps_ref = refs[:7]
        more = (len(load.operands), len(load.outs_like))
        refs = refs[7:]
        load_ins, g_ref, refs = refs[: more[0]], refs[more[0]], refs[more[0] + 1 :]
        load_outs, refs = refs[: more[1]], refs[more[1] :]
        dk_acc, dv_acc = refs[:2]
        place = Place()
        carried = load.begin(place, load_ins, load_outs, refs[2:])

        @pl.when(pl.program_id(0) == 0)
        def _():
            greet(load.peers(place, [place.core_peer]))
            for each in carried:
                each.start()
    else:
        q_ref, k_ref, v_ref, d_ref, log_ref, bias_ref, dq_ref, g_ref, dk_acc, dv_acc = refs
    scale = head_size ** (-0.5)
    length, width = q_ref.shape
    key_count = k_ref.shape[0]
    here = pl.program_id(0)
    key_rows = k_ref[...]
    value_rows = v_ref[...]
    keys_turned = key_rows.astype(F32).T.astype(BF)
    lane = lax.broadcasted_iota(jnp.int32, (query_block, width), 1)
    dk_acc[...] = jnp.zeros_like(dk_acc)
    dv_acc[...] = jnp.zeros_like(dv_acc)

    def back_turn(values, step):
        blocks = length // query_block
        index = lax.rem(step + place.core * (blocks // 2), blocks)
        return turned_block(values, base_ref, steps_ref, index, -1)

    @pl.loop(0, length // query_block)
    def _(step):
        rows = pl.ds(pl.multiple_of(step * query_block, query_block), query_block)
        block = q_ref[rows, :]
        grads = d_ref[rows, :]
        parts = []
        for head in range(2):
            mine = (lane >= head * head_size) & (lane < (head + 1) * head_size)
            q_mine = jnp.where(mine, block, jnp.zeros_like(block))
            d_mine = jnp.where(mine, grads, jnp.zeros_like(grads))
            scores = lax.dot_general(
                key_rows, q_mine, (((1,), (1,)), ((), ())), preferred_element_type=F32
            )
            scores = scores * scale
            if not turned:
                scores = scores + bias_ref[...]
            probs = jnp.exp(scores - log_ref[0, head : head + 1, rows])
            grad_probs = lax.dot_general(
                value_rows, d_mine, (((1,), (1,)), ((), ())), preferred_element_type=F32
            )
            delta = jnp.sum(probs * grad_probs, axis=0, keepdims=True)
            grad_scores = (probs * (grad_probs - delta)).astype(BF)
            dv_acc[...] += jnp.dot(probs.astype(BF), d_mine, preferred_element_type=F32)
            dk_acc[...] += jnp.dot(grad_scores, q_mine, preferred_element_type=F32)
            parts.append(
                jnp.dot(
                    keys_turned[head * head_size : (head + 1) * head_size, :],
                    grad_scores,
                    preferred_element_type=F32,
                )
            )
        grad_query = jnp.concatenate(parts, axis=0).T * scale
        if turned:
            columns = pl.ds(pl.multiple_of(here * width, width), width)
            g_ref[rows, columns] = back_turn(grad_query, step).astype(BF)
        else:
            dq_ref[rows, :] = grad_query.astype(BF)

    total_width = g_ref.shape[1] // (3 if turned else 2)
    first = total_width if turned else 0
    key_columns = pl.ds(pl.multiple_of(first + here * width, width), width)
    value_columns = pl.ds(pl.multiple_of(first + total_width + here * width, width), width)
    if turned:

        @pl.loop(0, key_count // query_block)
        def _(step):
            rows = pl.ds(pl.multiple_of(step * query_block, query_block), query_block)
            g_ref[rows, key_columns] = back_turn(dk_acc[rows, :] * scale, step).astype(BF)
            g_ref[rows, value_columns] = dv_acc[rows, :].astype(BF)

        @pl.when(here == pl.num_programs(0) - 1)
        def _():
            for each in carried:
                each.finish()
    else:
        g_ref[:, key_columns] = (dk_acc[...] * scale).astype(BF)
        g_ref[:, value_columns] = dv_acc[...].astype(BF)


def self_attention_back(place, queries, keys, values, grads, logs, load):
    length, total = queries.shape
    pairs = total // 128
    block = pl.BlockSpec((length, 128), lambda i: (0, i))
    whole = pl.BlockSpec(memory_space=pltpu.VMEM)
    tables = turn_tables(length, 256)
    return pl.pallas_call(
        functools.partial(attention_backward_kernel, HD, 256, True, load),
        grid=(pairs,),
        in_specs=[block] * 4
        + [pl.BlockSpec((1, 2, length), lambda i: (i, 0, 0))]
        + [whole] * 2
        + [ANYWHERE] * len(load.operands),
        out_specs=[pl.BlockSpec((length, 3 * total), lambda i: (0, 0))]
        + [ANYWHERE] * len(load.outs_like),
        out_shape=[jax.ShapeDtypeStruct((length, 3 * total), BF)] + load.outs_like,
        scratch_shapes=[pltpu.VMEM((length, 128), F32)] * 2 + load.scratch,
        compiler_params=pltpu.CompilerParams(collective_id=place, has_side_effects=True),
        cost_estimate=pl.CostEstimate(
            flops=10 * length * length * total,
            transcendentals=length * length * total // 64,
            bytes_accessed=100_000_000,
        ),
        name="self_attention_back",
    )(queries, keys, values, grads, logs, *tables, *load.operands)


def cross_attention(queries, context, bias):
    length, total = queries.shape
    slots = context.shape[0]
    pairs = total // 128
    block = pl.BlockSpec((length, 128), lambda i: (0, i))
    key_block = lambda shift: pl.BlockSpec((slots, 128), lambda i: (0, i + shift))
    return pl.pallas_call(
        cross_attention_kernel,
        grid=(pairs,),
        in_specs=[block, key_block(0), key_block(pairs), pl.BlockSpec((slots, 1), lambda i: (0, 0))],
        out_specs=[block, pl.BlockSpec((1, 2, length), lambda i: (i, 0, 0))],
        out_shape=[
            jax.ShapeDtypeStruct((length, total), BF),
            jax.ShapeDtypeStruct((pairs, 2, length), F32),
        ],
        cost_estimate=pl.CostEstimate(
            flops=4 * length * slots * total,
            transcendentals=length * slots * total // 64,
            bytes_accessed=length * total * 4,
        ),
        name="cross_attention",
    )(queries, context, context, bias)


def cross_attention_back(queries, context, bias, grads, logs):
    length, total = queries.shape
    slots = context.shape[0]
    pairs = total // 128
    block = pl.BlockSpec((length, 128), lambda i: (0, i))
    key_block = lambda shift: pl.BlockSpec((slots, 128), lambda i: (0, i + shift))
    return pl.pallas_call(
        functools.partial(attention_backward_kernel, HD, 512, False, None),
        grid=(pairs,),
        in_specs=[
            block,
            key_block(0),
            key_block(pairs),
            block,
            pl.BlockSpec((1, 2, length), lambda i: (i, 0, 0)),
            pl.BlockSpec((slots, 1), lambda i: (0, 0)),
        ],
        out_specs=[block, pl.BlockSpec((slots, 2 * total), lambda i: (0, 0))],
        out_shape=[
            jax.ShapeDtypeStruct((length, total), BF),
            jax.ShapeDtypeStruct((slots, 2 * total), BF),
        ],
        scratch_shapes=[pltpu.VMEM((slots, 128), F32)] * 2,
        cost_estimate=pl.CostEstimate(
            flops=10 * length * slots * total,
            transcendentals=length * slots * total // 64,
            bytes_accessed=length * total * 8,
        ),
        name="cross_attention_back",
    )(queries, context, context, grads, logs, bias)


def dot_nn(left, right):
    return lax.dot_general(left, right, (((1,), (0,)), ((), ())), preferred_element_type=F32)


def dot_nt(left, right):
    return lax.dot_general(left, right, (((1,), (1,)), ((), ())), preferred_element_type=F32)


def dot_tn(left, right):
    return lax.dot_general(left, right, (((0,), (0,)), ((), ())), preferred_element_type=F32)


PLANE = [[0, 2, 4, 6], [1, 3, 5, 7]]


def group_sum(partial):
    rows = partial.shape[0] // 2
    half = partial[:rows].astype(F32) + move(partial[rows:], SWAP_CORE).astype(F32)
    half = half.astype(BF)
    return half.astype(F32) + move(half, SWAP_Z).astype(F32)


def both_halves(half):
    return jnp.concatenate([half, move(half, SWAP_CORE)], axis=0)


def weight_order(one, two, pair):
    first = jnp.where(pair == 0, one, two)
    second = jnp.where(pair == 0, two, one)
    return jnp.concatenate([first, second], axis=0)


def plane_gather(mine):
    return lax.all_gather(mine, "dp", axis=0, tiled=True, axis_index_groups=PLANE)


def plane_sum(grad):
    return lax.psum_scatter(
        grad, "dp", scatter_dimension=0, tiled=True, axis_index_groups=PLANE
    )


def to_owners(total, pair):
    rows = total.shape[0] // 2
    first, second = total[:rows], total[rows:]
    one = move(jnp.where(pair == 0, first, second), ROUTE_A)
    two = move(jnp.where(pair == 0, second, first), RETURN_B)
    return one.astype(F32) + two.astype(F32)


def after(values, *others):
    return lax.optimization_barrier((values, *others))[0]


class Place:
    def __init__(self):
        d = lax.axis_index("dp")
        z = lax.axis_index("mp")
        self.d, self.z = d, z
        self.core = lax.rem(d, 2)
        self.column = d // 2
        self.pair = z // 2
        self.owner = self.core == self.pair
        self.core_peer = (d + 1 - 2 * self.core, z)
        self.near_z = (d, z + 1 - 2 * lax.rem(z, 2))
        self.far_z = z + 2 - 4 * self.pair
        self.far_same = (d, self.far_z)
        self.far_other = (self.core_peer[0], self.far_z)
        self.user = (2 * self.column + self.pair, self.far_z)
        self.x_peer = (d + 2 - 4 * lax.rem(self.column, 2), z)
        self.y_peer = (d + 4 - 8 * (self.column // 2), z)
        self.x_column = self.column + 1 - 2 * lax.rem(self.column, 2)
        self.y_column = self.column + 2 - 4 * (self.column // 2)


def greet(peers):
    barrier = pltpu.get_barrier_semaphore()
    for peer in peers:
        pl.semaphore_signal(
            barrier, inc=1, device_id=peer, device_id_type=pl.DeviceIdType.MESH
        )
    pl.semaphore_wait(barrier, len(peers))


def send(source, target, sent, got, peer):
    return pltpu.make_async_remote_copy(
        src_ref=source,
        dst_ref=target,
        send_sem=sent,
        recv_sem=got,
        device_id=peer,
        device_id_type=pl.DeviceIdType.MESH,
    )


class Spread:
    scratch = [pltpu.SemaphoreType.DMA((2,)), pltpu.SemaphoreType.DMA((3,)), pltpu.SemaphoreType.DMA]
    late = True

    @staticmethod
    def outs(part):
        return [jax.ShapeDtypeStruct((2 * part.shape[0], part.shape[1]), BF)]

    @staticmethod
    def peers(place):
        return [place.far_same, place.far_other]

    def __init__(self, place, ins, outs, sems):
        self.place = place
        (self.part,), (self.own,), (self.sent, self.got, self.here) = ins, outs, sems

    def target(self, sender):
        rows = self.part.shape[0]
        return self.own.at[pl.ds(pl.multiple_of(sender * rows, rows), rows)]

    def far(self, sender):
        return send(
            self.part, self.target(sender), self.sent.at[0], self.got.at[sender], self.place.user
        )

    def near(self, sender):
        return send(
            self.part, self.target(sender), self.sent.at[1], self.got.at[2], self.place.core_peer
        )

    def local(self):
        return pltpu.make_async_copy(self.part, self.target(self.place.core), self.here)

    def start(self):
        place = self.place
        self.far(place.core).start()

        @pl.when(place.owner)
        def _():
            self.local().start()

        @pl.when(jnp.logical_not(place.owner))
        def _():
            self.near(place.core).start()

    def middle(self):
        pass

    def finish(self):
        place = self.place

        @pl.when(place.owner)
        def _():
            self.local().wait()
            self.near(1 - place.core).wait_recv()

        @pl.when(jnp.logical_not(place.owner))
        def _():
            self.near(place.core).wait_send()
            self.far(0).wait_recv()
            self.far(1).wait_recv()

        self.far(place.core).wait_send()


class Plane:
    scratch = [
        pltpu.SemaphoreType.DMA((2, 3)),
        pltpu.SemaphoreType.DMA((2, 3)),
        pltpu.SemaphoreType.DMA,
    ]
    late = False

    @staticmethod
    def outs(own):
        return [jax.ShapeDtypeStruct((4 * own.shape[0], own.shape[1]), BF)]

    @staticmethod
    def peers(place):
        return [place.x_peer, place.y_peer]

    def __init__(self, place, ins, outs, sems):
        self.place = place
        (self.own,), (self.full,), (self.sent, self.got, self.here) = ins, outs, sems
        self.rows = self.own.shape[0] // 2

    def target(self, column, part):
        rows = self.rows
        return self.full.at[pl.ds(pl.multiple_of((2 * column + part) * rows, rows), rows)]

    def one(self, way, part):
        place = self.place
        peer = place.x_peer if way == 0 else place.y_peer
        return send(
            self.own.at[pl.ds(part * self.rows, self.rows)],
            self.target(place.column, part),
            self.sent.at[way, part],
            self.got.at[way, part],
            peer,
        )

    def two(self, way):
        place = self.place
        if way == 0:
            spot = self.target(place.y_column, 1)
            return send(spot, spot, self.sent.at[0, 2], self.got.at[0, 2], place.x_peer)
        spot = self.target(place.x_column, 0)
        return send(spot, spot, self.sent.at[1, 2], self.got.at[1, 2], place.y_peer)

    def local(self):
        rows = self.own.shape[0]
        place = self.full.at[pl.ds(pl.multiple_of(self.place.column * rows, rows), rows)]
        return pltpu.make_async_copy(self.own, place, self.here)

    def start(self):
        for way in range(2):
            self.one(way, way).start()
        for way in range(2):
            self.one(way, 1 - way).start()
        self.local().start()

    def middle(self):
        self.one(0, 0).wait_recv()
        self.two(1).start()
        self.one(1, 1).wait_recv()
        self.two(0).start()

    def finish(self):
        self.local().wait()
        for way in range(2):
            self.one(way, 1 - way).wait_recv()
            self.two(way).wait_recv()
            self.two(way).wait_send()
            for part in range(2):
                self.one(way, part).wait_send()


class Return:
    scratch = [pltpu.SemaphoreType.DMA((2,)), pltpu.SemaphoreType.DMA((2,))]
    late = True

    @staticmethod
    def outs(total):
        shape = jax.ShapeDtypeStruct((total.shape[0] // 2, total.shape[1]), BF)
        return [shape, shape]

    @staticmethod
    def peers(place):
        return [place.far_same, place.far_other]

    def __init__(self, place, ins, outs, sems):
        self.place = place
        (self.total,), (self.near, self.far), (self.sent, self.got) = ins, outs, sems

    def part(self, which):
        rows = self.near.shape[0]
        return self.total.at[pl.ds(pl.multiple_of(which * rows, rows), rows)]

    def to_near(self):
        place = self.place
        return send(
            self.part(1 - place.core), self.near, self.sent.at[0], self.got.at[0], place.core_peer
        )

    def to_far(self, same):
        place = self.place
        which = place.core if same else 1 - place.core
        peer = place.far_same if same else place.far_other
        return send(
            self.part(which), self.far, self.sent.at[0 if same else 1], self.got.at[1], peer
        )

    def start(self):
        place = self.place

        @pl.when(place.owner)
        def _():
            self.to_near().start()

        @pl.when(jnp.logical_not(place.owner))
        def _():
            self.to_far(True).start()
            self.to_far(False).start()

    def middle(self):
        pass

    def finish(self):
        place = self.place

        @pl.when(place.owner)
        def _():
            self.to_near().wait_send()
            self.to_far(True).wait_recv()

        @pl.when(jnp.logical_not(place.owner))
        def _():
            self.to_far(True).wait_send()
            self.to_far(False).wait_send()
            self.to_near().wait_recv()
            self.to_far(False).wait_recv()


class Swap:
    scratch = [pltpu.SemaphoreType.DMA, pltpu.SemaphoreType.DMA]
    late = True
    way = None

    @staticmethod
    def outs(values):
        return [jax.ShapeDtypeStruct(values.shape, values.dtype)]

    @classmethod
    def peers(cls, place):
        return {
            "core": [place.core_peer],
            "z": [place.near_z],
            "route": [place.far_same, place.far_other],
        }[cls.way]

    def __init__(self, place, ins, outs, sems):
        self.place = place
        peer = {"core": place.core_peer, "z": place.near_z, "route": place.far_other}[self.way]
        self.copy = send(ins[0], outs[0], sems[0], sems[1], peer)

    def each(self, act):
        if self.way != "route":
            act()
            return

        @pl.when(jnp.logical_not(self.place.owner))
        def _():
            act()

    def start(self):
        self.each(lambda: self.copy.start())

    def middle(self):
        pass

    def finish(self):
        self.each(lambda: self.copy.wait())


class SwapCore(Swap):
    way = "core"


class SwapCoreHalf(SwapCore):
    @staticmethod
    def outs(values):
        return [jax.ShapeDtypeStruct((values.shape[0] // 2,) + values.shape[1:], values.dtype)]

    def __init__(self, place, ins, outs, sems):
        rows = outs[0].shape[0]
        super().__init__(place, [ins[0].at[pl.ds(rows, rows)]], outs, sems)


class SwapNear(Swap):
    way = "z"


class SwapRoute(Swap):
    way = "route"


class Loads:
    def __init__(self, *loads):
        self.loads = loads
        self.operands = [operand for _, operand in loads]
        self.outs_like = [out for kind, operand in loads for out in kind.outs(operand)]
        self.scratch = [sem for kind, _ in loads for sem in kind.scratch]

    def peers(self, place, base):
        found = {id(peer): peer for peer in base}
        for kind, _ in self.loads:
            for peer in kind.peers(place):
                found[id(peer)] = peer
        return list(found.values())

    def begin(self, place, ins, outs, sems):
        result, at, sem_at = [], 0, 0
        for (kind, operand), source in zip(self.loads, ins):
            count, sem_count = len(kind.outs(operand)), len(kind.scratch)
            result.append(
                kind(
                    place,
                    [source],
                    outs[at : at + count],
                    sems[sem_at : sem_at + sem_count],
                )
            )
            at, sem_at = at + count, sem_at + sem_count
        return result


class Works:
    def __init__(self, *works):
        self.kinds = [kind for kind, _, _ in works]
        self.operands = [operand for _, left, right in works for operand in (left, right)]
        self.unique = []
        for operand in self.operands:
            if not any(operand is other for other in self.unique):
                self.unique.append(operand)
        self.places = [
            [at for at, other in enumerate(self.unique) if other is operand][0]
            for operand in self.operands
        ]
        self.outs_like = []
        for kind, left, right in works:
            if kind == "nt":
                shape = (left.shape[0], right.shape[0])
            else:
                shape = (left.shape[1], right.shape[1])
            self.outs_like.append(jax.ShapeDtypeStruct(shape, BF))
        self.scratch = (
            [pltpu.VMEM(operand.shape, BF) for operand in self.unique]
            + [pltpu.VMEM(out.shape, BF) for out in self.outs_like]
            + [pltpu.SemaphoreType.DMA((max(1, len(self.unique) + len(works)),))]
        )

    def begin(self, ins, outs, scratch):
        self_ins = list(scratch[: len(self.unique)])
        self_outs = list(scratch[len(self.unique) : -1])
        sems = scratch[-1]
        loads = [
            pltpu.make_async_copy(source, target, sems.at[k])
            for k, (source, target) in enumerate(zip(ins, self_ins))
        ]
        stores = [
            pltpu.make_async_copy(source, target, sems.at[len(loads) + k])
            for k, (source, target) in enumerate(zip(self_outs, outs))
        ]
        return loads, stores, self_ins, self_outs

    def run(self, state):
        loads, stores, ins, outs = state
        waited = set()
        for k, kind in enumerate(self.kinds):
            pair = self.places[2 * k : 2 * k + 2]
            for at in pair:
                if at not in waited:
                    loads[at].wait()
                    waited.add(at)
            left, right, out = ins[pair[0]], ins[pair[1]], outs[k]
            if kind == "nt":
                columns = out.shape[1] // 256

                @pl.loop(0, (out.shape[0] // 256) * columns)
                def _(step):
                    first = pl.ds(pl.multiple_of((step // columns) * 256, 256), 256)
                    second = pl.ds(pl.multiple_of(lax.rem(step, columns) * 256, 256), 256)
                    out[first, second] = lax.dot_general(
                        left[first, :],
                        right[second, :],
                        (((1,), (1,)), ((), ())),
                        preferred_element_type=F32,
                    ).astype(BF)
            else:

                @pl.loop(0, out.shape[0] // 256)
                def _(step):
                    spot = pl.ds(pl.multiple_of(step * 256, 256), 256)
                    out[spot, :] = lax.dot_general(
                        left[:, spot],
                        right[...],
                        (((0,), (0,)), ((), ())),
                        preferred_element_type=F32,
                    ).astype(BF)

            stores[k].start()


ANYWHERE = pl.BlockSpec(memory_space=pl.ANY)


def returned(total, near, far, core, owner):
    rows = near.shape[0]
    mine = jnp.where(core == 0, total[:rows], total[rows:])
    return jnp.where(owner, mine, near).astype(F32) + far.astype(F32)


def exchange_kernel(kind, chunks, window, load, works, *refs):
    refs = list(refs)
    place = Place()
    more = (len(load.operands), len(load.outs_like))
    todo = (len(works.unique), len(works.outs_like), len(works.scratch))
    w_count = len(refs) - 1 - 4 - more[0] - more[1] - todo[0] - todo[1] - todo[2]
    w_count -= 2 + 11 + 4 + (kind != "norm") + len(load.scratch) - 1
    w_from, refs = refs[1 : 1 + w_count], refs[:1] + refs[1 + w_count :]
    ins, refs = refs[:4], refs[4:]
    load_ins, refs = refs[: more[0]], refs[more[0] :]
    work_ins, refs = refs[: todo[0]], refs[todo[0] :]
    outs, refs = refs[:2], refs[2:]
    load_outs, refs = refs[: more[1]], refs[more[1] :]
    work_outs, refs = refs[: todo[1]], refs[todo[1] :]
    rest, refs = refs[:11], refs[11:]
    (a_ref, w_ref, res_ref, loads), refs = refs[:4], refs[4:]
    if kind == "norm":
        a_from, res_from, gain_ref, bias_ref = ins
        res_out, all_ref = outs
    else:
        a_from, res_from, up_from, gain_ref = ins
        all_ref, sum_ref = outs
        up_ref, refs = refs[0], refs[1:]
    carried = load.begin(place, load_ins, load_outs, refs)
    working = works.begin(work_ins, work_outs, refs[len(load.scratch) :])
    mine, given, near, half, far, send_near, got_near, send_far, got_far, send_all, got_all = rest
    rows = mine.shape[0]
    width = mine.shape[1]
    chunk = rows // chunks
    core_peer, far_peer = place.core_peer, place.near_z
    copy = send
    depth = a_ref.shape[1]
    block = 2 * chunk
    tile = 256
    tiles = width // tile

    def load_rows(k):
        first = (k // 2) * block + (0 if k % 2 else rows)
        spot = pl.ds(first, block)
        return pltpu.make_async_copy(a_from.at[spot], a_ref.at[spot], loads.at[2 * tiles + k])

    def load_weight(k):
        spot = pl.ds(k * tile, tile)
        share = depth // len(w_from)
        return [
            pltpu.make_async_copy(
                source.at[spot, pl.ds(window * depth, share)],
                w_ref.at[spot, pl.ds(at * share, share)],
                loads.at[at * tiles + k],
            )
            for at, source in enumerate(w_from)
        ]

    later = [pltpu.make_async_copy(res_from, res_ref, loads.at[2 * tiles + 2 * chunks])]
    if kind != "norm":
        later.append(
            pltpu.make_async_copy(
                up_from.at[pl.ds(0, rows)], up_ref, loads.at[2 * tiles + 2 * chunks + 1]
            )
        )
    load_rows(0).start()
    for k in range(tiles):
        for each in load_weight(k):
            each.start()
    for k in range(1, chunks):
        load_rows(k).start()
    for each in later + working[0]:
        each.start()
    greet(load.peers(place, [core_peer, far_peer]))
    for each in carried:
        if not each.late:
            each.start()

    def near_copy(k):
        part = pl.ds(k * chunk, chunk)
        return copy(given.at[part], near.at[part], send_near.at[k], got_near.at[k], core_peer)

    def far_copy(k):
        part = pl.ds(k * chunk, chunk)
        return copy(half.at[part], far.at[part], send_far.at[k], got_far.at[k], far_peer)

    def all_copy(k):
        return copy(
            all_ref.at[pl.ds(k * chunk, chunk)],
            all_ref.at[pl.ds(rows + k * chunk, chunk)],
            send_all.at[k],
            got_all.at[k],
            core_peer,
        )

    def tile_product(first, target, start, spot):
        target[pl.ds(start, block), spot] = lax.dot_general(
            a_ref[pl.ds(first, block), :],
            w_ref[spot, :],
            (((1,), (1,)), ((), ())),
            preferred_element_type=F32,
        ).astype(target.dtype)

    def product(first, target, start):
        @pl.loop(0, tiles)
        def _(step):
            spot = pl.ds(pl.multiple_of(step * tile, tile), tile)
            tile_product(first, target, start, spot)

    step_rows = 16
    for m in range(chunks // 2):
        load_rows(2 * m).wait()
        if m == 0:
            for k in range(tiles):
                for each in load_weight(k):
                    each.wait()
                tile_product(rows, given, 0, pl.ds(k * tile, tile))
        else:
            product(rows + m * block, given, m * block)
        for k in (2 * m, 2 * m + 1):
            near_copy(k).start()
        load_rows(2 * m + 1).wait()
        product(m * block, mine, m * block)
        for k in (2 * m, 2 * m + 1):
            near_copy(k).wait_recv()

            @pl.loop(0, chunk // step_rows)
            def _(step):
                part = pl.ds(pl.multiple_of(k * chunk + step * step_rows, step_rows), step_rows)
                half[part, :] = (mine[part, :] + near[part, :].astype(F32)).astype(BF)

            far_copy(k).start()
    for each in carried:
        if each.late:
            each.start()
    works.run(working)
    for each in later:
        each.wait()
    if kind != "norm":
        sum_ref[...] = jnp.zeros_like(sum_ref)
    for k in range(chunks):
        far_copy(k).wait_recv()

        @pl.loop(0, chunk // step_rows)
        def _(step):
            part = pl.ds(pl.multiple_of(k * chunk + step * step_rows, step_rows), step_rows)
            total = half[part, :].astype(F32) + far[part, :].astype(F32)
            if kind == "norm":
                values = res_ref[part, :] + total
                res_out[part, :] = values
            else:
                values = res_ref[part, :]
            centered = values - jnp.mean(values, axis=-1, keepdims=True)
            inverse = lax.rsqrt(jnp.mean(centered * centered, axis=-1, keepdims=True) + EPS)
            scaled = centered * inverse
            if kind == "norm":
                all_ref[part, :] = (scaled * gain_ref[...] + bias_ref[...]).astype(BF)
            else:
                grad_scaled = total * gain_ref[...]
                first_mean = jnp.mean(grad_scaled, axis=-1, keepdims=True)
                second_mean = jnp.mean(grad_scaled * scaled, axis=-1, keepdims=True)
                grads = inverse * (grad_scaled - first_mean - scaled * second_mean)
                all_ref[part, :] = (up_ref[part, :].astype(F32) + grads).astype(BF)
                product_rows = total * scaled
                sum_ref[0] += product_rows[:8] + product_rows[8:]
                sum_ref[1] += total[:8] + total[8:]

        if k == 1:
            for each in carried:
                each.middle()
        if kind != "half":
            all_copy(k).start()
    for k in range(chunks):
        near_copy(k).wait_send()
        far_copy(k).wait_send()
        if kind != "half":
            all_copy(k).wait_send()
            all_copy(k).wait_recv()
    for each in carried:
        each.finish()
    for each in working[1]:
        each.wait()


def exchange(kind, place, a, w, residual, *others, load=Loads(), window=0, works=Works()):
    length, depth = a.shape
    w = w if isinstance(w, tuple) else (w,)
    width = w[0].shape[0]
    rows = length // 2
    chunks = 4
    whole = pl.BlockSpec(memory_space=pltpu.VMEM)
    if kind == "norm":
        gain, bias = others
        operands = (a, *w, residual, gain[None], bias[None])
        outs = [
            jax.ShapeDtypeStruct((rows, width), F32),
            jax.ShapeDtypeStruct((length, width), BF),
        ]
    else:
        up, gain = others
        operands = (a, *w, residual, up, gain[None])
        outs = [
            jax.ShapeDtypeStruct((rows if kind == "half" else length, width), BF),
            jax.ShapeDtypeStruct((2, 8, width), F32),
        ]
    plain = 2 if kind == "norm" else 1
    specs = [ANYWHERE] * (len(operands) - plain) + [whole] * plain
    specs += [ANYWHERE] * (len(load.operands) + len(works.unique))
    tiles = width // 256
    more = [
        pltpu.VMEM((length, depth), BF),
        pltpu.VMEM((width, depth), BF),
        pltpu.VMEM((rows, width), F32),
        pltpu.SemaphoreType.DMA((2 * tiles + 2 * chunks + 2,)),
    ]
    if kind != "norm":
        more.append(pltpu.VMEM((rows, width), BF))
    out_specs = [whole] * 2 + [ANYWHERE] * (len(load.outs_like) + len(works.outs_like))
    operands += tuple(load.operands) + tuple(works.unique)
    outs = outs + load.outs_like + works.outs_like
    return pl.pallas_call(
        functools.partial(exchange_kernel, kind, chunks, window, load, works),
        in_specs=specs,
        out_specs=out_specs,
        out_shape=outs,
        scratch_shapes=[
            pltpu.VMEM((rows, width), F32),
            pltpu.VMEM((rows, width), BF),
            pltpu.VMEM((rows, width), BF),
            pltpu.VMEM((rows, width), BF),
            pltpu.VMEM((rows, width), BF),
        ]
        + [pltpu.SemaphoreType.DMA((chunks,))] * 6
        + more
        + load.scratch
        + works.scratch,
        compiler_params=pltpu.CompilerParams(
            collective_id=place, has_side_effects=True, vmem_limit_bytes=60 * 2**20
        ),
        cost_estimate=pl.CostEstimate(
            flops=2 * length * depth * width,
            transcendentals=0,
            bytes_accessed=100_000_000,
        ),
        name="exchange_" + kind,
    )(*operands)


def spread_kernel(load, chunks, *refs):
    refs = list(refs)
    more = (len(load.operands), len(load.outs_like))
    (half_ref, pieces_ref), refs = refs[:2], refs[2:]
    load_ins, refs = refs[: more[0]], refs[more[0] :]
    (out_ref, token_ref, share_ref), refs = refs[:3], refs[3:]
    load_outs, refs = refs[: more[1]], refs[more[1] :]
    (sent, got, send_token, got_token, send_share, got_share), refs = refs[:6], refs[6:]
    place = Place()
    carried = load.begin(place, load_ins, load_outs, refs)
    d, core, pair = place.d, place.core, place.pair
    inner_z = lax.rem(place.z, 2)
    plane_peers = [(lax.rem(d + j, 8), place.z) for j in range(1, 8)]
    far_peers = [(lax.rem(d + j, 8), place.far_z) for j in range(8)]
    greet([place.near_z] + far_peers + plane_peers)
    rows = half_ref.shape[0]
    chunk = rows // chunks

    def spot(which, k):
        return out_ref.at[pl.ds(pl.multiple_of(which * rows + k * chunk, chunk), chunk)]

    def owner_copy(k, which):
        source = half_ref.at[pl.ds(k * chunk, chunk)]
        return send(source, spot(which, k), sent.at[0, k], got.at[0, k], place.core_peer)

    def pair_copy(k, which):
        source = half_ref.at[pl.ds(k * chunk, chunk)]
        return send(source, spot(which, k), sent.at[1, k], got.at[1, k], place.user)

    def pass_copy(k, which):
        return send(spot(which, k), spot(which, k), sent.at[2, k], got.at[2, k], place.near_z)

    def share_copy(far, j):
        return send(
            pieces_ref.at[pl.ds(pl.multiple_of(lax.rem(d + j, 8) * 8, 8), 8)],
            share_ref.at[pl.ds((8 * far + j) * 8, 8)],
            send_share.at[far, j],
            got_share.at[far, j],
            far_peers[j] if far else plane_peers[j - 1],
        )

    for j in range(8):
        share_copy(1, j).start()
        if j:
            share_copy(0, j).start()
    share_ref[pl.ds(0, 8), :] = pieces_ref[pl.ds(pl.multiple_of(d * 8, 8), 8), :]

    @pl.when(core == inner_z)
    def _():
        for k in range(chunks):
            pair_copy(k, core).start()

    @pl.when(core != pair)
    def _():
        for k in range(chunks):
            owner_copy(k, core).start()

    @pl.when(core == pair)
    def _():
        @pl.loop(0, rows // 16)
        def _(step):
            first = pl.multiple_of(step * 16, 16)
            out_ref[pl.ds(pl.multiple_of(core * rows + first, 16), 16), :] = half_ref[
                pl.ds(first, 16), :
            ]

        for k in range(chunks):
            owner_copy(k, 1 - core).wait_recv()

    def pass_on(k):
        pair_copy(k, inner_z).wait_recv()
        pass_copy(k, inner_z).start()

    @pl.when(core != pair)
    def _():
        for k in range(chunks // 2):
            pass_on(k)

    for each in carried:
        each.start()

    @pl.when(core != pair)
    def _():
        for k in range(chunks // 2, chunks):
            pass_on(k)
        for k in range(chunks):
            pass_copy(k, 1 - inner_z).wait_recv()

    head = 16
    token_ref[pl.ds(pl.multiple_of(d * head, head), head), :] = out_ref[pl.ds(0, head), :]

    def token_copy(j, sender):
        return send(
            out_ref.at[pl.ds(0, head)],
            token_ref.at[pl.ds(pl.multiple_of(sender * head, head), head)],
            send_token.at[j - 1],
            got_token.at[j - 1],
            plane_peers[j - 1],
        )

    for j in range(1, 8):
        token_copy(j, d).start()

    @pl.when(core != pair)
    def _():
        for k in range(chunks):
            pass_copy(k, inner_z).wait_send()
            owner_copy(k, core).wait_send()

    @pl.when(core == inner_z)
    def _():
        for k in range(chunks):
            pair_copy(k, core).wait_send()

    for j in range(1, 8):
        token_copy(j, d).wait_send()
        token_copy(j, lax.rem(d + 8 - j, 8)).wait_recv()
    for j in range(8):
        share_copy(1, j).wait()
        if j:
            share_copy(0, j).wait()
    for each in carried:
        each.finish()


def spread_gradient(place, half, pieces, load):
    rows, width = half.shape
    chunks = 4
    whole = pl.BlockSpec(memory_space=pltpu.VMEM)
    return pl.pallas_call(
        functools.partial(spread_kernel, load, chunks),
        in_specs=[whole] * 2 + [ANYWHERE] * len(load.operands),
        out_specs=[whole] * 3 + [ANYWHERE] * len(load.outs_like),
        out_shape=[
            jax.ShapeDtypeStruct((2 * rows, width), BF),
            jax.ShapeDtypeStruct((8 * 16, width), BF),
            jax.ShapeDtypeStruct((2 * pieces.shape[0], pieces.shape[1]), F32),
        ]
        + load.outs_like,
        scratch_shapes=[
            pltpu.SemaphoreType.DMA((3, chunks)),
            pltpu.SemaphoreType.DMA((3, chunks)),
            pltpu.SemaphoreType.DMA((7,)),
            pltpu.SemaphoreType.DMA((7,)),
            pltpu.SemaphoreType.DMA((2, 8)),
            pltpu.SemaphoreType.DMA((2, 8)),
        ]
        + load.scratch,
        compiler_params=pltpu.CompilerParams(
            collective_id=place, has_side_effects=True, vmem_limit_bytes=60 * 2**20
        ),
        cost_estimate=pl.CostEstimate(flops=0, transcendentals=0, bytes_accessed=100_000_000),
        name="spread_gradient",
    )(half, pieces, *load.operands)


def feed_kernel(n_ref, cot_ref, gate_ref, up_ref, down_ref, hidden_ref, grad_ref):
    here = pl.program_id(0)
    length = n_ref.shape[0]
    tile = gate_ref.shape[1]
    half = grad_ref.shape[1] // 2
    block = 256
    gate_columns = pl.ds(pl.multiple_of(here * tile, tile), tile)
    up_columns = pl.ds(pl.multiple_of(half + here * tile, tile), tile)

    @pl.loop(0, length // block)
    def _(step):
        rows = pl.ds(pl.multiple_of(step * block, block), block)
        gate = jnp.dot(n_ref[rows, :], gate_ref[...], preferred_element_type=F32)
        up = jnp.dot(n_ref[rows, :], up_ref[...], preferred_element_type=F32)
        grad = jnp.dot(cot_ref[rows, :], down_ref[...], preferred_element_type=F32)
        sigmoid = jax.nn.sigmoid(gate)
        silu = gate * sigmoid
        hidden_ref[rows, :] = (silu * up).astype(BF)
        grad_ref[rows, gate_columns] = (
            grad * up * sigmoid * (1.0 + gate * (1.0 - sigmoid))
        ).astype(BF)
        grad_ref[rows, up_columns] = (grad * silu).astype(BF)


def feed_forward(normed, cot, gate_up, down):
    length, width = normed.shape
    hidden_width = down.shape[1]
    tile = 256
    steps = hidden_width // tile
    fixed = pl.BlockSpec((length, width), lambda j: (0, 0))
    return pl.pallas_call(
        feed_kernel,
        grid=(steps,),
        in_specs=[
            fixed,
            fixed,
            pl.BlockSpec((width, tile), lambda j: (0, j)),
            pl.BlockSpec((width, tile), lambda j: (0, j + steps)),
            pl.BlockSpec((width, tile), lambda j: (0, j)),
        ],
        out_specs=[
            pl.BlockSpec((length, tile), lambda j: (0, j)),
            pl.BlockSpec((length, 2 * hidden_width), lambda j: (0, 0)),
        ],
        out_shape=[
            jax.ShapeDtypeStruct((length, hidden_width), BF),
            jax.ShapeDtypeStruct((length, 2 * hidden_width), BF),
        ],
        compiler_params=pltpu.CompilerParams(vmem_limit_bytes=60 * 2**20),
        cost_estimate=pl.CostEstimate(
            flops=6 * length * width * hidden_width,
            transcendentals=length * hidden_width,
            bytes_accessed=30_000_000,
        ),
        name="feed_forward",
    )(normed, cot, gate_up, gate_up, down)


def turn_tables(length, block):
    rotated = HD // 2
    angles = np.exp(-np.log(10000.0) * np.arange(rotated // 2) * 2.0 / rotated)
    lanes = np.concatenate([angles, angles, np.zeros(HD - rotated)])
    lanes = np.concatenate([lanes, lanes])
    base = np.arange(block)[:, None] * lanes[None]
    steps = np.zeros((8, 128))
    steps[: length // block] = np.arange(0, length, block)[:, None] * lanes[None]
    pack = lambda table: np.stack([np.cos(table), np.sin(table)]).astype(np.float32)
    return jnp.asarray(pack(base)), jnp.asarray(pack(steps))


def turned_block(values, base_ref, steps_ref, here, sign):
    half = HD // 4
    first_cos, first_sin = steps_ref[0, pl.ds(here, 1), :], steps_ref[1, pl.ds(here, 1), :]
    cosine = first_cos * base_ref[0] - first_sin * base_ref[1]
    sine = first_sin * base_ref[0] + first_cos * base_ref[1]
    lane = lax.rem(lax.broadcasted_iota(jnp.int32, values.shape, 1), HD)
    lower = jnp.where(lane < half, sine, 0.0)
    upper = jnp.where((lane >= half) & (lane < 2 * half), sine, 0.0)
    ahead = pltpu.roll(values, 128 - half, 1)
    behind = pltpu.roll(values, half, 1)
    if sign > 0:
        return values * cosine - ahead * lower + behind * upper
    return values * cosine + ahead * lower - behind * upper


def opening_kernel(*refs):
    (qkv_part, side_part, feed_part, latents, prompt, time_part, feat, facts) = refs[:8]
    gain_ref, bias_ref, base_ref, steps_ref = refs[8:12]
    (n_ref, q_ref, k_ref, v_ref, o_ref, log_ref, res_ref, qkv_out) = refs[12:20]
    side_full, feed_own, prompt_too, facts_too, feat_out = refs[20:25]
    projected, item, time_full, qkv_full, feat_full = refs[25:30]
    sent_far, got_far, sent_near, got_near, here = refs[30:35]
    sent_plane, got_plane, sent_side, got_side = refs[35:39]
    sent_small, got_small, sent_swap, got_swap = refs[39:43]
    place = Place()
    d, core, column, owner = place.d, place.core, place.column, place.owner
    step_here = pl.program_id(0)
    plane_peers = [(lax.rem(d + j, 8), place.z) for j in range(1, 8)]
    rows = qkv_part.shape[0]
    piece = rows // 2
    length, width = item.shape
    total = qkv_full.shape[1]
    block = 256
    parts = range(4)

    def at(ref, index, count):
        return ref.at[pl.ds(pl.multiple_of(index * count, count), count)]

    def ends(k, sender):
        if k < 2:
            source = qkv_part.at[pl.ds(k * piece, piece)]
            spot = pl.multiple_of((2 * column + sender) * rows + k * piece, piece)
            return source, qkv_full.at[pl.ds(spot, piece)]
        if k == 2:
            return side_part, at(side_full, 2 * column + sender, rows)
        return feed_part, at(feed_own, sender, rows)

    def far(k, sender):
        source, target = ends(k, sender)
        return send(source, target, sent_far.at[k], got_far.at[sender, k], place.user)

    def near(k, sender):
        source, target = ends(k, sender)
        return send(source, target, sent_near.at[k], got_near.at[k], place.core_peer)

    def local(k):
        source, target = ends(k, core)
        return pltpu.make_async_copy(source, target, here.at[k])

    def await_part(k, sender):
        @pl.when(owner)
        def _():
            @pl.when(core == sender)
            def _():
                local(k).wait()

            @pl.when(core != sender)
            def _():
                near(k, sender).wait_recv()

        @pl.when(jnp.logical_not(owner))
        def _():
            far(k, sender).wait_recv()

    item_copy = send(latents, item, sent_swap.at[0], got_swap.at[0], place.core_peer)
    item_local = pltpu.make_async_copy(latents, item, here.at[4])
    outward = [
        pltpu.make_async_copy(qkv_full, qkv_out, here.at[7]),
        pltpu.make_async_copy(feat_full, feat_out, here.at[8]),
    ]
    swaps = [
        send(prompt, prompt_too, sent_swap.at[1], got_swap.at[1], place.core_peer),
        send(facts, facts_too, sent_swap.at[2], got_swap.at[2], place.core_peer),
    ]
    smalls = ((time_part, time_full), (feat, feat_full))

    def small(which, j, sender):
        part, whole = smalls[which]
        return send(
            part,
            at(whole, sender, part.shape[0]),
            sent_small.at[which, j - 1],
            got_small.at[which, j - 1],
            plane_peers[j - 1],
        )

    def small_local(which):
        part, whole = smalls[which]
        return pltpu.make_async_copy(part, at(whole, d, part.shape[0]), here.at[5 + which])

    def plane(stage, way, k, sender):
        peer = place.x_peer if way == 0 else place.y_peer
        source = column if stage == 0 else (place.y_column if way == 0 else place.x_column)
        spot = qkv_full.at[
            pl.ds(pl.multiple_of((2 * source + sender) * rows + k * piece, piece), piece)
        ]
        slot = 4 * stage + 2 * sender + k
        return send(spot, spot, sent_plane.at[way, slot], got_plane.at[way, slot], peer)

    def side(stage, way, sender):
        peer = place.x_peer if way == 0 else place.y_peer
        source = column if stage == 0 else (place.y_column if way == 0 else place.x_column)
        spot = at(side_full, 2 * source + sender, rows)
        slot = 2 * stage + sender
        return send(spot, spot, sent_side.at[way, slot], got_side.at[way, slot], peer)

    def side_one():
        for sender in range(2):
            await_part(2, sender)
            side(0, sender, sender).start()
        for sender in range(2):
            side(0, 1 - sender, sender).start()

    def side_two():
        side(0, 0, 0).wait_recv()
        side(1, 1, 0).start()
        side(0, 1, 1).wait_recv()
        side(1, 0, 1).start()

    @pl.when(step_here == 0)
    def _():
        greet([place.far_same, place.far_other] + plane_peers)
        for k in parts:
            far(k, core).start()

        @pl.when(owner)
        def _():
            item_copy.start()
            item_local.start()
            for k in parts:
                local(k).start()

        for which in range(2):
            small_local(which).start()
        for j in range(1, 8):
            for which in range(2):
                small(which, j, d).start()

        @pl.when(jnp.logical_not(owner))
        def _():
            for k in parts:
                near(k, core).start()

        for swap in swaps:
            swap.start()
        for which in range(2):
            small_local(which).wait()
        for j in range(1, 8):
            for which in range(2):
                small(which, j, lax.rem(d + 8 - j, 8)).wait_recv()

        @pl.when(owner)
        def _():
            item_local.wait()

        @pl.when(jnp.logical_not(owner))
        def _():
            item_copy.wait_recv()

        user = 2 * column + place.pair
        token_row = jnp.dot(
            feat_full[pl.ds(pl.multiple_of(user * 16, 16), 16), :],
            time_full[...],
            preferred_element_type=F32,
        )
        row_number = lax.broadcasted_iota(jnp.int32, (16, width), 0)

        def norm_rows(step, keep):
            local_row = pl.multiple_of(step * 16, 16)
            spot = pl.multiple_of(lax.rem(local_row + core * (length // 2), length), 16)
            values = item[pl.ds(spot, 16), :].astype(F32)
            values = jnp.where(row_number + spot == 0, token_row, values)
            if keep:
                res_ref[pl.ds(local_row, 16), :] = values
            centered = values - jnp.mean(values, axis=-1, keepdims=True)
            inverse = lax.rsqrt(jnp.mean(centered * centered, axis=-1, keepdims=True) + EPS)
            n_ref[pl.ds(local_row, 16), :] = (
                centered * inverse * gain_ref[...] + bias_ref[...]
            ).astype(BF)

        def forward(k):
            for sender in range(2):
                await_part(k, sender)
                plane(0, 0, k, sender).start()
                plane(0, 1, k, sender).start()

        steps = length // 16
        forward(0)

        @pl.loop(0, steps // 2)
        def _(step):
            norm_rows(step, True)

        forward(1)

        @pl.loop(steps // 2, steps)
        def _(step):
            norm_rows(step, False)

        for k in range(2):
            plane(0, 0, k, 0).wait_recv()
            plane(1, 1, k, 0).start()
            plane(0, 1, k, 1).wait_recv()
            plane(1, 0, k, 1).start()
            plane(0, 0, k, 1).wait_recv()
            plane(0, 1, k, 0).wait_recv()
        for k in range(2):
            plane(1, 1, k, 0).wait_recv()
            plane(1, 0, k, 1).wait_recv()

        side_one()

        for each in outward:
            each.start()
        third = total // 3
        for part in range(3):
            columns = pl.ds(part * third, third)

            @pl.loop(0, length // block)
            def _(step):
                spot = pl.ds(pl.multiple_of(step * block, block), block)
                projected[spot, columns] = jnp.dot(
                    n_ref[spot, :], qkv_full[:, columns], preferred_element_type=F32
                )

    @pl.when(step_here == 1)
    def _():
        side_two()

    def turn(first, target):
        columns = pl.ds(pl.multiple_of(first + step_here * 128, 128), 128)

        @pl.loop(0, length // block)
        def _(step):
            spot = pl.ds(pl.multiple_of(step * block, block), block)
            index = lax.rem(step + core * (length // block // 2), length // block)
            target[spot, :] = turned_block(
                projected[spot, columns], base_ref, steps_ref, index, 1
            ).astype(BF)

    turn(0, q_ref)
    turn(total // 3, k_ref)
    v_ref[...] = projected[
        :, pl.ds(pl.multiple_of(2 * (total // 3) + step_here * 128, 128), 128)
    ].astype(BF)
    attend_pair(HD, block, q_ref, k_ref, v_ref, None, o_ref, log_ref)

    @pl.when(step_here == pl.num_programs(0) - 1)
    def _():
        for sender in range(2):
            side(0, 1 - sender, sender).wait_recv()
        side(1, 1, 0).wait_recv()
        side(1, 0, 1).wait_recv()
        for sender in range(2):
            await_part(3, sender)
        for each in outward:
            each.wait()
        for swap in swaps:
            swap.wait()
        for j in range(1, 8):
            for which in range(2):
                small(which, j, d).wait_send()
        for k in parts:
            far(k, core).wait_send()

        @pl.when(owner)
        def _():
            item_copy.wait_send()

        @pl.when(jnp.logical_not(owner))
        def _():
            for k in parts:
                near(k, core).wait_send()

        for sender in range(2):
            for way in range(2):
                side(0, way, sender).wait_send()
                for k in range(2):
                    plane(0, way, k, sender).wait_send()
        side(1, 1, 0).wait_send()
        side(1, 0, 1).wait_send()
        for k in range(2):
            plane(1, 1, k, 0).wait_send()
            plane(1, 0, k, 1).wait_send()


def opening(place, qkv_part, side_part, feed_part, latents, prompt, time_part, feat, facts, gain, bias):
    length, width = latents.shape
    total = qkv_part.shape[1]
    rows = qkv_part.shape[0]
    pairs = total // 3 // 128
    base, steps = turn_tables(length, 256)
    block = pl.BlockSpec((length, 128), lambda i: (0, i))
    whole = pl.BlockSpec(memory_space=pltpu.VMEM)
    wide = jax.ShapeDtypeStruct((length, total // 3), BF)
    dma = pltpu.SemaphoreType.DMA
    return pl.pallas_call(
        opening_kernel,
        grid=(pairs,),
        in_specs=[ANYWHERE] * 8 + [whole] * 4,
        out_specs=[whole]
        + [block] * 4
        + [pl.BlockSpec((1, 2, length), lambda i: (i, 0, 0)), whole]
        + [ANYWHERE] * 6,
        out_shape=[jax.ShapeDtypeStruct((length, width), BF)]
        + [wide] * 4
        + [
            jax.ShapeDtypeStruct((pairs, 2, length), F32),
            jax.ShapeDtypeStruct((length // 2, width), F32),
            jax.ShapeDtypeStruct((8 * rows, total), BF),
            jax.ShapeDtypeStruct((8 * rows, side_part.shape[1]), BF),
            jax.ShapeDtypeStruct((2 * rows, feed_part.shape[1]), BF),
            jax.ShapeDtypeStruct(prompt.shape, BF),
            jax.ShapeDtypeStruct(facts.shape, facts.dtype),
            jax.ShapeDtypeStruct((8 * feat.shape[0], feat.shape[1]), BF),
        ],
        scratch_shapes=[
            pltpu.VMEM((length, total), F32),
            pltpu.VMEM((length, width), BF),
            pltpu.VMEM((8 * time_part.shape[0], width), BF),
            pltpu.VMEM((8 * rows, total), BF),
            pltpu.VMEM((8 * feat.shape[0], feat.shape[1]), BF),
            dma((4,)),
            dma((2, 4)),
            dma((4,)),
            dma((4,)),
            dma((9,)),
            dma((2, 8)),
            dma((2, 8)),
            dma((2, 4)),
            dma((2, 4)),
            dma((2, 7)),
            dma((2, 7)),
            dma((3,)),
            dma((3,)),
        ],
        compiler_params=pltpu.CompilerParams(
            collective_id=place, has_side_effects=True, vmem_limit_bytes=60 * 2**20
        ),
        cost_estimate=pl.CostEstimate(
            flops=4 * length * length * total // 3 + 2 * length * width * total,
            transcendentals=length * length * total // 192,
            bytes_accessed=200_000_000,
        ),
        name="opening",
    )(
        qkv_part,
        side_part,
        feed_part,
        latents,
        prompt,
        time_part,
        feat,
        facts,
        gain[None],
        bias[None],
        base,
        steps,
    )


def per_device_paired(
    latents,
    prompt_tokens,
    prompt_lengths,
    timesteps,
    time_weight,
    self_gain,
    self_bias,
    qkv_weight,
    self_out_weight,
    cross_gain,
    cross_bias,
    cross_query_weight,
    context_weight,
    cross_out_weight,
    feed_gain,
    feed_bias,
    gate_up_weight,
    down_weight,
    down_bias,
    cotangent,
):
    d = lax.axis_index("dp")
    z = lax.axis_index("mp")
    core, pair = d & 1, z >> 1
    owner = core == pair
    length = latents.shape[1] + 1
    rows = length // 4
    half_rows = length // 2
    part_rows = qkv_weight.shape[0]
    n = cross_query_weight.shape[1]

    side_part = jnp.concatenate(
        [
            self_out_weight.T,
            cross_query_weight,
            cross_out_weight.T,
            context_weight.reshape(part_rows, -1),
        ],
        axis=1,
    )
    feature_width = 8 * time_weight.shape[0]
    features = time_features(timesteps, feature_width).astype(BF)
    (
        normed_one,
        queries,
        keys,
        values,
        attended,
        self_logs,
        residual_mine,
        qkv_full,
        side_full,
        gate_up_own,
        prompt_too,
        facts_too,
        features_full,
    ) = opening(
        5,
        qkv_weight.reshape(part_rows, -1),
        side_part,
        gate_up_weight.reshape(part_rows, -1),
        jnp.pad(latents[0], ((1, 0), (0, 0))),
        prompt_tokens[0],
        time_weight,
        jnp.broadcast_to(features, (16, feature_width)),
        jnp.broadcast_to(prompt_lengths[:, None], (8, 128)),
        self_gain,
        self_bias,
    )
    gate_up_full = plane_gather(gate_up_own)
    self_out_full = side_full[:, :n]
    cross_query_full = side_full[:, n : 2 * n]
    cross_out_full = side_full[:, 2 * n : 3 * n]
    context_full = side_full[:, 3 * n :].reshape(context_weight.shape[0] * 8, -1)

    item_prompt = jnp.where(owner, prompt_tokens[0], prompt_too)
    item_length = jnp.where(owner, prompt_lengths[0], facts_too[0, 0])

    residual_one, normed_two_all, down_own, cot_too = exchange(
        "norm",
        0,
        attended,
        side_full,
        residual_mine,
        cross_gain,
        cross_bias,
        load=Loads((Spread, down_weight.T), (SwapRoute, cotangent[0])),
    )
    cot_shard = jnp.where(owner, cotangent[0], cot_too)
    cot_far = move(cot_shard, SWAP_Z)
    odd = (z & 1) == 1
    cross_q = dot_nn(normed_two_all, cross_query_full).astype(BF)
    context = dot_nn(item_prompt, context_full).astype(BF)
    slots = prompt_tokens.shape[1]
    mask = jnp.where(jnp.arange(slots, dtype=jnp.int32)[:, None] < item_length, 0.0, NEG)
    mask = mask.astype(F32)
    crossed, cross_logs = cross_attention(cross_q, context, mask)
    cot_far = after(cot_far, crossed)
    cot_mine = jnp.concatenate(
        [jnp.where(odd, cot_far, cot_shard), jnp.where(odd, cot_shard, cot_far)], axis=0
    )
    cot_other = move(cot_mine, SWAP_CORE)
    residual_two, normed_three_all, down_full = exchange(
        "norm",
        1,
        crossed,
        side_full,
        residual_one,
        feed_gain,
        feed_bias,
        load=Loads((Plane, down_own)),
        window=2,
    )
    cot_all = jnp.concatenate([cot_mine, after(cot_other, normed_three_all)], axis=0)
    hidden, grad_gate_up = feed_forward(normed_three_all, cot_all, gate_up_full, down_full)

    split = gate_up_weight.shape[2]
    gate_local = dot_tn(normed_three_all, grad_gate_up[:, :split]).astype(BF)
    gate_sums = plane_sum(gate_local)
    up_local = dot_tn(normed_three_all, after(grad_gate_up, gate_local)[:, split:]).astype(BF)
    up_sums = plane_sum(up_local)
    grad_two_all, feed_sums, feed, down_local = exchange(
        "back",
        2,
        after(grad_gate_up, up_local),
        gate_up_full,
        residual_two,
        cot_mine,
        feed_gain,
        works=Works(("nt", hidden, down_full), ("tn", cot_all, hidden)),
    )
    down_sums = plane_sum(down_local)
    grad_crossed = dot_nn(grad_two_all, cross_out_full).astype(BF)
    grad_cross_q, grad_context = cross_attention_back(
        cross_q, context, mask, grad_crossed, cross_logs
    )
    (
        grad_one_all,
        cross_sums,
        gate_near,
        gate_far,
        feed_near,
        cross_query_grad,
        cross_out_grad,
    ) = exchange(
        "back",
        3,
        grad_cross_q,
        side_full,
        residual_one,
        grad_two_all,
        cross_gain,
        load=Loads((Return, gate_sums), (SwapCoreHalf, feed)),
        window=1,
        works=Works(("tn", normed_two_all, grad_cross_q), ("tn", grad_two_all, crossed)),
    )
    context_grad = dot_tn(item_prompt, grad_context).astype(BF).reshape(side_full.shape[0], -1)
    cross_local = jnp.concatenate([cross_query_grad, cross_out_grad, context_grad], axis=1)
    feed_half = feed[:half_rows].astype(F32) + feed_near.astype(F32)
    feed_here = jnp.where(odd, feed_half[rows:], feed_half[:rows])
    feed_away = jnp.where(odd, feed_half[:rows], feed_half[rows:]).astype(BF)
    grad_attended = dot_nn(grad_one_all, self_out_full).astype(BF)
    grad_projected, up_near, up_far, feed_far = self_attention_back(
        7,
        queries,
        keys,
        values,
        grad_attended,
        self_logs,
        Loads((Return, up_sums), (SwapNear, feed_away)),
    )
    residual_here = jnp.where(odd, residual_two[rows:], residual_two[:rows])
    output_here = (residual_here + feed_here + feed_far.astype(F32) + down_bias).astype(BF)
    cross_total = plane_sum(cross_local)
    self_out_local = dot_tn(grad_one_all, attended).astype(BF)
    qkv_local = dot_tn(normed_one, grad_projected).astype(BF)
    self_local = jnp.concatenate([qkv_local, self_out_local], axis=1)
    self_total = plane_sum(self_local)
    grad_in, self_sums, down_near, down_far, output_far = exchange(
        "half",
        4,
        after(grad_projected, self_local),
        qkv_full,
        residual_mine,
        grad_one_all,
        self_gain,
        load=Loads((Return, down_sums), (SwapRoute, output_here)),
    )
    sums = jnp.concatenate(
        [
            jnp.sum(self_sums, axis=1),
            jnp.sum(cross_sums, axis=1),
            jnp.sum(feed_sums, axis=1),
            jnp.sum(cot_mine.astype(F32), axis=0)[None],
            jnp.zeros((1, grad_in.shape[1]), F32),
        ],
        axis=0,
    )
    share = sums.shape[1] // 8
    pieces = jnp.swapaxes(sums.reshape(8, 8, share), 0, 1)
    pieces = jnp.pad(pieces, ((0, 0), (0, 0), (0, 256 - share))).reshape(64, 256)
    whole, token_rows, sums, cross_near, cross_far, self_near, self_far = spread_gradient(
        8, grad_in, pieces, Loads((Return, cross_total), (Return, self_total))
    )
    sums = jnp.sum(sums.reshape(16, 8, 256), axis=0)[:, :share]
    output = jnp.where(owner, output_here, output_far)
    latents_grad = whole[1:]

    token_rows = token_rows.reshape(8, 16, -1)[:, 0]
    all_features = features_full.reshape(8, 16, -1)[:, 0]
    my_features = jnp.zeros((8, feature_width // 8), F32)
    for j in range(8):
        piece = all_features[:, j * (feature_width // 8) : (j + 1) * (feature_width // 8)]
        my_features = my_features + jnp.where(d == j, piece.astype(F32), 0.0)
    time_grad = lax.dot_general(
        my_features.astype(BF), token_rows, (((0,), (0,)), ((), ())), preferred_element_type=F32
    )

    cross_grads = returned(cross_total, cross_near, cross_far, core, owner)
    self_grads = returned(self_total, self_near, self_far, core, owner)
    qkv_columns = qkv_full.shape[1]
    gate_grad = returned(gate_sums, gate_near, gate_far, core, owner)
    up_grad = returned(up_sums, up_near, up_far, core, owner)
    down_grad = returned(down_sums, down_near, down_far, core, owner)
    return (
        output[None],
        latents_grad[None],
        time_grad,
        sums[0],
        sums[1],
        self_grads[:, :qkv_columns].reshape(qkv_weight.shape),
        self_grads[:, qkv_columns:].T,
        sums[2],
        sums[3],
        cross_grads[:, :n],
        cross_grads[:, 2 * n :].reshape(context_weight.shape),
        cross_grads[:, n : 2 * n].T,
        sums[4],
        sums[5],
        jnp.stack([gate_grad, up_grad], axis=1),
        down_grad.T,
        sums[6],
    )


def solution(mesh):
    placed = (
        P("dp", None, None),
        P("dp", None, None),
        P("dp"),
        P("dp"),
        P("dp", None),
        P(),
        P(),
        P("dp", None, "mp"),
        P("mp", "dp"),
        P(),
        P(),
        P("dp", "mp"),
        P("dp", None, "mp"),
        P("mp", "dp"),
        P(),
        P(),
        P("dp", None, "mp"),
        P("mp", "dp"),
        P(),
        P("dp", "mp", None),
    )
    paired = mesh.shape["dp"] == 8 and mesh.shape["mp"] == 4
    return jax.shard_map(
        per_device_paired if paired else per_device_general,
        mesh=mesh,
        in_specs=placed,
        out_specs=(
            P("dp", "mp", None),
            P("dp", None, None),
            P("dp", None),
            P("dp"),
            P("dp"),
            P("dp", None, "mp"),
            P("mp", "dp"),
            P("dp"),
            P("dp"),
            P("dp", "mp"),
            P("dp", None, "mp"),
            P("mp", "dp"),
            P("dp"),
            P("dp"),
            P("dp", None, "mp"),
            P("mp", "dp"),
            P("dp"),
        ),
        check_vma=False,
    )
```

```python
import functools
import math

import jax
import jax.numpy as jnp
import numpy as np
from jax import lax
from jax.experimental import pallas as pl
from jax.experimental.pallas import tpu as pltpu
from jax.sharding import PartitionSpec as P

HD = 64


EPS = 1e-05
NEG = -1e30


def time_features(steps_in, feature_width):
    half_width = feature_width // 2
    freqs = jnp.exp(-math.log(10000.0) * jnp.arange(half_width, dtype=jnp.float32) / half_width)
    angles = steps_in.astype(jnp.float32)[:, None] * freqs[None, :]
    return jnp.concatenate([jnp.cos(angles), jnp.sin(angles)], axis=-1)


def rope_tables(length, head_size):
    rotated_width = head_size // 2
    half_width = rotated_width // 2
    inverse = jnp.exp(
        -math.log(10000.0) * jnp.arange(half_width, dtype=jnp.float32) * 2.0 / rotated_width
    )
    angles = jnp.arange(length, dtype=jnp.float32)[:, None] * inverse[None, :]
    cosine = jnp.concatenate([jnp.cos(angles), jnp.cos(angles)], axis=-1)
    sine = jnp.concatenate([jnp.sin(angles), jnp.sin(angles)], axis=-1)
    return (cosine[:, None, :], sine[:, None, :])


def rotate(values, cosine, sine):
    rotated_width = cosine.shape[-1]
    half_width = rotated_width // 2
    first = values[..., :rotated_width]
    turned = jnp.concatenate([-first[..., half_width:], first[..., :half_width]], axis=-1)
    return jnp.concatenate([first * cosine + turned * sine, values[..., rotated_width:]], axis=-1)


def unrotate(grads_in, cosine, sine):
    rotated_width = cosine.shape[-1]
    half_width = rotated_width // 2
    first = grads_in[..., :rotated_width]
    scaled_in = first * sine
    turned = jnp.concatenate([scaled_in[..., half_width:], -scaled_in[..., :half_width]], axis=-1)
    return jnp.concatenate([first * cosine + turned, grads_in[..., rotated_width:]], axis=-1)


def layer_norm(values, gain, bias):
    centered = values - jnp.mean(values, axis=-1, keepdims=True)
    inverse = lax.rsqrt(jnp.mean(centered * centered, axis=-1, keepdims=True) + EPS)
    scaled = centered * inverse
    return (scaled * gain + bias, scaled, inverse)


def norm_back(grad_normed, scaled, inverse, gain):
    grad_scaled = grad_normed * gain
    first_mean = jnp.mean(grad_scaled, axis=-1, keepdims=True)
    second_mean = jnp.mean(grad_scaled * scaled, axis=-1, keepdims=True)
    grad_values = inverse * (grad_scaled - first_mean - scaled * second_mean)
    return (
        grad_values,
        jnp.sum(grad_normed * scaled, axis=(0, 1)),
        jnp.sum(grad_normed, axis=(0, 1)),
    )


def attend_forward(queries, key_rows, value_rows, bias_rows, block_size):
    score_scale = queries.shape[-1] ** (-0.5)

    def one_item(operands):
        item_query, item_key, item_value, item_bias = operands
        query_blocks = item_query.reshape(-1, block_size, item_query.shape[1], item_query.shape[2])

        def one_block(block_query):
            scores = jnp.einsum(
                "qhe,khe->hqk", block_query, item_key, preferred_element_type=jnp.float32
            )
            scores = scores * score_scale + item_bias[None, None, :]
            row_max = jnp.max(scores, axis=-1, keepdims=True)
            expos = jnp.exp(scores - row_max)
            row_total = jnp.sum(expos, axis=-1, keepdims=True)
            weights_p = (expos / row_total).astype(jnp.bfloat16)
            mixed = jnp.einsum(
                "hqk,khe->qhe", weights_p, item_value, preferred_element_type=jnp.float32
            )
            return (mixed, (row_max + jnp.log(row_total))[..., 0])

        mixed, log_total = lax.map(one_block, query_blocks)
        return (mixed.reshape(item_query.shape), log_total)

    return lax.map(one_item, (queries, key_rows, value_rows, bias_rows))


def attend_backward(queries, key_rows, value_rows, bias_rows, log_totals, grad_out, block_size):
    score_scale = queries.shape[-1] ** (-0.5)

    def one_item(operands):
        item_query, item_key, item_value, item_bias, item_log, item_grad = operands
        block_shape = (-1, block_size, item_query.shape[1], item_query.shape[2])
        query_blocks = item_query.reshape(block_shape)
        grad_blocks = item_grad.reshape(block_shape)

        def one_block(carry, operands_block):
            block_query, block_log, block_grad = operands_block
            scores = jnp.einsum(
                "qhe,khe->hqk", block_query, item_key, preferred_element_type=jnp.float32
            )
            scores = scores * score_scale + item_bias[None, None, :]
            probs_full = jnp.exp(scores - block_log[..., None])
            grad_probs = jnp.einsum(
                "qhe,khe->hqk", block_grad, item_value, preferred_element_type=jnp.float32
            )
            delta_row = jnp.sum(probs_full * grad_probs, axis=-1, keepdims=True)
            grad_scores = (probs_full * (grad_probs - delta_row)).astype(jnp.bfloat16)
            grad_query = (
                jnp.einsum(
                    "hqk,khe->qhe", grad_scores, item_key, preferred_element_type=jnp.float32
                )
                * score_scale
            )
            grad_key = (
                carry[0]
                + jnp.einsum(
                    "hqk,qhe->khe", grad_scores, block_query, preferred_element_type=jnp.float32
                )
                * score_scale
            )
            grad_value = carry[1] + jnp.einsum(
                "hqk,qhe->khe",
                probs_full.astype(jnp.bfloat16),
                block_grad,
                preferred_element_type=jnp.float32,
            )
            return ((grad_key, grad_value), grad_query)

        start_carry = (
            jnp.zeros(item_key.shape, jnp.float32),
            jnp.zeros(item_value.shape, jnp.float32),
        )
        (grad_key, grad_value), grad_query = lax.scan(
            one_block, start_carry, (query_blocks, item_log, grad_blocks)
        )
        return (grad_query.reshape(item_query.shape), grad_key, grad_value)

    return lax.map(one_item, (queries, key_rows, value_rows, bias_rows, log_totals, grad_out))


def per_device_general(
    latents,
    prompt_tokens,
    prompt_lengths,
    timesteps,
    time_weight,
    self_gain,
    self_bias,
    qkv_weight,
    self_out_weight,
    cross_gain,
    cross_bias,
    cross_query_weight,
    context_weight,
    cross_out_weight,
    feed_gain,
    feed_bias,
    gate_up_weight,
    down_weight,
    down_bias,
    cotangent,
):
    gathered = (
        lax.all_gather(time_weight, "dp", axis=0, tiled=True),
        lax.all_gather(qkv_weight, "dp", axis=0, tiled=True),
        lax.all_gather(self_out_weight, "dp", axis=1, tiled=True),
        lax.all_gather(cross_query_weight, "dp", axis=0, tiled=True),
        lax.all_gather(context_weight, "dp", axis=0, tiled=True),
        lax.all_gather(cross_out_weight, "dp", axis=1, tiled=True),
        lax.all_gather(gate_up_weight, "dp", axis=0, tiled=True),
        lax.all_gather(down_weight, "dp", axis=1, tiled=True),
    )
    (
        time_full,
        qkv_full,
        self_out_full,
        cross_query_full,
        context_full,
        cross_out_full,
        gate_up_full,
        down_full,
    ) = gathered
    items_here = latents.shape[0]
    seq_len = latents.shape[1] + 1
    shard_rows = seq_len // lax.axis_size("mp")
    first_row = lax.axis_index("mp") * shard_rows
    head_size = HD
    block_size = min(512, seq_len)
    features = time_features(timesteps, time_full.shape[0]).astype(jnp.bfloat16)
    token_row = jnp.dot(features, time_full, preferred_element_type=jnp.float32)
    residual_in = jnp.concatenate([token_row[:, None, :], latents.astype(jnp.float32)], axis=1)
    normed_one, scaled_one, inverse_one = layer_norm(residual_in, self_gain, self_bias)
    normed_one = normed_one.astype(jnp.bfloat16)
    projected = jnp.einsum(
        "bsd,dkc->bskc", normed_one, qkv_full, preferred_element_type=jnp.float32
    )
    heads_here = projected.shape[-1] // head_size
    head_shape = (items_here, seq_len, heads_here, head_size)
    cosine, sine = rope_tables(seq_len, head_size)
    queries = rotate(projected[:, :, 0].reshape(head_shape), cosine, sine).astype(jnp.bfloat16)
    key_rows = rotate(projected[:, :, 1].reshape(head_shape), cosine, sine).astype(jnp.bfloat16)
    value_rows = projected[:, :, 2].reshape(head_shape).astype(jnp.bfloat16)
    open_rows = jnp.zeros((items_here, seq_len), jnp.float32)
    attended, self_logs = attend_forward(queries, key_rows, value_rows, open_rows, block_size)
    attended = attended.reshape(items_here, seq_len, heads_here * head_size).astype(jnp.bfloat16)
    segment = attended
    self_branch = jnp.swapaxes(
        lax.psum_scatter(
            jnp.swapaxes(jnp.dot(segment, self_out_full, preferred_element_type=jnp.float32), 0, 1),
            "mp",
            scatter_dimension=0,
            tiled=True,
        ),
        0,
        1,
    )
    residual_one = lax.dynamic_slice_in_dim(residual_in, first_row, shard_rows, 1) + self_branch
    normed_two, scaled_two, inverse_two = layer_norm(residual_one, cross_gain, cross_bias)
    normed_two_all = lax.all_gather(normed_two.astype(jnp.bfloat16), "mp", axis=1, tiled=True)
    cross_q = (
        jnp.dot(normed_two_all, cross_query_full, preferred_element_type=jnp.float32)
        .astype(jnp.bfloat16)
        .reshape(head_shape)
    )
    context = jnp.einsum(
        "bpc,ckh->bpkh", prompt_tokens, context_full, preferred_element_type=jnp.float32
    ).astype(jnp.bfloat16)
    prompt_slots = prompt_tokens.shape[1]
    context_shape = (items_here, prompt_slots, heads_here, head_size)
    context_keys = context[:, :, 0].reshape(context_shape)
    context_values = context[:, :, 1].reshape(context_shape)
    slot_index = jnp.arange(prompt_slots, dtype=jnp.int32)
    mask_rows = jnp.where(slot_index[None, :] < prompt_lengths[:, None], 0.0, NEG).astype(
        jnp.float32
    )
    crossed, cross_logs = attend_forward(
        cross_q, context_keys, context_values, mask_rows, block_size
    )
    crossed = crossed.reshape(items_here, seq_len, heads_here * head_size).astype(jnp.bfloat16)
    segment = crossed
    cross_branch = jnp.swapaxes(
        lax.psum_scatter(
            jnp.swapaxes(
                jnp.dot(segment, cross_out_full, preferred_element_type=jnp.float32), 0, 1
            ).astype(jnp.bfloat16),
            "mp",
            scatter_dimension=0,
            tiled=True,
        ).astype(jnp.float32),
        0,
        1,
    )
    residual_two = residual_one + cross_branch
    normed_three, scaled_three, inverse_three = layer_norm(residual_two, feed_gain, feed_bias)
    normed_three_all = lax.all_gather(normed_three.astype(jnp.bfloat16), "mp", axis=1, tiled=True)
    gate_up = jnp.einsum(
        "bsd,dkf->bskf", normed_three_all, gate_up_full, preferred_element_type=jnp.float32
    )
    gate_part = gate_up[:, :, 0]
    up_part = gate_up[:, :, 1]
    hidden = (jax.nn.silu(gate_part) * up_part).astype(jnp.bfloat16)
    segment = hidden
    feed_branch = jnp.swapaxes(
        lax.psum_scatter(
            jnp.swapaxes(
                jnp.dot(segment, down_full, preferred_element_type=jnp.float32), 0, 1
            ).astype(jnp.bfloat16),
            "mp",
            scatter_dimension=0,
            tiled=True,
        ).astype(jnp.float32),
        0,
        1,
    )
    output = (residual_two + feed_branch + down_bias).astype(jnp.bfloat16)
    regathered = (
        lax.all_gather(qkv_weight, "dp", axis=0, tiled=True),
        lax.all_gather(self_out_weight, "dp", axis=1, tiled=True),
        lax.all_gather(cross_query_weight, "dp", axis=0, tiled=True),
        lax.all_gather(context_weight, "dp", axis=0, tiled=True),
        lax.all_gather(cross_out_weight, "dp", axis=1, tiled=True),
        lax.all_gather(gate_up_weight, "dp", axis=0, tiled=True),
        lax.all_gather(down_weight, "dp", axis=1, tiled=True),
    )
    (
        qkv_back,
        self_out_back,
        cross_query_back,
        context_back,
        cross_out_back,
        gate_up_back,
        down_back,
    ) = regathered
    grad_rows = lax.all_gather(cotangent, "mp", axis=1, tiled=True)
    grad_hidden = jnp.einsum(
        "bsd,fd->bsf", grad_rows, down_back, preferred_element_type=jnp.float32
    )
    sigmoid_gate = jax.nn.sigmoid(gate_part)
    grad_up = grad_hidden * gate_part * sigmoid_gate
    grad_gate = grad_hidden * up_part * sigmoid_gate * (1.0 + gate_part * (1.0 - sigmoid_gate))
    grad_gate_up = jnp.stack([grad_gate, grad_up], axis=2).astype(jnp.bfloat16)
    down_weight_grad = jnp.einsum(
        "bsf,bsd->fd", hidden, grad_rows, preferred_element_type=jnp.float32
    )
    gate_up_grad = jnp.einsum(
        "bsd,bskf->dkf", normed_three_all, grad_gate_up, preferred_element_type=jnp.float32
    )
    segment = grad_gate_up
    grad_normed_three = jnp.swapaxes(
        lax.psum_scatter(
            jnp.swapaxes(
                jnp.einsum(
                    "bskf,dkf->bsd", segment, gate_up_back, preferred_element_type=jnp.float32
                ),
                0,
                1,
            ).astype(jnp.bfloat16),
            "mp",
            scatter_dimension=0,
            tiled=True,
        ).astype(jnp.float32),
        0,
        1,
    )
    grad_two_norm, feed_gain_part, feed_bias_part = norm_back(
        grad_normed_three, scaled_three, inverse_three, feed_gain
    )
    grad_out_shard = cotangent.astype(jnp.float32)
    down_bias_part = jnp.sum(grad_out_shard, axis=(0, 1))
    grad_residual_two = (grad_out_shard + grad_two_norm).astype(jnp.bfloat16)
    grad_rows_two = lax.all_gather(grad_residual_two, "mp", axis=1, tiled=True)
    grad_crossed = jnp.einsum(
        "bsd,hd->bsh", grad_rows_two, cross_out_back, preferred_element_type=jnp.float32
    ).astype(jnp.bfloat16)
    cross_out_grad = jnp.einsum(
        "bsh,bsd->hd", crossed, grad_rows_two, preferred_element_type=jnp.float32
    )
    grad_cross_q, grad_cross_k, grad_cross_v = attend_backward(
        cross_q,
        context_keys,
        context_values,
        mask_rows,
        cross_logs,
        grad_crossed.reshape(head_shape),
        block_size,
    )
    grad_cross_q = grad_cross_q.reshape(items_here, seq_len, heads_here * head_size).astype(
        jnp.bfloat16
    )
    grad_context = (
        jnp.stack([grad_cross_k, grad_cross_v], axis=2)
        .reshape(items_here, prompt_slots, 2, heads_here * head_size)
        .astype(jnp.bfloat16)
    )
    cross_query_grad = jnp.einsum(
        "bsd,bsh->dh", normed_two_all, grad_cross_q, preferred_element_type=jnp.float32
    )
    context_weight_grad = jnp.einsum(
        "bpc,bpkh->ckh", prompt_tokens, grad_context, preferred_element_type=jnp.float32
    )
    segment = grad_cross_q
    grad_normed_two = jnp.swapaxes(
        lax.psum_scatter(
            jnp.swapaxes(
                jnp.einsum(
                    "bsh,dh->bsd", segment, cross_query_back, preferred_element_type=jnp.float32
                ),
                0,
                1,
            ).astype(jnp.bfloat16),
            "mp",
            scatter_dimension=0,
            tiled=True,
        ).astype(jnp.float32),
        0,
        1,
    )
    grad_one_norm, cross_gain_part, cross_bias_part = norm_back(
        grad_normed_two, scaled_two, inverse_two, cross_gain
    )
    grad_residual_one = (grad_residual_two.astype(jnp.float32) + grad_one_norm).astype(jnp.bfloat16)
    grad_rows_one = lax.all_gather(grad_residual_one, "mp", axis=1, tiled=True)
    grad_attended = jnp.einsum(
        "bsd,hd->bsh", grad_rows_one, self_out_back, preferred_element_type=jnp.float32
    ).astype(jnp.bfloat16)
    self_out_grad = jnp.einsum(
        "bsh,bsd->hd", attended, grad_rows_one, preferred_element_type=jnp.float32
    )
    grad_query, grad_key, grad_value = attend_backward(
        queries,
        key_rows,
        value_rows,
        open_rows,
        self_logs,
        grad_attended.reshape(head_shape),
        block_size,
    )
    grad_query = unrotate(grad_query, cosine, sine)
    grad_key = unrotate(grad_key, cosine, sine)
    grad_projected = (
        jnp.stack([grad_query, grad_key, grad_value], axis=2)
        .reshape(items_here, seq_len, 3, heads_here * head_size)
        .astype(jnp.bfloat16)
    )
    qkv_weight_grad = jnp.einsum(
        "bsd,bskc->dkc", normed_one, grad_projected, preferred_element_type=jnp.float32
    )
    grad_normed_part = jnp.einsum(
        "bskc,dkc->bsd", grad_projected, qkv_back, preferred_element_type=jnp.float32
    )
    summed = (
        lax.psum(grad_normed_part.astype(jnp.bfloat16), "mp").astype(jnp.float32),
        lax.psum(cross_gain_part.astype(jnp.bfloat16), "mp").astype(jnp.float32),
        lax.psum(cross_bias_part.astype(jnp.bfloat16), "mp").astype(jnp.float32),
        lax.psum(feed_gain_part.astype(jnp.bfloat16), "mp").astype(jnp.float32),
        lax.psum(feed_bias_part.astype(jnp.bfloat16), "mp").astype(jnp.float32),
        lax.psum(down_bias_part.astype(jnp.bfloat16), "mp").astype(jnp.float32),
    )
    grad_in_norm, self_gain_part, self_bias_part = norm_back(
        summed[0], scaled_one, inverse_one, self_gain
    )
    grad_residual_in = grad_rows_one.astype(jnp.float32) + grad_in_norm
    latents_grad = grad_residual_in[:, 1:].astype(jnp.bfloat16)
    time_weight_grad = jnp.dot(
        features.astype(jnp.float32).T, grad_residual_in[:, 0], precision=lax.Precision.HIGHEST
    )
    cross_gain_sum, cross_bias_sum, feed_gain_sum, feed_bias_sum, down_bias_sum = (
        summed[1],
        summed[2],
        summed[3],
        summed[4],
        summed[5],
    )
    reduced = (
        lax.psum_scatter(
            time_weight_grad.astype(jnp.bfloat16), "dp", scatter_dimension=0, tiled=True
        ).astype(jnp.float32),
        lax.psum_scatter(
            qkv_weight_grad.astype(jnp.bfloat16), "dp", scatter_dimension=0, tiled=True
        ).astype(jnp.float32),
        lax.psum_scatter(
            self_out_grad.astype(jnp.bfloat16), "dp", scatter_dimension=1, tiled=True
        ).astype(jnp.float32),
        lax.psum_scatter(
            cross_query_grad.astype(jnp.bfloat16), "dp", scatter_dimension=0, tiled=True
        ).astype(jnp.float32),
        lax.psum_scatter(
            context_weight_grad.astype(jnp.bfloat16), "dp", scatter_dimension=0, tiled=True
        ).astype(jnp.float32),
        lax.psum_scatter(
            cross_out_grad.astype(jnp.bfloat16), "dp", scatter_dimension=1, tiled=True
        ).astype(jnp.float32),
        lax.psum_scatter(
            gate_up_grad.astype(jnp.bfloat16), "dp", scatter_dimension=0, tiled=True
        ).astype(jnp.float32),
        lax.psum_scatter(
            down_weight_grad.astype(jnp.bfloat16), "dp", scatter_dimension=1, tiled=True
        ).astype(jnp.float32),
        lax.psum_scatter(
            self_gain_part.astype(jnp.bfloat16), "dp", scatter_dimension=0, tiled=True
        ).astype(jnp.float32),
        lax.psum_scatter(
            self_bias_part.astype(jnp.bfloat16), "dp", scatter_dimension=0, tiled=True
        ).astype(jnp.float32),
        lax.psum_scatter(
            cross_gain_sum.astype(jnp.bfloat16), "dp", scatter_dimension=0, tiled=True
        ).astype(jnp.float32),
        lax.psum_scatter(
            cross_bias_sum.astype(jnp.bfloat16), "dp", scatter_dimension=0, tiled=True
        ).astype(jnp.float32),
        lax.psum_scatter(
            feed_gain_sum.astype(jnp.bfloat16), "dp", scatter_dimension=0, tiled=True
        ).astype(jnp.float32),
        lax.psum_scatter(
            feed_bias_sum.astype(jnp.bfloat16), "dp", scatter_dimension=0, tiled=True
        ).astype(jnp.float32),
        lax.psum_scatter(
            down_bias_sum.astype(jnp.bfloat16), "dp", scatter_dimension=0, tiled=True
        ).astype(jnp.float32),
    )
    return (
        output,
        latents_grad,
        reduced[0],
        reduced[8],
        reduced[9],
        reduced[1],
        reduced[2],
        reduced[10],
        reduced[11],
        reduced[3],
        reduced[4],
        reduced[5],
        reduced[12],
        reduced[13],
        reduced[6],
        reduced[7],
        reduced[14],
    )


AXES = ("dp", "mp")
BF = jnp.bfloat16
F32 = jnp.float32


def flat_permutation(places):
    pairs = []
    for d in range(8):
        for z in range(4):
            target = places(d >> 1, d & 1, z & 1, z >> 1)
            if target is not None:
                s, c, zz, p = target
                pairs.append(((2 * s + c) * 4 + 2 * p + zz, (2 * (d >> 1) + (d & 1)) * 4 + z))
    return [(source, target) for target, source in pairs]


SWAP_CORE = flat_permutation(lambda s, c, zz, p: (s, 1 - c, zz, p))
SWAP_Z = flat_permutation(lambda s, c, zz, p: (s, c, 1 - zz, p))
SWAP_PAIR = flat_permutation(lambda s, c, zz, p: (s, c, zz, 1 - p))
SWAP_X = flat_permutation(lambda s, c, zz, p: (s ^ 1, c, zz, p))
SWAP_Y = flat_permutation(lambda s, c, zz, p: (s ^ 2, c, zz, p))
ROUTE_A = flat_permutation(lambda s, c, zz, p: (s, p, zz, c))
ROUTE_B = flat_permutation(lambda s, c, zz, p: (s, p, zz, 1 - c))
RETURN_B = flat_permutation(lambda s, c, zz, p: (s, 1 - p, zz, c))
OWNER_TO_PARTNER = flat_permutation(lambda s, c, zz, p: (s, 1 - c, zz, p) if c == p else None)
PARTNER_TO_OWNER = flat_permutation(lambda s, c, zz, p: (s, 1 - c, zz, p) if c != p else None)
OWNER_TO_PAIR = flat_permutation(lambda s, c, zz, p: (s, c, zz, 1 - p) if c == p else None)
OWNER_Z = flat_permutation(lambda s, c, zz, p: (s, c, 1 - zz, p) if c == p else None)
PARTNER_Z = flat_permutation(lambda s, c, zz, p: (s, c, 1 - zz, p) if c != p else None)


def move(values, pairs):
    return lax.ppermute(values, AXES, pairs)


def xor_blocks(values, axis, count, index):
    blocks = jnp.split(values, count, axis=axis)
    bit = 1
    while bit < count:
        flip = (index & bit) != 0
        blocks = [jnp.where(flip, blocks[j ^ bit], blocks[j]) for j in range(count)]
        bit *= 2
    return jnp.concatenate(blocks, axis=axis)


def attend_pair(head_size, query_block, queries, keys, values, bias, o_ref, log_ref):
    scale = head_size ** (-0.5)
    length, width = queries.shape
    key_rows = keys[...]
    values_turned = values[...].astype(F32).T.astype(BF)
    lane = lax.broadcasted_iota(jnp.int32, (query_block, width), 1)

    @pl.loop(0, length // query_block)
    def _(step):
        rows = pl.ds(pl.multiple_of(step * query_block, query_block), query_block)
        block = queries[rows, :]
        parts, logs = [], []
        for head in range(2):
            mine = (lane >= head * head_size) & (lane < (head + 1) * head_size)
            masked = jnp.where(mine, block, jnp.zeros_like(block))
            scores = lax.dot_general(
                key_rows, masked, (((1,), (1,)), ((), ())), preferred_element_type=F32
            )
            scores = scores * scale
            if bias is not None:
                scores = scores + bias[...]
            top = jnp.max(scores, axis=0, keepdims=True)
            expos = jnp.exp(scores - top)
            total = jnp.sum(expos, axis=0, keepdims=True)
            mixed = lax.dot_general(
                values_turned[head * head_size : (head + 1) * head_size, :],
                expos.astype(BF),
                (((1,), (0,)), ((), ())),
                preferred_element_type=F32,
            )
            parts.append(mixed * (1.0 / total))
            logs.append(top + jnp.log(total))
        o_ref[rows, :] = jnp.concatenate(parts, axis=0).T.astype(BF)
        log_ref[0, :, rows] = jnp.concatenate(logs, axis=0)


def cross_attention_kernel(q_ref, k_ref, v_ref, bias_ref, o_ref, log_ref):
    attend_pair(HD, 512, q_ref, k_ref, v_ref, bias_ref, o_ref, log_ref)


def attention_backward_kernel(head_size, query_block, turned, load, *refs):
    if turned:
        refs = list(refs)
        q_ref, k_ref, v_ref, d_ref, log_ref, base_ref, steps_ref = refs[:7]
        more = (len(load.operands), len(load.outs_like))
        refs = refs[7:]
        load_ins, g_ref, refs = refs[: more[0]], refs[more[0]], refs[more[0] + 1 :]
        load_outs, refs = refs[: more[1]], refs[more[1] :]
        dk_acc, dv_acc = refs[:2]
        place = Place()
        carried = load.begin(place, load_ins, load_outs, refs[2:])

        @pl.when(pl.program_id(0) == 0)
        def _():
            greet(load.peers(place, [place.core_peer]))
            for each in carried:
                each.start()
    else:
        q_ref, k_ref, v_ref, d_ref, log_ref, bias_ref, dq_ref, g_ref, dk_acc, dv_acc = refs
    scale = head_size ** (-0.5)
    length, width = q_ref.shape
    key_count = k_ref.shape[0]
    here = pl.program_id(0)
    key_rows = k_ref[...]
    value_rows = v_ref[...]
    keys_turned = key_rows.astype(F32).T.astype(BF)
    lane = lax.broadcasted_iota(jnp.int32, (query_block, width), 1)
    dk_acc[...] = jnp.zeros_like(dk_acc)
    dv_acc[...] = jnp.zeros_like(dv_acc)

    def back_turn(values, step):
        blocks = length // query_block
        index = lax.rem(step + place.core * (blocks // 2), blocks)
        return turned_block(values, base_ref, steps_ref, index, -1)

    @pl.loop(0, length // query_block)
    def _(step):
        rows = pl.ds(pl.multiple_of(step * query_block, query_block), query_block)
        block = q_ref[rows, :]
        grads = d_ref[rows, :]
        parts = []
        for head in range(2):
            mine = (lane >= head * head_size) & (lane < (head + 1) * head_size)
            q_mine = jnp.where(mine, block, jnp.zeros_like(block))
            d_mine = jnp.where(mine, grads, jnp.zeros_like(grads))
            scores = lax.dot_general(
                key_rows, q_mine, (((1,), (1,)), ((), ())), preferred_element_type=F32
            )
            scores = scores * scale
            if not turned:
                scores = scores + bias_ref[...]
            probs = jnp.exp(scores - log_ref[0, head : head + 1, rows])
            grad_probs = lax.dot_general(
                value_rows, d_mine, (((1,), (1,)), ((), ())), preferred_element_type=F32
            )
            delta = jnp.sum(probs * grad_probs, axis=0, keepdims=True)
            grad_scores = (probs * (grad_probs - delta)).astype(BF)
            dv_acc[...] += jnp.dot(probs.astype(BF), d_mine, preferred_element_type=F32)
            dk_acc[...] += jnp.dot(grad_scores, q_mine, preferred_element_type=F32)
            parts.append(
                jnp.dot(
                    keys_turned[head * head_size : (head + 1) * head_size, :],
                    grad_scores,
                    preferred_element_type=F32,
                )
            )
        grad_query = jnp.concatenate(parts, axis=0).T * scale
        if turned:
            columns = pl.ds(pl.multiple_of(here * width, width), width)
            g_ref[rows, columns] = back_turn(grad_query, step).astype(BF)
        else:
            dq_ref[rows, :] = grad_query.astype(BF)

    total_width = g_ref.shape[1] // (3 if turned else 2)
    first = total_width if turned else 0
    key_columns = pl.ds(pl.multiple_of(first + here * width, width), width)
    value_columns = pl.ds(pl.multiple_of(first + total_width + here * width, width), width)
    if turned:

        @pl.loop(0, key_count // query_block)
        def _(step):
            rows = pl.ds(pl.multiple_of(step * query_block, query_block), query_block)
            g_ref[rows, key_columns] = back_turn(dk_acc[rows, :] * scale, step).astype(BF)
            g_ref[rows, value_columns] = dv_acc[rows, :].astype(BF)

        @pl.when(here == pl.num_programs(0) - 1)
        def _():
            for each in carried:
                each.finish()
    else:
        g_ref[:, key_columns] = (dk_acc[...] * scale).astype(BF)
        g_ref[:, value_columns] = dv_acc[...].astype(BF)


def self_attention_back(place, queries, keys, values, grads, logs, load):
    length, total = queries.shape
    pairs = total // 128
    block = pl.BlockSpec((length, 128), lambda i: (0, i))
    whole = pl.BlockSpec(memory_space=pltpu.VMEM)
    tables = turn_tables(length, 256)
    return pl.pallas_call(
        functools.partial(attention_backward_kernel, HD, 256, True, load),
        grid=(pairs,),
        in_specs=[block] * 4
        + [pl.BlockSpec((1, 2, length), lambda i: (i, 0, 0))]
        + [whole] * 2
        + [ANYWHERE] * len(load.operands),
        out_specs=[pl.BlockSpec((length, 3 * total), lambda i: (0, 0))]
        + [ANYWHERE] * len(load.outs_like),
        out_shape=[jax.ShapeDtypeStruct((length, 3 * total), BF)] + load.outs_like,
        scratch_shapes=[pltpu.VMEM((length, 128), F32)] * 2 + load.scratch,
        compiler_params=pltpu.CompilerParams(collective_id=place, has_side_effects=True),
        cost_estimate=pl.CostEstimate(
            flops=10 * length * length * total,
            transcendentals=length * length * total // 64,
            bytes_accessed=100_000_000,
        ),
        name="self_attention_back",
    )(queries, keys, values, grads, logs, *tables, *load.operands)


def cross_attention(queries, context, bias):
    length, total = queries.shape
    slots = context.shape[0]
    pairs = total // 128
    block = pl.BlockSpec((length, 128), lambda i: (0, i))
    key_block = lambda shift: pl.BlockSpec((slots, 128), lambda i: (0, i + shift))
    return pl.pallas_call(
        cross_attention_kernel,
        grid=(pairs,),
        in_specs=[block, key_block(0), key_block(pairs), pl.BlockSpec((slots, 1), lambda i: (0, 0))],
        out_specs=[block, pl.BlockSpec((1, 2, length), lambda i: (i, 0, 0))],
        out_shape=[
            jax.ShapeDtypeStruct((length, total), BF),
            jax.ShapeDtypeStruct((pairs, 2, length), F32),
        ],
        cost_estimate=pl.CostEstimate(
            flops=4 * length * slots * total,
            transcendentals=length * slots * total // 64,
            bytes_accessed=length * total * 4,
        ),
        name="cross_attention",
    )(queries, context, context, bias)


def cross_attention_back(queries, context, bias, grads, logs):
    length, total = queries.shape
    slots = context.shape[0]
    pairs = total // 128
    block = pl.BlockSpec((length, 128), lambda i: (0, i))
    key_block = lambda shift: pl.BlockSpec((slots, 128), lambda i: (0, i + shift))
    return pl.pallas_call(
        functools.partial(attention_backward_kernel, HD, 512, False, None),
        grid=(pairs,),
        in_specs=[
            block,
            key_block(0),
            key_block(pairs),
            block,
            pl.BlockSpec((1, 2, length), lambda i: (i, 0, 0)),
            pl.BlockSpec((slots, 1), lambda i: (0, 0)),
        ],
        out_specs=[block, pl.BlockSpec((slots, 2 * total), lambda i: (0, 0))],
        out_shape=[
            jax.ShapeDtypeStruct((length, total), BF),
            jax.ShapeDtypeStruct((slots, 2 * total), BF),
        ],
        scratch_shapes=[pltpu.VMEM((slots, 128), F32)] * 2,
        cost_estimate=pl.CostEstimate(
            flops=10 * length * slots * total,
            transcendentals=length * slots * total // 64,
            bytes_accessed=length * total * 8,
        ),
        name="cross_attention_back",
    )(queries, context, context, grads, logs, bias)


def dot_nn(left, right):
    return lax.dot_general(left, right, (((1,), (0,)), ((), ())), preferred_element_type=F32)


def dot_nt(left, right):
    return lax.dot_general(left, right, (((1,), (1,)), ((), ())), preferred_element_type=F32)


def dot_tn(left, right):
    return lax.dot_general(left, right, (((0,), (0,)), ((), ())), preferred_element_type=F32)


PLANE = [[0, 2, 4, 6], [1, 3, 5, 7]]


def group_sum(partial):
    rows = partial.shape[0] // 2
    half = partial[:rows].astype(F32) + move(partial[rows:], SWAP_CORE).astype(F32)
    half = half.astype(BF)
    return half.astype(F32) + move(half, SWAP_Z).astype(F32)


def both_halves(half):
    return jnp.concatenate([half, move(half, SWAP_CORE)], axis=0)


def weight_order(one, two, pair):
    first = jnp.where(pair == 0, one, two)
    second = jnp.where(pair == 0, two, one)
    return jnp.concatenate([first, second], axis=0)


def plane_gather(mine):
    return lax.all_gather(mine, "dp", axis=0, tiled=True, axis_index_groups=PLANE)


def plane_sum(grad):
    return lax.psum_scatter(
        grad, "dp", scatter_dimension=0, tiled=True, axis_index_groups=PLANE
    )


def to_owners(total, pair):
    rows = total.shape[0] // 2
    first, second = total[:rows], total[rows:]
    one = move(jnp.where(pair == 0, first, second), ROUTE_A)
    two = move(jnp.where(pair == 0, second, first), RETURN_B)
    return one.astype(F32) + two.astype(F32)


def after(values, *others):
    return lax.optimization_barrier((values, *others))[0]


class Place:
    def __init__(self):
        d = lax.axis_index("dp")
        z = lax.axis_index("mp")
        self.d, self.z = d, z
        self.core = lax.rem(d, 2)
        self.column = d // 2
        self.pair = z // 2
        self.owner = self.core == self.pair
        self.core_peer = (d + 1 - 2 * self.core, z)
        self.near_z = (d, z + 1 - 2 * lax.rem(z, 2))
        self.far_z = z + 2 - 4 * self.pair
        self.far_same = (d, self.far_z)
        self.far_other = (self.core_peer[0], self.far_z)
        self.user = (2 * self.column + self.pair, self.far_z)
        self.x_peer = (d + 2 - 4 * lax.rem(self.column, 2), z)
        self.y_peer = (d + 4 - 8 * (self.column // 2), z)
        self.x_column = self.column + 1 - 2 * lax.rem(self.column, 2)
        self.y_column = self.column + 2 - 4 * (self.column // 2)


def greet(peers):
    barrier = pltpu.get_barrier_semaphore()
    for peer in peers:
        pl.semaphore_signal(
            barrier, inc=1, device_id=peer, device_id_type=pl.DeviceIdType.MESH
        )
    pl.semaphore_wait(barrier, len(peers))


def send(source, target, sent, got, peer):
    return pltpu.make_async_remote_copy(
        src_ref=source,
        dst_ref=target,
        send_sem=sent,
        recv_sem=got,
        device_id=peer,
        device_id_type=pl.DeviceIdType.MESH,
    )


class Spread:
    scratch = [pltpu.SemaphoreType.DMA((2,)), pltpu.SemaphoreType.DMA((3,)), pltpu.SemaphoreType.DMA]
    late = True

    @staticmethod
    def outs(part):
        return [jax.ShapeDtypeStruct((2 * part.shape[0], part.shape[1]), BF)]

    @staticmethod
    def peers(place):
        return [place.far_same, place.far_other]

    def __init__(self, place, ins, outs, sems):
        self.place = place
        (self.part,), (self.own,), (self.sent, self.got, self.here) = ins, outs, sems

    def target(self, sender):
        rows = self.part.shape[0]
        return self.own.at[pl.ds(pl.multiple_of(sender * rows, rows), rows)]

    def far(self, sender):
        return send(
            self.part, self.target(sender), self.sent.at[0], self.got.at[sender], self.place.user
        )

    def near(self, sender):
        return send(
            self.part, self.target(sender), self.sent.at[1], self.got.at[2], self.place.core_peer
        )

    def local(self):
        return pltpu.make_async_copy(self.part, self.target(self.place.core), self.here)

    def start(self):
        place = self.place
        self.far(place.core).start()

        @pl.when(place.owner)
        def _():
            self.local().start()

        @pl.when(jnp.logical_not(place.owner))
        def _():
            self.near(place.core).start()

    def middle(self):
        pass

    def finish(self):
        place = self.place

        @pl.when(place.owner)
        def _():
            self.local().wait()
            self.near(1 - place.core).wait_recv()

        @pl.when(jnp.logical_not(place.owner))
        def _():
            self.near(place.core).wait_send()
            self.far(0).wait_recv()
            self.far(1).wait_recv()

        self.far(place.core).wait_send()


class Plane:
    scratch = [
        pltpu.SemaphoreType.DMA((2, 3)),
        pltpu.SemaphoreType.DMA((2, 3)),
        pltpu.SemaphoreType.DMA,
    ]
    late = False

    @staticmethod
    def outs(own):
        return [jax.ShapeDtypeStruct((4 * own.shape[0], own.shape[1]), BF)]

    @staticmethod
    def peers(place):
        return [place.x_peer, place.y_peer]

    def __init__(self, place, ins, outs, sems):
        self.place = place
        (self.own,), (self.full,), (self.sent, self.got, self.here) = ins, outs, sems
        self.rows = self.own.shape[0] // 2

    def target(self, column, part):
        rows = self.rows
        return self.full.at[pl.ds(pl.multiple_of((2 * column + part) * rows, rows), rows)]

    def one(self, way, part):
        place = self.place
        peer = place.x_peer if way == 0 else place.y_peer
        return send(
            self.own.at[pl.ds(part * self.rows, self.rows)],
            self.target(place.column, part),
            self.sent.at[way, part],
            self.got.at[way, part],
            peer,
        )

    def two(self, way):
        place = self.place
        if way == 0:
            spot = self.target(place.y_column, 1)
            return send(spot, spot, self.sent.at[0, 2], self.got.at[0, 2], place.x_peer)
        spot = self.target(place.x_column, 0)
        return send(spot, spot, self.sent.at[1, 2], self.got.at[1, 2], place.y_peer)

    def local(self):
        rows = self.own.shape[0]
        place = self.full.at[pl.ds(pl.multiple_of(self.place.column * rows, rows), rows)]
        return pltpu.make_async_copy(self.own, place, self.here)

    def start(self):
        for way in range(2):
            self.one(way, way).start()
        for way in range(2):
            self.one(way, 1 - way).start()
        self.local().start()

    def middle(self):
        self.one(0, 0).wait_recv()
        self.two(1).start()
        self.one(1, 1).wait_recv()
        self.two(0).start()

    def finish(self):
        self.local().wait()
        for way in range(2):
            self.one(way, 1 - way).wait_recv()
            self.two(way).wait_recv()
            self.two(way).wait_send()
            for part in range(2):
                self.one(way, part).wait_send()


class Return:
    scratch = [pltpu.SemaphoreType.DMA((2,)), pltpu.SemaphoreType.DMA((2,))]
    late = True

    @staticmethod
    def outs(total):
        shape = jax.ShapeDtypeStruct((total.shape[0] // 2, total.shape[1]), BF)
        return [shape, shape]

    @staticmethod
    def peers(place):
        return [place.far_same, place.far_other]

    def __init__(self, place, ins, outs, sems):
        self.place = place
        (self.total,), (self.near, self.far), (self.sent, self.got) = ins, outs, sems

    def part(self, which):
        rows = self.near.shape[0]
        return self.total.at[pl.ds(pl.multiple_of(which * rows, rows), rows)]

    def to_near(self):
        place = self.place
        return send(
            self.part(1 - place.core), self.near, self.sent.at[0], self.got.at[0], place.core_peer
        )

    def to_far(self, same):
        place = self.place
        which = place.core if same else 1 - place.core
        peer = place.far_same if same else place.far_other
        return send(
            self.part(which), self.far, self.sent.at[0 if same else 1], self.got.at[1], peer
        )

    def start(self):
        place = self.place

        @pl.when(place.owner)
        def _():
            self.to_near().start()

        @pl.when(jnp.logical_not(place.owner))
        def _():
            self.to_far(True).start()
            self.to_far(False).start()

    def middle(self):
        pass

    def finish(self):
        place = self.place

        @pl.when(place.owner)
        def _():
            self.to_near().wait_send()
            self.to_far(True).wait_recv()

        @pl.when(jnp.logical_not(place.owner))
        def _():
            self.to_far(True).wait_send()
            self.to_far(False).wait_send()
            self.to_near().wait_recv()
            self.to_far(False).wait_recv()


class Swap:
    scratch = [pltpu.SemaphoreType.DMA, pltpu.SemaphoreType.DMA]
    late = True
    way = None

    @staticmethod
    def outs(values):
        return [jax.ShapeDtypeStruct(values.shape, values.dtype)]

    @classmethod
    def peers(cls, place):
        return {
            "core": [place.core_peer],
            "z": [place.near_z],
            "route": [place.far_same, place.far_other],
        }[cls.way]

    def __init__(self, place, ins, outs, sems):
        self.place = place
        peer = {"core": place.core_peer, "z": place.near_z, "route": place.far_other}[self.way]
        self.copy = send(ins[0], outs[0], sems[0], sems[1], peer)

    def each(self, act):
        if self.way != "route":
            act()
            return

        @pl.when(jnp.logical_not(self.place.owner))
        def _():
            act()

    def start(self):
        self.each(lambda: self.copy.start())

    def middle(self):
        pass

    def finish(self):
        self.each(lambda: self.copy.wait())


class SwapCore(Swap):
    way = "core"


class SwapCoreHalf(SwapCore):
    @staticmethod
    def outs(values):
        return [jax.ShapeDtypeStruct((values.shape[0] // 2,) + values.shape[1:], values.dtype)]

    def __init__(self, place, ins, outs, sems):
        rows = outs[0].shape[0]
        super().__init__(place, [ins[0].at[pl.ds(rows, rows)]], outs, sems)


class SwapNear(Swap):
    way = "z"


class SwapRoute(Swap):
    way = "route"


def scratch_of(kind, operand):
    return kind.scratch(operand) if callable(kind.scratch) else kind.scratch


class PlaneSum:
    late = False

    @staticmethod
    def scratch(grad):
        rows, width = grad.shape[0] // 4, grad.shape[1]
        return [
            pltpu.VMEM((rows, width), BF),
            pltpu.VMEM((2, rows, width), BF),
            pltpu.VMEM((2, rows, width), BF),
            pltpu.VMEM((rows, width), BF),
            pltpu.SemaphoreType.DMA((2, 2)),
            pltpu.SemaphoreType.DMA((2, 2)),
            pltpu.SemaphoreType.DMA((4,)),
        ]

    @staticmethod
    def outs(grad):
        return [jax.ShapeDtypeStruct((grad.shape[0] // 4, grad.shape[1]), BF)]

    @staticmethod
    def peers(place):
        return [place.x_peer, place.y_peer]

    def __init__(self, place, ins, outs, scratch):
        self.place = place
        (self.grad,), (self.out,) = ins, outs
        self.first, self.staged, self.second, self.own, self.sent, self.got, self.here = scratch
        self.rows = self.own.shape[0]
        self.ways = (place.x_peer, place.y_peer)
        self.columns = (place.x_column, place.y_column)
        self.diagonal = place.x_column + 2 - 4 * (place.x_column // 2)

    def block(self, column, start, count):
        first = pl.multiple_of(column * self.rows + start, count)
        return self.grad.at[pl.ds(first, count)]

    def one(self, way):
        count = self.rows // 2
        return send(
            self.block(self.diagonal, way * count, count),
            self.first.at[pl.ds(way * count, count)],
            self.sent.at[0, way],
            self.got.at[0, way],
            self.ways[way],
        )

    def two(self, way):
        return send(
            self.staged.at[way],
            self.second.at[way],
            self.sent.at[1, way],
            self.got.at[1, way],
            self.ways[way],
        )

    def load(self, way):
        source = self.block(self.columns[way], 0, self.rows)
        return pltpu.make_async_copy(source, self.staged.at[way], self.here.at[way])

    def load_own(self):
        source = self.block(self.place.column, 0, self.rows)
        return pltpu.make_async_copy(source, self.own, self.here.at[2])

    def store(self):
        return pltpu.make_async_copy(self.own, self.out, self.here.at[3])

    def start(self):
        for way in range(2):
            self.one(way).start()
        for way in range(2):
            self.load(way).start()
        self.load_own().start()

    def middle(self):
        count = self.rows // 2
        for way in range(2):
            self.one(way).wait_recv()
            self.load(1 - way).wait()

            @pl.loop(0, count // 16)
            def _(step):
                rows = pl.ds(pl.multiple_of(way * count + step * 16, 16), 16)
                self.staged[1 - way, rows, :] = (
                    self.staged[1 - way, rows, :].astype(F32) + self.first[rows, :].astype(F32)
                ).astype(BF)

            self.two(1 - way).start()

    def finish(self):
        self.load_own().wait()
        for way in range(2):
            self.two(way).wait_recv()

        @pl.loop(0, self.rows // 16)
        def _(step):
            rows = pl.ds(pl.multiple_of(step * 16, 16), 16)
            self.own[rows, :] = (
                self.own[rows, :].astype(F32)
                + self.second[0, rows, :].astype(F32)
                + self.second[1, rows, :].astype(F32)
            ).astype(BF)

        self.store().start()
        for way in range(2):
            self.one(way).wait_send()
            self.two(way).wait_send()
        self.store().wait()


class Loads:
    def __init__(self, *loads):
        self.loads = loads
        self.operands = [operand for _, operand in loads]
        self.outs_like = [out for kind, operand in loads for out in kind.outs(operand)]
        self.scratch = [item for kind, operand in loads for item in scratch_of(kind, operand)]

    def peers(self, place, base):
        found = {id(peer): peer for peer in base}
        for kind, _ in self.loads:
            for peer in kind.peers(place):
                found[id(peer)] = peer
        return list(found.values())

    def begin(self, place, ins, outs, sems):
        result, at, sem_at = [], 0, 0
        for (kind, operand), source in zip(self.loads, ins):
            count, sem_count = len(kind.outs(operand)), len(scratch_of(kind, operand))
            result.append(
                kind(
                    place,
                    [source],
                    outs[at : at + count],
                    sems[sem_at : sem_at + sem_count],
                )
            )
            at, sem_at = at + count, sem_at + sem_count
        return result


class Works:
    def __init__(self, *works):
        self.kinds = [kind for kind, _, _ in works]
        self.operands = [operand for _, left, right in works for operand in (left, right)]
        self.unique = []
        for operand in self.operands:
            if not any(operand is other for other in self.unique):
                self.unique.append(operand)
        self.places = [
            [at for at, other in enumerate(self.unique) if other is operand][0]
            for operand in self.operands
        ]
        self.outs_like = []
        for kind, left, right in works:
            if kind == "nt":
                shape = (left.shape[0], right.shape[0])
            else:
                shape = (left.shape[1], right.shape[1])
            self.outs_like.append(jax.ShapeDtypeStruct(shape, BF))
        self.scratch = (
            [pltpu.VMEM(operand.shape, BF) for operand in self.unique]
            + [pltpu.VMEM(out.shape, BF) for out in self.outs_like]
            + [pltpu.SemaphoreType.DMA((max(1, len(self.unique) + len(works)),))]
        )

    def begin(self, ins, outs, scratch):
        self_ins = list(scratch[: len(self.unique)])
        self_outs = list(scratch[len(self.unique) : -1])
        sems = scratch[-1]
        loads = [
            pltpu.make_async_copy(source, target, sems.at[k])
            for k, (source, target) in enumerate(zip(ins, self_ins))
        ]
        stores = [
            pltpu.make_async_copy(source, target, sems.at[len(loads) + k])
            for k, (source, target) in enumerate(zip(self_outs, outs))
        ]
        return loads, stores, self_ins, self_outs

    def run(self, state):
        loads, stores, ins, outs = state
        waited = set()
        for k, kind in enumerate(self.kinds):
            pair = self.places[2 * k : 2 * k + 2]
            for at in pair:
                if at not in waited:
                    loads[at].wait()
                    waited.add(at)
            left, right, out = ins[pair[0]], ins[pair[1]], outs[k]
            if kind == "nt":
                columns = out.shape[1] // 256

                @pl.loop(0, (out.shape[0] // 256) * columns)
                def _(step):
                    first = pl.ds(pl.multiple_of((step // columns) * 256, 256), 256)
                    second = pl.ds(pl.multiple_of(lax.rem(step, columns) * 256, 256), 256)
                    out[first, second] = lax.dot_general(
                        left[first, :],
                        right[second, :],
                        (((1,), (1,)), ((), ())),
                        preferred_element_type=F32,
                    ).astype(BF)
            else:

                @pl.loop(0, out.shape[0] // 256)
                def _(step):
                    spot = pl.ds(pl.multiple_of(step * 256, 256), 256)
                    out[spot, :] = lax.dot_general(
                        left[:, spot],
                        right[...],
                        (((0,), (0,)), ((), ())),
                        preferred_element_type=F32,
                    ).astype(BF)

            stores[k].start()


ANYWHERE = pl.BlockSpec(memory_space=pl.ANY)


def returned(total, near, far, core, owner):
    rows = near.shape[0]
    mine = jnp.where(core == 0, total[:rows], total[rows:])
    return jnp.where(owner, mine, near).astype(F32) + far.astype(F32)


def exchange_kernel(kind, chunks, window, load, works, *refs):
    refs = list(refs)
    place = Place()
    more = (len(load.operands), len(load.outs_like))
    todo = (len(works.unique), len(works.outs_like), len(works.scratch))
    w_count = len(refs) - 1 - 4 - more[0] - more[1] - todo[0] - todo[1] - todo[2]
    w_count -= 2 + 11 + 4 + (kind != "norm") + len(load.scratch) - 1
    w_from, refs = refs[1 : 1 + w_count], refs[:1] + refs[1 + w_count :]
    ins, refs = refs[:4], refs[4:]
    load_ins, refs = refs[: more[0]], refs[more[0] :]
    work_ins, refs = refs[: todo[0]], refs[todo[0] :]
    outs, refs = refs[:2], refs[2:]
    load_outs, refs = refs[: more[1]], refs[more[1] :]
    work_outs, refs = refs[: todo[1]], refs[todo[1] :]
    rest, refs = refs[:11], refs[11:]
    (a_ref, w_ref, res_ref, loads), refs = refs[:4], refs[4:]
    if kind == "norm":
        a_from, res_from, gain_ref, bias_ref = ins
        res_out, all_ref = outs
    else:
        a_from, res_from, up_from, gain_ref = ins
        all_ref, sum_ref = outs
        up_ref, refs = refs[0], refs[1:]
    carried = load.begin(place, load_ins, load_outs, refs)
    working = works.begin(work_ins, work_outs, refs[len(load.scratch) :])
    mine, given, near, half, far, send_near, got_near, send_far, got_far, send_all, got_all = rest
    rows = mine.shape[0]
    width = mine.shape[1]
    chunk = rows // chunks
    core_peer, far_peer = place.core_peer, place.near_z
    copy = send
    depth = a_ref.shape[1]
    block = 2 * chunk
    tile = 256
    tiles = width // tile

    def load_rows(k):
        first = (k // 2) * block + (0 if k % 2 else rows)
        spot = pl.ds(first, block)
        return pltpu.make_async_copy(a_from.at[spot], a_ref.at[spot], loads.at[2 * tiles + k])

    def load_weight(k):
        spot = pl.ds(k * tile, tile)
        share = depth // len(w_from)
        return [
            pltpu.make_async_copy(
                source.at[spot, pl.ds(window * depth, share)],
                w_ref.at[spot, pl.ds(at * share, share)],
                loads.at[at * tiles + k],
            )
            for at, source in enumerate(w_from)
        ]

    later = [pltpu.make_async_copy(res_from, res_ref, loads.at[2 * tiles + 2 * chunks])]
    if kind != "norm":
        later.append(
            pltpu.make_async_copy(
                up_from.at[pl.ds(0, rows)], up_ref, loads.at[2 * tiles + 2 * chunks + 1]
            )
        )
    load_rows(0).start()
    for k in range(tiles):
        for each in load_weight(k):
            each.start()
    for k in range(1, chunks):
        load_rows(k).start()
    for each in later + working[0]:
        each.start()
    greet(load.peers(place, [core_peer, far_peer]))
    for each in carried:
        if not each.late:
            each.start()

    def near_copy(k):
        part = pl.ds(k * chunk, chunk)
        return copy(given.at[part], near.at[part], send_near.at[k], got_near.at[k], core_peer)

    def far_copy(k):
        part = pl.ds(k * chunk, chunk)
        return copy(half.at[part], far.at[part], send_far.at[k], got_far.at[k], far_peer)

    def all_copy(k):
        return copy(
            all_ref.at[pl.ds(k * chunk, chunk)],
            all_ref.at[pl.ds(rows + k * chunk, chunk)],
            send_all.at[k],
            got_all.at[k],
            core_peer,
        )

    def tile_product(first, target, start, spot):
        target[pl.ds(start, block), spot] = lax.dot_general(
            a_ref[pl.ds(first, block), :],
            w_ref[spot, :],
            (((1,), (1,)), ((), ())),
            preferred_element_type=F32,
        ).astype(target.dtype)

    def product(first, target, start):
        @pl.loop(0, tiles)
        def _(step):
            spot = pl.ds(pl.multiple_of(step * tile, tile), tile)
            tile_product(first, target, start, spot)

    step_rows = 16
    for m in range(chunks // 2):
        load_rows(2 * m).wait()
        if m == 0:
            for k in range(tiles):
                for each in load_weight(k):
                    each.wait()
                tile_product(rows, given, 0, pl.ds(k * tile, tile))
        else:
            product(rows + m * block, given, m * block)
        for k in (2 * m, 2 * m + 1):
            near_copy(k).start()
        load_rows(2 * m + 1).wait()
        product(m * block, mine, m * block)
        for k in (2 * m, 2 * m + 1):
            near_copy(k).wait_recv()

            @pl.loop(0, chunk // step_rows)
            def _(step):
                part = pl.ds(pl.multiple_of(k * chunk + step * step_rows, step_rows), step_rows)
                half[part, :] = (mine[part, :] + near[part, :].astype(F32)).astype(BF)

            far_copy(k).start()
    for each in carried:
        if each.late:
            each.start()
    works.run(working)
    for each in later:
        each.wait()
    if kind != "norm":
        sum_ref[...] = jnp.zeros_like(sum_ref)
    for k in range(chunks):
        far_copy(k).wait_recv()

        @pl.loop(0, chunk // step_rows)
        def _(step):
            part = pl.ds(pl.multiple_of(k * chunk + step * step_rows, step_rows), step_rows)
            total = half[part, :].astype(F32) + far[part, :].astype(F32)
            if kind == "norm":
                values = res_ref[part, :] + total
                res_out[part, :] = values
            else:
                values = res_ref[part, :]
            centered = values - jnp.mean(values, axis=-1, keepdims=True)
            inverse = lax.rsqrt(jnp.mean(centered * centered, axis=-1, keepdims=True) + EPS)
            scaled = centered * inverse
            if kind == "norm":
                all_ref[part, :] = (scaled * gain_ref[...] + bias_ref[...]).astype(BF)
            else:
                grad_scaled = total * gain_ref[...]
                first_mean = jnp.mean(grad_scaled, axis=-1, keepdims=True)
                second_mean = jnp.mean(grad_scaled * scaled, axis=-1, keepdims=True)
                grads = inverse * (grad_scaled - first_mean - scaled * second_mean)
                all_ref[part, :] = (up_ref[part, :].astype(F32) + grads).astype(BF)
                product_rows = total * scaled
                sum_ref[0] += product_rows[:8] + product_rows[8:]
                sum_ref[1] += total[:8] + total[8:]

        if k == chunks // 4:
            for each in carried:
                each.middle()
        if kind != "half":
            all_copy(k).start()
    for k in range(chunks):
        near_copy(k).wait_send()
        far_copy(k).wait_send()
        if kind != "half":
            all_copy(k).wait_send()
            all_copy(k).wait_recv()
    for each in carried:
        each.finish()
    for each in working[1]:
        each.wait()


def exchange(kind, place, a, w, residual, *others, load=Loads(), window=0, works=Works()):
    length, depth = a.shape
    w = w if isinstance(w, tuple) else (w,)
    width = w[0].shape[0]
    rows = length // 2
    chunks = 8 if depth < 2048 else 4
    whole = pl.BlockSpec(memory_space=pltpu.VMEM)
    if kind == "norm":
        gain, bias = others
        operands = (a, *w, residual, gain[None], bias[None])
        outs = [
            jax.ShapeDtypeStruct((rows, width), F32),
            jax.ShapeDtypeStruct((length, width), BF),
        ]
    else:
        up, gain = others
        operands = (a, *w, residual, up, gain[None])
        outs = [
            jax.ShapeDtypeStruct((rows if kind == "half" else length, width), BF),
            jax.ShapeDtypeStruct((2, 8, width), F32),
        ]
    plain = 2 if kind == "norm" else 1
    specs = [ANYWHERE] * (len(operands) - plain) + [whole] * plain
    specs += [ANYWHERE] * (len(load.operands) + len(works.unique))
    tiles = width // 256
    more = [
        pltpu.VMEM((length, depth), BF),
        pltpu.VMEM((width, depth), BF),
        pltpu.VMEM((rows, width), F32),
        pltpu.SemaphoreType.DMA((2 * tiles + 2 * chunks + 2,)),
    ]
    if kind != "norm":
        more.append(pltpu.VMEM((rows, width), BF))
    out_specs = [whole] * 2 + [ANYWHERE] * (len(load.outs_like) + len(works.outs_like))
    operands += tuple(load.operands) + tuple(works.unique)
    outs = outs + load.outs_like + works.outs_like
    return pl.pallas_call(
        functools.partial(exchange_kernel, kind, chunks, window, load, works),
        in_specs=specs,
        out_specs=out_specs,
        out_shape=outs,
        scratch_shapes=[
            pltpu.VMEM((rows, width), F32),
            pltpu.VMEM((rows, width), BF),
            pltpu.VMEM((rows, width), BF),
            pltpu.VMEM((rows, width), BF),
            pltpu.VMEM((rows, width), BF),
        ]
        + [pltpu.SemaphoreType.DMA((chunks,))] * 6
        + more
        + load.scratch
        + works.scratch,
        compiler_params=pltpu.CompilerParams(
            collective_id=place, has_side_effects=True, vmem_limit_bytes=60 * 2**20
        ),
        cost_estimate=pl.CostEstimate(
            flops=2 * length * depth * width,
            transcendentals=0,
            bytes_accessed=100_000_000,
        ),
        name="exchange_" + kind,
    )(*operands)


def spread_kernel(load, chunks, *refs):
    refs = list(refs)
    more = (len(load.operands), len(load.outs_like))
    (half_ref, pieces_ref), refs = refs[:2], refs[2:]
    load_ins, refs = refs[: more[0]], refs[more[0] :]
    (out_ref, token_ref, share_ref), refs = refs[:3], refs[3:]
    load_outs, refs = refs[: more[1]], refs[more[1] :]
    (sent, got, send_token, got_token, send_share, got_share), refs = refs[:6], refs[6:]
    place = Place()
    carried = load.begin(place, load_ins, load_outs, refs)
    d, core, pair = place.d, place.core, place.pair
    inner_z = lax.rem(place.z, 2)
    plane_peers = [(lax.rem(d + j, 8), place.z) for j in range(1, 8)]
    far_peers = [(lax.rem(d + j, 8), place.far_z) for j in range(8)]
    greet([place.near_z] + far_peers + plane_peers)
    rows = half_ref.shape[0]
    chunk = rows // chunks

    def spot(which, k):
        return out_ref.at[pl.ds(pl.multiple_of(which * rows + k * chunk, chunk), chunk)]

    def owner_copy(k, which):
        source = half_ref.at[pl.ds(k * chunk, chunk)]
        return send(source, spot(which, k), sent.at[0, k], got.at[0, k], place.core_peer)

    def pair_copy(k, which):
        source = half_ref.at[pl.ds(k * chunk, chunk)]
        return send(source, spot(which, k), sent.at[1, k], got.at[1, k], place.user)

    def pass_copy(k, which):
        return send(spot(which, k), spot(which, k), sent.at[2, k], got.at[2, k], place.near_z)

    def share_copy(far, j):
        return send(
            pieces_ref.at[pl.ds(pl.multiple_of(lax.rem(d + j, 8) * 8, 8), 8)],
            share_ref.at[pl.ds((8 * far + j) * 8, 8)],
            send_share.at[far, j],
            got_share.at[far, j],
            far_peers[j] if far else plane_peers[j - 1],
        )

    for j in range(8):
        share_copy(1, j).start()
        if j:
            share_copy(0, j).start()
    share_ref[pl.ds(0, 8), :] = pieces_ref[pl.ds(pl.multiple_of(d * 8, 8), 8), :]

    @pl.when(core == inner_z)
    def _():
        for k in range(chunks):
            pair_copy(k, core).start()

    @pl.when(core != pair)
    def _():
        for k in range(chunks):
            owner_copy(k, core).start()

    @pl.when(core == pair)
    def _():
        @pl.loop(0, rows // 16)
        def _(step):
            first = pl.multiple_of(step * 16, 16)
            out_ref[pl.ds(pl.multiple_of(core * rows + first, 16), 16), :] = half_ref[
                pl.ds(first, 16), :
            ]

        for k in range(chunks):
            owner_copy(k, 1 - core).wait_recv()

    def pass_on(k):
        pair_copy(k, inner_z).wait_recv()
        pass_copy(k, inner_z).start()

    @pl.when(core != pair)
    def _():
        for k in range(chunks // 2):
            pass_on(k)

    for each in carried:
        each.start()

    @pl.when(core != pair)
    def _():
        for k in range(chunks // 2, chunks):
            pass_on(k)
        for k in range(chunks):
            pass_copy(k, 1 - inner_z).wait_recv()

    head = 16
    token_ref[pl.ds(pl.multiple_of(d * head, head), head), :] = out_ref[pl.ds(0, head), :]

    def token_copy(j, sender):
        return send(
            out_ref.at[pl.ds(0, head)],
            token_ref.at[pl.ds(pl.multiple_of(sender * head, head), head)],
            send_token.at[j - 1],
            got_token.at[j - 1],
            plane_peers[j - 1],
        )

    for j in range(1, 8):
        token_copy(j, d).start()

    @pl.when(core != pair)
    def _():
        for k in range(chunks):
            pass_copy(k, inner_z).wait_send()
            owner_copy(k, core).wait_send()

    @pl.when(core == inner_z)
    def _():
        for k in range(chunks):
            pair_copy(k, core).wait_send()

    for j in range(1, 8):
        token_copy(j, d).wait_send()
        token_copy(j, lax.rem(d + 8 - j, 8)).wait_recv()
    for j in range(8):
        share_copy(1, j).wait()
        if j:
            share_copy(0, j).wait()
    for each in carried:
        each.finish()


def spread_gradient(place, half, pieces, load):
    rows, width = half.shape
    chunks = 4
    whole = pl.BlockSpec(memory_space=pltpu.VMEM)
    return pl.pallas_call(
        functools.partial(spread_kernel, load, chunks),
        in_specs=[whole] * 2 + [ANYWHERE] * len(load.operands),
        out_specs=[whole] * 3 + [ANYWHERE] * len(load.outs_like),
        out_shape=[
            jax.ShapeDtypeStruct((2 * rows, width), BF),
            jax.ShapeDtypeStruct((8 * 16, width), BF),
            jax.ShapeDtypeStruct((2 * pieces.shape[0], pieces.shape[1]), F32),
        ]
        + load.outs_like,
        scratch_shapes=[
            pltpu.SemaphoreType.DMA((3, chunks)),
            pltpu.SemaphoreType.DMA((3, chunks)),
            pltpu.SemaphoreType.DMA((7,)),
            pltpu.SemaphoreType.DMA((7,)),
            pltpu.SemaphoreType.DMA((2, 8)),
            pltpu.SemaphoreType.DMA((2, 8)),
        ]
        + load.scratch,
        compiler_params=pltpu.CompilerParams(
            collective_id=place, has_side_effects=True, vmem_limit_bytes=60 * 2**20
        ),
        cost_estimate=pl.CostEstimate(flops=0, transcendentals=0, bytes_accessed=100_000_000),
        name="spread_gradient",
    )(half, pieces, *load.operands)


def feed_kernel(n_ref, cot_ref, gate_ref, up_ref, down_ref, hidden_ref, grad_ref):
    here = pl.program_id(0)
    length = n_ref.shape[0]
    tile = gate_ref.shape[1]
    half = grad_ref.shape[1] // 2
    block = 256
    gate_columns = pl.ds(pl.multiple_of(here * tile, tile), tile)
    up_columns = pl.ds(pl.multiple_of(half + here * tile, tile), tile)

    @pl.loop(0, length // block)
    def _(step):
        rows = pl.ds(pl.multiple_of(step * block, block), block)
        gate = jnp.dot(n_ref[rows, :], gate_ref[...], preferred_element_type=F32)
        up = jnp.dot(n_ref[rows, :], up_ref[...], preferred_element_type=F32)
        grad = jnp.dot(cot_ref[rows, :], down_ref[...], preferred_element_type=F32)
        sigmoid = jax.nn.sigmoid(gate)
        silu = gate * sigmoid
        hidden_ref[rows, :] = (silu * up).astype(BF)
        grad_ref[rows, gate_columns] = (
            grad * up * sigmoid * (1.0 + gate * (1.0 - sigmoid))
        ).astype(BF)
        grad_ref[rows, up_columns] = (grad * silu).astype(BF)


def feed_forward(normed, cot, gate_up, down):
    length, width = normed.shape
    hidden_width = down.shape[1]
    tile = 256
    steps = hidden_width // tile
    fixed = pl.BlockSpec((length, width), lambda j: (0, 0))
    return pl.pallas_call(
        feed_kernel,
        grid=(steps,),
        in_specs=[
            fixed,
            fixed,
            pl.BlockSpec((width, tile), lambda j: (0, j)),
            pl.BlockSpec((width, tile), lambda j: (0, j + steps)),
            pl.BlockSpec((width, tile), lambda j: (0, j)),
        ],
        out_specs=[
            pl.BlockSpec((length, tile), lambda j: (0, j)),
            pl.BlockSpec((length, 2 * hidden_width), lambda j: (0, 0)),
        ],
        out_shape=[
            jax.ShapeDtypeStruct((length, hidden_width), BF),
            jax.ShapeDtypeStruct((length, 2 * hidden_width), BF),
        ],
        compiler_params=pltpu.CompilerParams(vmem_limit_bytes=60 * 2**20),
        cost_estimate=pl.CostEstimate(
            flops=6 * length * width * hidden_width,
            transcendentals=length * hidden_width,
            bytes_accessed=30_000_000,
        ),
        name="feed_forward",
    )(normed, cot, gate_up, gate_up, down)


def turn_tables(length, block):
    rotated = HD // 2
    angles = np.exp(-np.log(10000.0) * np.arange(rotated // 2) * 2.0 / rotated)
    lanes = np.concatenate([angles, angles, np.zeros(HD - rotated)])
    lanes = np.concatenate([lanes, lanes])
    base = np.arange(block)[:, None] * lanes[None]
    steps = np.zeros((8, 128))
    steps[: length // block] = np.arange(0, length, block)[:, None] * lanes[None]
    pack = lambda table: np.stack([np.cos(table), np.sin(table)]).astype(np.float32)
    return jnp.asarray(pack(base)), jnp.asarray(pack(steps))


def turned_block(values, base_ref, steps_ref, here, sign):
    half = HD // 4
    first_cos, first_sin = steps_ref[0, pl.ds(here, 1), :], steps_ref[1, pl.ds(here, 1), :]
    cosine = first_cos * base_ref[0] - first_sin * base_ref[1]
    sine = first_sin * base_ref[0] + first_cos * base_ref[1]
    lane = lax.rem(lax.broadcasted_iota(jnp.int32, values.shape, 1), HD)
    lower = jnp.where(lane < half, sine, 0.0)
    upper = jnp.where((lane >= half) & (lane < 2 * half), sine, 0.0)
    ahead = pltpu.roll(values, 128 - half, 1)
    behind = pltpu.roll(values, half, 1)
    if sign > 0:
        return values * cosine - ahead * lower + behind * upper
    return values * cosine + ahead * lower - behind * upper


def opening_kernel(*refs):
    (qkv_part, side_part, feed_part, latents, prompt, time_part, feat, facts) = refs[:8]
    gain_ref, bias_ref, base_ref, steps_ref = refs[8:12]
    (n_ref, q_ref, k_ref, v_ref, o_ref, log_ref, res_ref, qkv_out) = refs[12:20]
    side_full, feed_own, prompt_too, facts_too, feat_out = refs[20:25]
    projected, item, time_full, qkv_full, feat_full = refs[25:30]
    sent_far, got_far, sent_near, got_near, here = refs[30:35]
    sent_plane, got_plane, sent_side, got_side = refs[35:39]
    sent_small, got_small, sent_swap, got_swap = refs[39:43]
    place = Place()
    d, core, column, owner = place.d, place.core, place.column, place.owner
    step_here = pl.program_id(0)
    plane_peers = [(lax.rem(d + j, 8), place.z) for j in range(1, 8)]
    rows = qkv_part.shape[0]
    piece = rows // 2
    length, width = item.shape
    total = qkv_full.shape[1]
    block = 256
    parts = range(4)

    def at(ref, index, count):
        return ref.at[pl.ds(pl.multiple_of(index * count, count), count)]

    def ends(k, sender):
        if k < 2:
            source = qkv_part.at[pl.ds(k * piece, piece)]
            spot = pl.multiple_of((2 * column + sender) * rows + k * piece, piece)
            return source, qkv_full.at[pl.ds(spot, piece)]
        if k == 2:
            return side_part, at(side_full, 2 * column + sender, rows)
        return feed_part, at(feed_own, sender, rows)

    def far(k, sender):
        source, target = ends(k, sender)
        return send(source, target, sent_far.at[k], got_far.at[sender, k], place.user)

    def near(k, sender):
        source, target = ends(k, sender)
        return send(source, target, sent_near.at[k], got_near.at[k], place.core_peer)

    def local(k):
        source, target = ends(k, core)
        return pltpu.make_async_copy(source, target, here.at[k])

    def await_part(k, sender):
        @pl.when(owner)
        def _():
            @pl.when(core == sender)
            def _():
                local(k).wait()

            @pl.when(core != sender)
            def _():
                near(k, sender).wait_recv()

        @pl.when(jnp.logical_not(owner))
        def _():
            far(k, sender).wait_recv()

    item_copy = send(latents, item, sent_swap.at[0], got_swap.at[0], place.core_peer)
    item_local = pltpu.make_async_copy(latents, item, here.at[4])
    outward = [
        pltpu.make_async_copy(qkv_full, qkv_out, here.at[7]),
        pltpu.make_async_copy(feat_full, feat_out, here.at[8]),
    ]
    swaps = [
        send(prompt, prompt_too, sent_swap.at[1], got_swap.at[1], place.core_peer),
        send(facts, facts_too, sent_swap.at[2], got_swap.at[2], place.core_peer),
    ]
    smalls = ((time_part, time_full), (feat, feat_full))

    def small(which, j, sender):
        part, whole = smalls[which]
        return send(
            part,
            at(whole, sender, part.shape[0]),
            sent_small.at[which, j - 1],
            got_small.at[which, j - 1],
            plane_peers[j - 1],
        )

    def small_local(which):
        part, whole = smalls[which]
        return pltpu.make_async_copy(part, at(whole, d, part.shape[0]), here.at[5 + which])

    def plane(stage, way, k, sender):
        peer = place.x_peer if way == 0 else place.y_peer
        source = column if stage == 0 else (place.y_column if way == 0 else place.x_column)
        spot = qkv_full.at[
            pl.ds(pl.multiple_of((2 * source + sender) * rows + k * piece, piece), piece)
        ]
        slot = 4 * stage + 2 * sender + k
        return send(spot, spot, sent_plane.at[way, slot], got_plane.at[way, slot], peer)

    def side(stage, way, sender):
        peer = place.x_peer if way == 0 else place.y_peer
        source = column if stage == 0 else (place.y_column if way == 0 else place.x_column)
        spot = at(side_full, 2 * source + sender, rows)
        slot = 2 * stage + sender
        return send(spot, spot, sent_side.at[way, slot], got_side.at[way, slot], peer)

    def side_one():
        for sender in range(2):
            await_part(2, sender)
            side(0, sender, sender).start()
        for sender in range(2):
            side(0, 1 - sender, sender).start()

    def side_two():
        side(0, 0, 0).wait_recv()
        side(1, 1, 0).start()
        side(0, 1, 1).wait_recv()
        side(1, 0, 1).start()

    @pl.when(step_here == 0)
    def _():
        greet([place.far_same, place.far_other] + plane_peers)
        for k in parts:
            far(k, core).start()

        @pl.when(owner)
        def _():
            item_copy.start()
            item_local.start()
            for k in parts:
                local(k).start()

        for which in range(2):
            small_local(which).start()
        for j in range(1, 8):
            for which in range(2):
                small(which, j, d).start()

        @pl.when(jnp.logical_not(owner))
        def _():
            for k in parts:
                near(k, core).start()

        for swap in swaps:
            swap.start()
        for which in range(2):
            small_local(which).wait()
        for j in range(1, 8):
            for which in range(2):
                small(which, j, lax.rem(d + 8 - j, 8)).wait_recv()

        @pl.when(owner)
        def _():
            item_local.wait()

        @pl.when(jnp.logical_not(owner))
        def _():
            item_copy.wait_recv()

        user = 2 * column + place.pair
        token_row = jnp.dot(
            feat_full[pl.ds(pl.multiple_of(user * 16, 16), 16), :],
            time_full[...],
            preferred_element_type=F32,
        )
        row_number = lax.broadcasted_iota(jnp.int32, (16, width), 0)

        def norm_rows(step, keep):
            local_row = pl.multiple_of(step * 16, 16)
            spot = pl.multiple_of(lax.rem(local_row + core * (length // 2), length), 16)
            values = item[pl.ds(spot, 16), :].astype(F32)
            values = jnp.where(row_number + spot == 0, token_row, values)
            if keep:
                res_ref[pl.ds(local_row, 16), :] = values
            centered = values - jnp.mean(values, axis=-1, keepdims=True)
            inverse = lax.rsqrt(jnp.mean(centered * centered, axis=-1, keepdims=True) + EPS)
            n_ref[pl.ds(local_row, 16), :] = (
                centered * inverse * gain_ref[...] + bias_ref[...]
            ).astype(BF)

        def forward(k):
            for sender in range(2):
                await_part(k, sender)
                plane(0, 0, k, sender).start()
                plane(0, 1, k, sender).start()

        steps = length // 16
        forward(0)

        @pl.loop(0, steps // 2)
        def _(step):
            norm_rows(step, True)

        forward(1)

        @pl.loop(steps // 2, steps)
        def _(step):
            norm_rows(step, False)

        for k in range(2):
            plane(0, 0, k, 0).wait_recv()
            plane(1, 1, k, 0).start()
            plane(0, 1, k, 1).wait_recv()
            plane(1, 0, k, 1).start()
            plane(0, 0, k, 1).wait_recv()
            plane(0, 1, k, 0).wait_recv()
        for k in range(2):
            plane(1, 1, k, 0).wait_recv()
            plane(1, 0, k, 1).wait_recv()

        side_one()

        for each in outward:
            each.start()
        third = total // 3
        for part in range(3):
            columns = pl.ds(part * third, third)

            @pl.loop(0, length // block)
            def _(step):
                spot = pl.ds(pl.multiple_of(step * block, block), block)
                projected[spot, columns] = jnp.dot(
                    n_ref[spot, :], qkv_full[:, columns], preferred_element_type=F32
                )

    @pl.when(step_here == 1)
    def _():
        side_two()

    def turn(first, target):
        columns = pl.ds(pl.multiple_of(first + step_here * 128, 128), 128)

        @pl.loop(0, length // block)
        def _(step):
            spot = pl.ds(pl.multiple_of(step * block, block), block)
            index = lax.rem(step + core * (length // block // 2), length // block)
            target[spot, :] = turned_block(
                projected[spot, columns], base_ref, steps_ref, index, 1
            ).astype(BF)

    turn(0, q_ref)
    turn(total // 3, k_ref)
    v_ref[...] = projected[
        :, pl.ds(pl.multiple_of(2 * (total // 3) + step_here * 128, 128), 128)
    ].astype(BF)
    attend_pair(HD, block, q_ref, k_ref, v_ref, None, o_ref, log_ref)

    @pl.when(step_here == pl.num_programs(0) - 1)
    def _():
        for sender in range(2):
            side(0, 1 - sender, sender).wait_recv()
        side(1, 1, 0).wait_recv()
        side(1, 0, 1).wait_recv()
        for sender in range(2):
            await_part(3, sender)
        for each in outward:
            each.wait()
        for swap in swaps:
            swap.wait()
        for j in range(1, 8):
            for which in range(2):
                small(which, j, d).wait_send()
        for k in parts:
            far(k, core).wait_send()

        @pl.when(owner)
        def _():
            item_copy.wait_send()

        @pl.when(jnp.logical_not(owner))
        def _():
            for k in parts:
                near(k, core).wait_send()

        for sender in range(2):
            for way in range(2):
                side(0, way, sender).wait_send()
                for k in range(2):
                    plane(0, way, k, sender).wait_send()
        side(1, 1, 0).wait_send()
        side(1, 0, 1).wait_send()
        for k in range(2):
            plane(1, 1, k, 0).wait_send()
            plane(1, 0, k, 1).wait_send()


def opening(place, qkv_part, side_part, feed_part, latents, prompt, time_part, feat, facts, gain, bias):
    length, width = latents.shape
    total = qkv_part.shape[1]
    rows = qkv_part.shape[0]
    pairs = total // 3 // 128
    base, steps = turn_tables(length, 256)
    block = pl.BlockSpec((length, 128), lambda i: (0, i))
    whole = pl.BlockSpec(memory_space=pltpu.VMEM)
    wide = jax.ShapeDtypeStruct((length, total // 3), BF)
    dma = pltpu.SemaphoreType.DMA
    return pl.pallas_call(
        opening_kernel,
        grid=(pairs,),
        in_specs=[ANYWHERE] * 8 + [whole] * 4,
        out_specs=[whole]
        + [block] * 4
        + [pl.BlockSpec((1, 2, length), lambda i: (i, 0, 0)), whole]
        + [ANYWHERE] * 6,
        out_shape=[jax.ShapeDtypeStruct((length, width), BF)]
        + [wide] * 4
        + [
            jax.ShapeDtypeStruct((pairs, 2, length), F32),
            jax.ShapeDtypeStruct((length // 2, width), F32),
            jax.ShapeDtypeStruct((8 * rows, total), BF),
            jax.ShapeDtypeStruct((8 * rows, side_part.shape[1]), BF),
            jax.ShapeDtypeStruct((2 * rows, feed_part.shape[1]), BF),
            jax.ShapeDtypeStruct(prompt.shape, BF),
            jax.ShapeDtypeStruct(facts.shape, facts.dtype),
            jax.ShapeDtypeStruct((8 * feat.shape[0], feat.shape[1]), BF),
        ],
        scratch_shapes=[
            pltpu.VMEM((length, total), F32),
            pltpu.VMEM((length, width), BF),
            pltpu.VMEM((8 * time_part.shape[0], width), BF),
            pltpu.VMEM((8 * rows, total), BF),
            pltpu.VMEM((8 * feat.shape[0], feat.shape[1]), BF),
            dma((4,)),
            dma((2, 4)),
            dma((4,)),
            dma((4,)),
            dma((9,)),
            dma((2, 8)),
            dma((2, 8)),
            dma((2, 4)),
            dma((2, 4)),
            dma((2, 7)),
            dma((2, 7)),
            dma((3,)),
            dma((3,)),
        ],
        compiler_params=pltpu.CompilerParams(
            collective_id=place, has_side_effects=True, vmem_limit_bytes=60 * 2**20
        ),
        cost_estimate=pl.CostEstimate(
            flops=4 * length * length * total // 3 + 2 * length * width * total,
            transcendentals=length * length * total // 192,
            bytes_accessed=200_000_000,
        ),
        name="opening",
    )(
        qkv_part,
        side_part,
        feed_part,
        latents,
        prompt,
        time_part,
        feat,
        facts,
        gain[None],
        bias[None],
        base,
        steps,
    )


def per_device_paired(
    latents,
    prompt_tokens,
    prompt_lengths,
    timesteps,
    time_weight,
    self_gain,
    self_bias,
    qkv_weight,
    self_out_weight,
    cross_gain,
    cross_bias,
    cross_query_weight,
    context_weight,
    cross_out_weight,
    feed_gain,
    feed_bias,
    gate_up_weight,
    down_weight,
    down_bias,
    cotangent,
):
    d = lax.axis_index("dp")
    z = lax.axis_index("mp")
    core, pair = d & 1, z >> 1
    owner = core == pair
    length = latents.shape[1] + 1
    rows = length // 4
    half_rows = length // 2
    part_rows = qkv_weight.shape[0]
    n = cross_query_weight.shape[1]

    side_part = jnp.concatenate(
        [
            self_out_weight.T,
            cross_query_weight,
            cross_out_weight.T,
            context_weight.reshape(part_rows, -1),
        ],
        axis=1,
    )
    feature_width = 8 * time_weight.shape[0]
    features = time_features(timesteps, feature_width).astype(BF)
    (
        normed_one,
        queries,
        keys,
        values,
        attended,
        self_logs,
        residual_mine,
        qkv_full,
        side_full,
        gate_up_own,
        prompt_too,
        facts_too,
        features_full,
    ) = opening(
        5,
        qkv_weight.reshape(part_rows, -1),
        side_part,
        gate_up_weight.reshape(part_rows, -1),
        jnp.pad(latents[0], ((1, 0), (0, 0))),
        prompt_tokens[0],
        time_weight,
        jnp.broadcast_to(features, (16, feature_width)),
        jnp.broadcast_to(prompt_lengths[:, None], (8, 128)),
        self_gain,
        self_bias,
    )
    gate_up_full = plane_gather(gate_up_own)
    self_out_full = side_full[:, :n]
    cross_query_full = side_full[:, n : 2 * n]
    cross_out_full = side_full[:, 2 * n : 3 * n]
    context_full = side_full[:, 3 * n :].reshape(context_weight.shape[0] * 8, -1)

    item_prompt = jnp.where(owner, prompt_tokens[0], prompt_too)
    item_length = jnp.where(owner, prompt_lengths[0], facts_too[0, 0])

    residual_one, normed_two_all, down_own, cot_too = exchange(
        "norm",
        0,
        attended,
        side_full,
        residual_mine,
        cross_gain,
        cross_bias,
        load=Loads((Spread, down_weight.T), (SwapRoute, cotangent[0])),
    )
    cot_shard = jnp.where(owner, cotangent[0], cot_too)
    cot_far = move(cot_shard, SWAP_Z)
    odd = (z & 1) == 1
    cross_q = dot_nn(normed_two_all, cross_query_full).astype(BF)
    context = dot_nn(item_prompt, context_full).astype(BF)
    slots = prompt_tokens.shape[1]
    mask = jnp.where(jnp.arange(slots, dtype=jnp.int32)[:, None] < item_length, 0.0, NEG)
    mask = mask.astype(F32)
    crossed, cross_logs = cross_attention(cross_q, context, mask)
    cot_far = after(cot_far, crossed)
    cot_mine = jnp.concatenate(
        [jnp.where(odd, cot_far, cot_shard), jnp.where(odd, cot_shard, cot_far)], axis=0
    )
    cot_other = move(cot_mine, SWAP_CORE)
    residual_two, normed_three_all, down_full = exchange(
        "norm",
        1,
        crossed,
        side_full,
        residual_one,
        feed_gain,
        feed_bias,
        load=Loads((Plane, down_own)),
        window=2,
    )
    cot_all = jnp.concatenate([cot_mine, after(cot_other, normed_three_all)], axis=0)
    hidden, grad_gate_up = feed_forward(normed_three_all, cot_all, gate_up_full, down_full)

    split = gate_up_weight.shape[2]
    gate_local = dot_tn(normed_three_all, grad_gate_up[:, :split]).astype(BF)
    gate_sums = plane_sum(gate_local)
    up_local = dot_tn(normed_three_all, after(grad_gate_up, gate_local)[:, split:]).astype(BF)
    up_sums = plane_sum(up_local)
    grad_two_all, feed_sums, feed, down_local = exchange(
        "back",
        2,
        after(grad_gate_up, up_local),
        gate_up_full,
        residual_two,
        cot_mine,
        feed_gain,
        works=Works(("nt", hidden, down_full), ("tn", cot_all, hidden)),
    )
    down_sums = plane_sum(down_local)
    grad_crossed = dot_nn(grad_two_all, cross_out_full).astype(BF)
    grad_cross_q, grad_context = cross_attention_back(
        cross_q, context, mask, grad_crossed, cross_logs
    )
    (
        grad_one_all,
        cross_sums,
        gate_near,
        gate_far,
        feed_near,
        cross_query_grad,
        cross_out_grad,
        context_grad,
    ) = exchange(
        "back",
        3,
        grad_cross_q,
        side_full,
        residual_one,
        grad_two_all,
        cross_gain,
        load=Loads((Return, gate_sums), (SwapCoreHalf, feed)),
        window=1,
        works=Works(
            ("tn", normed_two_all, grad_cross_q),
            ("tn", grad_two_all, crossed),
            ("tn", item_prompt, grad_context),
        ),
    )
    feed_half = feed[:half_rows].astype(F32) + feed_near.astype(F32)
    feed_here = jnp.where(odd, feed_half[rows:], feed_half[:rows])
    feed_away = jnp.where(odd, feed_half[:rows], feed_half[rows:]).astype(BF)
    grad_attended = dot_nn(grad_one_all, self_out_full).astype(BF)
    grad_projected, up_near, up_far, feed_far = self_attention_back(
        7,
        queries,
        keys,
        values,
        grad_attended,
        self_logs,
        Loads((Return, up_sums), (SwapNear, feed_away)),
    )
    residual_here = jnp.where(odd, residual_two[rows:], residual_two[:rows])
    output_here = (residual_here + feed_here + feed_far.astype(F32) + down_bias).astype(BF)
    self_out_local = dot_tn(grad_one_all, attended).astype(BF)
    qkv_local = dot_tn(normed_one, grad_projected).astype(BF)
    self_local = jnp.concatenate([qkv_local, self_out_local], axis=1)
    self_total = plane_sum(self_local)
    (
        grad_in,
        self_sums,
        down_near,
        down_far,
        output_far,
        cross_query_total,
        cross_out_total,
        context_total,
    ) = exchange(
        "half",
        4,
        after(grad_projected, self_local),
        qkv_full,
        residual_mine,
        grad_one_all,
        self_gain,
        load=Loads(
            (Return, down_sums),
            (SwapRoute, output_here),
            (PlaneSum, cross_query_grad),
            (PlaneSum, cross_out_grad),
            (PlaneSum, context_grad),
        ),
    )
    sums = jnp.concatenate(
        [
            jnp.sum(self_sums, axis=1),
            jnp.sum(cross_sums, axis=1),
            jnp.sum(feed_sums, axis=1),
            jnp.sum(cot_mine.astype(F32), axis=0)[None],
            jnp.zeros((1, grad_in.shape[1]), F32),
        ],
        axis=0,
    )
    share = sums.shape[1] // 8
    pieces = jnp.swapaxes(sums.reshape(8, 8, share), 0, 1)
    pieces = jnp.pad(pieces, ((0, 0), (0, 0), (0, 256 - share))).reshape(64, 256)
    totals = (cross_query_total, cross_out_total, context_total, self_total)
    whole, token_rows, sums, *ends = spread_gradient(
        8, grad_in, pieces, Loads(*[(Return, total) for total in totals])
    )
    cross_query_grad, cross_out_grad, context_grad, self_grads = [
        returned(total, ends[2 * k], ends[2 * k + 1], core, owner)
        for k, total in enumerate(totals)
    ]
    sums = jnp.sum(sums.reshape(16, 8, 256), axis=0)[:, :share]
    output = jnp.where(owner, output_here, output_far)
    latents_grad = whole[1:]

    token_rows = token_rows.reshape(8, 16, -1)[:, 0]
    all_features = features_full.reshape(8, 16, -1)[:, 0]
    my_features = jnp.zeros((8, feature_width // 8), F32)
    for j in range(8):
        piece = all_features[:, j * (feature_width // 8) : (j + 1) * (feature_width // 8)]
        my_features = my_features + jnp.where(d == j, piece.astype(F32), 0.0)
    time_grad = lax.dot_general(
        my_features.astype(BF), token_rows, (((0,), (0,)), ((), ())), preferred_element_type=F32
    )

    qkv_columns = qkv_full.shape[1]
    gate_grad = returned(gate_sums, gate_near, gate_far, core, owner)
    up_grad = returned(up_sums, up_near, up_far, core, owner)
    down_grad = returned(down_sums, down_near, down_far, core, owner)
    return (
        output[None],
        latents_grad[None],
        time_grad,
        sums[0],
        sums[1],
        self_grads[:, :qkv_columns].reshape(qkv_weight.shape),
        self_grads[:, qkv_columns:].T,
        sums[2],
        sums[3],
        cross_query_grad,
        context_grad.reshape(context_weight.shape),
        cross_out_grad.T,
        sums[4],
        sums[5],
        jnp.stack([gate_grad, up_grad], axis=1),
        down_grad.T,
        sums[6],
    )


def solution(mesh):
    placed = (
        P("dp", None, None),
        P("dp", None, None),
        P("dp"),
        P("dp"),
        P("dp", None),
        P(),
        P(),
        P("dp", None, "mp"),
        P("mp", "dp"),
        P(),
        P(),
        P("dp", "mp"),
        P("dp", None, "mp"),
        P("mp", "dp"),
        P(),
        P(),
        P("dp", None, "mp"),
        P("mp", "dp"),
        P(),
        P("dp", "mp", None),
    )
    paired = mesh.shape["dp"] == 8 and mesh.shape["mp"] == 4
    return jax.shard_map(
        per_device_paired if paired else per_device_general,
        mesh=mesh,
        in_specs=placed,
        out_specs=(
            P("dp", "mp", None),
            P("dp", None, None),
            P("dp", None),
            P("dp"),
            P("dp"),
            P("dp", None, "mp"),
            P("mp", "dp"),
            P("dp"),
            P("dp"),
            P("dp", "mp"),
            P("dp", None, "mp"),
            P("mp", "dp"),
            P("dp"),
            P("dp"),
            P("dp", None, "mp"),
            P("mp", "dp"),
            P("dp"),
        ),
        check_vma=False,
    )
```

```python
import functools
import math

import jax
import jax.numpy as jnp
import numpy as np
from jax import lax
from jax.experimental import pallas as pl
from jax.experimental.pallas import tpu as pltpu
from jax.sharding import PartitionSpec as P

HD = 64


EPS = 1e-05
NEG = -1e30


def time_features(steps_in, feature_width):
    half_width = feature_width // 2
    freqs = jnp.exp(-math.log(10000.0) * jnp.arange(half_width, dtype=jnp.float32) / half_width)
    angles = steps_in.astype(jnp.float32)[:, None] * freqs[None, :]
    return jnp.concatenate([jnp.cos(angles), jnp.sin(angles)], axis=-1)


def rope_tables(length, head_size):
    rotated_width = head_size // 2
    half_width = rotated_width // 2
    inverse = jnp.exp(
        -math.log(10000.0) * jnp.arange(half_width, dtype=jnp.float32) * 2.0 / rotated_width
    )
    angles = jnp.arange(length, dtype=jnp.float32)[:, None] * inverse[None, :]
    cosine = jnp.concatenate([jnp.cos(angles), jnp.cos(angles)], axis=-1)
    sine = jnp.concatenate([jnp.sin(angles), jnp.sin(angles)], axis=-1)
    return (cosine[:, None, :], sine[:, None, :])


def rotate(values, cosine, sine):
    rotated_width = cosine.shape[-1]
    half_width = rotated_width // 2
    first = values[..., :rotated_width]
    turned = jnp.concatenate([-first[..., half_width:], first[..., :half_width]], axis=-1)
    return jnp.concatenate([first * cosine + turned * sine, values[..., rotated_width:]], axis=-1)


def unrotate(grads_in, cosine, sine):
    rotated_width = cosine.shape[-1]
    half_width = rotated_width // 2
    first = grads_in[..., :rotated_width]
    scaled_in = first * sine
    turned = jnp.concatenate([scaled_in[..., half_width:], -scaled_in[..., :half_width]], axis=-1)
    return jnp.concatenate([first * cosine + turned, grads_in[..., rotated_width:]], axis=-1)


def layer_norm(values, gain, bias):
    centered = values - jnp.mean(values, axis=-1, keepdims=True)
    inverse = lax.rsqrt(jnp.mean(centered * centered, axis=-1, keepdims=True) + EPS)
    scaled = centered * inverse
    return (scaled * gain + bias, scaled, inverse)


def norm_back(grad_normed, scaled, inverse, gain):
    grad_scaled = grad_normed * gain
    first_mean = jnp.mean(grad_scaled, axis=-1, keepdims=True)
    second_mean = jnp.mean(grad_scaled * scaled, axis=-1, keepdims=True)
    grad_values = inverse * (grad_scaled - first_mean - scaled * second_mean)
    return (
        grad_values,
        jnp.sum(grad_normed * scaled, axis=(0, 1)),
        jnp.sum(grad_normed, axis=(0, 1)),
    )


def attend_forward(queries, key_rows, value_rows, bias_rows, block_size):
    score_scale = queries.shape[-1] ** (-0.5)

    def one_item(operands):
        item_query, item_key, item_value, item_bias = operands
        query_blocks = item_query.reshape(-1, block_size, item_query.shape[1], item_query.shape[2])

        def one_block(block_query):
            scores = jnp.einsum(
                "qhe,khe->hqk", block_query, item_key, preferred_element_type=jnp.float32
            )
            scores = scores * score_scale + item_bias[None, None, :]
            row_max = jnp.max(scores, axis=-1, keepdims=True)
            expos = jnp.exp(scores - row_max)
            row_total = jnp.sum(expos, axis=-1, keepdims=True)
            weights_p = (expos / row_total).astype(jnp.bfloat16)
            mixed = jnp.einsum(
                "hqk,khe->qhe", weights_p, item_value, preferred_element_type=jnp.float32
            )
            return (mixed, (row_max + jnp.log(row_total))[..., 0])

        mixed, log_total = lax.map(one_block, query_blocks)
        return (mixed.reshape(item_query.shape), log_total)

    return lax.map(one_item, (queries, key_rows, value_rows, bias_rows))


def attend_backward(queries, key_rows, value_rows, bias_rows, log_totals, grad_out, block_size):
    score_scale = queries.shape[-1] ** (-0.5)

    def one_item(operands):
        item_query, item_key, item_value, item_bias, item_log, item_grad = operands
        block_shape = (-1, block_size, item_query.shape[1], item_query.shape[2])
        query_blocks = item_query.reshape(block_shape)
        grad_blocks = item_grad.reshape(block_shape)

        def one_block(carry, operands_block):
            block_query, block_log, block_grad = operands_block
            scores = jnp.einsum(
                "qhe,khe->hqk", block_query, item_key, preferred_element_type=jnp.float32
            )
            scores = scores * score_scale + item_bias[None, None, :]
            probs_full = jnp.exp(scores - block_log[..., None])
            grad_probs = jnp.einsum(
                "qhe,khe->hqk", block_grad, item_value, preferred_element_type=jnp.float32
            )
            delta_row = jnp.sum(probs_full * grad_probs, axis=-1, keepdims=True)
            grad_scores = (probs_full * (grad_probs - delta_row)).astype(jnp.bfloat16)
            grad_query = (
                jnp.einsum(
                    "hqk,khe->qhe", grad_scores, item_key, preferred_element_type=jnp.float32
                )
                * score_scale
            )
            grad_key = (
                carry[0]
                + jnp.einsum(
                    "hqk,qhe->khe", grad_scores, block_query, preferred_element_type=jnp.float32
                )
                * score_scale
            )
            grad_value = carry[1] + jnp.einsum(
                "hqk,qhe->khe",
                probs_full.astype(jnp.bfloat16),
                block_grad,
                preferred_element_type=jnp.float32,
            )
            return ((grad_key, grad_value), grad_query)

        start_carry = (
            jnp.zeros(item_key.shape, jnp.float32),
            jnp.zeros(item_value.shape, jnp.float32),
        )
        (grad_key, grad_value), grad_query = lax.scan(
            one_block, start_carry, (query_blocks, item_log, grad_blocks)
        )
        return (grad_query.reshape(item_query.shape), grad_key, grad_value)

    return lax.map(one_item, (queries, key_rows, value_rows, bias_rows, log_totals, grad_out))


def per_device_general(
    latents,
    prompt_tokens,
    prompt_lengths,
    timesteps,
    time_weight,
    self_gain,
    self_bias,
    qkv_weight,
    self_out_weight,
    cross_gain,
    cross_bias,
    cross_query_weight,
    context_weight,
    cross_out_weight,
    feed_gain,
    feed_bias,
    gate_up_weight,
    down_weight,
    down_bias,
    cotangent,
):
    gathered = (
        lax.all_gather(time_weight, "dp", axis=0, tiled=True),
        lax.all_gather(qkv_weight, "dp", axis=0, tiled=True),
        lax.all_gather(self_out_weight, "dp", axis=1, tiled=True),
        lax.all_gather(cross_query_weight, "dp", axis=0, tiled=True),
        lax.all_gather(context_weight, "dp", axis=0, tiled=True),
        lax.all_gather(cross_out_weight, "dp", axis=1, tiled=True),
        lax.all_gather(gate_up_weight, "dp", axis=0, tiled=True),
        lax.all_gather(down_weight, "dp", axis=1, tiled=True),
    )
    (
        time_full,
        qkv_full,
        self_out_full,
        cross_query_full,
        context_full,
        cross_out_full,
        gate_up_full,
        down_full,
    ) = gathered
    items_here = latents.shape[0]
    seq_len = latents.shape[1] + 1
    shard_rows = seq_len // lax.axis_size("mp")
    first_row = lax.axis_index("mp") * shard_rows
    head_size = HD
    block_size = min(512, seq_len)
    features = time_features(timesteps, time_full.shape[0]).astype(jnp.bfloat16)
    token_row = jnp.dot(features, time_full, preferred_element_type=jnp.float32)
    residual_in = jnp.concatenate([token_row[:, None, :], latents.astype(jnp.float32)], axis=1)
    normed_one, scaled_one, inverse_one = layer_norm(residual_in, self_gain, self_bias)
    normed_one = normed_one.astype(jnp.bfloat16)
    projected = jnp.einsum(
        "bsd,dkc->bskc", normed_one, qkv_full, preferred_element_type=jnp.float32
    )
    heads_here = projected.shape[-1] // head_size
    head_shape = (items_here, seq_len, heads_here, head_size)
    cosine, sine = rope_tables(seq_len, head_size)
    queries = rotate(projected[:, :, 0].reshape(head_shape), cosine, sine).astype(jnp.bfloat16)
    key_rows = rotate(projected[:, :, 1].reshape(head_shape), cosine, sine).astype(jnp.bfloat16)
    value_rows = projected[:, :, 2].reshape(head_shape).astype(jnp.bfloat16)
    open_rows = jnp.zeros((items_here, seq_len), jnp.float32)
    attended, self_logs = attend_forward(queries, key_rows, value_rows, open_rows, block_size)
    attended = attended.reshape(items_here, seq_len, heads_here * head_size).astype(jnp.bfloat16)
    segment = attended
    self_branch = jnp.swapaxes(
        lax.psum_scatter(
            jnp.swapaxes(jnp.dot(segment, self_out_full, preferred_element_type=jnp.float32), 0, 1),
            "mp",
            scatter_dimension=0,
            tiled=True,
        ),
        0,
        1,
    )
    residual_one = lax.dynamic_slice_in_dim(residual_in, first_row, shard_rows, 1) + self_branch
    normed_two, scaled_two, inverse_two = layer_norm(residual_one, cross_gain, cross_bias)
    normed_two_all = lax.all_gather(normed_two.astype(jnp.bfloat16), "mp", axis=1, tiled=True)
    cross_q = (
        jnp.dot(normed_two_all, cross_query_full, preferred_element_type=jnp.float32)
        .astype(jnp.bfloat16)
        .reshape(head_shape)
    )
    context = jnp.einsum(
        "bpc,ckh->bpkh", prompt_tokens, context_full, preferred_element_type=jnp.float32
    ).astype(jnp.bfloat16)
    prompt_slots = prompt_tokens.shape[1]
    context_shape = (items_here, prompt_slots, heads_here, head_size)
    context_keys = context[:, :, 0].reshape(context_shape)
    context_values = context[:, :, 1].reshape(context_shape)
    slot_index = jnp.arange(prompt_slots, dtype=jnp.int32)
    mask_rows = jnp.where(slot_index[None, :] < prompt_lengths[:, None], 0.0, NEG).astype(
        jnp.float32
    )
    crossed, cross_logs = attend_forward(
        cross_q, context_keys, context_values, mask_rows, block_size
    )
    crossed = crossed.reshape(items_here, seq_len, heads_here * head_size).astype(jnp.bfloat16)
    segment = crossed
    cross_branch = jnp.swapaxes(
        lax.psum_scatter(
            jnp.swapaxes(
                jnp.dot(segment, cross_out_full, preferred_element_type=jnp.float32), 0, 1
            ).astype(jnp.bfloat16),
            "mp",
            scatter_dimension=0,
            tiled=True,
        ).astype(jnp.float32),
        0,
        1,
    )
    residual_two = residual_one + cross_branch
    normed_three, scaled_three, inverse_three = layer_norm(residual_two, feed_gain, feed_bias)
    normed_three_all = lax.all_gather(normed_three.astype(jnp.bfloat16), "mp", axis=1, tiled=True)
    gate_up = jnp.einsum(
        "bsd,dkf->bskf", normed_three_all, gate_up_full, preferred_element_type=jnp.float32
    )
    gate_part = gate_up[:, :, 0]
    up_part = gate_up[:, :, 1]
    hidden = (jax.nn.silu(gate_part) * up_part).astype(jnp.bfloat16)
    segment = hidden
    feed_branch = jnp.swapaxes(
        lax.psum_scatter(
            jnp.swapaxes(
                jnp.dot(segment, down_full, preferred_element_type=jnp.float32), 0, 1
            ).astype(jnp.bfloat16),
            "mp",
            scatter_dimension=0,
            tiled=True,
        ).astype(jnp.float32),
        0,
        1,
    )
    output = (residual_two + feed_branch + down_bias).astype(jnp.bfloat16)
    regathered = (
        lax.all_gather(qkv_weight, "dp", axis=0, tiled=True),
        lax.all_gather(self_out_weight, "dp", axis=1, tiled=True),
        lax.all_gather(cross_query_weight, "dp", axis=0, tiled=True),
        lax.all_gather(context_weight, "dp", axis=0, tiled=True),
        lax.all_gather(cross_out_weight, "dp", axis=1, tiled=True),
        lax.all_gather(gate_up_weight, "dp", axis=0, tiled=True),
        lax.all_gather(down_weight, "dp", axis=1, tiled=True),
    )
    (
        qkv_back,
        self_out_back,
        cross_query_back,
        context_back,
        cross_out_back,
        gate_up_back,
        down_back,
    ) = regathered
    grad_rows = lax.all_gather(cotangent, "mp", axis=1, tiled=True)
    grad_hidden = jnp.einsum(
        "bsd,fd->bsf", grad_rows, down_back, preferred_element_type=jnp.float32
    )
    sigmoid_gate = jax.nn.sigmoid(gate_part)
    grad_up = grad_hidden * gate_part * sigmoid_gate
    grad_gate = grad_hidden * up_part * sigmoid_gate * (1.0 + gate_part * (1.0 - sigmoid_gate))
    grad_gate_up = jnp.stack([grad_gate, grad_up], axis=2).astype(jnp.bfloat16)
    down_weight_grad = jnp.einsum(
        "bsf,bsd->fd", hidden, grad_rows, preferred_element_type=jnp.float32
    )
    gate_up_grad = jnp.einsum(
        "bsd,bskf->dkf", normed_three_all, grad_gate_up, preferred_element_type=jnp.float32
    )
    segment = grad_gate_up
    grad_normed_three = jnp.swapaxes(
        lax.psum_scatter(
            jnp.swapaxes(
                jnp.einsum(
                    "bskf,dkf->bsd", segment, gate_up_back, preferred_element_type=jnp.float32
                ),
                0,
                1,
            ).astype(jnp.bfloat16),
            "mp",
            scatter_dimension=0,
            tiled=True,
        ).astype(jnp.float32),
        0,
        1,
    )
    grad_two_norm, feed_gain_part, feed_bias_part = norm_back(
        grad_normed_three, scaled_three, inverse_three, feed_gain
    )
    grad_out_shard = cotangent.astype(jnp.float32)
    down_bias_part = jnp.sum(grad_out_shard, axis=(0, 1))
    grad_residual_two = (grad_out_shard + grad_two_norm).astype(jnp.bfloat16)
    grad_rows_two = lax.all_gather(grad_residual_two, "mp", axis=1, tiled=True)
    grad_crossed = jnp.einsum(
        "bsd,hd->bsh", grad_rows_two, cross_out_back, preferred_element_type=jnp.float32
    ).astype(jnp.bfloat16)
    cross_out_grad = jnp.einsum(
        "bsh,bsd->hd", crossed, grad_rows_two, preferred_element_type=jnp.float32
    )
    grad_cross_q, grad_cross_k, grad_cross_v = attend_backward(
        cross_q,
        context_keys,
        context_values,
        mask_rows,
        cross_logs,
        grad_crossed.reshape(head_shape),
        block_size,
    )
    grad_cross_q = grad_cross_q.reshape(items_here, seq_len, heads_here * head_size).astype(
        jnp.bfloat16
    )
    grad_context = (
        jnp.stack([grad_cross_k, grad_cross_v], axis=2)
        .reshape(items_here, prompt_slots, 2, heads_here * head_size)
        .astype(jnp.bfloat16)
    )
    cross_query_grad = jnp.einsum(
        "bsd,bsh->dh", normed_two_all, grad_cross_q, preferred_element_type=jnp.float32
    )
    context_weight_grad = jnp.einsum(
        "bpc,bpkh->ckh", prompt_tokens, grad_context, preferred_element_type=jnp.float32
    )
    segment = grad_cross_q
    grad_normed_two = jnp.swapaxes(
        lax.psum_scatter(
            jnp.swapaxes(
                jnp.einsum(
                    "bsh,dh->bsd", segment, cross_query_back, preferred_element_type=jnp.float32
                ),
                0,
                1,
            ).astype(jnp.bfloat16),
            "mp",
            scatter_dimension=0,
            tiled=True,
        ).astype(jnp.float32),
        0,
        1,
    )
    grad_one_norm, cross_gain_part, cross_bias_part = norm_back(
        grad_normed_two, scaled_two, inverse_two, cross_gain
    )
    grad_residual_one = (grad_residual_two.astype(jnp.float32) + grad_one_norm).astype(jnp.bfloat16)
    grad_rows_one = lax.all_gather(grad_residual_one, "mp", axis=1, tiled=True)
    grad_attended = jnp.einsum(
        "bsd,hd->bsh", grad_rows_one, self_out_back, preferred_element_type=jnp.float32
    ).astype(jnp.bfloat16)
    self_out_grad = jnp.einsum(
        "bsh,bsd->hd", attended, grad_rows_one, preferred_element_type=jnp.float32
    )
    grad_query, grad_key, grad_value = attend_backward(
        queries,
        key_rows,
        value_rows,
        open_rows,
        self_logs,
        grad_attended.reshape(head_shape),
        block_size,
    )
    grad_query = unrotate(grad_query, cosine, sine)
    grad_key = unrotate(grad_key, cosine, sine)
    grad_projected = (
        jnp.stack([grad_query, grad_key, grad_value], axis=2)
        .reshape(items_here, seq_len, 3, heads_here * head_size)
        .astype(jnp.bfloat16)
    )
    qkv_weight_grad = jnp.einsum(
        "bsd,bskc->dkc", normed_one, grad_projected, preferred_element_type=jnp.float32
    )
    grad_normed_part = jnp.einsum(
        "bskc,dkc->bsd", grad_projected, qkv_back, preferred_element_type=jnp.float32
    )
    summed = (
        lax.psum(grad_normed_part.astype(jnp.bfloat16), "mp").astype(jnp.float32),
        lax.psum(cross_gain_part.astype(jnp.bfloat16), "mp").astype(jnp.float32),
        lax.psum(cross_bias_part.astype(jnp.bfloat16), "mp").astype(jnp.float32),
        lax.psum(feed_gain_part.astype(jnp.bfloat16), "mp").astype(jnp.float32),
        lax.psum(feed_bias_part.astype(jnp.bfloat16), "mp").astype(jnp.float32),
        lax.psum(down_bias_part.astype(jnp.bfloat16), "mp").astype(jnp.float32),
    )
    grad_in_norm, self_gain_part, self_bias_part = norm_back(
        summed[0], scaled_one, inverse_one, self_gain
    )
    grad_residual_in = grad_rows_one.astype(jnp.float32) + grad_in_norm
    latents_grad = grad_residual_in[:, 1:].astype(jnp.bfloat16)
    time_weight_grad = jnp.dot(
        features.astype(jnp.float32).T, grad_residual_in[:, 0], precision=lax.Precision.HIGHEST
    )
    cross_gain_sum, cross_bias_sum, feed_gain_sum, feed_bias_sum, down_bias_sum = (
        summed[1],
        summed[2],
        summed[3],
        summed[4],
        summed[5],
    )
    reduced = (
        lax.psum_scatter(
            time_weight_grad.astype(jnp.bfloat16), "dp", scatter_dimension=0, tiled=True
        ).astype(jnp.float32),
        lax.psum_scatter(
            qkv_weight_grad.astype(jnp.bfloat16), "dp", scatter_dimension=0, tiled=True
        ).astype(jnp.float32),
        lax.psum_scatter(
            self_out_grad.astype(jnp.bfloat16), "dp", scatter_dimension=1, tiled=True
        ).astype(jnp.float32),
        lax.psum_scatter(
            cross_query_grad.astype(jnp.bfloat16), "dp", scatter_dimension=0, tiled=True
        ).astype(jnp.float32),
        lax.psum_scatter(
            context_weight_grad.astype(jnp.bfloat16), "dp", scatter_dimension=0, tiled=True
        ).astype(jnp.float32),
        lax.psum_scatter(
            cross_out_grad.astype(jnp.bfloat16), "dp", scatter_dimension=1, tiled=True
        ).astype(jnp.float32),
        lax.psum_scatter(
            gate_up_grad.astype(jnp.bfloat16), "dp", scatter_dimension=0, tiled=True
        ).astype(jnp.float32),
        lax.psum_scatter(
            down_weight_grad.astype(jnp.bfloat16), "dp", scatter_dimension=1, tiled=True
        ).astype(jnp.float32),
        lax.psum_scatter(
            self_gain_part.astype(jnp.bfloat16), "dp", scatter_dimension=0, tiled=True
        ).astype(jnp.float32),
        lax.psum_scatter(
            self_bias_part.astype(jnp.bfloat16), "dp", scatter_dimension=0, tiled=True
        ).astype(jnp.float32),
        lax.psum_scatter(
            cross_gain_sum.astype(jnp.bfloat16), "dp", scatter_dimension=0, tiled=True
        ).astype(jnp.float32),
        lax.psum_scatter(
            cross_bias_sum.astype(jnp.bfloat16), "dp", scatter_dimension=0, tiled=True
        ).astype(jnp.float32),
        lax.psum_scatter(
            feed_gain_sum.astype(jnp.bfloat16), "dp", scatter_dimension=0, tiled=True
        ).astype(jnp.float32),
        lax.psum_scatter(
            feed_bias_sum.astype(jnp.bfloat16), "dp", scatter_dimension=0, tiled=True
        ).astype(jnp.float32),
        lax.psum_scatter(
            down_bias_sum.astype(jnp.bfloat16), "dp", scatter_dimension=0, tiled=True
        ).astype(jnp.float32),
    )
    return (
        output,
        latents_grad,
        reduced[0],
        reduced[8],
        reduced[9],
        reduced[1],
        reduced[2],
        reduced[10],
        reduced[11],
        reduced[3],
        reduced[4],
        reduced[5],
        reduced[12],
        reduced[13],
        reduced[6],
        reduced[7],
        reduced[14],
    )


AXES = ("dp", "mp")
BF = jnp.bfloat16
F32 = jnp.float32


def flat_permutation(places):
    pairs = []
    for d in range(8):
        for z in range(4):
            target = places(d >> 1, d & 1, z & 1, z >> 1)
            if target is not None:
                s, c, zz, p = target
                pairs.append(((2 * s + c) * 4 + 2 * p + zz, (2 * (d >> 1) + (d & 1)) * 4 + z))
    return [(source, target) for target, source in pairs]


SWAP_CORE = flat_permutation(lambda s, c, zz, p: (s, 1 - c, zz, p))
SWAP_Z = flat_permutation(lambda s, c, zz, p: (s, c, 1 - zz, p))
SWAP_PAIR = flat_permutation(lambda s, c, zz, p: (s, c, zz, 1 - p))
SWAP_X = flat_permutation(lambda s, c, zz, p: (s ^ 1, c, zz, p))
SWAP_Y = flat_permutation(lambda s, c, zz, p: (s ^ 2, c, zz, p))
ROUTE_A = flat_permutation(lambda s, c, zz, p: (s, p, zz, c))
ROUTE_B = flat_permutation(lambda s, c, zz, p: (s, p, zz, 1 - c))
RETURN_B = flat_permutation(lambda s, c, zz, p: (s, 1 - p, zz, c))
OWNER_TO_PARTNER = flat_permutation(lambda s, c, zz, p: (s, 1 - c, zz, p) if c == p else None)
PARTNER_TO_OWNER = flat_permutation(lambda s, c, zz, p: (s, 1 - c, zz, p) if c != p else None)
OWNER_TO_PAIR = flat_permutation(lambda s, c, zz, p: (s, c, zz, 1 - p) if c == p else None)
OWNER_Z = flat_permutation(lambda s, c, zz, p: (s, c, 1 - zz, p) if c == p else None)
PARTNER_Z = flat_permutation(lambda s, c, zz, p: (s, c, 1 - zz, p) if c != p else None)


def move(values, pairs):
    return lax.ppermute(values, AXES, pairs)


def xor_blocks(values, axis, count, index):
    blocks = jnp.split(values, count, axis=axis)
    bit = 1
    while bit < count:
        flip = (index & bit) != 0
        blocks = [jnp.where(flip, blocks[j ^ bit], blocks[j]) for j in range(count)]
        bit *= 2
    return jnp.concatenate(blocks, axis=axis)


def attend_pair(head_size, query_block, queries, keys, values, bias, o_ref, log_ref):
    scale = head_size ** (-0.5)
    length, width = queries.shape
    key_rows = keys[...]
    values_turned = values[...].astype(F32).T.astype(BF)
    lane = lax.broadcasted_iota(jnp.int32, (query_block, width), 1)

    @pl.loop(0, length // query_block)
    def _(step):
        rows = pl.ds(pl.multiple_of(step * query_block, query_block), query_block)
        block = queries[rows, :]
        parts, logs = [], []
        for head in range(2):
            mine = (lane >= head * head_size) & (lane < (head + 1) * head_size)
            masked = jnp.where(mine, block, jnp.zeros_like(block))
            scores = lax.dot_general(
                key_rows, masked, (((1,), (1,)), ((), ())), preferred_element_type=F32
            )
            scores = scores * scale
            if bias is not None:
                scores = scores + bias[...]
            top = jnp.max(scores, axis=0, keepdims=True)
            expos = jnp.exp(scores - top)
            total = jnp.sum(expos, axis=0, keepdims=True)
            mixed = lax.dot_general(
                values_turned[head * head_size : (head + 1) * head_size, :],
                expos.astype(BF),
                (((1,), (0,)), ((), ())),
                preferred_element_type=F32,
            )
            parts.append(mixed * (1.0 / total))
            logs.append(top + jnp.log(total))
        o_ref[rows, :] = jnp.concatenate(parts, axis=0).T.astype(BF)
        log_ref[0, :, rows] = jnp.concatenate(logs, axis=0)


def cross_attention_kernel(q_ref, k_ref, v_ref, bias_ref, o_ref, log_ref):
    attend_pair(HD, 512, q_ref, k_ref, v_ref, bias_ref, o_ref, log_ref)


def attention_backward_kernel(head_size, query_block, turned, load, *refs):
    if turned:
        refs = list(refs)
        q_ref, k_ref, v_ref, d_ref, log_ref, base_ref, steps_ref = refs[:7]
        more = (len(load.operands), len(load.outs_like))
        refs = refs[7:]
        load_ins, g_ref, refs = refs[: more[0]], refs[more[0]], refs[more[0] + 1 :]
        load_outs, refs = refs[: more[1]], refs[more[1] :]
        dk_acc, dv_acc = refs[:2]
        place = Place()
        carried = load.begin(place, load_ins, load_outs, refs[2:])

        @pl.when(pl.program_id(0) == 0)
        def _():
            greet(load.peers(place, [place.core_peer]))
            for each in carried:
                each.start()
    else:
        q_ref, k_ref, v_ref, d_ref, log_ref, bias_ref, dq_ref, g_ref, dk_acc, dv_acc = refs
    scale = head_size ** (-0.5)
    length, width = q_ref.shape
    key_count = k_ref.shape[0]
    here = pl.program_id(0)
    key_rows = k_ref[...]
    value_rows = v_ref[...]
    keys_turned = key_rows.astype(F32).T.astype(BF)
    lane = lax.broadcasted_iota(jnp.int32, (query_block, width), 1)
    dk_acc[...] = jnp.zeros_like(dk_acc)
    dv_acc[...] = jnp.zeros_like(dv_acc)

    def back_turn(values, step):
        blocks = length // query_block
        index = lax.rem(step + place.core * (blocks // 2), blocks)
        return turned_block(values, base_ref, steps_ref, index, -1)

    @pl.loop(0, length // query_block)
    def _(step):
        rows = pl.ds(pl.multiple_of(step * query_block, query_block), query_block)
        block = q_ref[rows, :]
        grads = d_ref[rows, :]
        parts = []
        for head in range(2):
            mine = (lane >= head * head_size) & (lane < (head + 1) * head_size)
            q_mine = jnp.where(mine, block, jnp.zeros_like(block))
            d_mine = jnp.where(mine, grads, jnp.zeros_like(grads))
            scores = lax.dot_general(
                key_rows, q_mine, (((1,), (1,)), ((), ())), preferred_element_type=F32
            )
            scores = scores * scale
            if not turned:
                scores = scores + bias_ref[...]
            probs = jnp.exp(scores - log_ref[0, head : head + 1, rows])
            grad_probs = lax.dot_general(
                value_rows, d_mine, (((1,), (1,)), ((), ())), preferred_element_type=F32
            )
            delta = jnp.sum(probs * grad_probs, axis=0, keepdims=True)
            grad_scores = (probs * (grad_probs - delta)).astype(BF)
            dv_acc[...] += jnp.dot(probs.astype(BF), d_mine, preferred_element_type=F32)
            dk_acc[...] += jnp.dot(grad_scores, q_mine, preferred_element_type=F32)
            parts.append(
                jnp.dot(
                    keys_turned[head * head_size : (head + 1) * head_size, :],
                    grad_scores,
                    preferred_element_type=F32,
                )
            )
        grad_query = jnp.concatenate(parts, axis=0).T * scale
        if turned:
            columns = pl.ds(pl.multiple_of(here * width, width), width)
            g_ref[rows, columns] = back_turn(grad_query, step).astype(BF)
        else:
            dq_ref[rows, :] = grad_query.astype(BF)

    total_width = g_ref.shape[1] // (3 if turned else 2)
    first = total_width if turned else 0
    key_columns = pl.ds(pl.multiple_of(first + here * width, width), width)
    value_columns = pl.ds(pl.multiple_of(first + total_width + here * width, width), width)
    if turned:

        @pl.loop(0, key_count // query_block)
        def _(step):
            rows = pl.ds(pl.multiple_of(step * query_block, query_block), query_block)
            g_ref[rows, key_columns] = back_turn(dk_acc[rows, :] * scale, step).astype(BF)
            g_ref[rows, value_columns] = dv_acc[rows, :].astype(BF)

        @pl.when(here == pl.num_programs(0) - 1)
        def _():
            for each in carried:
                each.finish()
    else:
        g_ref[:, key_columns] = (dk_acc[...] * scale).astype(BF)
        g_ref[:, value_columns] = dv_acc[...].astype(BF)


def self_attention_back(place, queries, keys, values, grads, logs, load):
    length, total = queries.shape
    pairs = total // 128
    block = pl.BlockSpec((length, 128), lambda i: (0, i))
    whole = pl.BlockSpec(memory_space=pltpu.VMEM)
    tables = turn_tables(length, 256)
    return pl.pallas_call(
        functools.partial(attention_backward_kernel, HD, 256, True, load),
        grid=(pairs,),
        in_specs=[block] * 4
        + [pl.BlockSpec((1, 2, length), lambda i: (i, 0, 0))]
        + [whole] * 2
        + [ANYWHERE] * len(load.operands),
        out_specs=[pl.BlockSpec((length, 3 * total), lambda i: (0, 0))]
        + [ANYWHERE] * len(load.outs_like),
        out_shape=[jax.ShapeDtypeStruct((length, 3 * total), BF)] + load.outs_like,
        scratch_shapes=[pltpu.VMEM((length, 128), F32)] * 2 + load.scratch,
        compiler_params=pltpu.CompilerParams(collective_id=place, has_side_effects=True),
        cost_estimate=pl.CostEstimate(
            flops=10 * length * length * total,
            transcendentals=length * length * total // 64,
            bytes_accessed=100_000_000,
        ),
        name="self_attention_back",
    )(queries, keys, values, grads, logs, *tables, *load.operands)


def cross_attention(queries, context, bias):
    length, total = queries.shape
    slots = context.shape[0]
    pairs = total // 128
    block = pl.BlockSpec((length, 128), lambda i: (0, i))
    key_block = lambda shift: pl.BlockSpec((slots, 128), lambda i: (0, i + shift))
    return pl.pallas_call(
        cross_attention_kernel,
        grid=(pairs,),
        in_specs=[block, key_block(0), key_block(pairs), pl.BlockSpec((slots, 1), lambda i: (0, 0))],
        out_specs=[block, pl.BlockSpec((1, 2, length), lambda i: (i, 0, 0))],
        out_shape=[
            jax.ShapeDtypeStruct((length, total), BF),
            jax.ShapeDtypeStruct((pairs, 2, length), F32),
        ],
        cost_estimate=pl.CostEstimate(
            flops=4 * length * slots * total,
            transcendentals=length * slots * total // 64,
            bytes_accessed=length * total * 4,
        ),
        name="cross_attention",
    )(queries, context, context, bias)


def cross_attention_back(queries, context, bias, grads, logs):
    length, total = queries.shape
    slots = context.shape[0]
    pairs = total // 128
    block = pl.BlockSpec((length, 128), lambda i: (0, i))
    key_block = lambda shift: pl.BlockSpec((slots, 128), lambda i: (0, i + shift))
    return pl.pallas_call(
        functools.partial(attention_backward_kernel, HD, 512, False, None),
        grid=(pairs,),
        in_specs=[
            block,
            key_block(0),
            key_block(pairs),
            block,
            pl.BlockSpec((1, 2, length), lambda i: (i, 0, 0)),
            pl.BlockSpec((slots, 1), lambda i: (0, 0)),
        ],
        out_specs=[block, pl.BlockSpec((slots, 2 * total), lambda i: (0, 0))],
        out_shape=[
            jax.ShapeDtypeStruct((length, total), BF),
            jax.ShapeDtypeStruct((slots, 2 * total), BF),
        ],
        scratch_shapes=[pltpu.VMEM((slots, 128), F32)] * 2,
        cost_estimate=pl.CostEstimate(
            flops=10 * length * slots * total,
            transcendentals=length * slots * total // 64,
            bytes_accessed=length * total * 8,
        ),
        name="cross_attention_back",
    )(queries, context, context, grads, logs, bias)


def dot_nn(left, right):
    return lax.dot_general(left, right, (((1,), (0,)), ((), ())), preferred_element_type=F32)


def dot_nt(left, right):
    return lax.dot_general(left, right, (((1,), (1,)), ((), ())), preferred_element_type=F32)


def dot_tn(left, right):
    return lax.dot_general(left, right, (((0,), (0,)), ((), ())), preferred_element_type=F32)


PLANE = [[0, 2, 4, 6], [1, 3, 5, 7]]


def group_sum(partial):
    rows = partial.shape[0] // 2
    half = partial[:rows].astype(F32) + move(partial[rows:], SWAP_CORE).astype(F32)
    half = half.astype(BF)
    return half.astype(F32) + move(half, SWAP_Z).astype(F32)


def both_halves(half):
    return jnp.concatenate([half, move(half, SWAP_CORE)], axis=0)


def weight_order(one, two, pair):
    first = jnp.where(pair == 0, one, two)
    second = jnp.where(pair == 0, two, one)
    return jnp.concatenate([first, second], axis=0)


def plane_gather(mine):
    return lax.all_gather(mine, "dp", axis=0, tiled=True, axis_index_groups=PLANE)


def plane_sum(grad):
    return lax.psum_scatter(
        grad, "dp", scatter_dimension=0, tiled=True, axis_index_groups=PLANE
    )


def to_owners(total, pair):
    rows = total.shape[0] // 2
    first, second = total[:rows], total[rows:]
    one = move(jnp.where(pair == 0, first, second), ROUTE_A)
    two = move(jnp.where(pair == 0, second, first), RETURN_B)
    return one.astype(F32) + two.astype(F32)


def after(values, *others):
    return lax.optimization_barrier((values, *others))[0]


class Place:
    def __init__(self):
        d = lax.axis_index("dp")
        z = lax.axis_index("mp")
        self.d, self.z = d, z
        self.core = lax.rem(d, 2)
        self.column = d // 2
        self.pair = z // 2
        self.owner = self.core == self.pair
        self.core_peer = (d + 1 - 2 * self.core, z)
        self.near_z = (d, z + 1 - 2 * lax.rem(z, 2))
        self.far_z = z + 2 - 4 * self.pair
        self.far_same = (d, self.far_z)
        self.far_other = (self.core_peer[0], self.far_z)
        self.user = (2 * self.column + self.pair, self.far_z)
        self.x_peer = (d + 2 - 4 * lax.rem(self.column, 2), z)
        self.y_peer = (d + 4 - 8 * (self.column // 2), z)
        self.x_column = self.column + 1 - 2 * lax.rem(self.column, 2)
        self.y_column = self.column + 2 - 4 * (self.column // 2)


def greet(peers):
    barrier = pltpu.get_barrier_semaphore()
    for peer in peers:
        pl.semaphore_signal(
            barrier, inc=1, device_id=peer, device_id_type=pl.DeviceIdType.MESH
        )
    pl.semaphore_wait(barrier, len(peers))


def send(source, target, sent, got, peer):
    return pltpu.make_async_remote_copy(
        src_ref=source,
        dst_ref=target,
        send_sem=sent,
        recv_sem=got,
        device_id=peer,
        device_id_type=pl.DeviceIdType.MESH,
    )


class Spread:
    scratch = [pltpu.SemaphoreType.DMA((2,)), pltpu.SemaphoreType.DMA((3,)), pltpu.SemaphoreType.DMA]
    late = True

    @staticmethod
    def outs(part):
        return [jax.ShapeDtypeStruct((2 * part.shape[0], part.shape[1]), BF)]

    @staticmethod
    def peers(place):
        return [place.far_same, place.far_other]

    def __init__(self, place, ins, outs, sems):
        self.place = place
        (self.part,), (self.own,), (self.sent, self.got, self.here) = ins, outs, sems

    def target(self, sender):
        rows = self.part.shape[0]
        return self.own.at[pl.ds(pl.multiple_of(sender * rows, rows), rows)]

    def far(self, sender):
        return send(
            self.part, self.target(sender), self.sent.at[0], self.got.at[sender], self.place.user
        )

    def near(self, sender):
        return send(
            self.part, self.target(sender), self.sent.at[1], self.got.at[2], self.place.core_peer
        )

    def local(self):
        return pltpu.make_async_copy(self.part, self.target(self.place.core), self.here)

    def start(self):
        place = self.place
        self.far(place.core).start()

        @pl.when(place.owner)
        def _():
            self.local().start()

        @pl.when(jnp.logical_not(place.owner))
        def _():
            self.near(place.core).start()

    def middle(self):
        pass

    def finish(self):
        place = self.place

        @pl.when(place.owner)
        def _():
            self.local().wait()
            self.near(1 - place.core).wait_recv()

        @pl.when(jnp.logical_not(place.owner))
        def _():
            self.near(place.core).wait_send()
            self.far(0).wait_recv()
            self.far(1).wait_recv()

        self.far(place.core).wait_send()


class Plane:
    scratch = [
        pltpu.SemaphoreType.DMA((2, 3)),
        pltpu.SemaphoreType.DMA((2, 3)),
        pltpu.SemaphoreType.DMA,
    ]
    late = False

    @staticmethod
    def outs(own):
        return [jax.ShapeDtypeStruct((4 * own.shape[0], own.shape[1]), BF)]

    @staticmethod
    def peers(place):
        return [place.x_peer, place.y_peer]

    def __init__(self, place, ins, outs, sems):
        self.place = place
        (self.own,), (self.full,), (self.sent, self.got, self.here) = ins, outs, sems
        self.rows = self.own.shape[0] // 2

    def target(self, column, part):
        rows = self.rows
        return self.full.at[pl.ds(pl.multiple_of((2 * column + part) * rows, rows), rows)]

    def one(self, way, part):
        place = self.place
        peer = place.x_peer if way == 0 else place.y_peer
        return send(
            self.own.at[pl.ds(part * self.rows, self.rows)],
            self.target(place.column, part),
            self.sent.at[way, part],
            self.got.at[way, part],
            peer,
        )

    def two(self, way):
        place = self.place
        if way == 0:
            spot = self.target(place.y_column, 1)
            return send(spot, spot, self.sent.at[0, 2], self.got.at[0, 2], place.x_peer)
        spot = self.target(place.x_column, 0)
        return send(spot, spot, self.sent.at[1, 2], self.got.at[1, 2], place.y_peer)

    def local(self):
        rows = self.own.shape[0]
        place = self.full.at[pl.ds(pl.multiple_of(self.place.column * rows, rows), rows)]
        return pltpu.make_async_copy(self.own, place, self.here)

    def start(self):
        for way in range(2):
            self.one(way, way).start()
        for way in range(2):
            self.one(way, 1 - way).start()
        self.local().start()

    def middle(self):
        self.one(0, 0).wait_recv()
        self.two(1).start()
        self.one(1, 1).wait_recv()
        self.two(0).start()

    def finish(self):
        self.local().wait()
        for way in range(2):
            self.one(way, 1 - way).wait_recv()
            self.two(way).wait_recv()
            self.two(way).wait_send()
            for part in range(2):
                self.one(way, part).wait_send()


class Return:
    scratch = [pltpu.SemaphoreType.DMA((2,)), pltpu.SemaphoreType.DMA((2,))]
    late = True

    @staticmethod
    def outs(total):
        shape = jax.ShapeDtypeStruct((total.shape[0] // 2, total.shape[1]), BF)
        return [shape, shape]

    @staticmethod
    def peers(place):
        return [place.far_same, place.far_other]

    def __init__(self, place, ins, outs, sems):
        self.place = place
        (self.total,), (self.near, self.far), (self.sent, self.got) = ins, outs, sems

    def part(self, which):
        rows = self.near.shape[0]
        return self.total.at[pl.ds(pl.multiple_of(which * rows, rows), rows)]

    def to_near(self):
        place = self.place
        return send(
            self.part(1 - place.core), self.near, self.sent.at[0], self.got.at[0], place.core_peer
        )

    def to_far(self, same):
        place = self.place
        which = place.core if same else 1 - place.core
        peer = place.far_same if same else place.far_other
        return send(
            self.part(which), self.far, self.sent.at[0 if same else 1], self.got.at[1], peer
        )

    def start(self):
        place = self.place

        @pl.when(place.owner)
        def _():
            self.to_near().start()

        @pl.when(jnp.logical_not(place.owner))
        def _():
            self.to_far(True).start()
            self.to_far(False).start()

    def middle(self):
        pass

    def finish(self):
        place = self.place

        @pl.when(place.owner)
        def _():
            self.to_near().wait_send()
            self.to_far(True).wait_recv()

        @pl.when(jnp.logical_not(place.owner))
        def _():
            self.to_far(True).wait_send()
            self.to_far(False).wait_send()
            self.to_near().wait_recv()
            self.to_far(False).wait_recv()


class Swap:
    scratch = [pltpu.SemaphoreType.DMA, pltpu.SemaphoreType.DMA]
    late = True
    way = None

    @staticmethod
    def outs(values):
        return [jax.ShapeDtypeStruct(values.shape, values.dtype)]

    @classmethod
    def peers(cls, place):
        return {
            "core": [place.core_peer],
            "z": [place.near_z],
            "route": [place.far_same, place.far_other],
        }[cls.way]

    def __init__(self, place, ins, outs, sems):
        self.place = place
        peer = {"core": place.core_peer, "z": place.near_z, "route": place.far_other}[self.way]
        self.copy = send(ins[0], outs[0], sems[0], sems[1], peer)

    def each(self, act):
        if self.way != "route":
            act()
            return

        @pl.when(jnp.logical_not(self.place.owner))
        def _():
            act()

    def start(self):
        self.each(lambda: self.copy.start())

    def middle(self):
        pass

    def finish(self):
        self.each(lambda: self.copy.wait())


class SwapCore(Swap):
    way = "core"


class SwapCoreHalf(SwapCore):
    @staticmethod
    def outs(values):
        return [jax.ShapeDtypeStruct((values.shape[0] // 2,) + values.shape[1:], values.dtype)]

    def __init__(self, place, ins, outs, sems):
        rows = outs[0].shape[0]
        super().__init__(place, [ins[0].at[pl.ds(rows, rows)]], outs, sems)


class SwapNear(Swap):
    way = "z"


class SwapRoute(Swap):
    way = "route"


def scratch_of(kind, operand):
    return kind.scratch(operand) if callable(kind.scratch) else kind.scratch


class PlaneSum:
    late = False

    @staticmethod
    def scratch(grad):
        rows, width = grad.shape[0] // 4, grad.shape[1]
        return [
            pltpu.VMEM((rows, width), BF),
            pltpu.VMEM((2, rows, width), BF),
            pltpu.VMEM((2, rows, width), BF),
            pltpu.VMEM((rows, width), BF),
            pltpu.SemaphoreType.DMA((2, 2)),
            pltpu.SemaphoreType.DMA((2, 2)),
            pltpu.SemaphoreType.DMA((4,)),
        ]

    @staticmethod
    def outs(grad):
        return [jax.ShapeDtypeStruct((grad.shape[0] // 4, grad.shape[1]), BF)]

    @staticmethod
    def peers(place):
        return [place.x_peer, place.y_peer]

    def __init__(self, place, ins, outs, scratch):
        self.place = place
        (self.grad,), (self.out,) = ins, outs
        self.first, self.staged, self.second, self.own, self.sent, self.got, self.here = scratch
        self.rows = self.own.shape[0]
        self.ways = (place.x_peer, place.y_peer)
        self.columns = (place.x_column, place.y_column)
        self.diagonal = place.x_column + 2 - 4 * (place.x_column // 2)

    def block(self, column, start, count):
        first = pl.multiple_of(column * self.rows + start, count)
        return self.grad.at[pl.ds(first, count)]

    def one(self, way):
        count = self.rows // 2
        return send(
            self.block(self.diagonal, way * count, count),
            self.first.at[pl.ds(way * count, count)],
            self.sent.at[0, way],
            self.got.at[0, way],
            self.ways[way],
        )

    def two(self, way):
        return send(
            self.staged.at[way],
            self.second.at[way],
            self.sent.at[1, way],
            self.got.at[1, way],
            self.ways[way],
        )

    def load(self, way):
        source = self.block(self.columns[way], 0, self.rows)
        return pltpu.make_async_copy(source, self.staged.at[way], self.here.at[way])

    def load_own(self):
        source = self.block(self.place.column, 0, self.rows)
        return pltpu.make_async_copy(source, self.own, self.here.at[2])

    def store(self):
        return pltpu.make_async_copy(self.own, self.out, self.here.at[3])

    def start(self):
        for way in range(2):
            self.one(way).start()
        for way in range(2):
            self.load(way).start()
        self.load_own().start()

    def middle(self):
        count = self.rows // 2
        for way in range(2):
            self.one(way).wait_recv()
            self.load(1 - way).wait()

            @pl.loop(0, count // 16)
            def _(step):
                rows = pl.ds(pl.multiple_of(way * count + step * 16, 16), 16)
                self.staged[1 - way, rows, :] = (
                    self.staged[1 - way, rows, :].astype(F32) + self.first[rows, :].astype(F32)
                ).astype(BF)

            self.two(1 - way).start()

    def finish(self):
        self.load_own().wait()
        for way in range(2):
            self.two(way).wait_recv()

        @pl.loop(0, self.rows // 16)
        def _(step):
            rows = pl.ds(pl.multiple_of(step * 16, 16), 16)
            self.own[rows, :] = (
                self.own[rows, :].astype(F32)
                + self.second[0, rows, :].astype(F32)
                + self.second[1, rows, :].astype(F32)
            ).astype(BF)

        self.store().start()
        for way in range(2):
            self.one(way).wait_send()
            self.two(way).wait_send()
        self.store().wait()


class Loads:
    def __init__(self, *loads):
        self.loads = loads
        self.operands = [operand for _, operand in loads]
        self.outs_like = [out for kind, operand in loads for out in kind.outs(operand)]
        self.scratch = [item for kind, operand in loads for item in scratch_of(kind, operand)]

    def peers(self, place, base):
        found = {id(peer): peer for peer in base}
        for kind, _ in self.loads:
            for peer in kind.peers(place):
                found[id(peer)] = peer
        return list(found.values())

    def begin(self, place, ins, outs, sems):
        result, at, sem_at = [], 0, 0
        for (kind, operand), source in zip(self.loads, ins):
            count, sem_count = len(kind.outs(operand)), len(scratch_of(kind, operand))
            result.append(
                kind(
                    place,
                    [source],
                    outs[at : at + count],
                    sems[sem_at : sem_at + sem_count],
                )
            )
            at, sem_at = at + count, sem_at + sem_count
        return result


class Works:
    def __init__(self, *works):
        self.works = works
        self.unique = []
        for kind, left, right in works:
            for operand in (left,) if kind == "ta" else (left, right):
                if not any(operand is other for other in self.unique):
                    self.unique.append(operand)
        self.outs_like = []
        for kind, left, right in works:
            if kind == "nt":
                shape = (left.shape[0], right.shape[0])
            elif kind == "ta":
                shape = (left.shape[1], right[1])
            else:
                shape = (left.shape[1], right.shape[1])
            self.outs_like.append(jax.ShapeDtypeStruct(shape, BF))
        self.scratch = (
            [pltpu.VMEM(operand.shape, BF) for operand in self.unique]
            + [pltpu.VMEM(out.shape, BF) for out in self.outs_like]
            + [pltpu.SemaphoreType.DMA((max(1, len(self.unique) + len(works)),))]
        )

    def begin(self, ins, outs, scratch):
        self_ins = list(scratch[: len(self.unique)])
        self_outs = list(scratch[len(self.unique) : -1])
        sems = scratch[-1]
        loads = [
            pltpu.make_async_copy(source, target, sems.at[k])
            for k, (source, target) in enumerate(zip(ins, self_ins))
        ]
        stores = [
            pltpu.make_async_copy(source, target, sems.at[len(loads) + k])
            for k, (source, target) in enumerate(zip(self_outs, outs))
        ]
        return loads, stores, self_ins, self_outs

    def run(self, state, summed):
        loads, stores, ins, outs = state
        waited = set()

        def held(operand):
            at = [place for place, other in enumerate(self.unique) if other is operand][0]
            if at not in waited:
                loads[at].wait()
                waited.add(at)
            return ins[at]

        for k, (kind, left, right) in enumerate(self.works):
            left, out = held(left), outs[k]
            if kind == "ta":
                right = summed.at[:, pl.ds(right[0], right[1])]
            else:
                right = held(right)
            if kind == "nt":
                columns = out.shape[1] // 256

                @pl.loop(0, (out.shape[0] // 256) * columns)
                def _(step):
                    first = pl.ds(pl.multiple_of((step // columns) * 256, 256), 256)
                    second = pl.ds(pl.multiple_of(lax.rem(step, columns) * 256, 256), 256)
                    out[first, second] = lax.dot_general(
                        left[first, :],
                        right[second, :],
                        (((1,), (1,)), ((), ())),
                        preferred_element_type=F32,
                    ).astype(BF)
            else:

                @pl.loop(0, out.shape[0] // 256)
                def _(step):
                    spot = pl.ds(pl.multiple_of(step * 256, 256), 256)
                    out[spot, :] = lax.dot_general(
                        left[:, spot],
                        right[...],
                        (((0,), (0,)), ((), ())),
                        preferred_element_type=F32,
                    ).astype(BF)

            stores[k].start()


ANYWHERE = pl.BlockSpec(memory_space=pl.ANY)


def returned(total, near, far, core, owner):
    rows = near.shape[0]
    mine = jnp.where(core == 0, total[:rows], total[rows:])
    return jnp.where(owner, mine, near).astype(F32) + far.astype(F32)


def exchange_kernel(kind, chunks, window, load, works, *refs):
    refs = list(refs)
    place = Place()
    more = (len(load.operands), len(load.outs_like))
    todo = (len(works.unique), len(works.outs_like), len(works.scratch))
    w_count = len(refs) - 1 - 4 - more[0] - more[1] - todo[0] - todo[1] - todo[2]
    w_count -= 2 + 11 + 4 + (kind != "norm") + len(load.scratch) - 1
    w_from, refs = refs[1 : 1 + w_count], refs[:1] + refs[1 + w_count :]
    ins, refs = refs[:4], refs[4:]
    load_ins, refs = refs[: more[0]], refs[more[0] :]
    work_ins, refs = refs[: todo[0]], refs[todo[0] :]
    outs, refs = refs[:2], refs[2:]
    load_outs, refs = refs[: more[1]], refs[more[1] :]
    work_outs, refs = refs[: todo[1]], refs[todo[1] :]
    rest, refs = refs[:11], refs[11:]
    (a_ref, w_ref, res_ref, loads), refs = refs[:4], refs[4:]
    if kind == "norm":
        a_from, res_from, gain_ref, bias_ref = ins
        res_out, all_ref = outs
    else:
        a_from, res_from, up_from, gain_ref = ins
        all_ref, sum_ref = outs
        up_ref, refs = refs[0], refs[1:]
    carried = load.begin(place, load_ins, load_outs, refs)
    working = works.begin(work_ins, work_outs, refs[len(load.scratch) :])
    mine, given, near, half, far, send_near, got_near, send_far, got_far, send_all, got_all = rest
    rows = mine.shape[0]
    width = mine.shape[1]
    chunk = rows // chunks
    core_peer, far_peer = place.core_peer, place.near_z
    copy = send
    depth = a_ref.shape[1]
    block = 2 * chunk
    tile = 256
    tiles = width // tile

    def load_rows(k):
        first = (k // 2) * block + (0 if k % 2 else rows)
        spot = pl.ds(first, block)
        return pltpu.make_async_copy(a_from.at[spot], a_ref.at[spot], loads.at[2 * tiles + k])

    def load_weight(k):
        spot = pl.ds(k * tile, tile)
        share = depth // len(w_from)
        return [
            pltpu.make_async_copy(
                source.at[spot, pl.ds(window * depth, share)],
                w_ref.at[spot, pl.ds(at * share, share)],
                loads.at[at * tiles + k],
            )
            for at, source in enumerate(w_from)
        ]

    later = [pltpu.make_async_copy(res_from, res_ref, loads.at[2 * tiles + 2 * chunks])]
    if kind != "norm":
        later.append(
            pltpu.make_async_copy(
                up_from.at[pl.ds(0, rows)], up_ref, loads.at[2 * tiles + 2 * chunks + 1]
            )
        )
    load_rows(0).start()
    for k in range(tiles):
        for each in load_weight(k):
            each.start()
    for k in range(1, chunks):
        load_rows(k).start()
    for each in later + working[0]:
        each.start()
    greet(load.peers(place, [core_peer, far_peer]))
    for each in carried:
        if not each.late:
            each.start()

    def near_copy(k):
        part = pl.ds(k * chunk, chunk)
        return copy(given.at[part], near.at[part], send_near.at[k], got_near.at[k], core_peer)

    def far_copy(k):
        part = pl.ds(k * chunk, chunk)
        return copy(half.at[part], far.at[part], send_far.at[k], got_far.at[k], far_peer)

    def all_copy(k):
        return copy(
            all_ref.at[pl.ds(k * chunk, chunk)],
            all_ref.at[pl.ds(rows + k * chunk, chunk)],
            send_all.at[k],
            got_all.at[k],
            core_peer,
        )

    def tile_product(first, target, start, spot):
        target[pl.ds(start, block), spot] = lax.dot_general(
            a_ref[pl.ds(first, block), :],
            w_ref[spot, :],
            (((1,), (1,)), ((), ())),
            preferred_element_type=F32,
        ).astype(target.dtype)

    def product(first, target, start):
        @pl.loop(0, tiles)
        def _(step):
            spot = pl.ds(pl.multiple_of(step * tile, tile), tile)
            tile_product(first, target, start, spot)

    step_rows = 16
    for m in range(chunks // 2):
        load_rows(2 * m).wait()
        if m == 0:
            for k in range(tiles):
                for each in load_weight(k):
                    each.wait()
                tile_product(rows, given, 0, pl.ds(k * tile, tile))
        else:
            product(rows + m * block, given, m * block)
        for k in (2 * m, 2 * m + 1):
            near_copy(k).start()
        load_rows(2 * m + 1).wait()
        product(m * block, mine, m * block)
        for k in (2 * m, 2 * m + 1):
            near_copy(k).wait_recv()

            @pl.loop(0, chunk // step_rows)
            def _(step):
                part = pl.ds(pl.multiple_of(k * chunk + step * step_rows, step_rows), step_rows)
                half[part, :] = (mine[part, :] + near[part, :].astype(F32)).astype(BF)

            far_copy(k).start()
    for each in carried:
        if each.late:
            each.start()
    works.run(working, a_ref)
    for each in later:
        each.wait()
    if kind != "norm":
        sum_ref[...] = jnp.zeros_like(sum_ref)
    for k in range(chunks):
        far_copy(k).wait_recv()

        @pl.loop(0, chunk // step_rows)
        def _(step):
            part = pl.ds(pl.multiple_of(k * chunk + step * step_rows, step_rows), step_rows)
            total = half[part, :].astype(F32) + far[part, :].astype(F32)
            if kind == "norm":
                values = res_ref[part, :] + total
                res_out[part, :] = values
            else:
                values = res_ref[part, :]
            centered = values - jnp.mean(values, axis=-1, keepdims=True)
            inverse = lax.rsqrt(jnp.mean(centered * centered, axis=-1, keepdims=True) + EPS)
            scaled = centered * inverse
            if kind == "norm":
                all_ref[part, :] = (scaled * gain_ref[...] + bias_ref[...]).astype(BF)
            else:
                grad_scaled = total * gain_ref[...]
                first_mean = jnp.mean(grad_scaled, axis=-1, keepdims=True)
                second_mean = jnp.mean(grad_scaled * scaled, axis=-1, keepdims=True)
                grads = inverse * (grad_scaled - first_mean - scaled * second_mean)
                all_ref[part, :] = (up_ref[part, :].astype(F32) + grads).astype(BF)
                product_rows = total * scaled
                sum_ref[0] += product_rows[:8] + product_rows[8:]
                sum_ref[1] += total[:8] + total[8:]

        if k == chunks // 4:
            for each in carried:
                each.middle()
        if kind != "half":
            all_copy(k).start()
    for k in range(chunks):
        near_copy(k).wait_send()
        far_copy(k).wait_send()
        if kind != "half":
            all_copy(k).wait_send()
            all_copy(k).wait_recv()
    for each in carried:
        each.finish()
    for each in working[1]:
        each.wait()


def exchange(kind, place, a, w, residual, *others, load=Loads(), window=0, works=Works()):
    length, depth = a.shape
    w = w if isinstance(w, tuple) else (w,)
    width = w[0].shape[0]
    rows = length // 2
    chunks = 8 if depth < 2048 else 4
    whole = pl.BlockSpec(memory_space=pltpu.VMEM)
    if kind == "norm":
        gain, bias = others
        operands = (a, *w, residual, gain[None], bias[None])
        outs = [
            jax.ShapeDtypeStruct((rows, width), F32),
            jax.ShapeDtypeStruct((length, width), BF),
        ]
    else:
        up, gain = others
        operands = (a, *w, residual, up, gain[None])
        outs = [
            jax.ShapeDtypeStruct((rows if kind == "half" else length, width), BF),
            jax.ShapeDtypeStruct((2, 8, width), F32),
        ]
    plain = 2 if kind == "norm" else 1
    specs = [ANYWHERE] * (len(operands) - plain) + [whole] * plain
    specs += [ANYWHERE] * (len(load.operands) + len(works.unique))
    tiles = width // 256
    more = [
        pltpu.VMEM((length, depth), BF),
        pltpu.VMEM((width, depth), BF),
        pltpu.VMEM((rows, width), F32),
        pltpu.SemaphoreType.DMA((2 * tiles + 2 * chunks + 2,)),
    ]
    if kind != "norm":
        more.append(pltpu.VMEM((rows, width), BF))
    out_specs = [whole] * 2 + [ANYWHERE] * (len(load.outs_like) + len(works.outs_like))
    operands += tuple(load.operands) + tuple(works.unique)
    outs = outs + load.outs_like + works.outs_like
    return pl.pallas_call(
        functools.partial(exchange_kernel, kind, chunks, window, load, works),
        in_specs=specs,
        out_specs=out_specs,
        out_shape=outs,
        scratch_shapes=[
            pltpu.VMEM((rows, width), F32),
            pltpu.VMEM((rows, width), BF),
            pltpu.VMEM((rows, width), BF),
            pltpu.VMEM((rows, width), BF),
            pltpu.VMEM((rows, width), BF),
        ]
        + [pltpu.SemaphoreType.DMA((chunks,))] * 6
        + more
        + load.scratch
        + works.scratch,
        compiler_params=pltpu.CompilerParams(
            collective_id=place, has_side_effects=True, vmem_limit_bytes=63 * 2**20
        ),
        cost_estimate=pl.CostEstimate(
            flops=2 * length * depth * width,
            transcendentals=0,
            bytes_accessed=100_000_000,
        ),
        name="exchange_" + kind,
    )(*operands)


def spread_kernel(load, chunks, *refs):
    refs = list(refs)
    more = (len(load.operands), len(load.outs_like))
    (half_ref, pieces_ref), refs = refs[:2], refs[2:]
    load_ins, refs = refs[: more[0]], refs[more[0] :]
    (out_ref, token_ref, share_ref), refs = refs[:3], refs[3:]
    load_outs, refs = refs[: more[1]], refs[more[1] :]
    (sent, got, send_token, got_token, send_share, got_share), refs = refs[:6], refs[6:]
    place = Place()
    carried = load.begin(place, load_ins, load_outs, refs)
    d, core, pair = place.d, place.core, place.pair
    inner_z = lax.rem(place.z, 2)
    plane_peers = [(lax.rem(d + j, 8), place.z) for j in range(1, 8)]
    far_peers = [(lax.rem(d + j, 8), place.far_z) for j in range(8)]
    greet([place.near_z] + far_peers + plane_peers)
    rows = half_ref.shape[0]
    chunk = rows // chunks

    def spot(which, k):
        return out_ref.at[pl.ds(pl.multiple_of(which * rows + k * chunk, chunk), chunk)]

    def owner_copy(k, which):
        source = half_ref.at[pl.ds(k * chunk, chunk)]
        return send(source, spot(which, k), sent.at[0, k], got.at[0, k], place.core_peer)

    def pair_copy(k, which):
        source = half_ref.at[pl.ds(k * chunk, chunk)]
        return send(source, spot(which, k), sent.at[1, k], got.at[1, k], place.user)

    def pass_copy(k, which):
        return send(spot(which, k), spot(which, k), sent.at[2, k], got.at[2, k], place.near_z)

    def share_copy(far, j):
        return send(
            pieces_ref.at[pl.ds(pl.multiple_of(lax.rem(d + j, 8) * 8, 8), 8)],
            share_ref.at[pl.ds((8 * far + j) * 8, 8)],
            send_share.at[far, j],
            got_share.at[far, j],
            far_peers[j] if far else plane_peers[j - 1],
        )

    for j in range(8):
        share_copy(1, j).start()
        if j:
            share_copy(0, j).start()
    share_ref[pl.ds(0, 8), :] = pieces_ref[pl.ds(pl.multiple_of(d * 8, 8), 8), :]

    @pl.when(core == inner_z)
    def _():
        for k in range(chunks):
            pair_copy(k, core).start()

    @pl.when(core != pair)
    def _():
        for k in range(chunks):
            owner_copy(k, core).start()

    @pl.when(core == pair)
    def _():
        @pl.loop(0, rows // 16)
        def _(step):
            first = pl.multiple_of(step * 16, 16)
            out_ref[pl.ds(pl.multiple_of(core * rows + first, 16), 16), :] = half_ref[
                pl.ds(first, 16), :
            ]

        for k in range(chunks):
            owner_copy(k, 1 - core).wait_recv()

    def pass_on(k):
        pair_copy(k, inner_z).wait_recv()
        pass_copy(k, inner_z).start()

    @pl.when(core != pair)
    def _():
        for k in range(chunks // 2):
            pass_on(k)

    for each in carried:
        each.start()

    @pl.when(core != pair)
    def _():
        for k in range(chunks // 2, chunks):
            pass_on(k)
        for k in range(chunks):
            pass_copy(k, 1 - inner_z).wait_recv()

    head = 16
    token_ref[pl.ds(pl.multiple_of(d * head, head), head), :] = out_ref[pl.ds(0, head), :]

    def token_copy(j, sender):
        return send(
            out_ref.at[pl.ds(0, head)],
            token_ref.at[pl.ds(pl.multiple_of(sender * head, head), head)],
            send_token.at[j - 1],
            got_token.at[j - 1],
            plane_peers[j - 1],
        )

    for j in range(1, 8):
        token_copy(j, d).start()

    @pl.when(core != pair)
    def _():
        for k in range(chunks):
            pass_copy(k, inner_z).wait_send()
            owner_copy(k, core).wait_send()

    @pl.when(core == inner_z)
    def _():
        for k in range(chunks):
            pair_copy(k, core).wait_send()

    for j in range(1, 8):
        token_copy(j, d).wait_send()
        token_copy(j, lax.rem(d + 8 - j, 8)).wait_recv()
    for j in range(8):
        share_copy(1, j).wait()
        if j:
            share_copy(0, j).wait()
    for each in carried:
        each.finish()


def spread_gradient(place, half, pieces, load):
    rows, width = half.shape
    chunks = 4
    whole = pl.BlockSpec(memory_space=pltpu.VMEM)
    return pl.pallas_call(
        functools.partial(spread_kernel, load, chunks),
        in_specs=[whole] * 2 + [ANYWHERE] * len(load.operands),
        out_specs=[whole] * 3 + [ANYWHERE] * len(load.outs_like),
        out_shape=[
            jax.ShapeDtypeStruct((2 * rows, width), BF),
            jax.ShapeDtypeStruct((8 * 16, width), BF),
            jax.ShapeDtypeStruct((2 * pieces.shape[0], pieces.shape[1]), F32),
        ]
        + load.outs_like,
        scratch_shapes=[
            pltpu.SemaphoreType.DMA((3, chunks)),
            pltpu.SemaphoreType.DMA((3, chunks)),
            pltpu.SemaphoreType.DMA((7,)),
            pltpu.SemaphoreType.DMA((7,)),
            pltpu.SemaphoreType.DMA((2, 8)),
            pltpu.SemaphoreType.DMA((2, 8)),
        ]
        + load.scratch,
        compiler_params=pltpu.CompilerParams(
            collective_id=place, has_side_effects=True, vmem_limit_bytes=60 * 2**20
        ),
        cost_estimate=pl.CostEstimate(flops=0, transcendentals=0, bytes_accessed=100_000_000),
        name="spread_gradient",
    )(half, pieces, *load.operands)


def feed_kernel(
    n_ref, mine_ref, other_ref, gate_ref, up_ref, down_ref, hidden_ref, grad_ref, cot_out, here
):
    step_here = pl.program_id(0)
    length = n_ref.shape[0]
    tile = gate_ref.shape[1]
    half = grad_ref.shape[1] // 2
    block = 256
    gate_columns = pl.ds(pl.multiple_of(step_here * tile, tile), tile)
    up_columns = pl.ds(pl.multiple_of(half + step_here * tile, tile), tile)
    both = (mine_ref, other_ref)
    copies = [
        pltpu.make_async_copy(part, cot_out.at[pl.ds(k * (length // 2), length // 2)], here.at[k])
        for k, part in enumerate(both)
    ]

    @pl.when(step_here == 0)
    def _():
        for copy in copies:
            copy.start()

    for k, cot_ref in enumerate(both):

        @pl.loop(0, length // 2 // block)
        def _(step):
            source = pl.ds(pl.multiple_of(step * block, block), block)
            rows = pl.ds(pl.multiple_of(k * (length // 2) + step * block, block), block)
            gate = jnp.dot(n_ref[rows, :], gate_ref[...], preferred_element_type=F32)
            up = jnp.dot(n_ref[rows, :], up_ref[...], preferred_element_type=F32)
            grad = jnp.dot(cot_ref[source, :], down_ref[...], preferred_element_type=F32)
            sigmoid = jax.nn.sigmoid(gate)
            silu = gate * sigmoid
            hidden_ref[rows, :] = (silu * up).astype(BF)
            grad_ref[rows, gate_columns] = (
                grad * up * sigmoid * (1.0 + gate * (1.0 - sigmoid))
            ).astype(BF)
            grad_ref[rows, up_columns] = (grad * silu).astype(BF)

    @pl.when(step_here == pl.num_programs(0) - 1)
    def _():
        for copy in copies:
            copy.wait()


def feed_forward(normed, mine, other, gate_up, down):
    length, width = normed.shape
    hidden_width = down.shape[1]
    tile = 256
    steps = hidden_width // tile
    whole = pl.BlockSpec(memory_space=pltpu.VMEM)
    return pl.pallas_call(
        feed_kernel,
        grid=(steps,),
        in_specs=[
            whole,
            whole,
            whole,
            pl.BlockSpec((width, tile), lambda j: (0, j)),
            pl.BlockSpec((width, tile), lambda j: (0, j + steps)),
            pl.BlockSpec((width, tile), lambda j: (0, j)),
        ],
        out_specs=[
            pl.BlockSpec((length, tile), lambda j: (0, j)),
            pl.BlockSpec((length, 2 * hidden_width), lambda j: (0, 0)),
            ANYWHERE,
        ],
        out_shape=[
            jax.ShapeDtypeStruct((length, hidden_width), BF),
            jax.ShapeDtypeStruct((length, 2 * hidden_width), BF),
            jax.ShapeDtypeStruct((length, width), BF),
        ],
        scratch_shapes=[pltpu.SemaphoreType.DMA((2,))],
        compiler_params=pltpu.CompilerParams(vmem_limit_bytes=60 * 2**20),
        cost_estimate=pl.CostEstimate(
            flops=6 * length * width * hidden_width,
            transcendentals=length * hidden_width,
            bytes_accessed=30_000_000,
        ),
        name="feed_forward",
    )(normed, mine, other, gate_up, gate_up, down)


def turn_tables(length, block):
    rotated = HD // 2
    angles = np.exp(-np.log(10000.0) * np.arange(rotated // 2) * 2.0 / rotated)
    lanes = np.concatenate([angles, angles, np.zeros(HD - rotated)])
    lanes = np.concatenate([lanes, lanes])
    base = np.arange(block)[:, None] * lanes[None]
    steps = np.zeros((8, 128))
    steps[: length // block] = np.arange(0, length, block)[:, None] * lanes[None]
    pack = lambda table: np.stack([np.cos(table), np.sin(table)]).astype(np.float32)
    return jnp.asarray(pack(base)), jnp.asarray(pack(steps))


def turned_block(values, base_ref, steps_ref, here, sign):
    half = HD // 4
    first_cos, first_sin = steps_ref[0, pl.ds(here, 1), :], steps_ref[1, pl.ds(here, 1), :]
    cosine = first_cos * base_ref[0] - first_sin * base_ref[1]
    sine = first_sin * base_ref[0] + first_cos * base_ref[1]
    lane = lax.rem(lax.broadcasted_iota(jnp.int32, values.shape, 1), HD)
    lower = jnp.where(lane < half, sine, 0.0)
    upper = jnp.where((lane >= half) & (lane < 2 * half), sine, 0.0)
    ahead = pltpu.roll(values, 128 - half, 1)
    behind = pltpu.roll(values, half, 1)
    if sign > 0:
        return values * cosine - ahead * lower + behind * upper
    return values * cosine + ahead * lower - behind * upper


def opening_kernel(*refs):
    (qkv_part, side_part, feed_part, latents, prompt, time_part, feat, facts) = refs[:8]
    gain_ref, bias_ref, base_ref, steps_ref = refs[8:12]
    (n_ref, q_ref, k_ref, v_ref, o_ref, log_ref, res_ref, qkv_out) = refs[12:20]
    side_full, feed_own, prompt_too, facts_too, feat_out = refs[20:25]
    projected, item, time_full, qkv_full, feat_full = refs[25:30]
    sent_far, got_far, sent_near, got_near, here = refs[30:35]
    sent_plane, got_plane, sent_side, got_side = refs[35:39]
    sent_small, got_small, sent_swap, got_swap = refs[39:43]
    place = Place()
    d, core, column, owner = place.d, place.core, place.column, place.owner
    step_here = pl.program_id(0)
    plane_peers = [(lax.rem(d + j, 8), place.z) for j in range(1, 8)]
    rows = qkv_part.shape[0]
    piece = rows // 2
    length, width = item.shape
    total = qkv_full.shape[1]
    block = 256
    parts = range(4)

    def at(ref, index, count):
        return ref.at[pl.ds(pl.multiple_of(index * count, count), count)]

    def ends(k, sender):
        if k < 2:
            source = qkv_part.at[pl.ds(k * piece, piece)]
            spot = pl.multiple_of((2 * column + sender) * rows + k * piece, piece)
            return source, qkv_full.at[pl.ds(spot, piece)]
        if k == 2:
            return side_part, at(side_full, 2 * column + sender, rows)
        return feed_part, at(feed_own, sender, rows)

    def far(k, sender):
        source, target = ends(k, sender)
        return send(source, target, sent_far.at[k], got_far.at[sender, k], place.user)

    def near(k, sender):
        source, target = ends(k, sender)
        return send(source, target, sent_near.at[k], got_near.at[k], place.core_peer)

    def local(k):
        source, target = ends(k, core)
        return pltpu.make_async_copy(source, target, here.at[k])

    def await_part(k, sender):
        @pl.when(owner)
        def _():
            @pl.when(core == sender)
            def _():
                local(k).wait()

            @pl.when(core != sender)
            def _():
                near(k, sender).wait_recv()

        @pl.when(jnp.logical_not(owner))
        def _():
            far(k, sender).wait_recv()

    item_copy = send(latents, item, sent_swap.at[0], got_swap.at[0], place.core_peer)
    item_local = pltpu.make_async_copy(latents, item, here.at[4])
    outward = [
        pltpu.make_async_copy(qkv_full, qkv_out, here.at[7]),
        pltpu.make_async_copy(feat_full, feat_out, here.at[8]),
    ]
    swaps = [
        send(prompt, prompt_too, sent_swap.at[1], got_swap.at[1], place.core_peer),
        send(facts, facts_too, sent_swap.at[2], got_swap.at[2], place.core_peer),
    ]
    smalls = ((time_part, time_full), (feat, feat_full))

    def small(which, j, sender):
        part, whole = smalls[which]
        return send(
            part,
            at(whole, sender, part.shape[0]),
            sent_small.at[which, j - 1],
            got_small.at[which, j - 1],
            plane_peers[j - 1],
        )

    def small_local(which):
        part, whole = smalls[which]
        return pltpu.make_async_copy(part, at(whole, d, part.shape[0]), here.at[5 + which])

    def plane(stage, way, k, sender):
        peer = place.x_peer if way == 0 else place.y_peer
        source = column if stage == 0 else (place.y_column if way == 0 else place.x_column)
        spot = qkv_full.at[
            pl.ds(pl.multiple_of((2 * source + sender) * rows + k * piece, piece), piece)
        ]
        slot = 4 * stage + 2 * sender + k
        return send(spot, spot, sent_plane.at[way, slot], got_plane.at[way, slot], peer)

    def side(stage, way, sender):
        peer = place.x_peer if way == 0 else place.y_peer
        source = column if stage == 0 else (place.y_column if way == 0 else place.x_column)
        spot = at(side_full, 2 * source + sender, rows)
        slot = 2 * stage + sender
        return send(spot, spot, sent_side.at[way, slot], got_side.at[way, slot], peer)

    def side_one():
        for sender in range(2):
            await_part(2, sender)
            side(0, sender, sender).start()
        for sender in range(2):
            side(0, 1 - sender, sender).start()

    def side_two():
        side(0, 0, 0).wait_recv()
        side(1, 1, 0).start()
        side(0, 1, 1).wait_recv()
        side(1, 0, 1).start()

    @pl.when(step_here == 0)
    def _():
        greet([place.far_same, place.far_other] + plane_peers)
        for k in parts:
            far(k, core).start()

        @pl.when(owner)
        def _():
            item_copy.start()
            item_local.start()
            for k in parts:
                local(k).start()

        for which in range(2):
            small_local(which).start()
        for j in range(1, 8):
            for which in range(2):
                small(which, j, d).start()

        @pl.when(jnp.logical_not(owner))
        def _():
            for k in parts:
                near(k, core).start()

        for swap in swaps:
            swap.start()
        for which in range(2):
            small_local(which).wait()
        for j in range(1, 8):
            for which in range(2):
                small(which, j, lax.rem(d + 8 - j, 8)).wait_recv()

        @pl.when(owner)
        def _():
            item_local.wait()

        @pl.when(jnp.logical_not(owner))
        def _():
            item_copy.wait_recv()

        user = 2 * column + place.pair
        token_row = jnp.dot(
            feat_full[pl.ds(pl.multiple_of(user * 16, 16), 16), :],
            time_full[...],
            preferred_element_type=F32,
        )
        row_number = lax.broadcasted_iota(jnp.int32, (16, width), 0)

        def norm_rows(step, keep):
            local_row = pl.multiple_of(step * 16, 16)
            spot = pl.multiple_of(lax.rem(local_row + core * (length // 2), length), 16)
            values = item[pl.ds(spot, 16), :].astype(F32)
            values = jnp.where(row_number + spot == 0, token_row, values)
            if keep:
                res_ref[pl.ds(local_row, 16), :] = values
            centered = values - jnp.mean(values, axis=-1, keepdims=True)
            inverse = lax.rsqrt(jnp.mean(centered * centered, axis=-1, keepdims=True) + EPS)
            n_ref[pl.ds(local_row, 16), :] = (
                centered * inverse * gain_ref[...] + bias_ref[...]
            ).astype(BF)

        def forward(k):
            for sender in range(2):
                await_part(k, sender)
                plane(0, 0, k, sender).start()
                plane(0, 1, k, sender).start()

        steps = length // 16
        forward(0)

        @pl.loop(0, steps // 2)
        def _(step):
            norm_rows(step, True)

        forward(1)

        @pl.loop(steps // 2, steps)
        def _(step):
            norm_rows(step, False)

        for k in range(2):
            plane(0, 0, k, 0).wait_recv()
            plane(1, 1, k, 0).start()
            plane(0, 1, k, 1).wait_recv()
            plane(1, 0, k, 1).start()
            plane(0, 0, k, 1).wait_recv()
            plane(0, 1, k, 0).wait_recv()
        for k in range(2):
            plane(1, 1, k, 0).wait_recv()
            plane(1, 0, k, 1).wait_recv()

        side_one()

        for each in outward:
            each.start()
        third = total // 3
        for part in range(3):
            columns = pl.ds(part * third, third)

            @pl.loop(0, length // block)
            def _(step):
                spot = pl.ds(pl.multiple_of(step * block, block), block)
                projected[spot, columns] = jnp.dot(
                    n_ref[spot, :], qkv_full[:, columns], preferred_element_type=F32
                )

    @pl.when(step_here == 1)
    def _():
        side_two()

    def turn(first, target):
        columns = pl.ds(pl.multiple_of(first + step_here * 128, 128), 128)

        @pl.loop(0, length // block)
        def _(step):
            spot = pl.ds(pl.multiple_of(step * block, block), block)
            index = lax.rem(step + core * (length // block // 2), length // block)
            target[spot, :] = turned_block(
                projected[spot, columns], base_ref, steps_ref, index, 1
            ).astype(BF)

    turn(0, q_ref)
    turn(total // 3, k_ref)
    v_ref[...] = projected[
        :, pl.ds(pl.multiple_of(2 * (total // 3) + step_here * 128, 128), 128)
    ].astype(BF)
    attend_pair(HD, block, q_ref, k_ref, v_ref, None, o_ref, log_ref)

    @pl.when(step_here == pl.num_programs(0) - 1)
    def _():
        for sender in range(2):
            side(0, 1 - sender, sender).wait_recv()
        side(1, 1, 0).wait_recv()
        side(1, 0, 1).wait_recv()
        for sender in range(2):
            await_part(3, sender)
        for each in outward:
            each.wait()
        for swap in swaps:
            swap.wait()
        for j in range(1, 8):
            for which in range(2):
                small(which, j, d).wait_send()
        for k in parts:
            far(k, core).wait_send()

        @pl.when(owner)
        def _():
            item_copy.wait_send()

        @pl.when(jnp.logical_not(owner))
        def _():
            for k in parts:
                near(k, core).wait_send()

        for sender in range(2):
            for way in range(2):
                side(0, way, sender).wait_send()
                for k in range(2):
                    plane(0, way, k, sender).wait_send()
        side(1, 1, 0).wait_send()
        side(1, 0, 1).wait_send()
        for k in range(2):
            plane(1, 1, k, 0).wait_send()
            plane(1, 0, k, 1).wait_send()


def opening(place, qkv_part, side_part, feed_part, latents, prompt, time_part, feat, facts, gain, bias):
    length, width = latents.shape
    total = qkv_part.shape[1]
    rows = qkv_part.shape[0]
    pairs = total // 3 // 128
    base, steps = turn_tables(length, 256)
    block = pl.BlockSpec((length, 128), lambda i: (0, i))
    whole = pl.BlockSpec(memory_space=pltpu.VMEM)
    wide = jax.ShapeDtypeStruct((length, total // 3), BF)
    dma = pltpu.SemaphoreType.DMA
    return pl.pallas_call(
        opening_kernel,
        grid=(pairs,),
        in_specs=[ANYWHERE] * 8 + [whole] * 4,
        out_specs=[whole]
        + [block] * 4
        + [pl.BlockSpec((1, 2, length), lambda i: (i, 0, 0)), whole]
        + [ANYWHERE] * 6,
        out_shape=[jax.ShapeDtypeStruct((length, width), BF)]
        + [wide] * 4
        + [
            jax.ShapeDtypeStruct((pairs, 2, length), F32),
            jax.ShapeDtypeStruct((length // 2, width), F32),
            jax.ShapeDtypeStruct((8 * rows, total), BF),
            jax.ShapeDtypeStruct((8 * rows, side_part.shape[1]), BF),
            jax.ShapeDtypeStruct((2 * rows, feed_part.shape[1]), BF),
            jax.ShapeDtypeStruct(prompt.shape, BF),
            jax.ShapeDtypeStruct(facts.shape, facts.dtype),
            jax.ShapeDtypeStruct((8 * feat.shape[0], feat.shape[1]), BF),
        ],
        scratch_shapes=[
            pltpu.VMEM((length, total), F32),
            pltpu.VMEM((length, width), BF),
            pltpu.VMEM((8 * time_part.shape[0], width), BF),
            pltpu.VMEM((8 * rows, total), BF),
            pltpu.VMEM((8 * feat.shape[0], feat.shape[1]), BF),
            dma((4,)),
            dma((2, 4)),
            dma((4,)),
            dma((4,)),
            dma((9,)),
            dma((2, 8)),
            dma((2, 8)),
            dma((2, 4)),
            dma((2, 4)),
            dma((2, 7)),
            dma((2, 7)),
            dma((3,)),
            dma((3,)),
        ],
        compiler_params=pltpu.CompilerParams(
            collective_id=place, has_side_effects=True, vmem_limit_bytes=60 * 2**20
        ),
        cost_estimate=pl.CostEstimate(
            flops=4 * length * length * total // 3 + 2 * length * width * total,
            transcendentals=length * length * total // 192,
            bytes_accessed=200_000_000,
        ),
        name="opening",
    )(
        qkv_part,
        side_part,
        feed_part,
        latents,
        prompt,
        time_part,
        feat,
        facts,
        gain[None],
        bias[None],
        base,
        steps,
    )


def per_device_paired(
    latents,
    prompt_tokens,
    prompt_lengths,
    timesteps,
    time_weight,
    self_gain,
    self_bias,
    qkv_weight,
    self_out_weight,
    cross_gain,
    cross_bias,
    cross_query_weight,
    context_weight,
    cross_out_weight,
    feed_gain,
    feed_bias,
    gate_up_weight,
    down_weight,
    down_bias,
    cotangent,
):
    d = lax.axis_index("dp")
    z = lax.axis_index("mp")
    core, pair = d & 1, z >> 1
    owner = core == pair
    length = latents.shape[1] + 1
    rows = length // 4
    half_rows = length // 2
    part_rows = qkv_weight.shape[0]
    n = cross_query_weight.shape[1]

    side_part = jnp.concatenate(
        [
            self_out_weight.T,
            cross_query_weight,
            cross_out_weight.T,
            context_weight.reshape(part_rows, -1),
        ],
        axis=1,
    )
    feature_width = 8 * time_weight.shape[0]
    features = time_features(timesteps, feature_width).astype(BF)
    (
        normed_one,
        queries,
        keys,
        values,
        attended,
        self_logs,
        residual_mine,
        qkv_full,
        side_full,
        gate_up_own,
        prompt_too,
        facts_too,
        features_full,
    ) = opening(
        5,
        qkv_weight.reshape(part_rows, -1),
        side_part,
        gate_up_weight.reshape(part_rows, -1),
        jnp.pad(latents[0], ((1, 0), (0, 0))),
        prompt_tokens[0],
        time_weight,
        jnp.broadcast_to(features, (16, feature_width)),
        jnp.broadcast_to(prompt_lengths[:, None], (8, 128)),
        self_gain,
        self_bias,
    )
    gate_up_full = plane_gather(gate_up_own)
    self_out_full = side_full[:, :n]
    cross_query_full = side_full[:, n : 2 * n]
    cross_out_full = side_full[:, 2 * n : 3 * n]
    context_full = side_full[:, 3 * n :].reshape(context_weight.shape[0] * 8, -1)

    item_prompt = jnp.where(owner, prompt_tokens[0], prompt_too)
    item_length = jnp.where(owner, prompt_lengths[0], facts_too[0, 0])

    residual_one, normed_two_all, down_own, cot_too = exchange(
        "norm",
        0,
        attended,
        side_full,
        residual_mine,
        cross_gain,
        cross_bias,
        load=Loads((Spread, down_weight.T), (SwapRoute, cotangent[0])),
    )
    cot_shard = jnp.where(owner, cotangent[0], cot_too)
    cot_far = move(cot_shard, SWAP_Z)
    odd = (z & 1) == 1
    cross_q = dot_nn(normed_two_all, cross_query_full).astype(BF)
    context = dot_nn(item_prompt, context_full).astype(BF)
    slots = prompt_tokens.shape[1]
    mask = jnp.where(jnp.arange(slots, dtype=jnp.int32)[:, None] < item_length, 0.0, NEG)
    mask = mask.astype(F32)
    crossed, cross_logs = cross_attention(cross_q, context, mask)
    cot_far = after(cot_far, crossed)
    cot_mine = jnp.concatenate(
        [jnp.where(odd, cot_far, cot_shard), jnp.where(odd, cot_shard, cot_far)], axis=0
    )
    cot_other = move(cot_mine, SWAP_CORE)
    residual_two, normed_three_all, down_full = exchange(
        "norm",
        1,
        crossed,
        side_full,
        residual_one,
        feed_gain,
        feed_bias,
        load=Loads((Plane, down_own)),
        window=2,
    )
    hidden, grad_gate_up, cot_all = feed_forward(
        normed_three_all,
        cot_mine,
        after(cot_other, normed_three_all),
        gate_up_full,
        down_full,
    )

    split = gate_up_weight.shape[2]
    gate_local = dot_tn(normed_three_all, grad_gate_up[:, :split]).astype(BF)
    gate_sums = plane_sum(gate_local)
    grad_two_all, feed_sums, feed, down_local, up_local = exchange(
        "back",
        2,
        after(grad_gate_up, gate_local),
        gate_up_full,
        residual_two,
        cot_mine,
        feed_gain,
        works=Works(
            ("nt", hidden, down_full),
            ("tn", cot_all, hidden),
            ("ta", normed_three_all, (split, split)),
        ),
    )
    up_sums = plane_sum(up_local)
    down_sums = plane_sum(after(down_local, up_local))
    grad_crossed = dot_nn(grad_two_all, cross_out_full).astype(BF)
    grad_cross_q, grad_context = cross_attention_back(
        cross_q, context, mask, grad_crossed, cross_logs
    )
    (
        grad_one_all,
        cross_sums,
        gate_near,
        gate_far,
        feed_near,
        cross_query_grad,
        cross_out_grad,
        context_grad,
    ) = exchange(
        "back",
        3,
        grad_cross_q,
        side_full,
        residual_one,
        grad_two_all,
        cross_gain,
        load=Loads((Return, gate_sums), (SwapCoreHalf, feed)),
        window=1,
        works=Works(
            ("tn", normed_two_all, grad_cross_q),
            ("tn", grad_two_all, crossed),
            ("tn", item_prompt, grad_context),
        ),
    )
    feed_half = feed[:half_rows].astype(F32) + feed_near.astype(F32)
    feed_here = jnp.where(odd, feed_half[rows:], feed_half[:rows])
    feed_away = jnp.where(odd, feed_half[:rows], feed_half[rows:]).astype(BF)
    grad_attended = dot_nn(grad_one_all, self_out_full).astype(BF)
    grad_projected, up_near, up_far, feed_far = self_attention_back(
        7,
        queries,
        keys,
        values,
        grad_attended,
        self_logs,
        Loads((Return, up_sums), (SwapNear, feed_away)),
    )
    residual_here = jnp.where(odd, residual_two[rows:], residual_two[:rows])
    output_here = (residual_here + feed_here + feed_far.astype(F32) + down_bias).astype(BF)
    self_out_local = dot_tn(grad_one_all, attended).astype(BF)
    qkv_local = dot_tn(normed_one, grad_projected).astype(BF)
    qkv_total = plane_sum(qkv_local)
    (
        grad_in,
        self_sums,
        down_near,
        down_far,
        output_far,
        cross_query_total,
        cross_out_total,
        context_total,
        self_out_total,
    ) = exchange(
        "half",
        4,
        after(grad_projected, qkv_local),
        qkv_full,
        residual_mine,
        grad_one_all,
        self_gain,
        load=Loads(
            (Return, down_sums),
            (SwapRoute, output_here),
            (PlaneSum, cross_query_grad),
            (PlaneSum, cross_out_grad),
            (PlaneSum, context_grad),
            (PlaneSum, self_out_local),
        ),
    )
    sums = jnp.concatenate(
        [
            jnp.sum(self_sums, axis=1),
            jnp.sum(cross_sums, axis=1),
            jnp.sum(feed_sums, axis=1),
            jnp.sum(cot_mine.astype(F32), axis=0)[None],
            jnp.zeros((1, grad_in.shape[1]), F32),
        ],
        axis=0,
    )
    share = sums.shape[1] // 8
    pieces = jnp.swapaxes(sums.reshape(8, 8, share), 0, 1)
    pieces = jnp.pad(pieces, ((0, 0), (0, 0), (0, 256 - share))).reshape(64, 256)
    totals = (cross_query_total, cross_out_total, context_total, self_out_total, qkv_total)
    whole, token_rows, sums, *ends = spread_gradient(
        8, grad_in, pieces, Loads(*[(Return, total) for total in totals])
    )
    cross_query_grad, cross_out_grad, context_grad, self_out_grad, qkv_grad = [
        returned(total, ends[2 * k], ends[2 * k + 1], core, owner)
        for k, total in enumerate(totals)
    ]
    sums = jnp.sum(sums.reshape(16, 8, 256), axis=0)[:, :share]
    output = jnp.where(owner, output_here, output_far)
    latents_grad = whole[1:]

    token_rows = token_rows.reshape(8, 16, -1)[:, 0]
    all_features = features_full.reshape(8, 16, -1)[:, 0]
    my_features = jnp.zeros((8, feature_width // 8), F32)
    for j in range(8):
        piece = all_features[:, j * (feature_width // 8) : (j + 1) * (feature_width // 8)]
        my_features = my_features + jnp.where(d == j, piece.astype(F32), 0.0)
    time_grad = lax.dot_general(
        my_features.astype(BF), token_rows, (((0,), (0,)), ((), ())), preferred_element_type=F32
    )

    gate_grad = returned(gate_sums, gate_near, gate_far, core, owner)
    up_grad = returned(up_sums, up_near, up_far, core, owner)
    down_grad = returned(down_sums, down_near, down_far, core, owner)
    return (
        output[None],
        latents_grad[None],
        time_grad,
        sums[0],
        sums[1],
        qkv_grad.reshape(qkv_weight.shape),
        self_out_grad.T,
        sums[2],
        sums[3],
        cross_query_grad,
        context_grad.reshape(context_weight.shape),
        cross_out_grad.T,
        sums[4],
        sums[5],
        jnp.stack([gate_grad, up_grad], axis=1),
        down_grad.T,
        sums[6],
    )


def solution(mesh):
    placed = (
        P("dp", None, None),
        P("dp", None, None),
        P("dp"),
        P("dp"),
        P("dp", None),
        P(),
        P(),
        P("dp", None, "mp"),
        P("mp", "dp"),
        P(),
        P(),
        P("dp", "mp"),
        P("dp", None, "mp"),
        P("mp", "dp"),
        P(),
        P(),
        P("dp", None, "mp"),
        P("mp", "dp"),
        P(),
        P("dp", "mp", None),
    )
    paired = mesh.shape["dp"] == 8 and mesh.shape["mp"] == 4
    return jax.shard_map(
        per_device_paired if paired else per_device_general,
        mesh=mesh,
        in_specs=placed,
        out_specs=(
            P("dp", "mp", None),
            P("dp", None, None),
            P("dp", None),
            P("dp"),
            P("dp"),
            P("dp", None, "mp"),
            P("mp", "dp"),
            P("dp"),
            P("dp"),
            P("dp", "mp"),
            P("dp", None, "mp"),
            P("mp", "dp"),
            P("dp"),
            P("dp"),
            P("dp", None, "mp"),
            P("mp", "dp"),
            P("dp"),
        ),
        check_vma=False,
    )
```

```python
import functools
import math

import jax
import jax.numpy as jnp
import numpy as np
from jax import lax
from jax.experimental import pallas as pl
from jax.experimental.pallas import tpu as pltpu
from jax.sharding import PartitionSpec as P

HD = 64


EPS = 1e-05
NEG = -1e30


def time_features(steps_in, feature_width):
    half_width = feature_width // 2
    freqs = jnp.exp(-math.log(10000.0) * jnp.arange(half_width, dtype=jnp.float32) / half_width)
    angles = steps_in.astype(jnp.float32)[:, None] * freqs[None, :]
    return jnp.concatenate([jnp.cos(angles), jnp.sin(angles)], axis=-1)


def rope_tables(length, head_size):
    rotated_width = head_size // 2
    half_width = rotated_width // 2
    inverse = jnp.exp(
        -math.log(10000.0) * jnp.arange(half_width, dtype=jnp.float32) * 2.0 / rotated_width
    )
    angles = jnp.arange(length, dtype=jnp.float32)[:, None] * inverse[None, :]
    cosine = jnp.concatenate([jnp.cos(angles), jnp.cos(angles)], axis=-1)
    sine = jnp.concatenate([jnp.sin(angles), jnp.sin(angles)], axis=-1)
    return (cosine[:, None, :], sine[:, None, :])


def rotate(values, cosine, sine):
    rotated_width = cosine.shape[-1]
    half_width = rotated_width // 2
    first = values[..., :rotated_width]
    turned = jnp.concatenate([-first[..., half_width:], first[..., :half_width]], axis=-1)
    return jnp.concatenate([first * cosine + turned * sine, values[..., rotated_width:]], axis=-1)


def unrotate(grads_in, cosine, sine):
    rotated_width = cosine.shape[-1]
    half_width = rotated_width // 2
    first = grads_in[..., :rotated_width]
    scaled_in = first * sine
    turned = jnp.concatenate([scaled_in[..., half_width:], -scaled_in[..., :half_width]], axis=-1)
    return jnp.concatenate([first * cosine + turned, grads_in[..., rotated_width:]], axis=-1)


def layer_norm(values, gain, bias):
    centered = values - jnp.mean(values, axis=-1, keepdims=True)
    inverse = lax.rsqrt(jnp.mean(centered * centered, axis=-1, keepdims=True) + EPS)
    scaled = centered * inverse
    return (scaled * gain + bias, scaled, inverse)


def norm_back(grad_normed, scaled, inverse, gain):
    grad_scaled = grad_normed * gain
    first_mean = jnp.mean(grad_scaled, axis=-1, keepdims=True)
    second_mean = jnp.mean(grad_scaled * scaled, axis=-1, keepdims=True)
    grad_values = inverse * (grad_scaled - first_mean - scaled * second_mean)
    return (
        grad_values,
        jnp.sum(grad_normed * scaled, axis=(0, 1)),
        jnp.sum(grad_normed, axis=(0, 1)),
    )


def attend_forward(queries, key_rows, value_rows, bias_rows, block_size):
    score_scale = queries.shape[-1] ** (-0.5)

    def one_item(operands):
        item_query, item_key, item_value, item_bias = operands
        query_blocks = item_query.reshape(-1, block_size, item_query.shape[1], item_query.shape[2])

        def one_block(block_query):
            scores = jnp.einsum(
                "qhe,khe->hqk", block_query, item_key, preferred_element_type=jnp.float32
            )
            scores = scores * score_scale + item_bias[None, None, :]
            row_max = jnp.max(scores, axis=-1, keepdims=True)
            expos = jnp.exp(scores - row_max)
            row_total = jnp.sum(expos, axis=-1, keepdims=True)
            weights_p = (expos / row_total).astype(jnp.bfloat16)
            mixed = jnp.einsum(
                "hqk,khe->qhe", weights_p, item_value, preferred_element_type=jnp.float32
            )
            return (mixed, (row_max + jnp.log(row_total))[..., 0])

        mixed, log_total = lax.map(one_block, query_blocks)
        return (mixed.reshape(item_query.shape), log_total)

    return lax.map(one_item, (queries, key_rows, value_rows, bias_rows))


def attend_backward(queries, key_rows, value_rows, bias_rows, log_totals, grad_out, block_size):
    score_scale = queries.shape[-1] ** (-0.5)

    def one_item(operands):
        item_query, item_key, item_value, item_bias, item_log, item_grad = operands
        block_shape = (-1, block_size, item_query.shape[1], item_query.shape[2])
        query_blocks = item_query.reshape(block_shape)
        grad_blocks = item_grad.reshape(block_shape)

        def one_block(carry, operands_block):
            block_query, block_log, block_grad = operands_block
            scores = jnp.einsum(
                "qhe,khe->hqk", block_query, item_key, preferred_element_type=jnp.float32
            )
            scores = scores * score_scale + item_bias[None, None, :]
            probs_full = jnp.exp(scores - block_log[..., None])
            grad_probs = jnp.einsum(
                "qhe,khe->hqk", block_grad, item_value, preferred_element_type=jnp.float32
            )
            delta_row = jnp.sum(probs_full * grad_probs, axis=-1, keepdims=True)
            grad_scores = (probs_full * (grad_probs - delta_row)).astype(jnp.bfloat16)
            grad_query = (
                jnp.einsum(
                    "hqk,khe->qhe", grad_scores, item_key, preferred_element_type=jnp.float32
                )
                * score_scale
            )
            grad_key = (
                carry[0]
                + jnp.einsum(
                    "hqk,qhe->khe", grad_scores, block_query, preferred_element_type=jnp.float32
                )
                * score_scale
            )
            grad_value = carry[1] + jnp.einsum(
                "hqk,qhe->khe",
                probs_full.astype(jnp.bfloat16),
                block_grad,
                preferred_element_type=jnp.float32,
            )
            return ((grad_key, grad_value), grad_query)

        start_carry = (
            jnp.zeros(item_key.shape, jnp.float32),
            jnp.zeros(item_value.shape, jnp.float32),
        )
        (grad_key, grad_value), grad_query = lax.scan(
            one_block, start_carry, (query_blocks, item_log, grad_blocks)
        )
        return (grad_query.reshape(item_query.shape), grad_key, grad_value)

    return lax.map(one_item, (queries, key_rows, value_rows, bias_rows, log_totals, grad_out))


def per_device_general(
    latents,
    prompt_tokens,
    prompt_lengths,
    timesteps,
    time_weight,
    self_gain,
    self_bias,
    qkv_weight,
    self_out_weight,
    cross_gain,
    cross_bias,
    cross_query_weight,
    context_weight,
    cross_out_weight,
    feed_gain,
    feed_bias,
    gate_up_weight,
    down_weight,
    down_bias,
    cotangent,
):
    gathered = (
        lax.all_gather(time_weight, "dp", axis=0, tiled=True),
        lax.all_gather(qkv_weight, "dp", axis=0, tiled=True),
        lax.all_gather(self_out_weight, "dp", axis=1, tiled=True),
        lax.all_gather(cross_query_weight, "dp", axis=0, tiled=True),
        lax.all_gather(context_weight, "dp", axis=0, tiled=True),
        lax.all_gather(cross_out_weight, "dp", axis=1, tiled=True),
        lax.all_gather(gate_up_weight, "dp", axis=0, tiled=True),
        lax.all_gather(down_weight, "dp", axis=1, tiled=True),
    )
    (
        time_full,
        qkv_full,
        self_out_full,
        cross_query_full,
        context_full,
        cross_out_full,
        gate_up_full,
        down_full,
    ) = gathered
    items_here = latents.shape[0]
    seq_len = latents.shape[1] + 1
    shard_rows = seq_len // lax.axis_size("mp")
    first_row = lax.axis_index("mp") * shard_rows
    head_size = HD
    block_size = min(512, seq_len)
    features = time_features(timesteps, time_full.shape[0]).astype(jnp.bfloat16)
    token_row = jnp.dot(features, time_full, preferred_element_type=jnp.float32)
    residual_in = jnp.concatenate([token_row[:, None, :], latents.astype(jnp.float32)], axis=1)
    normed_one, scaled_one, inverse_one = layer_norm(residual_in, self_gain, self_bias)
    normed_one = normed_one.astype(jnp.bfloat16)
    projected = jnp.einsum(
        "bsd,dkc->bskc", normed_one, qkv_full, preferred_element_type=jnp.float32
    )
    heads_here = projected.shape[-1] // head_size
    head_shape = (items_here, seq_len, heads_here, head_size)
    cosine, sine = rope_tables(seq_len, head_size)
    queries = rotate(projected[:, :, 0].reshape(head_shape), cosine, sine).astype(jnp.bfloat16)
    key_rows = rotate(projected[:, :, 1].reshape(head_shape), cosine, sine).astype(jnp.bfloat16)
    value_rows = projected[:, :, 2].reshape(head_shape).astype(jnp.bfloat16)
    open_rows = jnp.zeros((items_here, seq_len), jnp.float32)
    attended, self_logs = attend_forward(queries, key_rows, value_rows, open_rows, block_size)
    attended = attended.reshape(items_here, seq_len, heads_here * head_size).astype(jnp.bfloat16)
    segment = attended
    self_branch = jnp.swapaxes(
        lax.psum_scatter(
            jnp.swapaxes(jnp.dot(segment, self_out_full, preferred_element_type=jnp.float32), 0, 1),
            "mp",
            scatter_dimension=0,
            tiled=True,
        ),
        0,
        1,
    )
    residual_one = lax.dynamic_slice_in_dim(residual_in, first_row, shard_rows, 1) + self_branch
    normed_two, scaled_two, inverse_two = layer_norm(residual_one, cross_gain, cross_bias)
    normed_two_all = lax.all_gather(normed_two.astype(jnp.bfloat16), "mp", axis=1, tiled=True)
    cross_q = (
        jnp.dot(normed_two_all, cross_query_full, preferred_element_type=jnp.float32)
        .astype(jnp.bfloat16)
        .reshape(head_shape)
    )
    context = jnp.einsum(
        "bpc,ckh->bpkh", prompt_tokens, context_full, preferred_element_type=jnp.float32
    ).astype(jnp.bfloat16)
    prompt_slots = prompt_tokens.shape[1]
    context_shape = (items_here, prompt_slots, heads_here, head_size)
    context_keys = context[:, :, 0].reshape(context_shape)
    context_values = context[:, :, 1].reshape(context_shape)
    slot_index = jnp.arange(prompt_slots, dtype=jnp.int32)
    mask_rows = jnp.where(slot_index[None, :] < prompt_lengths[:, None], 0.0, NEG).astype(
        jnp.float32
    )
    crossed, cross_logs = attend_forward(
        cross_q, context_keys, context_values, mask_rows, block_size
    )
    crossed = crossed.reshape(items_here, seq_len, heads_here * head_size).astype(jnp.bfloat16)
    segment = crossed
    cross_branch = jnp.swapaxes(
        lax.psum_scatter(
            jnp.swapaxes(
                jnp.dot(segment, cross_out_full, preferred_element_type=jnp.float32), 0, 1
            ).astype(jnp.bfloat16),
            "mp",
            scatter_dimension=0,
            tiled=True,
        ).astype(jnp.float32),
        0,
        1,
    )
    residual_two = residual_one + cross_branch
    normed_three, scaled_three, inverse_three = layer_norm(residual_two, feed_gain, feed_bias)
    normed_three_all = lax.all_gather(normed_three.astype(jnp.bfloat16), "mp", axis=1, tiled=True)
    gate_up = jnp.einsum(
        "bsd,dkf->bskf", normed_three_all, gate_up_full, preferred_element_type=jnp.float32
    )
    gate_part = gate_up[:, :, 0]
    up_part = gate_up[:, :, 1]
    hidden = (jax.nn.silu(gate_part) * up_part).astype(jnp.bfloat16)
    segment = hidden
    feed_branch = jnp.swapaxes(
        lax.psum_scatter(
            jnp.swapaxes(
                jnp.dot(segment, down_full, preferred_element_type=jnp.float32), 0, 1
            ).astype(jnp.bfloat16),
            "mp",
            scatter_dimension=0,
            tiled=True,
        ).astype(jnp.float32),
        0,
        1,
    )
    output = (residual_two + feed_branch + down_bias).astype(jnp.bfloat16)
    regathered = (
        lax.all_gather(qkv_weight, "dp", axis=0, tiled=True),
        lax.all_gather(self_out_weight, "dp", axis=1, tiled=True),
        lax.all_gather(cross_query_weight, "dp", axis=0, tiled=True),
        lax.all_gather(context_weight, "dp", axis=0, tiled=True),
        lax.all_gather(cross_out_weight, "dp", axis=1, tiled=True),
        lax.all_gather(gate_up_weight, "dp", axis=0, tiled=True),
        lax.all_gather(down_weight, "dp", axis=1, tiled=True),
    )
    (
        qkv_back,
        self_out_back,
        cross_query_back,
        context_back,
        cross_out_back,
        gate_up_back,
        down_back,
    ) = regathered
    grad_rows = lax.all_gather(cotangent, "mp", axis=1, tiled=True)
    grad_hidden = jnp.einsum(
        "bsd,fd->bsf", grad_rows, down_back, preferred_element_type=jnp.float32
    )
    sigmoid_gate = jax.nn.sigmoid(gate_part)
    grad_up = grad_hidden * gate_part * sigmoid_gate
    grad_gate = grad_hidden * up_part * sigmoid_gate * (1.0 + gate_part * (1.0 - sigmoid_gate))
    grad_gate_up = jnp.stack([grad_gate, grad_up], axis=2).astype(jnp.bfloat16)
    down_weight_grad = jnp.einsum(
        "bsf,bsd->fd", hidden, grad_rows, preferred_element_type=jnp.float32
    )
    gate_up_grad = jnp.einsum(
        "bsd,bskf->dkf", normed_three_all, grad_gate_up, preferred_element_type=jnp.float32
    )
    segment = grad_gate_up
    grad_normed_three = jnp.swapaxes(
        lax.psum_scatter(
            jnp.swapaxes(
                jnp.einsum(
                    "bskf,dkf->bsd", segment, gate_up_back, preferred_element_type=jnp.float32
                ),
                0,
                1,
            ).astype(jnp.bfloat16),
            "mp",
            scatter_dimension=0,
            tiled=True,
        ).astype(jnp.float32),
        0,
        1,
    )
    grad_two_norm, feed_gain_part, feed_bias_part = norm_back(
        grad_normed_three, scaled_three, inverse_three, feed_gain
    )
    grad_out_shard = cotangent.astype(jnp.float32)
    down_bias_part = jnp.sum(grad_out_shard, axis=(0, 1))
    grad_residual_two = (grad_out_shard + grad_two_norm).astype(jnp.bfloat16)
    grad_rows_two = lax.all_gather(grad_residual_two, "mp", axis=1, tiled=True)
    grad_crossed = jnp.einsum(
        "bsd,hd->bsh", grad_rows_two, cross_out_back, preferred_element_type=jnp.float32
    ).astype(jnp.bfloat16)
    cross_out_grad = jnp.einsum(
        "bsh,bsd->hd", crossed, grad_rows_two, preferred_element_type=jnp.float32
    )
    grad_cross_q, grad_cross_k, grad_cross_v = attend_backward(
        cross_q,
        context_keys,
        context_values,
        mask_rows,
        cross_logs,
        grad_crossed.reshape(head_shape),
        block_size,
    )
    grad_cross_q = grad_cross_q.reshape(items_here, seq_len, heads_here * head_size).astype(
        jnp.bfloat16
    )
    grad_context = (
        jnp.stack([grad_cross_k, grad_cross_v], axis=2)
        .reshape(items_here, prompt_slots, 2, heads_here * head_size)
        .astype(jnp.bfloat16)
    )
    cross_query_grad = jnp.einsum(
        "bsd,bsh->dh", normed_two_all, grad_cross_q, preferred_element_type=jnp.float32
    )
    context_weight_grad = jnp.einsum(
        "bpc,bpkh->ckh", prompt_tokens, grad_context, preferred_element_type=jnp.float32
    )
    segment = grad_cross_q
    grad_normed_two = jnp.swapaxes(
        lax.psum_scatter(
            jnp.swapaxes(
                jnp.einsum(
                    "bsh,dh->bsd", segment, cross_query_back, preferred_element_type=jnp.float32
                ),
                0,
                1,
            ).astype(jnp.bfloat16),
            "mp",
            scatter_dimension=0,
            tiled=True,
        ).astype(jnp.float32),
        0,
        1,
    )
    grad_one_norm, cross_gain_part, cross_bias_part = norm_back(
        grad_normed_two, scaled_two, inverse_two, cross_gain
    )
    grad_residual_one = (grad_residual_two.astype(jnp.float32) + grad_one_norm).astype(jnp.bfloat16)
    grad_rows_one = lax.all_gather(grad_residual_one, "mp", axis=1, tiled=True)
    grad_attended = jnp.einsum(
        "bsd,hd->bsh", grad_rows_one, self_out_back, preferred_element_type=jnp.float32
    ).astype(jnp.bfloat16)
    self_out_grad = jnp.einsum(
        "bsh,bsd->hd", attended, grad_rows_one, preferred_element_type=jnp.float32
    )
    grad_query, grad_key, grad_value = attend_backward(
        queries,
        key_rows,
        value_rows,
        open_rows,
        self_logs,
        grad_attended.reshape(head_shape),
        block_size,
    )
    grad_query = unrotate(grad_query, cosine, sine)
    grad_key = unrotate(grad_key, cosine, sine)
    grad_projected = (
        jnp.stack([grad_query, grad_key, grad_value], axis=2)
        .reshape(items_here, seq_len, 3, heads_here * head_size)
        .astype(jnp.bfloat16)
    )
    qkv_weight_grad = jnp.einsum(
        "bsd,bskc->dkc", normed_one, grad_projected, preferred_element_type=jnp.float32
    )
    grad_normed_part = jnp.einsum(
        "bskc,dkc->bsd", grad_projected, qkv_back, preferred_element_type=jnp.float32
    )
    summed = (
        lax.psum(grad_normed_part.astype(jnp.bfloat16), "mp").astype(jnp.float32),
        lax.psum(cross_gain_part.astype(jnp.bfloat16), "mp").astype(jnp.float32),
        lax.psum(cross_bias_part.astype(jnp.bfloat16), "mp").astype(jnp.float32),
        lax.psum(feed_gain_part.astype(jnp.bfloat16), "mp").astype(jnp.float32),
        lax.psum(feed_bias_part.astype(jnp.bfloat16), "mp").astype(jnp.float32),
        lax.psum(down_bias_part.astype(jnp.bfloat16), "mp").astype(jnp.float32),
    )
    grad_in_norm, self_gain_part, self_bias_part = norm_back(
        summed[0], scaled_one, inverse_one, self_gain
    )
    grad_residual_in = grad_rows_one.astype(jnp.float32) + grad_in_norm
    latents_grad = grad_residual_in[:, 1:].astype(jnp.bfloat16)
    time_weight_grad = jnp.dot(
        features.astype(jnp.float32).T, grad_residual_in[:, 0], precision=lax.Precision.HIGHEST
    )
    cross_gain_sum, cross_bias_sum, feed_gain_sum, feed_bias_sum, down_bias_sum = (
        summed[1],
        summed[2],
        summed[3],
        summed[4],
        summed[5],
    )
    reduced = (
        lax.psum_scatter(
            time_weight_grad.astype(jnp.bfloat16), "dp", scatter_dimension=0, tiled=True
        ).astype(jnp.float32),
        lax.psum_scatter(
            qkv_weight_grad.astype(jnp.bfloat16), "dp", scatter_dimension=0, tiled=True
        ).astype(jnp.float32),
        lax.psum_scatter(
            self_out_grad.astype(jnp.bfloat16), "dp", scatter_dimension=1, tiled=True
        ).astype(jnp.float32),
        lax.psum_scatter(
            cross_query_grad.astype(jnp.bfloat16), "dp", scatter_dimension=0, tiled=True
        ).astype(jnp.float32),
        lax.psum_scatter(
            context_weight_grad.astype(jnp.bfloat16), "dp", scatter_dimension=0, tiled=True
        ).astype(jnp.float32),
        lax.psum_scatter(
            cross_out_grad.astype(jnp.bfloat16), "dp", scatter_dimension=1, tiled=True
        ).astype(jnp.float32),
        lax.psum_scatter(
            gate_up_grad.astype(jnp.bfloat16), "dp", scatter_dimension=0, tiled=True
        ).astype(jnp.float32),
        lax.psum_scatter(
            down_weight_grad.astype(jnp.bfloat16), "dp", scatter_dimension=1, tiled=True
        ).astype(jnp.float32),
        lax.psum_scatter(
            self_gain_part.astype(jnp.bfloat16), "dp", scatter_dimension=0, tiled=True
        ).astype(jnp.float32),
        lax.psum_scatter(
            self_bias_part.astype(jnp.bfloat16), "dp", scatter_dimension=0, tiled=True
        ).astype(jnp.float32),
        lax.psum_scatter(
            cross_gain_sum.astype(jnp.bfloat16), "dp", scatter_dimension=0, tiled=True
        ).astype(jnp.float32),
        lax.psum_scatter(
            cross_bias_sum.astype(jnp.bfloat16), "dp", scatter_dimension=0, tiled=True
        ).astype(jnp.float32),
        lax.psum_scatter(
            feed_gain_sum.astype(jnp.bfloat16), "dp", scatter_dimension=0, tiled=True
        ).astype(jnp.float32),
        lax.psum_scatter(
            feed_bias_sum.astype(jnp.bfloat16), "dp", scatter_dimension=0, tiled=True
        ).astype(jnp.float32),
        lax.psum_scatter(
            down_bias_sum.astype(jnp.bfloat16), "dp", scatter_dimension=0, tiled=True
        ).astype(jnp.float32),
    )
    return (
        output,
        latents_grad,
        reduced[0],
        reduced[8],
        reduced[9],
        reduced[1],
        reduced[2],
        reduced[10],
        reduced[11],
        reduced[3],
        reduced[4],
        reduced[5],
        reduced[12],
        reduced[13],
        reduced[6],
        reduced[7],
        reduced[14],
    )


AXES = ("dp", "mp")
BF = jnp.bfloat16
F32 = jnp.float32


def flat_permutation(places):
    pairs = []
    for d in range(8):
        for z in range(4):
            target = places(d >> 1, d & 1, z & 1, z >> 1)
            if target is not None:
                s, c, zz, p = target
                pairs.append(((2 * s + c) * 4 + 2 * p + zz, (2 * (d >> 1) + (d & 1)) * 4 + z))
    return [(source, target) for target, source in pairs]


SWAP_CORE = flat_permutation(lambda s, c, zz, p: (s, 1 - c, zz, p))
SWAP_Z = flat_permutation(lambda s, c, zz, p: (s, c, 1 - zz, p))
SWAP_PAIR = flat_permutation(lambda s, c, zz, p: (s, c, zz, 1 - p))
SWAP_X = flat_permutation(lambda s, c, zz, p: (s ^ 1, c, zz, p))
SWAP_Y = flat_permutation(lambda s, c, zz, p: (s ^ 2, c, zz, p))
ROUTE_A = flat_permutation(lambda s, c, zz, p: (s, p, zz, c))
ROUTE_B = flat_permutation(lambda s, c, zz, p: (s, p, zz, 1 - c))
RETURN_B = flat_permutation(lambda s, c, zz, p: (s, 1 - p, zz, c))
OWNER_TO_PARTNER = flat_permutation(lambda s, c, zz, p: (s, 1 - c, zz, p) if c == p else None)
PARTNER_TO_OWNER = flat_permutation(lambda s, c, zz, p: (s, 1 - c, zz, p) if c != p else None)
OWNER_TO_PAIR = flat_permutation(lambda s, c, zz, p: (s, c, zz, 1 - p) if c == p else None)
OWNER_Z = flat_permutation(lambda s, c, zz, p: (s, c, 1 - zz, p) if c == p else None)
PARTNER_Z = flat_permutation(lambda s, c, zz, p: (s, c, 1 - zz, p) if c != p else None)


def move(values, pairs):
    return lax.ppermute(values, AXES, pairs)


def xor_blocks(values, axis, count, index):
    blocks = jnp.split(values, count, axis=axis)
    bit = 1
    while bit < count:
        flip = (index & bit) != 0
        blocks = [jnp.where(flip, blocks[j ^ bit], blocks[j]) for j in range(count)]
        bit *= 2
    return jnp.concatenate(blocks, axis=axis)


def attend_pair(head_size, query_block, queries, keys, values, bias, o_ref, log_ref):
    scale = head_size ** (-0.5)
    length, width = queries.shape
    key_rows = keys[...]
    values_turned = values[...].astype(F32).T.astype(BF)
    lane = lax.broadcasted_iota(jnp.int32, (query_block, width), 1)

    @pl.loop(0, length // query_block)
    def _(step):
        rows = pl.ds(pl.multiple_of(step * query_block, query_block), query_block)
        block = queries[rows, :]
        parts, logs = [], []
        for head in range(2):
            mine = (lane >= head * head_size) & (lane < (head + 1) * head_size)
            masked = jnp.where(mine, block, jnp.zeros_like(block))
            scores = lax.dot_general(
                key_rows, masked, (((1,), (1,)), ((), ())), preferred_element_type=F32
            )
            scores = scores * scale
            if bias is not None:
                scores = scores + bias[...]
            top = jnp.max(scores, axis=0, keepdims=True)
            expos = jnp.exp(scores - top)
            total = jnp.sum(expos, axis=0, keepdims=True)
            mixed = lax.dot_general(
                values_turned[head * head_size : (head + 1) * head_size, :],
                expos.astype(BF),
                (((1,), (0,)), ((), ())),
                preferred_element_type=F32,
            )
            parts.append(mixed * (1.0 / total))
            logs.append(top + jnp.log(total))
        o_ref[rows, :] = jnp.concatenate(parts, axis=0).T.astype(BF)
        log_ref[0, :, rows] = jnp.concatenate(logs, axis=0)


def cross_attention_kernel(q_ref, k_ref, v_ref, bias_ref, o_ref, log_ref):
    attend_pair(HD, 512, q_ref, k_ref, v_ref, bias_ref, o_ref, log_ref)


def attention_backward_kernel(head_size, query_block, turned, load, *refs):
    if turned:
        refs = list(refs)
        q_ref, k_ref, v_ref, d_ref, log_ref, base_ref, steps_ref = refs[:7]
        more = (len(load.operands), len(load.outs_like))
        refs = refs[7:]
        load_ins, g_ref, refs = refs[: more[0]], refs[more[0]], refs[more[0] + 1 :]
        load_outs, refs = refs[: more[1]], refs[more[1] :]
        dk_acc, dv_acc = refs[:2]
        place = Place()
        carried = load.begin(place, load_ins, load_outs, refs[2:])

        @pl.when(pl.program_id(0) == 0)
        def _():
            greet(load.peers(place, [place.core_peer]))
            for each in carried:
                each.start()
    else:
        q_ref, k_ref, v_ref, d_ref, log_ref, bias_ref, dq_ref, g_ref, dk_acc, dv_acc = refs
    scale = head_size ** (-0.5)
    length, width = q_ref.shape
    key_count = k_ref.shape[0]
    here = pl.program_id(0)
    key_rows = k_ref[...]
    value_rows = v_ref[...]
    keys_turned = key_rows.astype(F32).T.astype(BF)
    lane = lax.broadcasted_iota(jnp.int32, (query_block, width), 1)
    dk_acc[...] = jnp.zeros_like(dk_acc)
    dv_acc[...] = jnp.zeros_like(dv_acc)

    def back_turn(values, step):
        blocks = length // query_block
        index = lax.rem(step + place.core * (blocks // 2), blocks)
        return turned_block(values, base_ref, steps_ref, index, -1)

    @pl.loop(0, length // query_block)
    def _(step):
        rows = pl.ds(pl.multiple_of(step * query_block, query_block), query_block)
        block = q_ref[rows, :]
        grads = d_ref[rows, :]
        parts = []
        for head in range(2):
            mine = (lane >= head * head_size) & (lane < (head + 1) * head_size)
            q_mine = jnp.where(mine, block, jnp.zeros_like(block))
            d_mine = jnp.where(mine, grads, jnp.zeros_like(grads))
            scores = lax.dot_general(
                key_rows, q_mine, (((1,), (1,)), ((), ())), preferred_element_type=F32
            )
            scores = scores * scale
            if not turned:
                scores = scores + bias_ref[...]
            probs = jnp.exp(scores - log_ref[0, head : head + 1, rows])
            grad_probs = lax.dot_general(
                value_rows, d_mine, (((1,), (1,)), ((), ())), preferred_element_type=F32
            )
            delta = jnp.sum(probs * grad_probs, axis=0, keepdims=True)
            grad_scores = (probs * (grad_probs - delta)).astype(BF)
            dv_acc[...] += jnp.dot(probs.astype(BF), d_mine, preferred_element_type=F32)
            dk_acc[...] += jnp.dot(grad_scores, q_mine, preferred_element_type=F32)
            parts.append(
                jnp.dot(
                    keys_turned[head * head_size : (head + 1) * head_size, :],
                    grad_scores,
                    preferred_element_type=F32,
                )
            )
        grad_query = jnp.concatenate(parts, axis=0).T * scale
        if turned:
            columns = pl.ds(pl.multiple_of(here * width, width), width)
            g_ref[rows, columns] = back_turn(grad_query, step).astype(BF)
        else:
            dq_ref[rows, :] = grad_query.astype(BF)

    total_width = g_ref.shape[1] // (3 if turned else 2)
    first = total_width if turned else 0
    key_columns = pl.ds(pl.multiple_of(first + here * width, width), width)
    value_columns = pl.ds(pl.multiple_of(first + total_width + here * width, width), width)
    if turned:

        @pl.loop(0, key_count // query_block)
        def _(step):
            rows = pl.ds(pl.multiple_of(step * query_block, query_block), query_block)
            g_ref[rows, key_columns] = back_turn(dk_acc[rows, :] * scale, step).astype(BF)
            g_ref[rows, value_columns] = dv_acc[rows, :].astype(BF)

        @pl.when(here == pl.num_programs(0) - 1)
        def _():
            for each in carried:
                each.finish()
    else:
        g_ref[:, key_columns] = (dk_acc[...] * scale).astype(BF)
        g_ref[:, value_columns] = dv_acc[...].astype(BF)


def self_attention_back(place, queries, keys, values, grads, logs, load):
    length, total = queries.shape
    pairs = total // 128
    block = pl.BlockSpec((length, 128), lambda i: (0, i))
    whole = pl.BlockSpec(memory_space=pltpu.VMEM)
    tables = turn_tables(length, 256)
    return pl.pallas_call(
        functools.partial(attention_backward_kernel, HD, 256, True, load),
        grid=(pairs,),
        in_specs=[block] * 4
        + [pl.BlockSpec((1, 2, length), lambda i: (i, 0, 0))]
        + [whole] * 2
        + [ANYWHERE] * len(load.operands),
        out_specs=[pl.BlockSpec((length, 3 * total), lambda i: (0, 0))]
        + [ANYWHERE] * len(load.outs_like),
        out_shape=[jax.ShapeDtypeStruct((length, 3 * total), BF)] + load.outs_like,
        scratch_shapes=[pltpu.VMEM((length, 128), F32)] * 2 + load.scratch,
        compiler_params=pltpu.CompilerParams(collective_id=place, has_side_effects=True),
        cost_estimate=pl.CostEstimate(
            flops=10 * length * length * total,
            transcendentals=length * length * total // 64,
            bytes_accessed=100_000_000,
        ),
        name="self_attention_back",
    )(queries, keys, values, grads, logs, *tables, *load.operands)


def cross_attention(queries, context, bias):
    length, total = queries.shape
    slots = context.shape[0]
    pairs = total // 128
    block = pl.BlockSpec((length, 128), lambda i: (0, i))
    key_block = lambda shift: pl.BlockSpec((slots, 128), lambda i: (0, i + shift))
    return pl.pallas_call(
        cross_attention_kernel,
        grid=(pairs,),
        in_specs=[block, key_block(0), key_block(pairs), pl.BlockSpec((slots, 1), lambda i: (0, 0))],
        out_specs=[block, pl.BlockSpec((1, 2, length), lambda i: (i, 0, 0))],
        out_shape=[
            jax.ShapeDtypeStruct((length, total), BF),
            jax.ShapeDtypeStruct((pairs, 2, length), F32),
        ],
        cost_estimate=pl.CostEstimate(
            flops=4 * length * slots * total,
            transcendentals=length * slots * total // 64,
            bytes_accessed=length * total * 4,
        ),
        name="cross_attention",
    )(queries, context, context, bias)


def cross_attention_back(queries, context, bias, grads, logs):
    length, total = queries.shape
    slots = context.shape[0]
    pairs = total // 128
    block = pl.BlockSpec((length, 128), lambda i: (0, i))
    key_block = lambda shift: pl.BlockSpec((slots, 128), lambda i: (0, i + shift))
    return pl.pallas_call(
        functools.partial(attention_backward_kernel, HD, 512, False, None),
        grid=(pairs,),
        in_specs=[
            block,
            key_block(0),
            key_block(pairs),
            block,
            pl.BlockSpec((1, 2, length), lambda i: (i, 0, 0)),
            pl.BlockSpec((slots, 1), lambda i: (0, 0)),
        ],
        out_specs=[block, pl.BlockSpec((slots, 2 * total), lambda i: (0, 0))],
        out_shape=[
            jax.ShapeDtypeStruct((length, total), BF),
            jax.ShapeDtypeStruct((slots, 2 * total), BF),
        ],
        scratch_shapes=[pltpu.VMEM((slots, 128), F32)] * 2,
        cost_estimate=pl.CostEstimate(
            flops=10 * length * slots * total,
            transcendentals=length * slots * total // 64,
            bytes_accessed=length * total * 8,
        ),
        name="cross_attention_back",
    )(queries, context, context, grads, logs, bias)


def dot_nn(left, right):
    return lax.dot_general(left, right, (((1,), (0,)), ((), ())), preferred_element_type=F32)


def dot_nt(left, right):
    return lax.dot_general(left, right, (((1,), (1,)), ((), ())), preferred_element_type=F32)


def dot_tn(left, right):
    return lax.dot_general(left, right, (((0,), (0,)), ((), ())), preferred_element_type=F32)


PLANE = [[0, 2, 4, 6], [1, 3, 5, 7]]


def group_sum(partial):
    rows = partial.shape[0] // 2
    half = partial[:rows].astype(F32) + move(partial[rows:], SWAP_CORE).astype(F32)
    half = half.astype(BF)
    return half.astype(F32) + move(half, SWAP_Z).astype(F32)


def both_halves(half):
    return jnp.concatenate([half, move(half, SWAP_CORE)], axis=0)


def weight_order(one, two, pair):
    first = jnp.where(pair == 0, one, two)
    second = jnp.where(pair == 0, two, one)
    return jnp.concatenate([first, second], axis=0)


def plane_gather(mine):
    return lax.all_gather(mine, "dp", axis=0, tiled=True, axis_index_groups=PLANE)


def plane_sum(grad):
    return lax.psum_scatter(
        grad, "dp", scatter_dimension=0, tiled=True, axis_index_groups=PLANE
    )


def to_owners(total, pair):
    rows = total.shape[0] // 2
    first, second = total[:rows], total[rows:]
    one = move(jnp.where(pair == 0, first, second), ROUTE_A)
    two = move(jnp.where(pair == 0, second, first), RETURN_B)
    return one.astype(F32) + two.astype(F32)


def after(values, *others):
    return lax.optimization_barrier((values, *others))[0]


class Place:
    def __init__(self):
        d = lax.axis_index("dp")
        z = lax.axis_index("mp")
        self.d, self.z = d, z
        self.core = lax.rem(d, 2)
        self.column = d // 2
        self.pair = z // 2
        self.owner = self.core == self.pair
        self.core_peer = (d + 1 - 2 * self.core, z)
        self.near_z = (d, z + 1 - 2 * lax.rem(z, 2))
        self.far_z = z + 2 - 4 * self.pair
        self.far_same = (d, self.far_z)
        self.far_other = (self.core_peer[0], self.far_z)
        self.user = (2 * self.column + self.pair, self.far_z)
        self.x_peer = (d + 2 - 4 * lax.rem(self.column, 2), z)
        self.y_peer = (d + 4 - 8 * (self.column // 2), z)
        self.x_column = self.column + 1 - 2 * lax.rem(self.column, 2)
        self.y_column = self.column + 2 - 4 * (self.column // 2)


def greet(peers):
    barrier = pltpu.get_barrier_semaphore()
    for peer in peers:
        pl.semaphore_signal(
            barrier, inc=1, device_id=peer, device_id_type=pl.DeviceIdType.MESH
        )
    pl.semaphore_wait(barrier, len(peers))


def send(source, target, sent, got, peer):
    return pltpu.make_async_remote_copy(
        src_ref=source,
        dst_ref=target,
        send_sem=sent,
        recv_sem=got,
        device_id=peer,
        device_id_type=pl.DeviceIdType.MESH,
    )


class Spread:
    scratch = [pltpu.SemaphoreType.DMA((2,)), pltpu.SemaphoreType.DMA((3,)), pltpu.SemaphoreType.DMA]
    late = True

    @staticmethod
    def outs(part):
        return [jax.ShapeDtypeStruct((2 * part.shape[0], part.shape[1]), BF)]

    @staticmethod
    def peers(place):
        return [place.far_same, place.far_other]

    def __init__(self, place, ins, outs, sems):
        self.place = place
        (self.part,), (self.own,), (self.sent, self.got, self.here) = ins, outs, sems

    def target(self, sender):
        rows = self.part.shape[0]
        return self.own.at[pl.ds(pl.multiple_of(sender * rows, rows), rows)]

    def far(self, sender):
        return send(
            self.part, self.target(sender), self.sent.at[0], self.got.at[sender], self.place.user
        )

    def near(self, sender):
        return send(
            self.part, self.target(sender), self.sent.at[1], self.got.at[2], self.place.core_peer
        )

    def local(self):
        return pltpu.make_async_copy(self.part, self.target(self.place.core), self.here)

    def start(self):
        place = self.place
        self.far(place.core).start()

        @pl.when(place.owner)
        def _():
            self.local().start()

        @pl.when(jnp.logical_not(place.owner))
        def _():
            self.near(place.core).start()

    def middle(self):
        pass

    def finish(self):
        place = self.place

        @pl.when(place.owner)
        def _():
            self.local().wait()
            self.near(1 - place.core).wait_recv()

        @pl.when(jnp.logical_not(place.owner))
        def _():
            self.near(place.core).wait_send()
            self.far(0).wait_recv()
            self.far(1).wait_recv()

        self.far(place.core).wait_send()


class Plane:
    scratch = [
        pltpu.SemaphoreType.DMA((2, 3)),
        pltpu.SemaphoreType.DMA((2, 3)),
        pltpu.SemaphoreType.DMA,
    ]
    late = False

    @staticmethod
    def outs(own):
        return [jax.ShapeDtypeStruct((4 * own.shape[0], own.shape[1]), BF)]

    @staticmethod
    def peers(place):
        return [place.x_peer, place.y_peer]

    def __init__(self, place, ins, outs, sems):
        self.place = place
        (self.own,), (self.full,), (self.sent, self.got, self.here) = ins, outs, sems
        self.rows = self.own.shape[0] // 2

    def target(self, column, part):
        rows = self.rows
        return self.full.at[pl.ds(pl.multiple_of((2 * column + part) * rows, rows), rows)]

    def one(self, way, part):
        place = self.place
        peer = place.x_peer if way == 0 else place.y_peer
        return send(
            self.own.at[pl.ds(part * self.rows, self.rows)],
            self.target(place.column, part),
            self.sent.at[way, part],
            self.got.at[way, part],
            peer,
        )

    def two(self, way):
        place = self.place
        if way == 0:
            spot = self.target(place.y_column, 1)
            return send(spot, spot, self.sent.at[0, 2], self.got.at[0, 2], place.x_peer)
        spot = self.target(place.x_column, 0)
        return send(spot, spot, self.sent.at[1, 2], self.got.at[1, 2], place.y_peer)

    def local(self):
        rows = self.own.shape[0]
        place = self.full.at[pl.ds(pl.multiple_of(self.place.column * rows, rows), rows)]
        return pltpu.make_async_copy(self.own, place, self.here)

    def start(self):
        for way in range(2):
            self.one(way, way).start()
        for way in range(2):
            self.one(way, 1 - way).start()
        self.local().start()

    def middle(self):
        self.one(0, 0).wait_recv()
        self.two(1).start()
        self.one(1, 1).wait_recv()
        self.two(0).start()

    def finish(self):
        self.local().wait()
        for way in range(2):
            self.one(way, 1 - way).wait_recv()
            self.two(way).wait_recv()
            self.two(way).wait_send()
            for part in range(2):
                self.one(way, part).wait_send()


class Return:
    scratch = [pltpu.SemaphoreType.DMA((2,)), pltpu.SemaphoreType.DMA((2,))]
    late = True

    @staticmethod
    def outs(total):
        shape = jax.ShapeDtypeStruct((total.shape[0] // 2, total.shape[1]), BF)
        return [shape, shape]

    @staticmethod
    def peers(place):
        return [place.far_same, place.far_other]

    def __init__(self, place, ins, outs, sems):
        self.place = place
        (self.total,), (self.near, self.far), (self.sent, self.got) = ins, outs, sems

    def part(self, which):
        rows = self.near.shape[0]
        return self.total.at[pl.ds(pl.multiple_of(which * rows, rows), rows)]

    def to_near(self):
        place = self.place
        return send(
            self.part(1 - place.core), self.near, self.sent.at[0], self.got.at[0], place.core_peer
        )

    def to_far(self, same):
        place = self.place
        which = place.core if same else 1 - place.core
        peer = place.far_same if same else place.far_other
        return send(
            self.part(which), self.far, self.sent.at[0 if same else 1], self.got.at[1], peer
        )

    def start(self):
        place = self.place

        @pl.when(place.owner)
        def _():
            self.to_near().start()

        @pl.when(jnp.logical_not(place.owner))
        def _():
            self.to_far(True).start()
            self.to_far(False).start()

    def middle(self):
        pass

    def finish(self):
        place = self.place

        @pl.when(place.owner)
        def _():
            self.to_near().wait_send()
            self.to_far(True).wait_recv()

        @pl.when(jnp.logical_not(place.owner))
        def _():
            self.to_far(True).wait_send()
            self.to_far(False).wait_send()
            self.to_near().wait_recv()
            self.to_far(False).wait_recv()


class Swap:
    scratch = [pltpu.SemaphoreType.DMA, pltpu.SemaphoreType.DMA]
    late = True
    way = None

    @staticmethod
    def outs(values):
        return [jax.ShapeDtypeStruct(values.shape, values.dtype)]

    @classmethod
    def peers(cls, place):
        return {
            "core": [place.core_peer],
            "z": [place.near_z],
            "route": [place.far_same, place.far_other],
        }[cls.way]

    def __init__(self, place, ins, outs, sems):
        self.place = place
        peer = {"core": place.core_peer, "z": place.near_z, "route": place.far_other}[self.way]
        self.copy = send(ins[0], outs[0], sems[0], sems[1], peer)

    def each(self, act):
        if self.way != "route":
            act()
            return

        @pl.when(jnp.logical_not(self.place.owner))
        def _():
            act()

    def start(self):
        self.each(lambda: self.copy.start())

    def middle(self):
        pass

    def finish(self):
        self.each(lambda: self.copy.wait())


class SwapCore(Swap):
    way = "core"


class SwapCoreHalf(SwapCore):
    @staticmethod
    def outs(values):
        return [jax.ShapeDtypeStruct((values.shape[0] // 2,) + values.shape[1:], values.dtype)]

    def __init__(self, place, ins, outs, sems):
        rows = outs[0].shape[0]
        super().__init__(place, [ins[0].at[pl.ds(rows, rows)]], outs, sems)


class SwapNear(Swap):
    way = "z"


class SwapRoute(Swap):
    way = "route"


def scratch_of(kind, operand):
    return kind.scratch(operand) if callable(kind.scratch) else kind.scratch


class PlaneSum:
    late = False

    @staticmethod
    def scratch(grad):
        rows, width = grad.shape[0] // 4, grad.shape[1]
        return [
            pltpu.VMEM((rows, width), BF),
            pltpu.VMEM((2, rows, width), BF),
            pltpu.VMEM((2, rows, width), BF),
            pltpu.VMEM((rows, width), BF),
            pltpu.SemaphoreType.DMA((2, 2)),
            pltpu.SemaphoreType.DMA((2, 2)),
            pltpu.SemaphoreType.DMA((4,)),
        ]

    @staticmethod
    def outs(grad):
        return [jax.ShapeDtypeStruct((grad.shape[0] // 4, grad.shape[1]), BF)]

    @staticmethod
    def peers(place):
        return [place.x_peer, place.y_peer]

    def __init__(self, place, ins, outs, scratch):
        self.place = place
        (self.grad,), (self.out,) = ins, outs
        self.first, self.staged, self.second, self.own, self.sent, self.got, self.here = scratch
        self.rows = self.own.shape[0]
        self.ways = (place.x_peer, place.y_peer)
        self.columns = (place.x_column, place.y_column)
        self.diagonal = place.x_column + 2 - 4 * (place.x_column // 2)

    def block(self, column, start, count):
        first = pl.multiple_of(column * self.rows + start, count)
        return self.grad.at[pl.ds(first, count)]

    def one(self, way):
        count = self.rows // 2
        return send(
            self.block(self.diagonal, way * count, count),
            self.first.at[pl.ds(way * count, count)],
            self.sent.at[0, way],
            self.got.at[0, way],
            self.ways[way],
        )

    def two(self, way):
        return send(
            self.staged.at[way],
            self.second.at[way],
            self.sent.at[1, way],
            self.got.at[1, way],
            self.ways[way],
        )

    def load(self, way):
        source = self.block(self.columns[way], 0, self.rows)
        return pltpu.make_async_copy(source, self.staged.at[way], self.here.at[way])

    def load_own(self):
        source = self.block(self.place.column, 0, self.rows)
        return pltpu.make_async_copy(source, self.own, self.here.at[2])

    def store(self):
        return pltpu.make_async_copy(self.own, self.out, self.here.at[3])

    def start(self):
        for way in range(2):
            self.one(way).start()
        for way in range(2):
            self.load(way).start()
        self.load_own().start()

    def middle(self):
        count = self.rows // 2
        for way in range(2):
            self.one(way).wait_recv()
            self.load(1 - way).wait()

            @pl.loop(0, count // 16)
            def _(step):
                rows = pl.ds(pl.multiple_of(way * count + step * 16, 16), 16)
                self.staged[1 - way, rows, :] = (
                    self.staged[1 - way, rows, :].astype(F32) + self.first[rows, :].astype(F32)
                ).astype(BF)

            self.two(1 - way).start()

    def finish(self):
        self.load_own().wait()
        for way in range(2):
            self.two(way).wait_recv()

        @pl.loop(0, self.rows // 16)
        def _(step):
            rows = pl.ds(pl.multiple_of(step * 16, 16), 16)
            self.own[rows, :] = (
                self.own[rows, :].astype(F32)
                + self.second[0, rows, :].astype(F32)
                + self.second[1, rows, :].astype(F32)
            ).astype(BF)

        self.store().start()
        for way in range(2):
            self.one(way).wait_send()
            self.two(way).wait_send()
        self.store().wait()


class Loads:
    def __init__(self, *loads):
        self.loads = loads
        self.operands = [operand for _, operand in loads]
        self.outs_like = [out for kind, operand in loads for out in kind.outs(operand)]
        self.scratch = [item for kind, operand in loads for item in scratch_of(kind, operand)]

    def peers(self, place, base):
        found = {id(peer): peer for peer in base}
        for kind, _ in self.loads:
            for peer in kind.peers(place):
                found[id(peer)] = peer
        return list(found.values())

    def begin(self, place, ins, outs, sems):
        result, at, sem_at = [], 0, 0
        for (kind, operand), source in zip(self.loads, ins):
            count, sem_count = len(kind.outs(operand)), len(scratch_of(kind, operand))
            result.append(
                kind(
                    place,
                    [source],
                    outs[at : at + count],
                    sems[sem_at : sem_at + sem_count],
                )
            )
            at, sem_at = at + count, sem_at + sem_count
        return result


class Works:
    def __init__(self, *works):
        self.works = works
        self.unique = []
        for kind, left, right in works:
            for operand in (left,) if kind == "ta" else (left, right):
                if not any(operand is other for other in self.unique):
                    self.unique.append(operand)
        self.outs_like = []
        for kind, left, right in works:
            if kind == "nt":
                shape = (left.shape[0], right.shape[0])
            elif kind == "ta":
                shape = (left.shape[1], right[1])
            else:
                shape = (left.shape[1], right.shape[1])
            self.outs_like.append(jax.ShapeDtypeStruct(shape, BF))
        self.scratch = (
            [pltpu.VMEM(operand.shape, BF) for operand in self.unique]
            + [pltpu.VMEM(out.shape, BF) for out in self.outs_like]
            + [pltpu.SemaphoreType.DMA((max(1, len(self.unique) + len(works)),))]
        )

    def begin(self, ins, outs, scratch):
        self_ins = list(scratch[: len(self.unique)])
        self_outs = list(scratch[len(self.unique) : -1])
        sems = scratch[-1]
        loads = [
            pltpu.make_async_copy(source, target, sems.at[k])
            for k, (source, target) in enumerate(zip(ins, self_ins))
        ]
        stores = [
            pltpu.make_async_copy(source, target, sems.at[len(loads) + k])
            for k, (source, target) in enumerate(zip(self_outs, outs))
        ]
        return loads, stores, self_ins, self_outs

    def run(self, state, summed):
        loads, stores, ins, outs = state
        waited = set()

        def held(operand):
            at = [place for place, other in enumerate(self.unique) if other is operand][0]
            if at not in waited:
                loads[at].wait()
                waited.add(at)
            return ins[at]

        for k, (kind, left, right) in enumerate(self.works):
            left, out = held(left), outs[k]
            if kind == "ta":
                right = summed.at[:, pl.ds(right[0], right[1])]
            else:
                right = held(right)
            if kind == "nt":
                columns = out.shape[1] // 256

                @pl.loop(0, (out.shape[0] // 256) * columns)
                def _(step):
                    first = pl.ds(pl.multiple_of((step // columns) * 256, 256), 256)
                    second = pl.ds(pl.multiple_of(lax.rem(step, columns) * 256, 256), 256)
                    out[first, second] = lax.dot_general(
                        left[first, :],
                        right[second, :],
                        (((1,), (1,)), ((), ())),
                        preferred_element_type=F32,
                    ).astype(BF)
            else:

                @pl.loop(0, out.shape[0] // 256)
                def _(step):
                    spot = pl.ds(pl.multiple_of(step * 256, 256), 256)
                    out[spot, :] = lax.dot_general(
                        left[:, spot],
                        right[...],
                        (((0,), (0,)), ((), ())),
                        preferred_element_type=F32,
                    ).astype(BF)

            stores[k].start()


ANYWHERE = pl.BlockSpec(memory_space=pl.ANY)


def returned(total, near, far, core, owner):
    rows = near.shape[0]
    mine = jnp.where(core == 0, total[:rows], total[rows:])
    return jnp.where(owner, mine, near).astype(F32) + far.astype(F32)


def exchange_kernel(kind, chunks, window, load, works, *refs):
    refs = list(refs)
    place = Place()
    more = (len(load.operands), len(load.outs_like))
    todo = (len(works.unique), len(works.outs_like), len(works.scratch))
    w_count = len(refs) - 1 - 4 - more[0] - more[1] - todo[0] - todo[1] - todo[2]
    w_count -= 2 + 11 + 4 + (kind != "norm") + len(load.scratch) - 1
    w_from, refs = refs[1 : 1 + w_count], refs[:1] + refs[1 + w_count :]
    ins, refs = refs[:4], refs[4:]
    load_ins, refs = refs[: more[0]], refs[more[0] :]
    work_ins, refs = refs[: todo[0]], refs[todo[0] :]
    outs, refs = refs[:2], refs[2:]
    load_outs, refs = refs[: more[1]], refs[more[1] :]
    work_outs, refs = refs[: todo[1]], refs[todo[1] :]
    rest, refs = refs[:11], refs[11:]
    (a_ref, w_ref, res_ref, loads), refs = refs[:4], refs[4:]
    if kind == "norm":
        a_from, res_from, gain_ref, bias_ref = ins
        res_out, all_ref = outs
    else:
        a_from, res_from, up_from, gain_ref = ins
        all_ref, sum_ref = outs
        up_ref, refs = refs[0], refs[1:]
    carried = load.begin(place, load_ins, load_outs, refs)
    working = works.begin(work_ins, work_outs, refs[len(load.scratch) :])
    mine, given, near, half, far, send_near, got_near, send_far, got_far, send_all, got_all = rest
    rows = mine.shape[0]
    width = mine.shape[1]
    chunk = rows // chunks
    core_peer, far_peer = place.core_peer, place.near_z
    copy = send
    depth = a_ref.shape[1]
    block = 2 * chunk
    tile = 256
    tiles = width // tile

    def load_rows(k):
        first = (k // 2) * block + (0 if k % 2 else rows)
        spot = pl.ds(first, block)
        return pltpu.make_async_copy(a_from.at[spot], a_ref.at[spot], loads.at[2 * tiles + k])

    def load_weight(k):
        spot = pl.ds(k * tile, tile)
        share = depth // len(w_from)
        return [
            pltpu.make_async_copy(
                source.at[spot, pl.ds(window * depth, share)],
                w_ref.at[spot, pl.ds(at * share, share)],
                loads.at[at * tiles + k],
            )
            for at, source in enumerate(w_from)
        ]

    later = [pltpu.make_async_copy(res_from, res_ref, loads.at[2 * tiles + 2 * chunks])]
    if kind != "norm":
        later.append(
            pltpu.make_async_copy(
                up_from.at[pl.ds(0, rows)], up_ref, loads.at[2 * tiles + 2 * chunks + 1]
            )
        )
    load_rows(0).start()
    for k in range(tiles):
        for each in load_weight(k):
            each.start()
    for k in range(1, chunks):
        load_rows(k).start()
    for each in later + working[0]:
        each.start()
    greet(load.peers(place, [core_peer, far_peer]))
    for each in carried:
        if not each.late:
            each.start()

    def near_copy(k):
        part = pl.ds(k * chunk, chunk)
        return copy(given.at[part], near.at[part], send_near.at[k], got_near.at[k], core_peer)

    def far_copy(k):
        part = pl.ds(k * chunk, chunk)
        return copy(half.at[part], far.at[part], send_far.at[k], got_far.at[k], far_peer)

    def all_copy(k):
        return copy(
            all_ref.at[pl.ds(k * chunk, chunk)],
            all_ref.at[pl.ds(rows + k * chunk, chunk)],
            send_all.at[k],
            got_all.at[k],
            core_peer,
        )

    def tile_product(first, target, start, spot):
        target[pl.ds(start, block), spot] = lax.dot_general(
            a_ref[pl.ds(first, block), :],
            w_ref[spot, :],
            (((1,), (1,)), ((), ())),
            preferred_element_type=F32,
        ).astype(target.dtype)

    def product(first, target, start):
        @pl.loop(0, tiles)
        def _(step):
            spot = pl.ds(pl.multiple_of(step * tile, tile), tile)
            tile_product(first, target, start, spot)

    step_rows = 16
    for m in range(chunks // 2):
        load_rows(2 * m).wait()
        if m == 0:
            for k in range(tiles):
                for each in load_weight(k):
                    each.wait()
                tile_product(rows, given, 0, pl.ds(k * tile, tile))
        else:
            product(rows + m * block, given, m * block)
        for k in (2 * m, 2 * m + 1):
            near_copy(k).start()
        load_rows(2 * m + 1).wait()
        product(m * block, mine, m * block)
        for k in (2 * m, 2 * m + 1):
            near_copy(k).wait_recv()

            @pl.loop(0, chunk // step_rows)
            def _(step):
                part = pl.ds(pl.multiple_of(k * chunk + step * step_rows, step_rows), step_rows)
                half[part, :] = (mine[part, :] + near[part, :].astype(F32)).astype(BF)

            far_copy(k).start()
    for each in carried:
        if each.late:
            each.start()
    works.run(working, a_ref)
    for each in later:
        each.wait()
    if kind != "norm":
        sum_ref[...] = jnp.zeros_like(sum_ref)
    for k in range(chunks):
        far_copy(k).wait_recv()

        @pl.loop(0, chunk // step_rows)
        def _(step):
            part = pl.ds(pl.multiple_of(k * chunk + step * step_rows, step_rows), step_rows)
            total = half[part, :].astype(F32) + far[part, :].astype(F32)
            if kind == "norm":
                values = res_ref[part, :] + total
                res_out[part, :] = values
            else:
                values = res_ref[part, :]
            centered = values - jnp.mean(values, axis=-1, keepdims=True)
            inverse = lax.rsqrt(jnp.mean(centered * centered, axis=-1, keepdims=True) + EPS)
            scaled = centered * inverse
            if kind == "norm":
                all_ref[part, :] = (scaled * gain_ref[...] + bias_ref[...]).astype(BF)
            else:
                grad_scaled = total * gain_ref[...]
                first_mean = jnp.mean(grad_scaled, axis=-1, keepdims=True)
                second_mean = jnp.mean(grad_scaled * scaled, axis=-1, keepdims=True)
                grads = inverse * (grad_scaled - first_mean - scaled * second_mean)
                all_ref[part, :] = (up_ref[part, :].astype(F32) + grads).astype(BF)
                product_rows = total * scaled
                sum_ref[0] += product_rows[:8] + product_rows[8:]
                sum_ref[1] += total[:8] + total[8:]

        if k == chunks // 4:
            for each in carried:
                each.middle()
        if kind != "half":
            all_copy(k).start()
    for k in range(chunks):
        near_copy(k).wait_send()
        far_copy(k).wait_send()
        if kind != "half":
            all_copy(k).wait_send()
            all_copy(k).wait_recv()
    for each in carried:
        each.finish()
    for each in working[1]:
        each.wait()


def exchange(kind, place, a, w, residual, *others, load=Loads(), window=0, works=Works()):
    length, depth = a.shape
    w = w if isinstance(w, tuple) else (w,)
    width = w[0].shape[0]
    rows = length // 2
    chunks = 8 if depth < 2048 else 4
    whole = pl.BlockSpec(memory_space=pltpu.VMEM)
    if kind == "norm":
        gain, bias = others
        operands = (a, *w, residual, gain[None], bias[None])
        outs = [
            jax.ShapeDtypeStruct((rows, width), F32),
            jax.ShapeDtypeStruct((length, width), BF),
        ]
    else:
        up, gain = others
        operands = (a, *w, residual, up, gain[None])
        outs = [
            jax.ShapeDtypeStruct((rows if kind == "half" else length, width), BF),
            jax.ShapeDtypeStruct((2, 8, width), F32),
        ]
    plain = 2 if kind == "norm" else 1
    specs = [ANYWHERE] * (len(operands) - plain) + [whole] * plain
    specs += [ANYWHERE] * (len(load.operands) + len(works.unique))
    tiles = width // 256
    more = [
        pltpu.VMEM((length, depth), BF),
        pltpu.VMEM((width, depth), BF),
        pltpu.VMEM((rows, width), F32),
        pltpu.SemaphoreType.DMA((2 * tiles + 2 * chunks + 2,)),
    ]
    if kind != "norm":
        more.append(pltpu.VMEM((rows, width), BF))
    out_specs = [whole] * 2 + [ANYWHERE] * (len(load.outs_like) + len(works.outs_like))
    operands += tuple(load.operands) + tuple(works.unique)
    outs = outs + load.outs_like + works.outs_like
    return pl.pallas_call(
        functools.partial(exchange_kernel, kind, chunks, window, load, works),
        in_specs=specs,
        out_specs=out_specs,
        out_shape=outs,
        scratch_shapes=[
            pltpu.VMEM((rows, width), F32),
            pltpu.VMEM((rows, width), BF),
            pltpu.VMEM((rows, width), BF),
            pltpu.VMEM((rows, width), BF),
            pltpu.VMEM((rows, width), BF),
        ]
        + [pltpu.SemaphoreType.DMA((chunks,))] * 6
        + more
        + load.scratch
        + works.scratch,
        compiler_params=pltpu.CompilerParams(
            collective_id=place, has_side_effects=True, vmem_limit_bytes=63 * 2**20
        ),
        cost_estimate=pl.CostEstimate(
            flops=2 * length * depth * width,
            transcendentals=0,
            bytes_accessed=100_000_000,
        ),
        name="exchange_" + kind,
    )(*operands)


def spread_kernel(load, chunks, *refs):
    refs = list(refs)
    more = (len(load.operands), len(load.outs_like))
    (half_ref, pieces_ref), refs = refs[:2], refs[2:]
    load_ins, refs = refs[: more[0]], refs[more[0] :]
    (out_ref, token_ref, share_ref), refs = refs[:3], refs[3:]
    load_outs, refs = refs[: more[1]], refs[more[1] :]
    (sent, got, send_token, got_token, send_share, got_share), refs = refs[:6], refs[6:]
    place = Place()
    carried = load.begin(place, load_ins, load_outs, refs)
    d, core, pair = place.d, place.core, place.pair
    inner_z = lax.rem(place.z, 2)
    plane_peers = [(lax.rem(d + j, 8), place.z) for j in range(1, 8)]
    far_peers = [(lax.rem(d + j, 8), place.far_z) for j in range(8)]
    greet([place.near_z] + far_peers + plane_peers)
    rows = half_ref.shape[0]
    chunk = rows // chunks

    def spot(which, k):
        return out_ref.at[pl.ds(pl.multiple_of(which * rows + k * chunk, chunk), chunk)]

    def owner_copy(k, which):
        source = half_ref.at[pl.ds(k * chunk, chunk)]
        return send(source, spot(which, k), sent.at[0, k], got.at[0, k], place.core_peer)

    def pair_copy(k, which):
        source = half_ref.at[pl.ds(k * chunk, chunk)]
        return send(source, spot(which, k), sent.at[1, k], got.at[1, k], place.user)

    def pass_copy(k, which):
        return send(spot(which, k), spot(which, k), sent.at[2, k], got.at[2, k], place.near_z)

    def share_copy(far, j):
        return send(
            pieces_ref.at[pl.ds(pl.multiple_of(lax.rem(d + j, 8) * 8, 8), 8)],
            share_ref.at[pl.ds((8 * far + j) * 8, 8)],
            send_share.at[far, j],
            got_share.at[far, j],
            far_peers[j] if far else plane_peers[j - 1],
        )

    for j in range(8):
        share_copy(1, j).start()
        if j:
            share_copy(0, j).start()
    share_ref[pl.ds(0, 8), :] = pieces_ref[pl.ds(pl.multiple_of(d * 8, 8), 8), :]

    @pl.when(core == inner_z)
    def _():
        for k in range(chunks):
            pair_copy(k, core).start()

    @pl.when(core != pair)
    def _():
        for k in range(chunks):
            owner_copy(k, core).start()

    @pl.when(core == pair)
    def _():
        @pl.loop(0, rows // 16)
        def _(step):
            first = pl.multiple_of(step * 16, 16)
            out_ref[pl.ds(pl.multiple_of(core * rows + first, 16), 16), :] = half_ref[
                pl.ds(first, 16), :
            ]

        for k in range(chunks):
            owner_copy(k, 1 - core).wait_recv()

    def pass_on(k):
        pair_copy(k, inner_z).wait_recv()
        pass_copy(k, inner_z).start()

    @pl.when(core != pair)
    def _():
        for k in range(chunks // 2):
            pass_on(k)

    for each in carried:
        each.start()

    @pl.when(core != pair)
    def _():
        for k in range(chunks // 2, chunks):
            pass_on(k)
        for k in range(chunks):
            pass_copy(k, 1 - inner_z).wait_recv()

    head = 16
    token_ref[pl.ds(pl.multiple_of(d * head, head), head), :] = out_ref[pl.ds(0, head), :]

    def token_copy(j, sender):
        return send(
            out_ref.at[pl.ds(0, head)],
            token_ref.at[pl.ds(pl.multiple_of(sender * head, head), head)],
            send_token.at[j - 1],
            got_token.at[j - 1],
            plane_peers[j - 1],
        )

    for j in range(1, 8):
        token_copy(j, d).start()

    @pl.when(core != pair)
    def _():
        for k in range(chunks):
            pass_copy(k, inner_z).wait_send()
            owner_copy(k, core).wait_send()

    @pl.when(core == inner_z)
    def _():
        for k in range(chunks):
            pair_copy(k, core).wait_send()

    for j in range(1, 8):
        token_copy(j, d).wait_send()
        token_copy(j, lax.rem(d + 8 - j, 8)).wait_recv()
    for j in range(8):
        share_copy(1, j).wait()
        if j:
            share_copy(0, j).wait()
    for each in carried:
        each.finish()


def spread_gradient(place, half, pieces, load):
    rows, width = half.shape
    chunks = 8
    whole = pl.BlockSpec(memory_space=pltpu.VMEM)
    return pl.pallas_call(
        functools.partial(spread_kernel, load, chunks),
        in_specs=[whole] * 2 + [ANYWHERE] * len(load.operands),
        out_specs=[whole] * 3 + [ANYWHERE] * len(load.outs_like),
        out_shape=[
            jax.ShapeDtypeStruct((2 * rows, width), BF),
            jax.ShapeDtypeStruct((8 * 16, width), BF),
            jax.ShapeDtypeStruct((2 * pieces.shape[0], pieces.shape[1]), F32),
        ]
        + load.outs_like,
        scratch_shapes=[
            pltpu.SemaphoreType.DMA((3, chunks)),
            pltpu.SemaphoreType.DMA((3, chunks)),
            pltpu.SemaphoreType.DMA((7,)),
            pltpu.SemaphoreType.DMA((7,)),
            pltpu.SemaphoreType.DMA((2, 8)),
            pltpu.SemaphoreType.DMA((2, 8)),
        ]
        + load.scratch,
        compiler_params=pltpu.CompilerParams(
            collective_id=place, has_side_effects=True, vmem_limit_bytes=60 * 2**20
        ),
        cost_estimate=pl.CostEstimate(flops=0, transcendentals=0, bytes_accessed=100_000_000),
        name="spread_gradient",
    )(half, pieces, *load.operands)


def feed_kernel(
    n_ref, mine_ref, other_ref, gate_ref, up_ref, down_ref, hidden_ref, grad_ref, cot_out, here
):
    step_here = pl.program_id(0)
    length = n_ref.shape[0]
    tile = gate_ref.shape[1]
    half = grad_ref.shape[1] // 2
    block = 256
    gate_columns = pl.ds(pl.multiple_of(step_here * tile, tile), tile)
    up_columns = pl.ds(pl.multiple_of(half + step_here * tile, tile), tile)
    both = (mine_ref, other_ref)
    copies = [
        pltpu.make_async_copy(part, cot_out.at[pl.ds(k * (length // 2), length // 2)], here.at[k])
        for k, part in enumerate(both)
    ]

    @pl.when(step_here == 0)
    def _():
        for copy in copies:
            copy.start()

    for k, cot_ref in enumerate(both):

        @pl.loop(0, length // 2 // block)
        def _(step):
            source = pl.ds(pl.multiple_of(step * block, block), block)
            rows = pl.ds(pl.multiple_of(k * (length // 2) + step * block, block), block)
            gate = jnp.dot(n_ref[rows, :], gate_ref[...], preferred_element_type=F32)
            up = jnp.dot(n_ref[rows, :], up_ref[...], preferred_element_type=F32)
            grad = jnp.dot(cot_ref[source, :], down_ref[...], preferred_element_type=F32)
            sigmoid = jax.nn.sigmoid(gate)
            silu = gate * sigmoid
            hidden_ref[rows, :] = (silu * up).astype(BF)
            grad_ref[rows, gate_columns] = (
                grad * up * sigmoid * (1.0 + gate * (1.0 - sigmoid))
            ).astype(BF)
            grad_ref[rows, up_columns] = (grad * silu).astype(BF)

    @pl.when(step_here == pl.num_programs(0) - 1)
    def _():
        for copy in copies:
            copy.wait()


def feed_forward(normed, mine, other, gate_up, down):
    length, width = normed.shape
    hidden_width = down.shape[1]
    tile = 256
    steps = hidden_width // tile
    whole = pl.BlockSpec(memory_space=pltpu.VMEM)
    return pl.pallas_call(
        feed_kernel,
        grid=(steps,),
        in_specs=[
            whole,
            whole,
            whole,
            pl.BlockSpec((width, tile), lambda j: (0, j)),
            pl.BlockSpec((width, tile), lambda j: (0, j + steps)),
            pl.BlockSpec((width, tile), lambda j: (0, j)),
        ],
        out_specs=[
            pl.BlockSpec((length, tile), lambda j: (0, j)),
            pl.BlockSpec((length, 2 * hidden_width), lambda j: (0, 0)),
            ANYWHERE,
        ],
        out_shape=[
            jax.ShapeDtypeStruct((length, hidden_width), BF),
            jax.ShapeDtypeStruct((length, 2 * hidden_width), BF),
            jax.ShapeDtypeStruct((length, width), BF),
        ],
        scratch_shapes=[pltpu.SemaphoreType.DMA((2,))],
        compiler_params=pltpu.CompilerParams(vmem_limit_bytes=60 * 2**20),
        cost_estimate=pl.CostEstimate(
            flops=6 * length * width * hidden_width,
            transcendentals=length * hidden_width,
            bytes_accessed=30_000_000,
        ),
        name="feed_forward",
    )(normed, mine, other, gate_up, gate_up, down)


def turn_tables(length, block):
    rotated = HD // 2
    angles = np.exp(-np.log(10000.0) * np.arange(rotated // 2) * 2.0 / rotated)
    lanes = np.concatenate([angles, angles, np.zeros(HD - rotated)])
    lanes = np.concatenate([lanes, lanes])
    base = np.arange(block)[:, None] * lanes[None]
    steps = np.zeros((8, 128))
    steps[: length // block] = np.arange(0, length, block)[:, None] * lanes[None]
    pack = lambda table: np.stack([np.cos(table), np.sin(table)]).astype(np.float32)
    return jnp.asarray(pack(base)), jnp.asarray(pack(steps))


def turned_block(values, base_ref, steps_ref, here, sign):
    half = HD // 4
    first_cos, first_sin = steps_ref[0, pl.ds(here, 1), :], steps_ref[1, pl.ds(here, 1), :]
    cosine = first_cos * base_ref[0] - first_sin * base_ref[1]
    sine = first_sin * base_ref[0] + first_cos * base_ref[1]
    lane = lax.rem(lax.broadcasted_iota(jnp.int32, values.shape, 1), HD)
    lower = jnp.where(lane < half, sine, 0.0)
    upper = jnp.where((lane >= half) & (lane < 2 * half), sine, 0.0)
    ahead = pltpu.roll(values, 128 - half, 1)
    behind = pltpu.roll(values, half, 1)
    if sign > 0:
        return values * cosine - ahead * lower + behind * upper
    return values * cosine + ahead * lower - behind * upper


def opening_kernel(*refs):
    (qkv_part, side_part, feed_part, latents, prompt, time_part, feat, facts) = refs[:8]
    gain_ref, bias_ref, base_ref, steps_ref = refs[8:12]
    (n_ref, q_ref, k_ref, v_ref, o_ref, log_ref, res_ref, qkv_out) = refs[12:20]
    side_full, feed_own, prompt_too, facts_too, feat_out = refs[20:25]
    projected, item, time_full, qkv_full, feat_full = refs[25:30]
    sent_far, got_far, sent_near, got_near, here = refs[30:35]
    sent_plane, got_plane, sent_side, got_side = refs[35:39]
    sent_small, got_small, sent_swap, got_swap = refs[39:43]
    place = Place()
    d, core, column, owner = place.d, place.core, place.column, place.owner
    step_here = pl.program_id(0)
    plane_peers = [(lax.rem(d + j, 8), place.z) for j in range(1, 8)]
    rows = qkv_part.shape[0]
    piece = rows // 2
    length, width = item.shape
    total = qkv_full.shape[1]
    block = 256
    parts = range(4)

    def at(ref, index, count):
        return ref.at[pl.ds(pl.multiple_of(index * count, count), count)]

    def ends(k, sender):
        if k < 2:
            source = qkv_part.at[pl.ds(k * piece, piece)]
            spot = pl.multiple_of((2 * column + sender) * rows + k * piece, piece)
            return source, qkv_full.at[pl.ds(spot, piece)]
        if k == 2:
            return side_part, at(side_full, 2 * column + sender, rows)
        return feed_part, at(feed_own, sender, rows)

    def far(k, sender):
        source, target = ends(k, sender)
        return send(source, target, sent_far.at[k], got_far.at[sender, k], place.user)

    def near(k, sender):
        source, target = ends(k, sender)
        return send(source, target, sent_near.at[k], got_near.at[k], place.core_peer)

    def local(k):
        source, target = ends(k, core)
        return pltpu.make_async_copy(source, target, here.at[k])

    def await_part(k, sender):
        @pl.when(owner)
        def _():
            @pl.when(core == sender)
            def _():
                local(k).wait()

            @pl.when(core != sender)
            def _():
                near(k, sender).wait_recv()

        @pl.when(jnp.logical_not(owner))
        def _():
            far(k, sender).wait_recv()

    item_copy = send(latents, item, sent_swap.at[0], got_swap.at[0], place.core_peer)
    item_local = pltpu.make_async_copy(latents, item, here.at[4])
    outward = [
        pltpu.make_async_copy(qkv_full, qkv_out, here.at[7]),
        pltpu.make_async_copy(feat_full, feat_out, here.at[8]),
    ]
    swaps = [
        send(prompt, prompt_too, sent_swap.at[1], got_swap.at[1], place.core_peer),
        send(facts, facts_too, sent_swap.at[2], got_swap.at[2], place.core_peer),
    ]
    smalls = ((time_part, time_full), (feat, feat_full))

    def small(which, j, sender):
        part, whole = smalls[which]
        return send(
            part,
            at(whole, sender, part.shape[0]),
            sent_small.at[which, j - 1],
            got_small.at[which, j - 1],
            plane_peers[j - 1],
        )

    def small_local(which):
        part, whole = smalls[which]
        return pltpu.make_async_copy(part, at(whole, d, part.shape[0]), here.at[5 + which])

    def plane(stage, way, k, sender):
        peer = place.x_peer if way == 0 else place.y_peer
        source = column if stage == 0 else (place.y_column if way == 0 else place.x_column)
        spot = qkv_full.at[
            pl.ds(pl.multiple_of((2 * source + sender) * rows + k * piece, piece), piece)
        ]
        slot = 4 * stage + 2 * sender + k
        return send(spot, spot, sent_plane.at[way, slot], got_plane.at[way, slot], peer)

    def side(stage, way, sender):
        peer = place.x_peer if way == 0 else place.y_peer
        source = column if stage == 0 else (place.y_column if way == 0 else place.x_column)
        spot = at(side_full, 2 * source + sender, rows)
        slot = 2 * stage + sender
        return send(spot, spot, sent_side.at[way, slot], got_side.at[way, slot], peer)

    def side_one():
        for sender in range(2):
            await_part(2, sender)
            side(0, sender, sender).start()
        for sender in range(2):
            side(0, 1 - sender, sender).start()

    def side_two():
        side(0, 0, 0).wait_recv()
        side(1, 1, 0).start()
        side(0, 1, 1).wait_recv()
        side(1, 0, 1).start()

    @pl.when(step_here == 0)
    def _():
        greet([place.far_same, place.far_other] + plane_peers)
        for k in parts:
            far(k, core).start()

        @pl.when(owner)
        def _():
            item_copy.start()
            item_local.start()
            for k in parts:
                local(k).start()

        for which in range(2):
            small_local(which).start()
        for j in range(1, 8):
            for which in range(2):
                small(which, j, d).start()

        @pl.when(jnp.logical_not(owner))
        def _():
            for k in parts:
                near(k, core).start()

        for swap in swaps:
            swap.start()
        for which in range(2):
            small_local(which).wait()
        for j in range(1, 8):
            for which in range(2):
                small(which, j, lax.rem(d + 8 - j, 8)).wait_recv()

        @pl.when(owner)
        def _():
            item_local.wait()

        @pl.when(jnp.logical_not(owner))
        def _():
            item_copy.wait_recv()

        user = 2 * column + place.pair
        token_row = jnp.dot(
            feat_full[pl.ds(pl.multiple_of(user * 16, 16), 16), :],
            time_full[...],
            preferred_element_type=F32,
        )
        row_number = lax.broadcasted_iota(jnp.int32, (16, width), 0)

        def norm_rows(step, keep):
            local_row = pl.multiple_of(step * 16, 16)
            spot = pl.multiple_of(lax.rem(local_row + core * (length // 2), length), 16)
            values = item[pl.ds(spot, 16), :].astype(F32)
            values = jnp.where(row_number + spot == 0, token_row, values)
            if keep:
                res_ref[pl.ds(local_row, 16), :] = values
            centered = values - jnp.mean(values, axis=-1, keepdims=True)
            inverse = lax.rsqrt(jnp.mean(centered * centered, axis=-1, keepdims=True) + EPS)
            n_ref[pl.ds(local_row, 16), :] = (
                centered * inverse * gain_ref[...] + bias_ref[...]
            ).astype(BF)

        def forward(k):
            for sender in range(2):
                await_part(k, sender)
                plane(0, 0, k, sender).start()
                plane(0, 1, k, sender).start()

        steps = length // 16
        forward(0)

        @pl.loop(0, steps // 2)
        def _(step):
            norm_rows(step, True)

        forward(1)

        @pl.loop(steps // 2, steps)
        def _(step):
            norm_rows(step, False)

        for k in range(2):
            plane(0, 0, k, 0).wait_recv()
            plane(1, 1, k, 0).start()
            plane(0, 1, k, 1).wait_recv()
            plane(1, 0, k, 1).start()
            plane(0, 0, k, 1).wait_recv()
            plane(0, 1, k, 0).wait_recv()
        for k in range(2):
            plane(1, 1, k, 0).wait_recv()
            plane(1, 0, k, 1).wait_recv()

        side_one()

        for each in outward:
            each.start()
        third = total // 3
        for part in range(3):
            columns = pl.ds(part * third, third)

            @pl.loop(0, length // block)
            def _(step):
                spot = pl.ds(pl.multiple_of(step * block, block), block)
                projected[spot, columns] = jnp.dot(
                    n_ref[spot, :], qkv_full[:, columns], preferred_element_type=F32
                )

    @pl.when(step_here == 1)
    def _():
        side_two()

    def turn(first, target):
        columns = pl.ds(pl.multiple_of(first + step_here * 128, 128), 128)

        @pl.loop(0, length // block)
        def _(step):
            spot = pl.ds(pl.multiple_of(step * block, block), block)
            index = lax.rem(step + core * (length // block // 2), length // block)
            target[spot, :] = turned_block(
                projected[spot, columns], base_ref, steps_ref, index, 1
            ).astype(BF)

    turn(0, q_ref)
    turn(total // 3, k_ref)
    v_ref[...] = projected[
        :, pl.ds(pl.multiple_of(2 * (total // 3) + step_here * 128, 128), 128)
    ].astype(BF)
    attend_pair(HD, block, q_ref, k_ref, v_ref, None, o_ref, log_ref)

    @pl.when(step_here == pl.num_programs(0) - 1)
    def _():
        for sender in range(2):
            side(0, 1 - sender, sender).wait_recv()
        side(1, 1, 0).wait_recv()
        side(1, 0, 1).wait_recv()
        for sender in range(2):
            await_part(3, sender)
        for each in outward:
            each.wait()
        for swap in swaps:
            swap.wait()
        for j in range(1, 8):
            for which in range(2):
                small(which, j, d).wait_send()
        for k in parts:
            far(k, core).wait_send()

        @pl.when(owner)
        def _():
            item_copy.wait_send()

        @pl.when(jnp.logical_not(owner))
        def _():
            for k in parts:
                near(k, core).wait_send()

        for sender in range(2):
            for way in range(2):
                side(0, way, sender).wait_send()
                for k in range(2):
                    plane(0, way, k, sender).wait_send()
        side(1, 1, 0).wait_send()
        side(1, 0, 1).wait_send()
        for k in range(2):
            plane(1, 1, k, 0).wait_send()
            plane(1, 0, k, 1).wait_send()


def opening(place, qkv_part, side_part, feed_part, latents, prompt, time_part, feat, facts, gain, bias):
    length, width = latents.shape
    total = qkv_part.shape[1]
    rows = qkv_part.shape[0]
    pairs = total // 3 // 128
    base, steps = turn_tables(length, 256)
    block = pl.BlockSpec((length, 128), lambda i: (0, i))
    whole = pl.BlockSpec(memory_space=pltpu.VMEM)
    wide = jax.ShapeDtypeStruct((length, total // 3), BF)
    dma = pltpu.SemaphoreType.DMA
    return pl.pallas_call(
        opening_kernel,
        grid=(pairs,),
        in_specs=[ANYWHERE] * 8 + [whole] * 4,
        out_specs=[whole]
        + [block] * 4
        + [pl.BlockSpec((1, 2, length), lambda i: (i, 0, 0)), whole]
        + [ANYWHERE] * 6,
        out_shape=[jax.ShapeDtypeStruct((length, width), BF)]
        + [wide] * 4
        + [
            jax.ShapeDtypeStruct((pairs, 2, length), F32),
            jax.ShapeDtypeStruct((length // 2, width), F32),
            jax.ShapeDtypeStruct((8 * rows, total), BF),
            jax.ShapeDtypeStruct((8 * rows, side_part.shape[1]), BF),
            jax.ShapeDtypeStruct((2 * rows, feed_part.shape[1]), BF),
            jax.ShapeDtypeStruct(prompt.shape, BF),
            jax.ShapeDtypeStruct(facts.shape, facts.dtype),
            jax.ShapeDtypeStruct((8 * feat.shape[0], feat.shape[1]), BF),
        ],
        scratch_shapes=[
            pltpu.VMEM((length, total), F32),
            pltpu.VMEM((length, width), BF),
            pltpu.VMEM((8 * time_part.shape[0], width), BF),
            pltpu.VMEM((8 * rows, total), BF),
            pltpu.VMEM((8 * feat.shape[0], feat.shape[1]), BF),
            dma((4,)),
            dma((2, 4)),
            dma((4,)),
            dma((4,)),
            dma((9,)),
            dma((2, 8)),
            dma((2, 8)),
            dma((2, 4)),
            dma((2, 4)),
            dma((2, 7)),
            dma((2, 7)),
            dma((3,)),
            dma((3,)),
        ],
        compiler_params=pltpu.CompilerParams(
            collective_id=place, has_side_effects=True, vmem_limit_bytes=60 * 2**20
        ),
        cost_estimate=pl.CostEstimate(
            flops=4 * length * length * total // 3 + 2 * length * width * total,
            transcendentals=length * length * total // 192,
            bytes_accessed=200_000_000,
        ),
        name="opening",
    )(
        qkv_part,
        side_part,
        feed_part,
        latents,
        prompt,
        time_part,
        feat,
        facts,
        gain[None],
        bias[None],
        base,
        steps,
    )


def per_device_paired(
    latents,
    prompt_tokens,
    prompt_lengths,
    timesteps,
    time_weight,
    self_gain,
    self_bias,
    qkv_weight,
    self_out_weight,
    cross_gain,
    cross_bias,
    cross_query_weight,
    context_weight,
    cross_out_weight,
    feed_gain,
    feed_bias,
    gate_up_weight,
    down_weight,
    down_bias,
    cotangent,
):
    d = lax.axis_index("dp")
    z = lax.axis_index("mp")
    core, pair = d & 1, z >> 1
    owner = core == pair
    length = latents.shape[1] + 1
    rows = length // 4
    half_rows = length // 2
    part_rows = qkv_weight.shape[0]
    n = cross_query_weight.shape[1]

    side_part = jnp.concatenate(
        [
            self_out_weight.T,
            cross_query_weight,
            cross_out_weight.T,
            context_weight.reshape(part_rows, -1),
        ],
        axis=1,
    )
    feature_width = 8 * time_weight.shape[0]
    features = time_features(timesteps, feature_width).astype(BF)
    (
        normed_one,
        queries,
        keys,
        values,
        attended,
        self_logs,
        residual_mine,
        qkv_full,
        side_full,
        gate_up_own,
        prompt_too,
        facts_too,
        features_full,
    ) = opening(
        5,
        qkv_weight.reshape(part_rows, -1),
        side_part,
        gate_up_weight.reshape(part_rows, -1),
        jnp.pad(latents[0], ((1, 0), (0, 0))),
        prompt_tokens[0],
        time_weight,
        jnp.broadcast_to(features, (16, feature_width)),
        jnp.broadcast_to(prompt_lengths[:, None], (8, 128)),
        self_gain,
        self_bias,
    )
    gate_up_full = plane_gather(gate_up_own)
    self_out_full = side_full[:, :n]
    cross_query_full = side_full[:, n : 2 * n]
    cross_out_full = side_full[:, 2 * n : 3 * n]
    context_full = side_full[:, 3 * n :].reshape(context_weight.shape[0] * 8, -1)

    item_prompt = jnp.where(owner, prompt_tokens[0], prompt_too)
    item_length = jnp.where(owner, prompt_lengths[0], facts_too[0, 0])

    residual_one, normed_two_all, down_own, cot_too = exchange(
        "norm",
        0,
        attended,
        side_full,
        residual_mine,
        cross_gain,
        cross_bias,
        load=Loads((Spread, down_weight.T), (SwapRoute, cotangent[0])),
    )
    cot_shard = jnp.where(owner, cotangent[0], cot_too)
    cot_far = move(cot_shard, SWAP_Z)
    odd = (z & 1) == 1
    cross_q = dot_nn(normed_two_all, cross_query_full).astype(BF)
    context = dot_nn(item_prompt, context_full).astype(BF)
    slots = prompt_tokens.shape[1]
    mask = jnp.where(jnp.arange(slots, dtype=jnp.int32)[:, None] < item_length, 0.0, NEG)
    mask = mask.astype(F32)
    crossed, cross_logs = cross_attention(cross_q, context, mask)
    cot_far = after(cot_far, crossed)
    cot_mine = jnp.concatenate(
        [jnp.where(odd, cot_far, cot_shard), jnp.where(odd, cot_shard, cot_far)], axis=0
    )
    cot_other = move(cot_mine, SWAP_CORE)
    residual_two, normed_three_all, down_full = exchange(
        "norm",
        1,
        crossed,
        side_full,
        residual_one,
        feed_gain,
        feed_bias,
        load=Loads((Plane, down_own)),
        window=2,
    )
    hidden, grad_gate_up, cot_all = feed_forward(
        normed_three_all,
        cot_mine,
        after(cot_other, normed_three_all),
        gate_up_full,
        down_full,
    )

    split = gate_up_weight.shape[2]
    gate_local = dot_tn(normed_three_all, grad_gate_up[:, :split]).astype(BF)
    gate_sums = plane_sum(gate_local)
    grad_two_all, feed_sums, feed, down_local, up_local = exchange(
        "back",
        2,
        after(grad_gate_up, gate_local),
        gate_up_full,
        residual_two,
        cot_mine,
        feed_gain,
        works=Works(
            ("nt", hidden, down_full),
            ("tn", cot_all, hidden),
            ("ta", normed_three_all, (split, split)),
        ),
    )
    up_sums = plane_sum(up_local)
    down_sums = plane_sum(after(down_local, up_local))
    grad_crossed = dot_nn(grad_two_all, cross_out_full).astype(BF)
    grad_cross_q, grad_context = cross_attention_back(
        cross_q, context, mask, grad_crossed, cross_logs
    )
    (
        grad_one_all,
        cross_sums,
        gate_near,
        gate_far,
        feed_near,
        cross_query_grad,
        cross_out_grad,
        context_grad,
    ) = exchange(
        "back",
        3,
        grad_cross_q,
        side_full,
        residual_one,
        grad_two_all,
        cross_gain,
        load=Loads((Return, gate_sums), (SwapCoreHalf, feed)),
        window=1,
        works=Works(
            ("tn", normed_two_all, grad_cross_q),
            ("tn", grad_two_all, crossed),
            ("tn", item_prompt, grad_context),
        ),
    )
    feed_half = feed[:half_rows].astype(F32) + feed_near.astype(F32)
    feed_here = jnp.where(odd, feed_half[rows:], feed_half[:rows])
    feed_away = jnp.where(odd, feed_half[:rows], feed_half[rows:]).astype(BF)
    grad_attended = dot_nn(grad_one_all, self_out_full).astype(BF)
    grad_projected, up_near, up_far, feed_far = self_attention_back(
        7,
        queries,
        keys,
        values,
        grad_attended,
        self_logs,
        Loads((Return, up_sums), (SwapNear, feed_away)),
    )
    residual_here = jnp.where(odd, residual_two[rows:], residual_two[:rows])
    output_here = (residual_here + feed_here + feed_far.astype(F32) + down_bias).astype(BF)
    self_out_local = dot_tn(grad_one_all, attended).astype(BF)
    qkv_local = dot_tn(normed_one, grad_projected).astype(BF)
    qkv_total = plane_sum(qkv_local)
    (
        grad_in,
        self_sums,
        down_near,
        down_far,
        output_far,
        cross_query_total,
        cross_out_total,
        context_total,
        self_out_total,
    ) = exchange(
        "half",
        4,
        after(grad_projected, qkv_local),
        qkv_full,
        residual_mine,
        grad_one_all,
        self_gain,
        load=Loads(
            (Return, down_sums),
            (SwapRoute, output_here),
            (PlaneSum, cross_query_grad),
            (PlaneSum, cross_out_grad),
            (PlaneSum, context_grad),
            (PlaneSum, self_out_local),
        ),
    )
    sums = jnp.concatenate(
        [
            jnp.sum(self_sums, axis=1),
            jnp.sum(cross_sums, axis=1),
            jnp.sum(feed_sums, axis=1),
            jnp.sum(cot_mine.astype(F32), axis=0)[None],
            jnp.zeros((1, grad_in.shape[1]), F32),
        ],
        axis=0,
    )
    share = sums.shape[1] // 8
    pieces = jnp.swapaxes(sums.reshape(8, 8, share), 0, 1)
    pieces = jnp.pad(pieces, ((0, 0), (0, 0), (0, 256 - share))).reshape(64, 256)
    totals = (cross_query_total, cross_out_total, context_total, self_out_total, qkv_total)
    whole, token_rows, sums, *ends = spread_gradient(
        8, grad_in, pieces, Loads(*[(Return, total) for total in totals])
    )
    cross_query_grad, cross_out_grad, context_grad, self_out_grad, qkv_grad = [
        returned(total, ends[2 * k], ends[2 * k + 1], core, owner)
        for k, total in enumerate(totals)
    ]
    sums = jnp.sum(sums.reshape(16, 8, 256), axis=0)[:, :share]
    output = jnp.where(owner, output_here, output_far)
    latents_grad = whole[1:]

    token_rows = token_rows.reshape(8, 16, -1)[:, 0]
    all_features = features_full.reshape(8, 16, -1)[:, 0]
    my_features = jnp.zeros((8, feature_width // 8), F32)
    for j in range(8):
        piece = all_features[:, j * (feature_width // 8) : (j + 1) * (feature_width // 8)]
        my_features = my_features + jnp.where(d == j, piece.astype(F32), 0.0)
    time_grad = lax.dot_general(
        my_features.astype(BF), token_rows, (((0,), (0,)), ((), ())), preferred_element_type=F32
    )

    gate_grad = returned(gate_sums, gate_near, gate_far, core, owner)
    up_grad = returned(up_sums, up_near, up_far, core, owner)
    down_grad = returned(down_sums, down_near, down_far, core, owner)
    return (
        output[None],
        latents_grad[None],
        time_grad,
        sums[0],
        sums[1],
        qkv_grad.reshape(qkv_weight.shape),
        self_out_grad.T,
        sums[2],
        sums[3],
        cross_query_grad,
        context_grad.reshape(context_weight.shape),
        cross_out_grad.T,
        sums[4],
        sums[5],
        jnp.stack([gate_grad, up_grad], axis=1),
        down_grad.T,
        sums[6],
    )


def solution(mesh):
    placed = (
        P("dp", None, None),
        P("dp", None, None),
        P("dp"),
        P("dp"),
        P("dp", None),
        P(),
        P(),
        P("dp", None, "mp"),
        P("mp", "dp"),
        P(),
        P(),
        P("dp", "mp"),
        P("dp", None, "mp"),
        P("mp", "dp"),
        P(),
        P(),
        P("dp", None, "mp"),
        P("mp", "dp"),
        P(),
        P("dp", "mp", None),
    )
    paired = mesh.shape["dp"] == 8 and mesh.shape["mp"] == 4
    return jax.shard_map(
        per_device_paired if paired else per_device_general,
        mesh=mesh,
        in_specs=placed,
        out_specs=(
            P("dp", "mp", None),
            P("dp", None, None),
            P("dp", None),
            P("dp"),
            P("dp"),
            P("dp", None, "mp"),
            P("mp", "dp"),
            P("dp"),
            P("dp"),
            P("dp", "mp"),
            P("dp", None, "mp"),
            P("mp", "dp"),
            P("dp"),
            P("dp"),
            P("dp", None, "mp"),
            P("mp", "dp"),
            P("dp"),
        ),
        check_vma=False,
    )
```
